32 devices in a mesh: exp: 4 (over y, core), fsdp: 8 (over z, x).
Axes of the slice: x: 2, y: 2, z: 4, core: 2. Of those that a mesh axis runs over, the one named last changes fastest.
Arguments:
- tokens: bfloat16 [8, 2048, 768], P('fsdp', 'exp'), may hold values from -6 to 6
- gate_res: float32 [8, 2048, 8], P('fsdp', 'exp'), may hold values from -3 to 3
- routes: int32 [8, 2048, 2], P('fsdp', 'exp'), may hold values from 0 to 7, all different within a row; in each aligned block of 512 rows (0 to 511, 512 to 1023, ..., all dimensions but the last counted through in order) at most 160 rows name the same one
- piece_starts: int32 [8, 4], P('fsdp'), may hold values from 0 to 1792, as said below
- norm_attn: float32 [768], replicated, may hold values from 0.5 to 1.5
- norm_ffn: float32 [768], replicated, may hold values from 0.5 to 1.5
- w_query: bfloat16 [768, 768], P('fsdp'), may hold values from -0.21875 to 0.21875
- w_key: bfloat16 [768, 768], P('fsdp'), may hold values from -0.21875 to 0.21875
- w_value: bfloat16 [768, 768], P('fsdp'), may hold values from -0.21875 to 0.21875
- w_out: bfloat16 [768, 768], P('fsdp'), may hold values from -1.25 to 1.25
- router: float32 [768, 8], replicated, may hold values from -0.15625 to 0.15625
- mixing: float32 [8, 8], replicated, may hold values from -2 to 2
- const_proj: float32 [768, 4], replicated, may hold values from -0.21875 to 0.21875
- const_vec: float32 [2, 768], replicated, may hold values from -6 to 6
- w_gate: bfloat16 [4, 768, 2048], P('exp', 'fsdp'), may hold values from -0.21875 to 0.21875
- w_up: bfloat16 [4, 768, 2048], P('exp', 'fsdp'), may hold values from -0.21875 to 0.21875
- w_down: bfloat16 [4, 2048, 768], P('exp', 'fsdp'), may hold values from -0.1875 to 0.1875
- cotangent: bfloat16 [8, 2048, 768], P('fsdp', 'exp'), may hold values from -6 to 6
Outputs:
- layer_out: bfloat16 [8, 2048, 768], P('fsdp', 'exp')
- grad_tokens: bfloat16 [8, 2048, 768], P('fsdp', 'exp')
- grad_gate_res: float32 [8, 2048, 8], P('fsdp', 'exp')
- grad_norm_attn: float32 [768], replicated
- grad_norm_ffn: float32 [768], replicated
- grad_query: float32 [768, 768], P('fsdp')
- grad_key: float32 [768, 768], P('fsdp')
- grad_value: float32 [768, 768], P('fsdp')
- grad_out: float32 [768, 768], P('fsdp')
- grad_router: float32 [768, 8], replicated
- grad_mixing: float32 [8, 8], replicated
- grad_const_proj: float32 [768, 4], replicated
- grad_const_vec: float32 [2, 768], replicated
- grad_gate: float32 [4, 768, 2048], P('exp', 'fsdp')
- grad_up: float32 [4, 768, 2048], P('exp', 'fsdp')
- grad_down: float32 [4, 2048, 768], P('exp', 'fsdp')
The draws below stay inside these ranges and needn't reach their ends.
Inputs may be any that keep to these rules, and one draw needn't show every extreme that they name: `routes`: each row names two different experts. Numbers below 4 are the feed-forward experts (expert e is owned by index e of exp), 4 is the zero expert, 5 the copy expert, 6 and 7 the constant experts. Within the 512 positions of one device no number is named by more than 160 rows, a bound that some block reaches. `piece_starts`: each sequence has 4 image pieces of 256 positions; piece j starts between j * 512 and (j + 1) * 512 - 256, so pieces never intersect.
All inputs are finite; a program needn't handle non-finite values.
Results may differ from the reference program's by a relative error of at most 0.02.
Values may be sent and summed in bfloat16 or wider, within the bound.
A program may use at most 192 MiB of HBM per device.

```python
import math
import jax
import jax.numpy as jnp
import numpy as np
from jax import lax

D = 768
H = 12
HD = 64
FF = 2048
TOK_DEV = 512
PIECE = 256
PIECES = 4
KBLK = 512
LENGTH = 2048
SEQS = 8
EXPERTS = 4
NE = 8
CAP = 160
SLOT = 512


def draw_piece_starts(key, part):
    offsets = jax.random.randint(key, (SEQS, PIECES), 0, SLOT - PIECE + 1)
    row_index = jnp.arange(SEQS, dtype=jnp.int32)[:, None]
    col_index = jnp.arange(PIECES, dtype=jnp.int32)[None, :]
    offsets = jnp.where((row_index == 0) & (col_index == 0), 0, offsets)
    offsets = jnp.where((row_index == 0) & (col_index == PIECES - 1), SLOT - PIECE, offsets)
    return (col_index * SLOT + offsets).astype(jnp.int32)


def level_of(key, shape, cuts, smallest, high):
    factor_of, own = 1.0, jax.random.fold_in(key, 6)
    for position, blocks in cuts:
        steps = jnp.exp(jax.random.uniform(jax.random.fold_in(own, position), (blocks,), jnp.float32, smallest / len(cuts), high / len(cuts)))
        factor_of = factor_of * jnp.repeat(steps, shape[position] // blocks).reshape([-1 if axis == position else 1 for axis in range(len(shape))])
    return factor_of


def shared_out(key, own, number, rows, amount, top, reach, slope):
    ranking = jax.random.permutation(key, amount)
    packed, ordinary = load_shares(amount, rows * top, reach, slope, True), load_shares(amount, rows * top, reach, slope, False)
    places = jnp.arange(amount)

    def named(tallies, turn):
        used = int((tallies > 0).sum())
        fixed = max(1, used // 4)
        passed = fixed + (places - fixed + turn * (used - fixed)) % max(1, amount - fixed)
        return jnp.zeros((amount,), jnp.int32).at[ranking[jnp.where(places < fixed, places, passed)]].set(jnp.asarray(tallies, jnp.int32))

    tallies = jnp.where(number % 4 == 0, named(packed, number // 4), named(ordinary, number - number // 4 - 1))
    mixed = jax.random.permutation(jax.random.fold_in(own, 3), amount)
    giver, taker = mixed[0:amount // 2 * 2:2], mixed[1:amount // 2 * 2:2]
    margin = jnp.minimum(tallies[giver] - 1, reach - tallies[taker]) // 2
    margin = jnp.where((giver == ranking[0]) | (taker == ranking[0]) | (tallies[taker] == 0), 0, jnp.maximum(margin, 0))
    passed = jax.random.randint(jax.random.fold_in(own, 4), (amount // 2,), 0, 1 << 20) % (margin + 1)
    tallies = tallies.at[giver].add(-passed).at[taker].add(passed)
    members = jnp.searchsorted(jnp.cumsum(tallies), jnp.arange(rows * top), side="right").astype(jnp.int32)
    grid = members.reshape(top, rows).T
    grid = grid[jax.random.permutation(jax.random.fold_in(own, 1), rows)]
    turn = jax.random.randint(jax.random.fold_in(own, 2), (rows, 1), 0, top)
    return jnp.take_along_axis(grid, (jnp.arange(top)[None, :] + turn) % top, axis=1)


def load_shares(amount, total, bound, slope, full):
    weights = [(1 << 20) // math.isqrt(grade ** slope) + 1 for grade in range(1, amount + 1)]
    largest = bound if full else min(bound, max(-(-total // amount), total * weights[0] // sum(weights)))
    least = 1 if total - largest >= amount - 1 else 0
    counts, rest = [largest] + [least] * (amount - 1), total - largest - least * (amount - 1)
    while rest > 0:
        free = [i for i in range(1, amount) if counts[i] < largest] or [i for i in range(1, amount) if counts[i] < bound]
        pool, budget = sum([weights[i] for i in free]), rest
        for i in free:
            extra = min(bound - counts[i], max(1, budget * weights[i] // pool), rest)
            counts[i] = counts[i] + extra
            rest = rest - extra
    return np.array(counts)


def noise(own_key, shape, spread, most, cuts=(), kind=jnp.bfloat16):
    level = level_of(own_key, shape, cuts, -0.22, 0.18) if cuts else 1.0
    values = jax.random.normal(own_key, shape, jnp.float32) * spread * level
    return jnp.minimum(jnp.maximum(values, -most), most).astype(kind)


def setup_inputs(seed: int = 0) -> dict:
    arg_keys = jax.random.split(jax.random.key(seed), 19)
    tokens = noise(arg_keys[0], (SEQS, LENGTH, D), 1.0, 6.0, ((0, 8), (1, 4)))
    gate_res = noise(arg_keys[1], (SEQS, LENGTH, NE), 0.5, 3.0, ((0, 8), (1, 4)), jnp.float32)
    routes_keys = jax.random.split(jax.random.fold_in(arg_keys[2], 1), SEQS * LENGTH // TOK_DEV)
    routes_turns = jax.random.permutation(jax.random.fold_in(arg_keys[2], 3), SEQS * LENGTH // TOK_DEV)
    routes = jax.vmap(lambda own, number: shared_out(jax.random.fold_in(arg_keys[2], 2), own, number, TOK_DEV, NE, 2, CAP, 1))(routes_keys, routes_turns).reshape((SEQS, LENGTH, 2))
    piece_starts = draw_piece_starts(jax.random.fold_in(arg_keys[18], 71), 0)
    norm_attn = jnp.clip(1.0 + 0.1 * jax.random.normal(arg_keys[4], (D,), jnp.float32), 0.5, 1.5)
    norm_ffn = jnp.clip(1.0 + 0.1 * jax.random.normal(arg_keys[5], (D,), jnp.float32), 0.5, 1.5)
    w_query = noise(arg_keys[6], (D, D), D ** -0.5, 0.21875, ((0, 8),))
    w_key = noise(arg_keys[7], (D, D), D ** -0.5, 0.21875, ((0, 8),))
    w_value = noise(arg_keys[8], (D, D), D ** -0.5, 0.21875, ((0, 8),))
    w_out = noise(arg_keys[9], (D, D), (D // 32) ** -0.5, 1.25, ((0, 8),))
    router = noise(arg_keys[10], (D, NE), (2 * D) ** -0.5, 0.15625, (), jnp.float32)
    mixing = noise(arg_keys[11], (NE, NE), NE ** -0.5, 2.0, (), jnp.float32)
    const_proj = noise(arg_keys[12], (D, 4), D ** -0.5, 0.21875, (), jnp.float32)
    const_vec = noise(arg_keys[13], (2, D), 1.0, 6.0, (), jnp.float32)
    w_gate = noise(arg_keys[14], (EXPERTS, D, FF), D ** -0.5, 0.21875, ((0, 4), (1, 8)))
    w_up = noise(arg_keys[15], (EXPERTS, D, FF), D ** -0.5, 0.21875, ((0, 4), (1, 8)))
    w_down = noise(arg_keys[16], (EXPERTS, FF, D), (FF // 2) ** -0.5, 0.1875, ((0, 4), (1, 8)))
    cotangent = noise(arg_keys[17], (SEQS, LENGTH, D), 1.0, 6.0, ((0, 8), (1, 4)))
    return dict(tokens=tokens, gate_res=gate_res, routes=routes, piece_starts=piece_starts, norm_attn=norm_attn, norm_ffn=norm_ffn, w_query=w_query, w_key=w_key, w_value=w_value, w_out=w_out, router=router, mixing=mixing, const_proj=const_proj, const_vec=const_vec, w_gate=w_gate, w_up=w_up, w_down=w_down, cotangent=cotangent)


EPS = 1e-05
HIGH = lax.Precision.HIGHEST
NEG = -1e+30

@jax.custom_vjp
def low(v):
    return lax.optimization_barrier(v.astype(jnp.bfloat16)).astype(jnp.float32)

@jax.custom_vjp
def low_back(v):
    return v

def low_keep(v):
    return (low(v), None)

def low_pass(kept, grad):
    return (grad,)

def back_keep(v):
    return (v, None)

def back_low(kept, grad):
    return (low(grad),)
low.defvjp(low_keep, low_pass)
low_back.defvjp(back_keep, back_low)

def rms_scale(values, gain_vec):
    inverse = lax.rsqrt(lax.optimization_barrier(jnp.mean(values * values, axis=-1, keepdims=True)) + EPS)
    return values * inverse * gain_vec

def piece_ids(positions, starts, extent):
    inside = (positions[:, None] >= starts[None, :]) & (positions[:, None] < starts[None, :] + extent)
    labels = jnp.arange(1, starts.shape[0] + 1, dtype=jnp.int32)
    return lax.optimization_barrier(jnp.sum(jnp.where(inside, labels[None, :], 0), axis=1)).astype(jnp.int32)

def allowed_mask(query_pos, query_ids, key_pos, key_ids):
    causal = key_pos[None, :] <= query_pos[:, None]
    shared = (key_ids[None, :] == query_ids[:, None]) & (query_ids[:, None] > 0)
    return causal | shared

def slot_dest(route_ids, n_ffn, capacity):
    flat_ids = route_ids.reshape(-1).astype(jnp.int32)
    onehot = (flat_ids[:, None] == jnp.arange(n_ffn, dtype=jnp.int32)[None, :]).astype(jnp.int32)
    earlier = jnp.cumsum(onehot, axis=0) - onehot
    slot_pos = lax.optimization_barrier(jnp.sum(earlier * onehot, axis=1))
    return jnp.where(flat_ids < n_ffn, flat_ids * capacity + slot_pos, n_ffn * capacity).astype(jnp.int32)

def local_mix(normed, res_logits, router, mixing, const_proj, const_vec, expert_rows, route_ids, n_ffn):
    n_all = router.shape[1]
    logits = jnp.dot(normed, router, precision=HIGH) + jnp.dot(res_logits, mixing, precision=HIGH)
    probs = jax.nn.softmax(logits, axis=-1)
    labels = jnp.arange(n_all, dtype=jnp.int32)
    chosen = lax.optimization_barrier(jnp.sum(jnp.where(route_ids[:, :, None] == labels[None, None, :], probs[:, None, :], 0.0), axis=-1))
    gates = chosen / lax.optimization_barrier(jnp.sum(chosen, axis=1, keepdims=True))
    pair_logits = jnp.dot(normed, const_proj, precision=HIGH)
    first_pair = jax.nn.softmax(pair_logits[:, 0:2], axis=-1)
    second_pair = jax.nn.softmax(pair_logits[:, 2:4], axis=-1)
    first_const = first_pair[:, 0:1] * normed + first_pair[:, 1:2] * const_vec[0][None, :]
    second_const = second_pair[:, 0:1] * normed + second_pair[:, 1:2] * const_vec[1][None, :]
    mixed = jnp.zeros_like(normed)
    for route_k in range(2):
        route_id = route_ids[:, route_k:route_k + 1]
        entry = jnp.where(route_id < n_ffn, expert_rows[:, route_k], 0.0)
        entry = entry + jnp.where(route_id == n_ffn + 1, normed, 0.0)
        entry = entry + jnp.where(route_id == n_ffn + 2, first_const, 0.0)
        entry = entry + jnp.where(route_id == n_ffn + 3, second_const, 0.0)
        mixed = mixed + gates[:, route_k:route_k + 1] * entry
    return mixed

def expert_ffn(operands):
    slot_rows, gate_mat, up_mat, down_mat = operands
    gate_pre = low_back(jnp.dot(slot_rows, gate_mat, precision=HIGH))
    up_pre = low_back(jnp.dot(slot_rows, up_mat, precision=HIGH))
    inner_act = low(jax.nn.silu(gate_pre) * up_pre)
    return low_back(low(jnp.dot(inner_act, down_mat, precision=HIGH)))

def attend_sequence(operands):
    query, key_all, value_all, starts = operands
    score_scale = 1.0 / math.sqrt(HD)
    key_pos = jnp.arange(LENGTH, dtype=jnp.int32)
    key_ids = piece_ids(key_pos, starts, PIECE)

    def one_block(block_ops):
        query_block, first_row = block_ops
        query_pos = (first_row + jnp.arange(KBLK, dtype=jnp.int32)).astype(jnp.int32)
        query_ids = piece_ids(query_pos, starts, PIECE)
        scores = jnp.einsum('qhd,khd->hqk', query_block, key_all, precision=HIGH) * score_scale
        scores = low_back(scores)
        allowed = allowed_mask(query_pos, query_ids, key_pos, key_ids)[None]
        scores = jnp.where(allowed, scores, NEG)
        attn_probs = low(jax.nn.softmax(scores, axis=-1))
        return jnp.einsum('hqk,khd->qhd', attn_probs, value_all, precision=HIGH)
    n_blocks = LENGTH // KBLK
    query_blocks = query.reshape(n_blocks, KBLK, H, HD)
    first_rows = (jnp.arange(n_blocks, dtype=jnp.int32) * KBLK).astype(jnp.int32)
    outputs = lax.map(jax.checkpoint(one_block), (query_blocks, first_rows))
    return outputs.reshape(LENGTH, H, HD)

def forward(tokens, gate_res, norm_attn, norm_ffn, w_query, w_key, w_value, w_out, router, mixing, const_proj, const_vec, w_gate, w_up, w_down, routes, piece_starts):
    n_tok = SEQS * LENGTH
    inputs_f = tokens.reshape(n_tok, D)
    attn_in = low(rms_scale(inputs_f, norm_attn))
    query = low_back(low(jnp.dot(attn_in, w_query, precision=HIGH)))
    key = low_back(low(jnp.dot(attn_in, w_key, precision=HIGH)))
    value = low_back(low(jnp.dot(attn_in, w_value, precision=HIGH)))
    heads_shape = (SEQS, LENGTH, H, HD)
    attn_seq = lax.map(attend_sequence, (query.reshape(heads_shape), key.reshape(heads_shape), value.reshape(heads_shape), piece_starts))
    attn_flat = low_back(low(attn_seq.reshape(n_tok, D)))
    hidden = inputs_f + low_back(jnp.dot(attn_flat, w_out, precision=HIGH))
    normed = rms_scale(hidden, norm_ffn)
    n_blocks = n_tok // TOK_DEV
    route_blocks = routes.reshape(n_blocks, TOK_DEV, 2)
    dests = jax.vmap(lambda part_routes: slot_dest(part_routes, EXPERTS, CAP))(route_blocks)
    sources = (jnp.arange(2 * TOK_DEV, dtype=jnp.int32) // 2).astype(jnp.int32)
    tables = jax.vmap(lambda dest_row: jnp.full((EXPERTS * CAP,), TOK_DEV, jnp.int32).at[dest_row].set(sources, mode='drop'))(dests)
    low_rows = low(normed).reshape(n_blocks, TOK_DEV, D)
    padded = jnp.concatenate([low_rows, jnp.zeros((n_blocks, 1, D), low_rows.dtype)], axis=1)
    slot_rows = jax.vmap(lambda block_rows, table_row: block_rows[table_row])(padded, tables)
    slot_rows = slot_rows.reshape(n_blocks, EXPERTS, CAP, D).transpose(1, 0, 2, 3).reshape(EXPERTS, n_blocks * CAP, D)
    slot_rows = low_back(slot_rows)
    expert_out = lax.map(jax.checkpoint(expert_ffn), (slot_rows, w_gate, w_up, w_down))
    expert_out = expert_out.reshape(EXPERTS, n_blocks, CAP, D).transpose(1, 0, 2, 3).reshape(n_blocks, EXPERTS * CAP, D)
    out_pad = jnp.concatenate([expert_out, jnp.zeros((n_blocks, 1, D), expert_out.dtype)], axis=1)
    expert_rows = jax.vmap(lambda block_out, dest_row: block_out[dest_row])(out_pad, dests).reshape(n_tok, 2, D)
    mixed = local_mix(normed, gate_res.reshape(n_tok, NE), router, mixing, const_proj, const_vec, expert_rows, routes.reshape(n_tok, 2), EXPERTS)
    return (hidden + mixed).reshape(SEQS, LENGTH, D)

def reference(tokens, gate_res, routes, piece_starts, norm_attn, norm_ffn, w_query, w_key, w_value, w_out, router, mixing, const_proj, const_vec, w_gate, w_up, w_down, cotangent):
    floats = (tokens.astype(jnp.float32), gate_res, norm_attn, norm_ffn, w_query.astype(jnp.float32), w_key.astype(jnp.float32), w_value.astype(jnp.float32), w_out.astype(jnp.float32), router, mixing, const_proj, const_vec, w_gate.astype(jnp.float32), w_up.astype(jnp.float32), w_down.astype(jnp.float32))

    def closed(*params):
        return forward(*params, routes, piece_starts)
    layer_out, pullback = jax.vjp(closed, *floats)
    gradients = pullback(cotangent.astype(jnp.float32))
    return (layer_out.astype(jnp.bfloat16), gradients[0].astype(jnp.bfloat16), gradients[1], gradients[2], gradients[3], gradients[4], gradients[5], gradients[6], gradients[7], gradients[8], gradients[9], gradients[10], gradients[11], gradients[12], gradients[13], gradients[14])
```

```python
import functools, math
import jax, jax.numpy as jnp
from jax import lax
from jax.experimental import pallas as pl
from jax.experimental.pallas import tpu as pltpu

from jax.sharding import PartitionSpec as P

H = 12
HD = 64
PIECE = 256
KBLK = 512
CAP = 160


EPS = 1e-05
HIGH = lax.Precision.HIGHEST
NEG = -1e30


def rms_scale(values, gain_vec):
    inverse = lax.rsqrt(jnp.mean(values * values, axis=-1, keepdims=True) + EPS)
    return values * inverse * gain_vec


def piece_ids(positions, starts, extent):
    inside = (positions[:, None] >= starts[None, :]) & (
        positions[:, None] < starts[None, :] + extent
    )
    labels = jnp.arange(1, starts.shape[0] + 1, dtype=jnp.int32)
    return jnp.sum(jnp.where(inside, labels[None, :], 0), axis=1)


def reach_bounds(positions, starts, extent):
    inside = (positions[:, None] >= starts[None, :]) & (
        positions[:, None] < starts[None, :] + extent
    )
    piece_last = jnp.max(jnp.where(inside, starts[None, :] + extent - 1, 0))
    piece_first = jnp.min(jnp.where(inside, starts[None, :], positions[0]))
    upper = jnp.maximum(positions[-1], piece_last)
    lower = jnp.minimum(positions[0], piece_first)
    return (upper, lower)


def allowed_mask(query_pos, query_ids, key_pos, key_ids):
    causal = key_pos[None, :] <= query_pos[:, None]
    shared = (key_ids[None, :] == query_ids[:, None]) & (query_ids[:, None] > 0)
    return causal | shared


def slot_dest(route_ids, n_ffn, capacity):
    flat_ids = route_ids.reshape(-1)
    onehot = (flat_ids[:, None] == jnp.arange(n_ffn, dtype=jnp.int32)[None, :]).astype(jnp.int32)
    earlier = jnp.cumsum(onehot, axis=0) - onehot
    slot_pos = jnp.sum(earlier * onehot, axis=1)
    return jnp.where(flat_ids < n_ffn, flat_ids * capacity + slot_pos, n_ffn * capacity)


def local_mix(
    normed, res_logits, router, mixing, const_proj, const_vec, expert_rows, route_ids, n_ffn
):
    n_all = router.shape[1]
    logits = jnp.dot(normed, router, precision=HIGH) + jnp.dot(res_logits, mixing, precision=HIGH)
    probs = jax.nn.softmax(logits, axis=-1)
    labels = jnp.arange(n_all, dtype=jnp.int32)
    chosen = jnp.sum(
        jnp.where(route_ids[:, :, None] == labels[None, None, :], probs[:, None, :], 0.0), axis=-1
    )
    gates = chosen / jnp.sum(chosen, axis=1, keepdims=True)
    pair_logits = jnp.dot(normed, const_proj, precision=HIGH)
    first_pair = jax.nn.softmax(pair_logits[:, 0:2], axis=-1)
    second_pair = jax.nn.softmax(pair_logits[:, 2:4], axis=-1)
    first_const = first_pair[:, 0:1] * normed + first_pair[:, 1:2] * const_vec[0][None, :]
    second_const = second_pair[:, 0:1] * normed + second_pair[:, 1:2] * const_vec[1][None, :]
    mixed = jnp.zeros_like(normed)
    for route_k in range(2):
        route_id = route_ids[:, route_k : route_k + 1]
        entry = jnp.where(route_id < n_ffn, expert_rows[:, route_k], 0.0)
        entry = entry + jnp.where(route_id == n_ffn + 1, normed, 0.0)
        entry = entry + jnp.where(route_id == n_ffn + 2, first_const, 0.0)
        entry = entry + jnp.where(route_id == n_ffn + 3, second_const, 0.0)
        mixed = mixed + gates[:, route_k : route_k + 1] * entry
    return mixed


def swiglu_act(gate_pre, up_pre):
    return jax.nn.silu(gate_pre) * up_pre


MESH = pl.DeviceIdType.MESH
BF = jnp.bfloat16
F32 = jnp.float32
LOG2E = 1.4426950408889634
QSCALE = LOG2E / math.sqrt(HD)


class Place:
    def __init__(self):
        self.e = lax.axis_index("exp")
        self.f = lax.axis_index("fsdp")
        self.z = self.f // 2
        self.x = self.f % 2
        self.sib = self.e + 1 - 2 * (self.e % 2)
        self.yp = (self.e + 2) % 4
        self.diag = (self.sib + 2) % 4
        self.xf = self.f + 1 - 2 * self.x
        self.exp_peers = (self.sib, self.yp, self.diag)

    def zf(self, d):
        return ((self.z + d) % 4) * 2 + self.x

    def barrier(self):
        sem = pltpu.get_barrier_semaphore()
        for p in self.exp_peers:
            pl.semaphore_signal(sem, inc=1, device_id=(p, self.f), device_id_type=MESH)
        for d in (1, 2, 3):
            pl.semaphore_signal(sem, inc=1, device_id=(self.e, self.zf(d)), device_id_type=MESH)
        pl.semaphore_signal(sem, inc=1, device_id=(self.e, self.xf), device_id_type=MESH)
        pl.semaphore_wait(sem, 7)

    def send(self, src, dst, ss, rs, e=None, f=None):
        return pltpu.make_async_remote_copy(
            src_ref=src,
            dst_ref=dst,
            send_sem=ss,
            recv_sem=rs,
            device_id=(self.e if e is None else e, self.f if f is None else f),
            device_id_type=MESH,
        )


def lane_of(shape):
    return lax.broadcasted_iota(jnp.int32, shape, len(shape) - 1)


def ka_kernel(
    x_ref, u_ref, wq_ref, wo_ref, wg_ref, wu_ref, wd_ref, gres_ref, routes_ref, routes_t_ref, starts_ref,
    gain_a_ref, gain_f_ref, router_ref, proj_ref, mix_ref,
    attn_all, q_s, k_s, v_s, o_s, lse_s, hidden_ref, logit_ref, pair_ref, place_ref, recv, wo_full, wq_full,
    gate_full, up_full, down_full,
    attn_recv, nb, snd, m_s, l_s, acc_s, gsel,
    wq_ss, wq_rs, wo_ss, wo_rs, at_ss, at_rs, o_ss, o_rs, d_ss, d_rs,
    us, ur, ds, dr, xs, xr, loc,
):
    me = Place()
    e, f, z, xf = me.e, me.f, me.z, me.xf
    T, D = x_ref.shape
    C = D // 4
    R = wo_ref.shape[0]
    me.barrier()

    def rows(ref, index):
        return ref.at[pl.ds(pl.multiple_of(index * R, 32), R)]

    early = ((wq_ref, wq_full, wq_ss, wq_rs, 0), (wo_ref, wo_full, wo_ss, wo_rs, 1))
    for src, dst, ss, rs, li in early:
        for d in (1, 3, 2):
            me.send(src, rows(dst, f), ss.at[d], rs.at[d], f=me.zf(d)).start()
        me.send(src, rows(dst, f), ss.at[0], rs.at[0], f=xf).start()
        pltpu.make_async_copy(src, rows(dst, f), loc.at[li]).start()

    xv = x_ref[...].astype(F32)
    inv = lax.rsqrt(jnp.mean(xv * xv, axis=-1, keepdims=True) + EPS)
    attn_all[e] = (xv * inv * gain_a_ref[...]).astype(BF)
    to_sib = me.send(attn_all.at[e], attn_all.at[e], at_ss.at[0], at_rs.at[0], e=me.sib)
    to_yp = me.send(attn_all.at[e], attn_all.at[e], at_ss.at[1], at_rs.at[1], e=me.yp)
    to_yp.start()
    to_sib.start()

    def early_in(dst, ss, rs, d):
        return me.send(rows(dst, f), rows(dst, ((z - d + 4) % 4) * 2 + me.x), ss.at[d], rs.at[d])

    def early_fwd(dst, ss, rs, d):
        slot = rows(dst, ((z - d + 4) % 4) * 2 + me.x)
        return me.send(slot, slot, ss.at[3 + d], rs.at[3 + d], f=xf)

    for src, dst, ss, rs, li in early:
        for d in (1, 3, 2):
            early_in(dst, ss, rs, d).wait_recv()
            early_fwd(dst, ss, rs, d).start()

    shards = ((wg_ref, gate_full), (wu_ref, up_full), (wd_ref, down_full))

    def up_send(w, p, src, slot):
        full = shards[w][1]
        return me.send(src, full.at[slot], us.at[w, p], ur.at[w, p], f=f + 2)

    def down_send(w, p, src, slot):
        full = shards[w][1]
        return me.send(src, full.at[slot], ds.at[w, p], dr.at[w, p], f=f - 2)

    def x_send(w, i, src, slot):
        full = shards[w][1]
        return me.send(src, full.at[slot], xs.at[w, i], xr.at[w, i], f=xf)

    def experts(p):
        for w, (src, full) in enumerate(shards):
            if p == 0:
                x_send(w, 0, src, f).start()

                @pl.when(z <= 2)
                def _():
                    up_send(w, 0, src, f).start()

                @pl.when(z >= 1)
                def _():
                    down_send(w, 0, src, f).start()

                pltpu.make_async_copy(src, full.at[f], loc.at[2 + w]).start()
            else:

                @pl.when(z >= p)
                def _():
                    slot = f - 2 * p
                    up_send(w, p - 1, full.at[slot], slot).wait_recv()
                    if p <= 2:

                        @pl.when(z <= 2)
                        def _():
                            up_send(w, p, full.at[slot], slot).start()

                    x_send(w, p, full.at[slot], slot).start()

                @pl.when(z + p <= 3)
                def _():
                    slot = f + 2 * p
                    down_send(w, p - 1, full.at[slot], slot).wait_recv()
                    if p <= 2:

                        @pl.when(z >= 1)
                        def _():
                            down_send(w, p, full.at[slot], slot).start()

                    x_send(w, 3 + p, full.at[slot], slot).start()

    experts(0)

    me.send(attn_all.at[me.yp], attn_all.at[me.yp], at_ss.at[1], at_rs.at[1]).wait_recv()
    fwd = me.send(attn_all.at[me.yp], attn_all.at[me.yp], at_ss.at[2], at_rs.at[2], e=me.sib)
    fwd.start()
    me.send(attn_all.at[me.sib], attn_all.at[me.sib], at_ss.at[0], at_rs.at[0]).wait_recv()
    me.send(attn_all.at[me.diag], attn_all.at[me.diag], at_ss.at[2], at_rs.at[2]).wait_recv()

    def early_wait(src, dst, ss, rs, li):
        pltpu.make_async_copy(src, rows(dst, f), loc.at[li]).wait()
        me.send(rows(dst, xf), rows(dst, xf), ss.at[0], rs.at[0]).wait_recv()
        for d in (1, 2, 3):
            slot = rows(dst, ((z - d + 4) % 4) * 2 + 1 - me.x)
            me.send(slot, slot, ss.at[3 + d], rs.at[3 + d]).wait_recv()

    early_wait(*early[0])

    def qkv_step(i, _):
        b = i // 2
        r = pl.ds(pl.multiple_of((i % 2) * 256, 256), 256)
        out = jnp.dot(attn_all[b, r, :], wq_full[...], preferred_element_type=F32)
        q_s[b, r, :] = (out[:, 0:C] * QSCALE).astype(BF)
        k_s[b, r, :] = pltpu.roll(out[:, 128:384], 192, 1)[:, 0:C].astype(BF)
        v_s[b, r, :] = out[:, 2 * C : 3 * C].astype(BF)
        return 0

    lax.fori_loop(0, 8, qkv_step, 0)
    experts(1)

    head_of = lane_of((T, C)) // HD

    def head_step(i, _):
        qb = i // 3
        h = i % 3
        qh = jnp.where(head_of == h, q_s[qb], jnp.zeros((T, C), BF))
        s = lax.dot_general(qh, k_s[qb], (((1,), (1,)), ((), ())), preferred_element_type=F32)
        col = lane_of((T, T))
        row = lax.broadcasted_iota(jnp.int32, (T, T), 0)
        first = starts_ref[0, qb] - qb * T
        inside_c = (col >= first) & (col < first + PIECE)
        inside_r = (row >= first) & (row < first + PIECE)
        s = jnp.where((col <= row) | (inside_c & inside_r), s, NEG)
        m = jnp.max(s, axis=-1, keepdims=True)
        p = jnp.exp2(s - m)
        m_s[...] = m
        l_s[...] = jnp.sum(p, axis=-1, keepdims=True)
        acc_s[...] = jnp.dot(p.astype(BF), v_s[qb], preferred_element_type=F32)

        def kv_step(kb, _):
            s = lax.dot_general(qh, k_s[kb], (((1,), (1,)), ((), ())), preferred_element_type=F32)
            m_old = m_s[...]
            m = jnp.maximum(m_old, jnp.max(s, axis=-1, keepdims=True))
            scale = jnp.exp2(m_old - m)
            p = jnp.exp2(s - m)
            m_s[...] = m
            l_s[...] = l_s[...] * scale + jnp.sum(p, axis=-1, keepdims=True)
            acc_s[...] = acc_s[...] * scale + jnp.dot(p.astype(BF), v_s[kb], preferred_element_type=F32)
            return 0

        lax.fori_loop(0, qb, kv_step, 0)
        total = l_s[...]
        o_s[qb] = jnp.where(head_of == h, (acc_s[...] / total).astype(BF), o_s[qb])
        lse = m_s[...] + jnp.log2(total)
        lse_s[qb] = jnp.where(lane_of((T, 8)) == h, lse, lse_s[qb])
        return 0

    lax.fori_loop(0, 12, head_step, 0)

    for i, p in enumerate(me.exp_peers):
        me.send(o_s.at[p], attn_recv.at[e], o_ss.at[i], o_rs.at[i], e=p).start()
    attn_recv[e] = o_s[e]
    experts(2)

    r0, r1 = routes_t_ref[0:1, :], routes_t_ref[1:2, :]
    expert = lax.broadcasted_iota(jnp.int32, (8, T), 0)
    has = (expert == r0) | (expert == r1)
    earlier = (lax.broadcasted_iota(jnp.int32, (T, T), 0) < lane_of((T, T))).astype(BF)
    count = jnp.dot(has.astype(BF), earlier, preferred_element_type=F32).astype(jnp.int32)
    count = jnp.where(has, count, -1)
    slot_id = lax.broadcasted_iota(jnp.int32, (CAP, T), 0)
    for k in range(4):
        place_ref[k] = jnp.where(slot_id == count[k : k + 1, :], 1.0, 0.0).astype(BF)

    early_wait(*early[1])
    for i, p in enumerate(me.exp_peers):
        me.send(attn_recv.at[p], attn_recv.at[p], o_ss.at[i], o_rs.at[i]).wait_recv()

    def hidden_step(i, _):
        r = pl.ds(pl.multiple_of(i * 256, 256), 256)
        h = x_ref[r, :].astype(F32)
        for b in range(4):
            h = h + jnp.dot(attn_recv[b, r, :], wo_full[b * C : (b + 1) * C, :], preferred_element_type=F32)
        hidden_ref[r, :] = h
        n = h * lax.rsqrt(jnp.mean(h * h, axis=-1, keepdims=True) + EPS) * gain_f_ref[...]
        nb[r, :] = n.astype(BF)
        logits = jnp.dot(n, router_ref[...], precision=HIGH, preferred_element_type=F32)
        logits = logits + jnp.dot(gres_ref[r, :], mix_ref[...], precision=HIGH, preferred_element_type=F32)
        logit_ref[r, :] = logits
        pair_ref[r, :] = jnp.dot(n, proj_ref[...], precision=HIGH, preferred_element_type=F32)
        gsel[r, :] = gates_of(logits, routes_ref[r, :])
        return 0

    lax.fori_loop(0, 2, hidden_step, 0)

    def dispatch_step(k, _):
        place = place_ref[k]
        snd[k, 0] = jnp.dot(place, nb[...], preferred_element_type=F32).astype(BF)
        gate = jnp.sum(jnp.where(lane_of((T, 8)) == k, gsel[...], 0.0), axis=-1, keepdims=True)
        gu = (gate * u_ref[...].astype(F32)).astype(BF)
        snd[k, 1] = jnp.dot(place, gu, preferred_element_type=F32).astype(BF)
        return 0

    lax.fori_loop(0, 4, dispatch_step, 0)
    for i, p in enumerate(me.exp_peers):
        me.send(snd.at[p], recv.at[e], d_ss.at[i], d_rs.at[i], e=p).start()
    recv[e] = snd[e]
    experts(3)

    for src, dst, ss, rs, li in early:
        for j in range(4):
            me.send(src, rows(dst, f), ss.at[j], rs.at[j]).wait_send()
        for d in (1, 2, 3):
            early_fwd(dst, ss, rs, d).wait_send()
    to_sib.wait_send()
    to_yp.wait_send()
    fwd.wait_send()
    for i, p in enumerate(me.exp_peers):
        me.send(o_s.at[p], attn_recv.at[e], o_ss.at[i], o_rs.at[i]).wait_send()
        me.send(snd.at[p], recv.at[p], d_ss.at[i], d_rs.at[i]).wait()
    for w, (src, full) in enumerate(shards):
        pltpu.make_async_copy(src, full.at[f], loc.at[2 + w]).wait()
        x_send(w, 0, src, xf).wait()

        @pl.when(z <= 2)
        def _():
            up_send(w, 0, src, f).wait_send()

        @pl.when(z >= 1)
        def _():
            down_send(w, 0, src, f).wait_send()

        for p in (1, 2, 3):

            @pl.when(z >= p)
            def _():
                slot = f - 2 * p
                if p <= 2:

                    @pl.when(z <= 2)
                    def _():
                        up_send(w, p, full.at[slot], slot).wait_send()

                x_send(w, p, full.at[slot], xf - 2 * p).wait()

            @pl.when(z + p <= 3)
            def _():
                slot = f + 2 * p
                if p <= 2:

                    @pl.when(z >= 1)
                    def _():
                        down_send(w, p, full.at[slot], slot).wait_send()

                x_send(w, 3 + p, full.at[slot], xf + 2 * p).wait()


def gates_of(logits, routes):
    lane = lane_of(logits.shape)
    chosen = (lane == routes[:, 0:1]) | (lane == routes[:, 1:2])
    top = jnp.max(jnp.where(chosen, logits, NEG), axis=-1, keepdims=True)
    weight = jnp.where(chosen, jnp.exp(logits - top), 0.0)
    return weight / jnp.sum(weight, axis=-1, keepdims=True)


def sds(shape, dtype):
    return jax.ShapeDtypeStruct(shape, dtype)


def vmem():
    return pl.BlockSpec(memory_space=pltpu.VMEM)


def anyspace():
    return pl.BlockSpec(memory_space=pl.ANY)


def call_ka(x, u, wq, wo, wg, wu, wd, gres, routes, routes_t, starts, gain_a, gain_f, router, proj, mix):
    T, D = x.shape
    C = D // 4
    FF = wg.shape[1]
    R = wo.shape[0]
    dma = pltpu.SemaphoreType.DMA
    return pl.pallas_call(
        ka_kernel,
        name="forward",
        out_shape=(
            sds((4, T, D), BF),
            sds((4, T, C), BF), sds((4, T, C), BF), sds((4, T, C), BF), sds((4, T, C), BF),
            sds((4, T, 8), F32),
            sds((T, D), F32),
            sds((T, 8), F32), sds((T, 4), F32),
            sds((4, CAP, T), BF),
            sds((4, 2, CAP, D), BF),
            sds((D, D), BF),
            sds((D, 3 * C), BF),
            sds((8, R, FF), BF), sds((8, R, FF), BF), sds((8, FF // 8, D), BF),
        ),
        in_specs=[vmem(), vmem(), anyspace(), anyspace(), anyspace(), anyspace(), anyspace(), vmem(), vmem(), vmem(),
                  pl.BlockSpec(memory_space=pltpu.SMEM)] + [vmem()] * 5,
        out_specs=tuple([vmem()] * 13 + [anyspace()] * 3),
        scratch_shapes=[
            pltpu.VMEM((4, T, C), BF),
            pltpu.VMEM((T, D), BF),
            pltpu.VMEM((4, 2, CAP, D), BF),
            pltpu.VMEM((T, 1), F32),
            pltpu.VMEM((T, 1), F32),
            pltpu.VMEM((T, C), F32),
            pltpu.VMEM((T, 8), F32),
            dma((7,)), dma((7,)), dma((7,)), dma((7,)),
            dma((3,)), dma((3,)), dma((3,)), dma((3,)), dma((3,)), dma((3,)),
            dma((3, 3)), dma((3, 3)), dma((3, 3)), dma((3, 3)), dma((3, 7)), dma((3, 7)),
            dma((5,)),
        ],
        compiler_params=pltpu.CompilerParams(collective_id=0, has_side_effects=True, vmem_limit_bytes=56 << 20),
    )(x, u, wq, wo, wg, wu, wd, gres, routes, routes_t, starts, gain_a, gain_f, router, proj, mix)


def body(
    tokens,
    gate_res,
    routes,
    piece_starts,
    norm_attn,
    norm_ffn,
    w_query,
    w_key,
    w_value,
    w_out,
    router,
    mixing,
    const_proj,
    const_vec,
    w_gate,
    w_up,
    w_down,
    cotangent,
):
    n_ffn = lax.axis_size("exp")
    rows_dev = tokens.shape[1]
    model_width = tokens.shape[2]
    seq_length = rows_dev * n_ffn
    score_scale = 1.0 / math.sqrt(HD)
    inputs_f = tokens[0].astype(jnp.float32)
    res_logits = gate_res[0]
    route_ids = routes[0]
    starts = piece_starts[0]
    full_query, full_key, full_value, full_out = (
        lax.all_gather(w_query, "fsdp", axis=0, tiled=True),
        lax.all_gather(w_key, "fsdp", axis=0, tiled=True),
        lax.all_gather(w_value, "fsdp", axis=0, tiled=True),
        lax.all_gather(w_out, "fsdp", axis=0, tiled=True),
    )
    attn_in = rms_scale(inputs_f, norm_attn).astype(jnp.bfloat16)
    query = jnp.dot(attn_in, full_query, preferred_element_type=jnp.float32).astype(jnp.bfloat16)
    key = jnp.dot(attn_in, full_key, preferred_element_type=jnp.float32).astype(jnp.bfloat16)
    value = jnp.dot(attn_in, full_value, preferred_element_type=jnp.float32).astype(jnp.bfloat16)
    keys_all, values_all = (
        lax.all_gather(key, "exp", axis=0, tiled=True),
        lax.all_gather(value, "exp", axis=0, tiled=True),
    )
    query_heads = query.reshape(rows_dev, H, HD)
    key_heads = keys_all.reshape(seq_length, H, HD)
    value_heads = values_all.reshape(seq_length, H, HD)
    query_pos = lax.axis_index("exp") * rows_dev + jnp.arange(rows_dev, dtype=jnp.int32)
    query_ids = piece_ids(query_pos, starts, PIECE)
    key_upper, query_lower = reach_bounds(query_pos, starts, PIECE)
    block_list = jnp.arange(seq_length // KBLK, dtype=jnp.int32)

    def score_block(block_index):
        key_first = block_index * KBLK
        key_block = lax.dynamic_slice_in_dim(key_heads, key_first, KBLK, 0)
        value_block = lax.dynamic_slice_in_dim(value_heads, key_first, KBLK, 0)
        key_pos = key_first + jnp.arange(KBLK, dtype=jnp.int32)
        key_ids = piece_ids(key_pos, starts, PIECE)
        scores = (
            jnp.einsum("qhd,khd->hqk", query_heads, key_block, preferred_element_type=jnp.float32)
            * score_scale
        )
        allowed = allowed_mask(query_pos, query_ids, key_pos, key_ids)[None]
        return (scores, allowed, key_block, value_block)

    def needed(block_index):
        return block_index * KBLK <= key_upper

    def lse_step(carry, block_index):

        def lse_active(state):
            run_max, run_sum = state
            scores, allowed, _, _ = score_block(block_index)
            scores = jnp.where(allowed, scores, NEG)
            new_max = jnp.maximum(run_max, jnp.max(scores, axis=-1))
            exp_terms = jnp.where(allowed, jnp.exp(scores - new_max[..., None]), 0.0)
            return (new_max, run_sum * jnp.exp(run_max - new_max) + jnp.sum(exp_terms, axis=-1))

        return (lax.cond(needed(block_index), lse_active, lambda state: state, carry), None)

    start_carry = (jnp.full((H, rows_dev), NEG, jnp.float32), jnp.zeros((H, rows_dev), jnp.float32))
    (run_max, run_sum), _ = lax.scan(lse_step, start_carry, block_list)
    log_norm = run_max + jnp.log(run_sum)

    def block_probs(scores, allowed):
        return jnp.where(allowed, jnp.exp(scores - log_norm[..., None]), 0.0)

    def out_step(accum, block_index):

        def out_active(total):
            scores, allowed, _, value_block = score_block(block_index)
            probs_low = block_probs(scores, allowed).astype(jnp.bfloat16)
            return total + jnp.einsum(
                "hqk,khd->qhd", probs_low, value_block, preferred_element_type=jnp.float32
            )

        return (lax.cond(needed(block_index), out_active, lambda total: total, accum), None)

    attn_sum, _ = lax.scan(out_step, jnp.zeros((rows_dev, H, HD), jnp.float32), block_list)
    attn_low = attn_sum.astype(jnp.bfloat16).reshape(rows_dev, model_width)
    hidden = inputs_f + jnp.dot(attn_low, full_out, preferred_element_type=jnp.float32)
    normed = rms_scale(hidden, norm_ffn)
    destination = slot_dest(route_ids, n_ffn, CAP)
    sources = jnp.arange(2 * rows_dev, dtype=jnp.int32) // 2
    slot_table = (
        jnp.full((n_ffn * CAP,), rows_dev, jnp.int32).at[destination].set(sources, mode="drop")
    )
    padded = jnp.concatenate(
        [normed.astype(jnp.bfloat16), jnp.zeros((1, model_width), jnp.bfloat16)], axis=0
    )
    dispatched = padded[slot_table].reshape(n_ffn, CAP, model_width)
    received = lax.all_to_all(dispatched, "exp", split_axis=0, concat_axis=0, tiled=True)
    full_gate, full_up, full_down = (
        lax.all_gather(w_gate[0], "fsdp", axis=0, tiled=True),
        lax.all_gather(w_up[0], "fsdp", axis=0, tiled=True),
        lax.all_gather(w_down[0], "fsdp", axis=0, tiled=True),
    )
    slot_rows = received.reshape(n_ffn * CAP, model_width)
    gate_pre = jnp.dot(slot_rows, full_gate, preferred_element_type=jnp.float32)
    up_pre = jnp.dot(slot_rows, full_up, preferred_element_type=jnp.float32)
    inner_act = swiglu_act(gate_pre, up_pre).astype(jnp.bfloat16)
    expert_result = jnp.dot(inner_act, full_down, preferred_element_type=jnp.float32).astype(
        jnp.bfloat16
    )
    returned = lax.all_to_all(
        expert_result.reshape(n_ffn, CAP, model_width),
        "exp",
        split_axis=0,
        concat_axis=0,
        tiled=True,
    )
    returned_pad = jnp.concatenate(
        [returned.reshape(n_ffn * CAP, model_width), jnp.zeros((1, model_width), jnp.bfloat16)],
        axis=0,
    )
    expert_rows = returned_pad[destination].astype(jnp.float32).reshape(rows_dev, 2, model_width)

    def mix_local(normed_in, logits_in, router_in, mixing_in, proj_in, vec_in, rows_in):
        return local_mix(
            normed_in, logits_in, router_in, mixing_in, proj_in, vec_in, rows_in, route_ids, n_ffn
        )

    moe_out, mix_pull = jax.vjp(
        mix_local, normed, res_logits, router, mixing, const_proj, const_vec, expert_rows
    )
    layer_out = (hidden + moe_out).astype(jnp.bfloat16)
    upstream = cotangent[0].astype(jnp.float32)
    d_normed_local, d_res_logits, d_router, d_mixing, d_const_proj, d_const_vec, d_expert_rows = (
        mix_pull(upstream)
    )
    d_rows_low = d_expert_rows.reshape(2 * rows_dev, model_width).astype(jnp.bfloat16)
    d_dispatched = (
        jnp.zeros((n_ffn * CAP, model_width), jnp.bfloat16)
        .at[destination]
        .set(d_rows_low, mode="drop")
    )
    d_received = lax.all_to_all(
        d_dispatched.reshape(n_ffn, CAP, model_width),
        "exp",
        split_axis=0,
        concat_axis=0,
        tiled=True,
    )
    d_received = d_received.reshape(n_ffn * CAP, model_width)
    d_inner = jnp.einsum("rd,fd->rf", d_received, full_down, preferred_element_type=jnp.float32)
    _, act_pull = jax.vjp(swiglu_act, gate_pre, up_pre)
    d_gate_pre, d_up_pre = act_pull(d_inner)
    d_gate_low = d_gate_pre.astype(jnp.bfloat16)
    d_up_low = d_up_pre.astype(jnp.bfloat16)
    grad_down_full = jnp.einsum(
        "rf,rd->fd", inner_act, d_received, preferred_element_type=jnp.float32
    )
    grad_gate_full = jnp.einsum(
        "rd,rf->df", slot_rows, d_gate_low, preferred_element_type=jnp.float32
    )
    grad_up_full = jnp.einsum("rd,rf->df", slot_rows, d_up_low, preferred_element_type=jnp.float32)
    d_slot_rows = (
        jnp.einsum("rf,df->rd", d_gate_low, full_gate, preferred_element_type=jnp.float32)
        + jnp.einsum("rf,df->rd", d_up_low, full_up, preferred_element_type=jnp.float32)
    ).astype(jnp.bfloat16)
    d_sent = lax.all_to_all(
        d_slot_rows.reshape(n_ffn, CAP, model_width), "exp", split_axis=0, concat_axis=0, tiled=True
    )
    d_sent_pad = jnp.concatenate(
        [d_sent.reshape(n_ffn * CAP, model_width), jnp.zeros((1, model_width), jnp.bfloat16)],
        axis=0,
    )
    d_normed_sent = jnp.sum(
        d_sent_pad[destination].astype(jnp.float32).reshape(rows_dev, 2, model_width), axis=1
    )
    _, norm_ffn_pull = jax.vjp(rms_scale, hidden, norm_ffn)
    d_hidden_part, d_norm_ffn = norm_ffn_pull(d_normed_local + d_normed_sent)
    d_hidden = upstream + d_hidden_part
    d_hidden_low = d_hidden.astype(jnp.bfloat16)
    grad_out_full = jnp.einsum(
        "td,te->de", attn_low, d_hidden_low, preferred_element_type=jnp.float32
    )
    d_attn = jnp.einsum(
        "te,de->td", d_hidden_low, full_out, preferred_element_type=jnp.float32
    ).astype(jnp.bfloat16)
    d_attn_heads = d_attn.reshape(rows_dev, H, HD)
    zero_block = jnp.zeros((KBLK, H, HD), jnp.float32)

    def delta_terms(block_index):
        scores, allowed, _, value_block = score_block(block_index)
        probs = block_probs(scores, allowed)
        d_probs = jnp.einsum(
            "qhd,khd->hqk", d_attn_heads, value_block, preferred_element_type=jnp.float32
        )
        part = jnp.sum(probs * d_probs, axis=-1)
        return (
            part,
            jnp.einsum(
                "hqk,qhd->khd",
                probs.astype(jnp.bfloat16),
                d_attn_heads,
                preferred_element_type=jnp.float32,
            ),
        )

    def query_terms(block_index, row_delta):
        scores, allowed, key_block, value_block = score_block(block_index)
        probs = block_probs(scores, allowed)
        d_probs = jnp.einsum(
            "qhd,khd->hqk", d_attn_heads, value_block, preferred_element_type=jnp.float32
        )
        d_scores = (probs * (d_probs - row_delta[..., None])).astype(jnp.bfloat16)
        part = (
            jnp.einsum("hqk,khd->qhd", d_scores, key_block, preferred_element_type=jnp.float32)
            * score_scale
        )
        return (
            part,
            jnp.einsum("hqk,qhd->khd", d_scores, query_heads, preferred_element_type=jnp.float32)
            * score_scale,
        )

    def delta_step(total, block_index):

        def delta_active(running):
            part, grad_block = delta_terms(block_index)
            return (running + part, grad_block)

        return lax.cond(
            needed(block_index), delta_active, lambda running: (running, zero_block), total
        )

    row_delta, grad_values = lax.scan(delta_step, jnp.zeros((H, rows_dev), jnp.float32), block_list)

    def query_step(total, block_index):

        def query_active(running):
            part, grad_block = query_terms(block_index, row_delta)
            return (running + part, grad_block)

        return lax.cond(
            needed(block_index), query_active, lambda running: (running, zero_block), total
        )

    d_query_sum, grad_keys = lax.scan(
        query_step, jnp.zeros((rows_dev, H, HD), jnp.float32), block_list
    )
    grad_keys = grad_keys.reshape(seq_length, model_width)
    grad_values = grad_values.reshape(seq_length, model_width)
    d_key_sum, d_value_sum = (
        lax.psum_scatter(
            grad_keys.astype(jnp.bfloat16), "exp", scatter_dimension=0, tiled=True
        ).astype(jnp.float32),
        lax.psum_scatter(
            grad_values.astype(jnp.bfloat16), "exp", scatter_dimension=0, tiled=True
        ).astype(jnp.float32),
    )
    d_query_low = d_query_sum.reshape(rows_dev, model_width).astype(jnp.bfloat16)
    d_key_low = d_key_sum.astype(jnp.bfloat16)
    d_value_low = d_value_sum.astype(jnp.bfloat16)
    d_attn_in = (
        jnp.einsum("te,de->td", d_query_low, full_query, preferred_element_type=jnp.float32)
        + jnp.einsum("te,de->td", d_key_low, full_key, preferred_element_type=jnp.float32)
        + jnp.einsum("te,de->td", d_value_low, full_value, preferred_element_type=jnp.float32)
    )
    grad_query_full = jnp.einsum(
        "td,te->de", attn_in, d_query_low, preferred_element_type=jnp.float32
    )
    grad_key_full = jnp.einsum("td,te->de", attn_in, d_key_low, preferred_element_type=jnp.float32)
    grad_value_full = jnp.einsum(
        "td,te->de", attn_in, d_value_low, preferred_element_type=jnp.float32
    )
    _, norm_attn_pull = jax.vjp(rms_scale, inputs_f, norm_attn)
    d_inputs_part, d_norm_attn = norm_attn_pull(d_attn_in)
    grad_tokens = (d_hidden + d_inputs_part).astype(jnp.bfloat16)
    attn_shards = (
        lax.psum_scatter(
            grad_query_full.astype(jnp.bfloat16), "fsdp", scatter_dimension=0, tiled=True
        ).astype(jnp.float32),
        lax.psum_scatter(
            grad_key_full.astype(jnp.bfloat16), "fsdp", scatter_dimension=0, tiled=True
        ).astype(jnp.float32),
        lax.psum_scatter(
            grad_value_full.astype(jnp.bfloat16), "fsdp", scatter_dimension=0, tiled=True
        ).astype(jnp.float32),
        lax.psum_scatter(
            grad_out_full.astype(jnp.bfloat16), "fsdp", scatter_dimension=0, tiled=True
        ).astype(jnp.float32),
    )
    attn_shards = (
        lax.psum(attn_shards[0].astype(jnp.bfloat16), "exp").astype(jnp.float32),
        lax.psum(attn_shards[1].astype(jnp.bfloat16), "exp").astype(jnp.float32),
        lax.psum(attn_shards[2].astype(jnp.bfloat16), "exp").astype(jnp.float32),
        lax.psum(attn_shards[3].astype(jnp.bfloat16), "exp").astype(jnp.float32),
    )
    expert_shards = (
        lax.psum_scatter(
            grad_gate_full.astype(jnp.bfloat16), "fsdp", scatter_dimension=0, tiled=True
        ).astype(jnp.float32),
        lax.psum_scatter(
            grad_up_full.astype(jnp.bfloat16), "fsdp", scatter_dimension=0, tiled=True
        ).astype(jnp.float32),
        lax.psum_scatter(
            grad_down_full.astype(jnp.bfloat16), "fsdp", scatter_dimension=0, tiled=True
        ).astype(jnp.float32),
    )
    small_sums = lax.psum(
        (d_norm_attn, d_norm_ffn, d_router, d_mixing, d_const_proj, d_const_vec), ("exp", "fsdp")
    )
    return (
        layer_out[None],
        grad_tokens[None],
        d_res_logits[None],
        small_sums[0],
        small_sums[1],
        attn_shards[0],
        attn_shards[1],
        attn_shards[2],
        attn_shards[3],
        small_sums[2],
        small_sums[3],
        small_sums[4],
        small_sums[5],
        expert_shards[0][None],
        expert_shards[1][None],
        expert_shards[2][None],
    )


def body_fast(
    tokens,
    gate_res,
    routes,
    piece_starts,
    norm_attn,
    norm_ffn,
    w_query,
    w_key,
    w_value,
    w_out,
    router,
    mixing,
    const_proj,
    const_vec,
    w_gate,
    w_up,
    w_down,
    cotangent,
):
    n_ffn = lax.axis_size("exp")
    rows_dev = tokens.shape[1]
    model_width = tokens.shape[2]
    seq_length = rows_dev * n_ffn
    score_scale = 1.0 / math.sqrt(HD)
    inputs_f = tokens[0].astype(jnp.float32)
    res_logits = gate_res[0]
    route_ids = routes[0]
    starts = piece_starts[0]
    full_query, full_key, full_value, full_out = (
        lax.all_gather(w_query, "fsdp", axis=0, tiled=True),
        lax.all_gather(w_key, "fsdp", axis=0, tiled=True),
        lax.all_gather(w_value, "fsdp", axis=0, tiled=True),
        lax.all_gather(w_out, "fsdp", axis=0, tiled=True),
    )
    attn_in = rms_scale(inputs_f, norm_attn).astype(jnp.bfloat16)
    query = jnp.dot(attn_in, full_query, preferred_element_type=jnp.float32).astype(jnp.bfloat16)
    key = jnp.dot(attn_in, full_key, preferred_element_type=jnp.float32).astype(jnp.bfloat16)
    value = jnp.dot(attn_in, full_value, preferred_element_type=jnp.float32).astype(jnp.bfloat16)
    keys_all, values_all = (
        lax.all_gather(key, "exp", axis=0, tiled=True),
        lax.all_gather(value, "exp", axis=0, tiled=True),
    )
    query_heads = query.reshape(rows_dev, H, HD)
    key_heads = keys_all.reshape(seq_length, H, HD)
    value_heads = values_all.reshape(seq_length, H, HD)
    query_pos = lax.axis_index("exp") * rows_dev + jnp.arange(rows_dev, dtype=jnp.int32)
    query_ids = piece_ids(query_pos, starts, PIECE)
    key_upper, query_lower = reach_bounds(query_pos, starts, PIECE)
    block_list = jnp.arange(seq_length // KBLK, dtype=jnp.int32)

    def score_block(block_index):
        key_first = block_index * KBLK
        key_block = lax.dynamic_slice_in_dim(key_heads, key_first, KBLK, 0)
        value_block = lax.dynamic_slice_in_dim(value_heads, key_first, KBLK, 0)
        key_pos = key_first + jnp.arange(KBLK, dtype=jnp.int32)
        key_ids = piece_ids(key_pos, starts, PIECE)
        scores = (
            jnp.einsum("qhd,khd->hqk", query_heads, key_block, preferred_element_type=jnp.float32)
            * score_scale
        )
        allowed = allowed_mask(query_pos, query_ids, key_pos, key_ids)[None]
        return (scores, allowed, key_block, value_block)

    def needed(block_index):
        return block_index * KBLK <= key_upper

    def lse_step(carry, block_index):

        def lse_active(state):
            run_max, run_sum = state
            scores, allowed, _, _ = score_block(block_index)
            scores = jnp.where(allowed, scores, NEG)
            new_max = jnp.maximum(run_max, jnp.max(scores, axis=-1))
            exp_terms = jnp.where(allowed, jnp.exp(scores - new_max[..., None]), 0.0)
            return (new_max, run_sum * jnp.exp(run_max - new_max) + jnp.sum(exp_terms, axis=-1))

        return (lax.cond(needed(block_index), lse_active, lambda state: state, carry), None)

    start_carry = (jnp.full((H, rows_dev), NEG, jnp.float32), jnp.zeros((H, rows_dev), jnp.float32))
    (run_max, run_sum), _ = lax.scan(lse_step, start_carry, block_list)
    log_norm = run_max + jnp.log(run_sum)

    def block_probs(scores, allowed):
        return jnp.where(allowed, jnp.exp(scores - log_norm[..., None]), 0.0)

    exp_index = lax.axis_index("exp")
    wqkv = jnp.concatenate(
        [lax.dynamic_slice_in_dim(w, exp_index * 192, 192, 1) for w in (w_query, w_key, w_value)], axis=1
    )
    ka_out = call_ka(
        tokens[0], cotangent[0], wqkv, w_out, w_gate[0], w_up[0], w_down[0], res_logits, route_ids, route_ids.T,
        piece_starts, norm_attn[None], norm_ffn[None], router, const_proj, mixing,
    )
    def block_probs(scores, allowed):
        return jnp.where(allowed, jnp.exp(scores - log_norm[..., None]), 0.0)

    o_heads, hidden, recv = ka_out[4], ka_out[6], ka_out[10]
    full_gate = ka_out[13].reshape(model_width, -1)
    full_up = ka_out[14].reshape(model_width, -1)
    full_down = ka_out[15].reshape(-1, model_width)
    attn_low = lax.all_to_all(o_heads, "exp", split_axis=0, concat_axis=2, tiled=True).reshape(rows_dev, model_width)
    normed = rms_scale(hidden, norm_ffn)
    destination = slot_dest(route_ids, n_ffn, CAP)
    sources = jnp.arange(2 * rows_dev, dtype=jnp.int32) // 2
    received = recv[:, 0]
    slot_rows = received.reshape(n_ffn * CAP, model_width)
    gate_pre = jnp.dot(slot_rows, full_gate, preferred_element_type=jnp.float32)
    up_pre = jnp.dot(slot_rows, full_up, preferred_element_type=jnp.float32)
    inner_act = swiglu_act(gate_pre, up_pre).astype(jnp.bfloat16)
    expert_result = jnp.dot(inner_act, full_down, preferred_element_type=jnp.float32).astype(
        jnp.bfloat16
    )
    returned = lax.all_to_all(
        expert_result.reshape(n_ffn, CAP, model_width),
        "exp",
        split_axis=0,
        concat_axis=0,
        tiled=True,
    )
    returned_pad = jnp.concatenate(
        [returned.reshape(n_ffn * CAP, model_width), jnp.zeros((1, model_width), jnp.bfloat16)],
        axis=0,
    )
    expert_rows = returned_pad[destination].astype(jnp.float32).reshape(rows_dev, 2, model_width)

    def mix_local(normed_in, logits_in, router_in, mixing_in, proj_in, vec_in, rows_in):
        return local_mix(
            normed_in, logits_in, router_in, mixing_in, proj_in, vec_in, rows_in, route_ids, n_ffn
        )

    moe_out, mix_pull = jax.vjp(
        mix_local, normed, res_logits, router, mixing, const_proj, const_vec, expert_rows
    )
    layer_out = (hidden + moe_out).astype(jnp.bfloat16)
    upstream = cotangent[0].astype(jnp.float32)
    d_normed_local, d_res_logits, d_router, d_mixing, d_const_proj, d_const_vec, d_expert_rows = (
        mix_pull(upstream)
    )
    d_received = recv[:, 1].reshape(n_ffn * CAP, model_width)
    d_inner = jnp.einsum("rd,fd->rf", d_received, full_down, preferred_element_type=jnp.float32)
    _, act_pull = jax.vjp(swiglu_act, gate_pre, up_pre)
    d_gate_pre, d_up_pre = act_pull(d_inner)
    d_gate_low = d_gate_pre.astype(jnp.bfloat16)
    d_up_low = d_up_pre.astype(jnp.bfloat16)
    grad_down_full = jnp.einsum(
        "rf,rd->fd", inner_act, d_received, preferred_element_type=jnp.float32
    )
    grad_gate_full = jnp.einsum(
        "rd,rf->df", slot_rows, d_gate_low, preferred_element_type=jnp.float32
    )
    grad_up_full = jnp.einsum("rd,rf->df", slot_rows, d_up_low, preferred_element_type=jnp.float32)
    d_slot_rows = (
        jnp.einsum("rf,df->rd", d_gate_low, full_gate, preferred_element_type=jnp.float32)
        + jnp.einsum("rf,df->rd", d_up_low, full_up, preferred_element_type=jnp.float32)
    ).astype(jnp.bfloat16)
    d_sent = lax.all_to_all(
        d_slot_rows.reshape(n_ffn, CAP, model_width), "exp", split_axis=0, concat_axis=0, tiled=True
    )
    d_sent_pad = jnp.concatenate(
        [d_sent.reshape(n_ffn * CAP, model_width), jnp.zeros((1, model_width), jnp.bfloat16)],
        axis=0,
    )
    d_normed_sent = jnp.sum(
        d_sent_pad[destination].astype(jnp.float32).reshape(rows_dev, 2, model_width), axis=1
    )
    _, norm_ffn_pull = jax.vjp(rms_scale, hidden, norm_ffn)
    d_hidden_part, d_norm_ffn = norm_ffn_pull(d_normed_local + d_normed_sent)
    d_hidden = upstream + d_hidden_part
    d_hidden_low = d_hidden.astype(jnp.bfloat16)
    grad_out_full = jnp.einsum(
        "td,te->de", attn_low, d_hidden_low, preferred_element_type=jnp.float32
    )
    d_attn = jnp.einsum(
        "te,de->td", d_hidden_low, full_out, preferred_element_type=jnp.float32
    ).astype(jnp.bfloat16)
    d_attn_heads = d_attn.reshape(rows_dev, H, HD)
    zero_block = jnp.zeros((KBLK, H, HD), jnp.float32)

    def delta_terms(block_index):
        scores, allowed, _, value_block = score_block(block_index)
        probs = block_probs(scores, allowed)
        d_probs = jnp.einsum(
            "qhd,khd->hqk", d_attn_heads, value_block, preferred_element_type=jnp.float32
        )
        part = jnp.sum(probs * d_probs, axis=-1)
        return (
            part,
            jnp.einsum(
                "hqk,qhd->khd",
                probs.astype(jnp.bfloat16),
                d_attn_heads,
                preferred_element_type=jnp.float32,
            ),
        )

    def query_terms(block_index, row_delta):
        scores, allowed, key_block, value_block = score_block(block_index)
        probs = block_probs(scores, allowed)
        d_probs = jnp.einsum(
            "qhd,khd->hqk", d_attn_heads, value_block, preferred_element_type=jnp.float32
        )
        d_scores = (probs * (d_probs - row_delta[..., None])).astype(jnp.bfloat16)
        part = (
            jnp.einsum("hqk,khd->qhd", d_scores, key_block, preferred_element_type=jnp.float32)
            * score_scale
        )
        return (
            part,
            jnp.einsum("hqk,qhd->khd", d_scores, query_heads, preferred_element_type=jnp.float32)
            * score_scale,
        )

    def delta_step(total, block_index):

        def delta_active(running):
            part, grad_block = delta_terms(block_index)
            return (running + part, grad_block)

        return lax.cond(
            needed(block_index), delta_active, lambda running: (running, zero_block), total
        )

    row_delta, grad_values = lax.scan(delta_step, jnp.zeros((H, rows_dev), jnp.float32), block_list)

    def query_step(total, block_index):

        def query_active(running):
            part, grad_block = query_terms(block_index, row_delta)
            return (running + part, grad_block)

        return lax.cond(
            needed(block_index), query_active, lambda running: (running, zero_block), total
        )

    d_query_sum, grad_keys = lax.scan(
        query_step, jnp.zeros((rows_dev, H, HD), jnp.float32), block_list
    )
    grad_keys = grad_keys.reshape(seq_length, model_width)
    grad_values = grad_values.reshape(seq_length, model_width)
    d_key_sum, d_value_sum = (
        lax.psum_scatter(
            grad_keys.astype(jnp.bfloat16), "exp", scatter_dimension=0, tiled=True
        ).astype(jnp.float32),
        lax.psum_scatter(
            grad_values.astype(jnp.bfloat16), "exp", scatter_dimension=0, tiled=True
        ).astype(jnp.float32),
    )
    d_query_low = d_query_sum.reshape(rows_dev, model_width).astype(jnp.bfloat16)
    d_key_low = d_key_sum.astype(jnp.bfloat16)
    d_value_low = d_value_sum.astype(jnp.bfloat16)
    d_attn_in = (
        jnp.einsum("te,de->td", d_query_low, full_query, preferred_element_type=jnp.float32)
        + jnp.einsum("te,de->td", d_key_low, full_key, preferred_element_type=jnp.float32)
        + jnp.einsum("te,de->td", d_value_low, full_value, preferred_element_type=jnp.float32)
    )
    grad_query_full = jnp.einsum(
        "td,te->de", attn_in, d_query_low, preferred_element_type=jnp.float32
    )
    grad_key_full = jnp.einsum("td,te->de", attn_in, d_key_low, preferred_element_type=jnp.float32)
    grad_value_full = jnp.einsum(
        "td,te->de", attn_in, d_value_low, preferred_element_type=jnp.float32
    )
    _, norm_attn_pull = jax.vjp(rms_scale, inputs_f, norm_attn)
    d_inputs_part, d_norm_attn = norm_attn_pull(d_attn_in)
    grad_tokens = (d_hidden + d_inputs_part).astype(jnp.bfloat16)
    attn_shards = (
        lax.psum_scatter(
            grad_query_full.astype(jnp.bfloat16), "fsdp", scatter_dimension=0, tiled=True
        ).astype(jnp.float32),
        lax.psum_scatter(
            grad_key_full.astype(jnp.bfloat16), "fsdp", scatter_dimension=0, tiled=True
        ).astype(jnp.float32),
        lax.psum_scatter(
            grad_value_full.astype(jnp.bfloat16), "fsdp", scatter_dimension=0, tiled=True
        ).astype(jnp.float32),
        lax.psum_scatter(
            grad_out_full.astype(jnp.bfloat16), "fsdp", scatter_dimension=0, tiled=True
        ).astype(jnp.float32),
    )
    attn_shards = (
        lax.psum(attn_shards[0].astype(jnp.bfloat16), "exp").astype(jnp.float32),
        lax.psum(attn_shards[1].astype(jnp.bfloat16), "exp").astype(jnp.float32),
        lax.psum(attn_shards[2].astype(jnp.bfloat16), "exp").astype(jnp.float32),
        lax.psum(attn_shards[3].astype(jnp.bfloat16), "exp").astype(jnp.float32),
    )
    expert_shards = (
        lax.psum_scatter(
            grad_gate_full.astype(jnp.bfloat16), "fsdp", scatter_dimension=0, tiled=True
        ).astype(jnp.float32),
        lax.psum_scatter(
            grad_up_full.astype(jnp.bfloat16), "fsdp", scatter_dimension=0, tiled=True
        ).astype(jnp.float32),
        lax.psum_scatter(
            grad_down_full.astype(jnp.bfloat16), "fsdp", scatter_dimension=0, tiled=True
        ).astype(jnp.float32),
    )
    small_sums = lax.psum(
        (d_norm_attn, d_norm_ffn, d_router, d_mixing, d_const_proj, d_const_vec), ("exp", "fsdp")
    )
    return (
        layer_out[None],
        grad_tokens[None],
        d_res_logits[None],
        small_sums[0],
        small_sums[1],
        attn_shards[0],
        attn_shards[1],
        attn_shards[2],
        attn_shards[3],
        small_sums[2],
        small_sums[3],
        small_sums[4],
        small_sums[5],
        expert_shards[0][None],
        expert_shards[1][None],
        expert_shards[2][None],
    )


def solution(mesh):
    placed = (
        P("fsdp", "exp", None),
        P("fsdp", "exp", None),
        P("fsdp", "exp", None),
        P("fsdp", None),
        P(),
        P(),
        P("fsdp", None),
        P("fsdp", None),
        P("fsdp", None),
        P("fsdp", None),
        P(),
        P(),
        P(),
        P(),
        P("exp", "fsdp", None),
        P("exp", "fsdp", None),
        P("exp", "fsdp", None),
        P("fsdp", "exp", None),
    )
    return jax.shard_map(
        body_fast if (mesh.shape['exp'], mesh.shape['fsdp']) == (4, 8) else body,
        mesh=mesh,
        in_specs=placed,
        out_specs=(
            P("fsdp", "exp", None),
            P("fsdp", "exp", None),
            P("fsdp", "exp", None),
            P(),
            P(),
            P("fsdp", None),
            P("fsdp", None),
            P("fsdp", None),
            P("fsdp", None),
            P(),
            P(),
            P(),
            P(),
            P("exp", "fsdp", None),
            P("exp", "fsdp", None),
            P("exp", "fsdp", None),
        ),
        check_vma=False,
    )
```

```python
import functools, math
import jax, jax.numpy as jnp
from jax import lax
from jax.experimental import pallas as pl
from jax.experimental.pallas import tpu as pltpu

from jax.sharding import PartitionSpec as P

H = 12
HD = 64
PIECE = 256
KBLK = 512
CAP = 160


EPS = 1e-05
HIGH = lax.Precision.HIGHEST
NEG = -1e30


def rms_scale(values, gain_vec):
    inverse = lax.rsqrt(jnp.mean(values * values, axis=-1, keepdims=True) + EPS)
    return values * inverse * gain_vec


def piece_ids(positions, starts, extent):
    inside = (positions[:, None] >= starts[None, :]) & (
        positions[:, None] < starts[None, :] + extent
    )
    labels = jnp.arange(1, starts.shape[0] + 1, dtype=jnp.int32)
    return jnp.sum(jnp.where(inside, labels[None, :], 0), axis=1)


def reach_bounds(positions, starts, extent):
    inside = (positions[:, None] >= starts[None, :]) & (
        positions[:, None] < starts[None, :] + extent
    )
    piece_last = jnp.max(jnp.where(inside, starts[None, :] + extent - 1, 0))
    piece_first = jnp.min(jnp.where(inside, starts[None, :], positions[0]))
    upper = jnp.maximum(positions[-1], piece_last)
    lower = jnp.minimum(positions[0], piece_first)
    return (upper, lower)


def allowed_mask(query_pos, query_ids, key_pos, key_ids):
    causal = key_pos[None, :] <= query_pos[:, None]
    shared = (key_ids[None, :] == query_ids[:, None]) & (query_ids[:, None] > 0)
    return causal | shared


def slot_dest(route_ids, n_ffn, capacity):
    flat_ids = route_ids.reshape(-1)
    onehot = (flat_ids[:, None] == jnp.arange(n_ffn, dtype=jnp.int32)[None, :]).astype(jnp.int32)
    earlier = jnp.cumsum(onehot, axis=0) - onehot
    slot_pos = jnp.sum(earlier * onehot, axis=1)
    return jnp.where(flat_ids < n_ffn, flat_ids * capacity + slot_pos, n_ffn * capacity)


def local_mix(
    normed, res_logits, router, mixing, const_proj, const_vec, expert_rows, route_ids, n_ffn
):
    n_all = router.shape[1]
    logits = jnp.dot(normed, router, precision=HIGH) + jnp.dot(res_logits, mixing, precision=HIGH)
    probs = jax.nn.softmax(logits, axis=-1)
    labels = jnp.arange(n_all, dtype=jnp.int32)
    chosen = jnp.sum(
        jnp.where(route_ids[:, :, None] == labels[None, None, :], probs[:, None, :], 0.0), axis=-1
    )
    gates = chosen / jnp.sum(chosen, axis=1, keepdims=True)
    pair_logits = jnp.dot(normed, const_proj, precision=HIGH)
    first_pair = jax.nn.softmax(pair_logits[:, 0:2], axis=-1)
    second_pair = jax.nn.softmax(pair_logits[:, 2:4], axis=-1)
    first_const = first_pair[:, 0:1] * normed + first_pair[:, 1:2] * const_vec[0][None, :]
    second_const = second_pair[:, 0:1] * normed + second_pair[:, 1:2] * const_vec[1][None, :]
    mixed = jnp.zeros_like(normed)
    for route_k in range(2):
        route_id = route_ids[:, route_k : route_k + 1]
        entry = jnp.where(route_id < n_ffn, expert_rows[:, route_k], 0.0)
        entry = entry + jnp.where(route_id == n_ffn + 1, normed, 0.0)
        entry = entry + jnp.where(route_id == n_ffn + 2, first_const, 0.0)
        entry = entry + jnp.where(route_id == n_ffn + 3, second_const, 0.0)
        mixed = mixed + gates[:, route_k : route_k + 1] * entry
    return mixed


def swiglu_act(gate_pre, up_pre):
    return jax.nn.silu(gate_pre) * up_pre


def body(
    tokens,
    gate_res,
    routes,
    piece_starts,
    norm_attn,
    norm_ffn,
    w_query,
    w_key,
    w_value,
    w_out,
    router,
    mixing,
    const_proj,
    const_vec,
    w_gate,
    w_up,
    w_down,
    cotangent,
):
    n_ffn = lax.axis_size("exp")
    rows_dev = tokens.shape[1]
    model_width = tokens.shape[2]
    seq_length = rows_dev * n_ffn
    score_scale = 1.0 / math.sqrt(HD)
    inputs_f = tokens[0].astype(jnp.float32)
    res_logits = gate_res[0]
    route_ids = routes[0]
    starts = piece_starts[0]
    full_query, full_key, full_value, full_out = (
        lax.all_gather(w_query, "fsdp", axis=0, tiled=True),
        lax.all_gather(w_key, "fsdp", axis=0, tiled=True),
        lax.all_gather(w_value, "fsdp", axis=0, tiled=True),
        lax.all_gather(w_out, "fsdp", axis=0, tiled=True),
    )
    attn_in = rms_scale(inputs_f, norm_attn).astype(jnp.bfloat16)
    query = jnp.dot(attn_in, full_query, preferred_element_type=jnp.float32).astype(jnp.bfloat16)
    key = jnp.dot(attn_in, full_key, preferred_element_type=jnp.float32).astype(jnp.bfloat16)
    value = jnp.dot(attn_in, full_value, preferred_element_type=jnp.float32).astype(jnp.bfloat16)
    keys_all, values_all = (
        lax.all_gather(key, "exp", axis=0, tiled=True),
        lax.all_gather(value, "exp", axis=0, tiled=True),
    )
    query_heads = query.reshape(rows_dev, H, HD)
    key_heads = keys_all.reshape(seq_length, H, HD)
    value_heads = values_all.reshape(seq_length, H, HD)
    query_pos = lax.axis_index("exp") * rows_dev + jnp.arange(rows_dev, dtype=jnp.int32)
    query_ids = piece_ids(query_pos, starts, PIECE)
    key_upper, query_lower = reach_bounds(query_pos, starts, PIECE)
    block_list = jnp.arange(seq_length // KBLK, dtype=jnp.int32)

    def score_block(block_index):
        key_first = block_index * KBLK
        key_block = lax.dynamic_slice_in_dim(key_heads, key_first, KBLK, 0)
        value_block = lax.dynamic_slice_in_dim(value_heads, key_first, KBLK, 0)
        key_pos = key_first + jnp.arange(KBLK, dtype=jnp.int32)
        key_ids = piece_ids(key_pos, starts, PIECE)
        scores = (
            jnp.einsum("qhd,khd->hqk", query_heads, key_block, preferred_element_type=jnp.float32)
            * score_scale
        )
        allowed = allowed_mask(query_pos, query_ids, key_pos, key_ids)[None]
        return (scores, allowed, key_block, value_block)

    def needed(block_index):
        return block_index * KBLK <= key_upper

    def lse_step(carry, block_index):

        def lse_active(state):
            run_max, run_sum = state
            scores, allowed, _, _ = score_block(block_index)
            scores = jnp.where(allowed, scores, NEG)
            new_max = jnp.maximum(run_max, jnp.max(scores, axis=-1))
            exp_terms = jnp.where(allowed, jnp.exp(scores - new_max[..., None]), 0.0)
            return (new_max, run_sum * jnp.exp(run_max - new_max) + jnp.sum(exp_terms, axis=-1))

        return (lax.cond(needed(block_index), lse_active, lambda state: state, carry), None)

    start_carry = (jnp.full((H, rows_dev), NEG, jnp.float32), jnp.zeros((H, rows_dev), jnp.float32))
    (run_max, run_sum), _ = lax.scan(lse_step, start_carry, block_list)
    log_norm = run_max + jnp.log(run_sum)

    def block_probs(scores, allowed):
        return jnp.where(allowed, jnp.exp(scores - log_norm[..., None]), 0.0)

    def out_step(accum, block_index):

        def out_active(total):
            scores, allowed, _, value_block = score_block(block_index)
            probs_low = block_probs(scores, allowed).astype(jnp.bfloat16)
            return total + jnp.einsum(
                "hqk,khd->qhd", probs_low, value_block, preferred_element_type=jnp.float32
            )

        return (lax.cond(needed(block_index), out_active, lambda total: total, accum), None)

    attn_sum, _ = lax.scan(out_step, jnp.zeros((rows_dev, H, HD), jnp.float32), block_list)
    attn_low = attn_sum.astype(jnp.bfloat16).reshape(rows_dev, model_width)
    hidden = inputs_f + jnp.dot(attn_low, full_out, preferred_element_type=jnp.float32)
    normed = rms_scale(hidden, norm_ffn)
    destination = slot_dest(route_ids, n_ffn, CAP)
    sources = jnp.arange(2 * rows_dev, dtype=jnp.int32) // 2
    slot_table = (
        jnp.full((n_ffn * CAP,), rows_dev, jnp.int32).at[destination].set(sources, mode="drop")
    )
    padded = jnp.concatenate(
        [normed.astype(jnp.bfloat16), jnp.zeros((1, model_width), jnp.bfloat16)], axis=0
    )
    dispatched = padded[slot_table].reshape(n_ffn, CAP, model_width)
    received = lax.all_to_all(dispatched, "exp", split_axis=0, concat_axis=0, tiled=True)
    full_gate, full_up, full_down = (
        lax.all_gather(w_gate[0], "fsdp", axis=0, tiled=True),
        lax.all_gather(w_up[0], "fsdp", axis=0, tiled=True),
        lax.all_gather(w_down[0], "fsdp", axis=0, tiled=True),
    )
    slot_rows = received.reshape(n_ffn * CAP, model_width)
    gate_pre = jnp.dot(slot_rows, full_gate, preferred_element_type=jnp.float32)
    up_pre = jnp.dot(slot_rows, full_up, preferred_element_type=jnp.float32)
    inner_act = swiglu_act(gate_pre, up_pre).astype(jnp.bfloat16)
    expert_result = jnp.dot(inner_act, full_down, preferred_element_type=jnp.float32).astype(
        jnp.bfloat16
    )
    returned = lax.all_to_all(
        expert_result.reshape(n_ffn, CAP, model_width),
        "exp",
        split_axis=0,
        concat_axis=0,
        tiled=True,
    )
    returned_pad = jnp.concatenate(
        [returned.reshape(n_ffn * CAP, model_width), jnp.zeros((1, model_width), jnp.bfloat16)],
        axis=0,
    )
    expert_rows = returned_pad[destination].astype(jnp.float32).reshape(rows_dev, 2, model_width)

    def mix_local(normed_in, logits_in, router_in, mixing_in, proj_in, vec_in, rows_in):
        return local_mix(
            normed_in, logits_in, router_in, mixing_in, proj_in, vec_in, rows_in, route_ids, n_ffn
        )

    moe_out, mix_pull = jax.vjp(
        mix_local, normed, res_logits, router, mixing, const_proj, const_vec, expert_rows
    )
    layer_out = (hidden + moe_out).astype(jnp.bfloat16)
    upstream = cotangent[0].astype(jnp.float32)
    d_normed_local, d_res_logits, d_router, d_mixing, d_const_proj, d_const_vec, d_expert_rows = (
        mix_pull(upstream)
    )
    d_rows_low = d_expert_rows.reshape(2 * rows_dev, model_width).astype(jnp.bfloat16)
    d_dispatched = (
        jnp.zeros((n_ffn * CAP, model_width), jnp.bfloat16)
        .at[destination]
        .set(d_rows_low, mode="drop")
    )
    d_received = lax.all_to_all(
        d_dispatched.reshape(n_ffn, CAP, model_width),
        "exp",
        split_axis=0,
        concat_axis=0,
        tiled=True,
    )
    d_received = d_received.reshape(n_ffn * CAP, model_width)
    d_inner = jnp.einsum("rd,fd->rf", d_received, full_down, preferred_element_type=jnp.float32)
    _, act_pull = jax.vjp(swiglu_act, gate_pre, up_pre)
    d_gate_pre, d_up_pre = act_pull(d_inner)
    d_gate_low = d_gate_pre.astype(jnp.bfloat16)
    d_up_low = d_up_pre.astype(jnp.bfloat16)
    grad_down_full = jnp.einsum(
        "rf,rd->fd", inner_act, d_received, preferred_element_type=jnp.float32
    )
    grad_gate_full = jnp.einsum(
        "rd,rf->df", slot_rows, d_gate_low, preferred_element_type=jnp.float32
    )
    grad_up_full = jnp.einsum("rd,rf->df", slot_rows, d_up_low, preferred_element_type=jnp.float32)
    d_slot_rows = (
        jnp.einsum("rf,df->rd", d_gate_low, full_gate, preferred_element_type=jnp.float32)
        + jnp.einsum("rf,df->rd", d_up_low, full_up, preferred_element_type=jnp.float32)
    ).astype(jnp.bfloat16)
    d_sent = lax.all_to_all(
        d_slot_rows.reshape(n_ffn, CAP, model_width), "exp", split_axis=0, concat_axis=0, tiled=True
    )
    d_sent_pad = jnp.concatenate(
        [d_sent.reshape(n_ffn * CAP, model_width), jnp.zeros((1, model_width), jnp.bfloat16)],
        axis=0,
    )
    d_normed_sent = jnp.sum(
        d_sent_pad[destination].astype(jnp.float32).reshape(rows_dev, 2, model_width), axis=1
    )
    _, norm_ffn_pull = jax.vjp(rms_scale, hidden, norm_ffn)
    d_hidden_part, d_norm_ffn = norm_ffn_pull(d_normed_local + d_normed_sent)
    d_hidden = upstream + d_hidden_part
    d_hidden_low = d_hidden.astype(jnp.bfloat16)
    grad_out_full = jnp.einsum(
        "td,te->de", attn_low, d_hidden_low, preferred_element_type=jnp.float32
    )
    d_attn = jnp.einsum(
        "te,de->td", d_hidden_low, full_out, preferred_element_type=jnp.float32
    ).astype(jnp.bfloat16)
    d_attn_heads = d_attn.reshape(rows_dev, H, HD)
    zero_block = jnp.zeros((KBLK, H, HD), jnp.float32)

    def delta_terms(block_index):
        scores, allowed, _, value_block = score_block(block_index)
        probs = block_probs(scores, allowed)
        d_probs = jnp.einsum(
            "qhd,khd->hqk", d_attn_heads, value_block, preferred_element_type=jnp.float32
        )
        part = jnp.sum(probs * d_probs, axis=-1)
        return (
            part,
            jnp.einsum(
                "hqk,qhd->khd",
                probs.astype(jnp.bfloat16),
                d_attn_heads,
                preferred_element_type=jnp.float32,
            ),
        )

    def query_terms(block_index, row_delta):
        scores, allowed, key_block, value_block = score_block(block_index)
        probs = block_probs(scores, allowed)
        d_probs = jnp.einsum(
            "qhd,khd->hqk", d_attn_heads, value_block, preferred_element_type=jnp.float32
        )
        d_scores = (probs * (d_probs - row_delta[..., None])).astype(jnp.bfloat16)
        part = (
            jnp.einsum("hqk,khd->qhd", d_scores, key_block, preferred_element_type=jnp.float32)
            * score_scale
        )
        return (
            part,
            jnp.einsum("hqk,qhd->khd", d_scores, query_heads, preferred_element_type=jnp.float32)
            * score_scale,
        )

    def delta_step(total, block_index):

        def delta_active(running):
            part, grad_block = delta_terms(block_index)
            return (running + part, grad_block)

        return lax.cond(
            needed(block_index), delta_active, lambda running: (running, zero_block), total
        )

    row_delta, grad_values = lax.scan(delta_step, jnp.zeros((H, rows_dev), jnp.float32), block_list)

    def query_step(total, block_index):

        def query_active(running):
            part, grad_block = query_terms(block_index, row_delta)
            return (running + part, grad_block)

        return lax.cond(
            needed(block_index), query_active, lambda running: (running, zero_block), total
        )

    d_query_sum, grad_keys = lax.scan(
        query_step, jnp.zeros((rows_dev, H, HD), jnp.float32), block_list
    )
    grad_keys = grad_keys.reshape(seq_length, model_width)
    grad_values = grad_values.reshape(seq_length, model_width)
    d_key_sum, d_value_sum = (
        lax.psum_scatter(
            grad_keys.astype(jnp.bfloat16), "exp", scatter_dimension=0, tiled=True
        ).astype(jnp.float32),
        lax.psum_scatter(
            grad_values.astype(jnp.bfloat16), "exp", scatter_dimension=0, tiled=True
        ).astype(jnp.float32),
    )
    d_query_low = d_query_sum.reshape(rows_dev, model_width).astype(jnp.bfloat16)
    d_key_low = d_key_sum.astype(jnp.bfloat16)
    d_value_low = d_value_sum.astype(jnp.bfloat16)
    d_attn_in = (
        jnp.einsum("te,de->td", d_query_low, full_query, preferred_element_type=jnp.float32)
        + jnp.einsum("te,de->td", d_key_low, full_key, preferred_element_type=jnp.float32)
        + jnp.einsum("te,de->td", d_value_low, full_value, preferred_element_type=jnp.float32)
    )
    grad_query_full = jnp.einsum(
        "td,te->de", attn_in, d_query_low, preferred_element_type=jnp.float32
    )
    grad_key_full = jnp.einsum("td,te->de", attn_in, d_key_low, preferred_element_type=jnp.float32)
    grad_value_full = jnp.einsum(
        "td,te->de", attn_in, d_value_low, preferred_element_type=jnp.float32
    )
    _, norm_attn_pull = jax.vjp(rms_scale, inputs_f, norm_attn)
    d_inputs_part, d_norm_attn = norm_attn_pull(d_attn_in)
    grad_tokens = (d_hidden + d_inputs_part).astype(jnp.bfloat16)
    attn_shards = (
        lax.psum_scatter(
            grad_query_full.astype(jnp.bfloat16), "fsdp", scatter_dimension=0, tiled=True
        ).astype(jnp.float32),
        lax.psum_scatter(
            grad_key_full.astype(jnp.bfloat16), "fsdp", scatter_dimension=0, tiled=True
        ).astype(jnp.float32),
        lax.psum_scatter(
            grad_value_full.astype(jnp.bfloat16), "fsdp", scatter_dimension=0, tiled=True
        ).astype(jnp.float32),
        lax.psum_scatter(
            grad_out_full.astype(jnp.bfloat16), "fsdp", scatter_dimension=0, tiled=True
        ).astype(jnp.float32),
    )
    attn_shards = (
        lax.psum(attn_shards[0].astype(jnp.bfloat16), "exp").astype(jnp.float32),
        lax.psum(attn_shards[1].astype(jnp.bfloat16), "exp").astype(jnp.float32),
        lax.psum(attn_shards[2].astype(jnp.bfloat16), "exp").astype(jnp.float32),
        lax.psum(attn_shards[3].astype(jnp.bfloat16), "exp").astype(jnp.float32),
    )
    expert_shards = (
        lax.psum_scatter(
            grad_gate_full.astype(jnp.bfloat16), "fsdp", scatter_dimension=0, tiled=True
        ).astype(jnp.float32),
        lax.psum_scatter(
            grad_up_full.astype(jnp.bfloat16), "fsdp", scatter_dimension=0, tiled=True
        ).astype(jnp.float32),
        lax.psum_scatter(
            grad_down_full.astype(jnp.bfloat16), "fsdp", scatter_dimension=0, tiled=True
        ).astype(jnp.float32),
    )
    small_sums = lax.psum(
        (d_norm_attn, d_norm_ffn, d_router, d_mixing, d_const_proj, d_const_vec), ("exp", "fsdp")
    )
    return (
        layer_out[None],
        grad_tokens[None],
        d_res_logits[None],
        small_sums[0],
        small_sums[1],
        attn_shards[0],
        attn_shards[1],
        attn_shards[2],
        attn_shards[3],
        small_sums[2],
        small_sums[3],
        small_sums[4],
        small_sums[5],
        expert_shards[0][None],
        expert_shards[1][None],
        expert_shards[2][None],
    )


MESH = pl.DeviceIdType.MESH
BF = jnp.bfloat16
F32 = jnp.float32
LOG2E = 1.4426950408889634
QSCALE = LOG2E / math.sqrt(HD)


class Place:
    def __init__(self):
        self.e = lax.axis_index("exp")
        self.f = lax.axis_index("fsdp")
        self.z = self.f // 2
        self.x = self.f % 2
        self.sib = self.e + 1 - 2 * (self.e % 2)
        self.yp = (self.e + 2) % 4
        self.diag = (self.sib + 2) % 4
        self.xf = self.f + 1 - 2 * self.x
        self.exp_peers = (self.sib, self.yp, self.diag)

    def zf(self, d):
        return ((self.z + d) % 4) * 2 + self.x

    def barrier(self):
        sem = pltpu.get_barrier_semaphore()
        for p in self.exp_peers:
            pl.semaphore_signal(sem, inc=1, device_id=(p, self.f), device_id_type=MESH)
        for d in (1, 2, 3):
            pl.semaphore_signal(sem, inc=1, device_id=(self.e, self.zf(d)), device_id_type=MESH)
        pl.semaphore_signal(sem, inc=1, device_id=(self.e, self.xf), device_id_type=MESH)
        pl.semaphore_wait(sem, 7)

    def send(self, src, dst, ss, rs, e=None, f=None):
        return pltpu.make_async_remote_copy(
            src_ref=src,
            dst_ref=dst,
            send_sem=ss,
            recv_sem=rs,
            device_id=(self.e if e is None else e, self.f if f is None else f),
            device_id_type=MESH,
        )


def lane_of(shape):
    return lax.broadcasted_iota(jnp.int32, shape, len(shape) - 1)


def ka_kernel(
    x_ref, u_ref, wq_ref, wo_ref, wg_ref, wu_ref, wd_ref, gres_ref, routes_ref, routes_t_ref, starts_ref,
    gain_a_ref, gain_f_ref, router_ref, proj_ref, mix_ref,
    attn_all, q_s, k_s, v_s, o_s, lse_s, hidden_ref, logit_ref, pair_ref, place_ref, recv, wo_full, wq_full,
    gate_full, up_full, down_full,
    attn_recv, nb, snd, m_s, l_s, acc_s, gsel,
    wq_ss, wq_rs, wo_ss, wo_rs, at_ss, at_rs, o_ss, o_rs, d_ss, d_rs,
    us, ur, ds, dr, xs, xr, loc,
):
    me = Place()
    e, f, z, xf = me.e, me.f, me.z, me.xf
    T, D = x_ref.shape
    C = D // 4
    R = wo_ref.shape[0]
    me.barrier()

    def rows(ref, index):
        return ref.at[pl.ds(pl.multiple_of(index * R, 32), R)]

    early = ((wq_ref, wq_full, wq_ss, wq_rs, 0), (wo_ref, wo_full, wo_ss, wo_rs, 1))
    for src, dst, ss, rs, li in early:
        for d in (1, 3, 2):
            me.send(src, rows(dst, f), ss.at[d], rs.at[d], f=me.zf(d)).start()
        me.send(src, rows(dst, f), ss.at[0], rs.at[0], f=xf).start()
        pltpu.make_async_copy(src, rows(dst, f), loc.at[li]).start()

    xv = x_ref[...].astype(F32)
    inv = lax.rsqrt(jnp.mean(xv * xv, axis=-1, keepdims=True) + EPS)
    attn_all[e] = (xv * inv * gain_a_ref[...]).astype(BF)
    to_sib = me.send(attn_all.at[e], attn_all.at[e], at_ss.at[0], at_rs.at[0], e=me.sib)
    to_yp = me.send(attn_all.at[e], attn_all.at[e], at_ss.at[1], at_rs.at[1], e=me.yp)
    to_yp.start()
    to_sib.start()

    def early_in(dst, ss, rs, d):
        return me.send(rows(dst, f), rows(dst, ((z - d + 4) % 4) * 2 + me.x), ss.at[d], rs.at[d])

    def early_fwd(dst, ss, rs, d):
        slot = rows(dst, ((z - d + 4) % 4) * 2 + me.x)
        return me.send(slot, slot, ss.at[3 + d], rs.at[3 + d], f=xf)

    for src, dst, ss, rs, li in early:
        for d in (1, 3, 2):
            early_in(dst, ss, rs, d).wait_recv()
            early_fwd(dst, ss, rs, d).start()

    shards = ((wg_ref, gate_full), (wu_ref, up_full), (wd_ref, down_full))

    def up_send(w, p, src, slot):
        full = shards[w][1]
        return me.send(src, full.at[slot], us.at[w, p], ur.at[w, p], f=f + 2)

    def down_send(w, p, src, slot):
        full = shards[w][1]
        return me.send(src, full.at[slot], ds.at[w, p], dr.at[w, p], f=f - 2)

    def x_send(w, i, src, slot):
        full = shards[w][1]
        return me.send(src, full.at[slot], xs.at[w, i], xr.at[w, i], f=xf)

    def experts(p):
        for w, (src, full) in enumerate(shards):
            if p == 0:
                x_send(w, 0, src, f).start()

                @pl.when(z <= 2)
                def _():
                    up_send(w, 0, src, f).start()

                @pl.when(z >= 1)
                def _():
                    down_send(w, 0, src, f).start()

                pltpu.make_async_copy(src, full.at[f], loc.at[2 + w]).start()
            else:

                @pl.when(z >= p)
                def _():
                    slot = f - 2 * p
                    up_send(w, p - 1, full.at[slot], slot).wait_recv()
                    if p <= 2:

                        @pl.when(z <= 2)
                        def _():
                            up_send(w, p, full.at[slot], slot).start()

                    x_send(w, p, full.at[slot], slot).start()

                @pl.when(z + p <= 3)
                def _():
                    slot = f + 2 * p
                    down_send(w, p - 1, full.at[slot], slot).wait_recv()
                    if p <= 2:

                        @pl.when(z >= 1)
                        def _():
                            down_send(w, p, full.at[slot], slot).start()

                    x_send(w, 3 + p, full.at[slot], slot).start()

    experts(0)

    me.send(attn_all.at[me.yp], attn_all.at[me.yp], at_ss.at[1], at_rs.at[1]).wait_recv()
    fwd = me.send(attn_all.at[me.yp], attn_all.at[me.yp], at_ss.at[2], at_rs.at[2], e=me.sib)
    fwd.start()
    me.send(attn_all.at[me.sib], attn_all.at[me.sib], at_ss.at[0], at_rs.at[0]).wait_recv()
    me.send(attn_all.at[me.diag], attn_all.at[me.diag], at_ss.at[2], at_rs.at[2]).wait_recv()

    def early_wait(src, dst, ss, rs, li):
        pltpu.make_async_copy(src, rows(dst, f), loc.at[li]).wait()
        me.send(rows(dst, xf), rows(dst, xf), ss.at[0], rs.at[0]).wait_recv()
        for d in (1, 2, 3):
            slot = rows(dst, ((z - d + 4) % 4) * 2 + 1 - me.x)
            me.send(slot, slot, ss.at[3 + d], rs.at[3 + d]).wait_recv()

    early_wait(*early[0])

    def qkv_step(i, _):
        b = i // 2
        r = pl.ds(pl.multiple_of((i % 2) * 256, 256), 256)
        out = jnp.dot(attn_all[b, r, :], wq_full[...], preferred_element_type=F32)
        q_s[b, r, :] = (out[:, 0:C] * QSCALE).astype(BF)
        k_s[b, r, :] = pltpu.roll(out[:, 128:384], 192, 1)[:, 0:C].astype(BF)
        v_s[b, r, :] = out[:, 2 * C : 3 * C].astype(BF)
        return 0

    lax.fori_loop(0, 8, qkv_step, 0)
    experts(1)

    lse_s[...] = jnp.zeros_like(lse_s)
    head_of = lane_of((T, C)) // HD

    def head_step(i, _):
        qb = i // 3
        h = i % 3
        qh = jnp.where(head_of == h, q_s[qb], jnp.zeros((T, C), BF))
        s = lax.dot_general(qh, k_s[qb], (((1,), (1,)), ((), ())), preferred_element_type=F32)
        col = lane_of((T, T))
        row = lax.broadcasted_iota(jnp.int32, (T, T), 0)
        first = starts_ref[0, qb] - qb * T
        inside_c = (col >= first) & (col < first + PIECE)
        inside_r = (row >= first) & (row < first + PIECE)
        s = jnp.where((col <= row) | (inside_c & inside_r), s, NEG)
        m = jnp.max(s, axis=-1, keepdims=True)
        p = jnp.exp2(s - m)
        m_s[...] = m
        l_s[...] = jnp.sum(p, axis=-1, keepdims=True)
        acc_s[...] = jnp.dot(p.astype(BF), v_s[qb], preferred_element_type=F32)

        def kv_step(kb, _):
            s = lax.dot_general(qh, k_s[kb], (((1,), (1,)), ((), ())), preferred_element_type=F32)
            m_old = m_s[...]
            m = jnp.maximum(m_old, jnp.max(s, axis=-1, keepdims=True))
            scale = jnp.exp2(m_old - m)
            p = jnp.exp2(s - m)
            m_s[...] = m
            l_s[...] = l_s[...] * scale + jnp.sum(p, axis=-1, keepdims=True)
            acc_s[...] = acc_s[...] * scale + jnp.dot(p.astype(BF), v_s[kb], preferred_element_type=F32)
            return 0

        lax.fori_loop(0, qb, kv_step, 0)
        total = l_s[...]
        o_s[qb] = jnp.where(head_of == h, (acc_s[...] / total).astype(BF), o_s[qb])
        lse = m_s[...] + jnp.log2(total)
        lse_s[qb] = jnp.where(lane_of((T, 8)) == h, lse, lse_s[qb])
        return 0

    lax.fori_loop(0, 12, head_step, 0)

    for i, p in enumerate(me.exp_peers):
        me.send(o_s.at[p], attn_recv.at[e], o_ss.at[i], o_rs.at[i], e=p).start()
    attn_recv[e] = o_s[e]
    experts(2)

    r0, r1 = routes_t_ref[0:1, :], routes_t_ref[1:2, :]
    expert = lax.broadcasted_iota(jnp.int32, (8, T), 0)
    has = (expert == r0) | (expert == r1)
    earlier = (lax.broadcasted_iota(jnp.int32, (T, T), 0) < lane_of((T, T))).astype(BF)
    count = jnp.dot(has.astype(BF), earlier, preferred_element_type=F32).astype(jnp.int32)
    count = jnp.where(has, count, -1)
    slot_id = lax.broadcasted_iota(jnp.int32, (CAP, T), 0)
    for k in range(4):
        place_ref[k] = jnp.where(slot_id == count[k : k + 1, :], 1.0, 0.0).astype(BF)

    early_wait(*early[1])
    for i, p in enumerate(me.exp_peers):
        me.send(attn_recv.at[p], attn_recv.at[p], o_ss.at[i], o_rs.at[i]).wait_recv()

    def hidden_step(i, _):
        r = pl.ds(pl.multiple_of(i * 256, 256), 256)
        h = x_ref[r, :].astype(F32)
        for b in range(4):
            h = h + jnp.dot(attn_recv[b, r, :], wo_full[b * C : (b + 1) * C, :], preferred_element_type=F32)
        hidden_ref[r, :] = h
        n = h * lax.rsqrt(jnp.mean(h * h, axis=-1, keepdims=True) + EPS) * gain_f_ref[...]
        nb[r, :] = n.astype(BF)
        logits = jnp.dot(n, router_ref[...], precision=HIGH, preferred_element_type=F32)
        logits = logits + jnp.dot(gres_ref[r, :], mix_ref[...], precision=HIGH, preferred_element_type=F32)
        logit_ref[r, :] = logits
        pair_ref[r, :] = jnp.dot(n, proj_ref[...], precision=HIGH, preferred_element_type=F32)
        gsel[r, :] = gates_of(logits, routes_ref[r, :])
        return 0

    lax.fori_loop(0, 2, hidden_step, 0)

    def dispatch_step(k, _):
        place = place_ref[k]
        snd[k, 0] = jnp.dot(place, nb[...], preferred_element_type=F32).astype(BF)
        gate = jnp.sum(jnp.where(lane_of((T, 8)) == k, gsel[...], 0.0), axis=-1, keepdims=True)
        gu = (gate * u_ref[...].astype(F32)).astype(BF)
        snd[k, 1] = jnp.dot(place, gu, preferred_element_type=F32).astype(BF)
        return 0

    lax.fori_loop(0, 4, dispatch_step, 0)
    for i, p in enumerate(me.exp_peers):
        me.send(snd.at[p], recv.at[e], d_ss.at[i], d_rs.at[i], e=p).start()
    recv[e] = snd[e]
    experts(3)

    for src, dst, ss, rs, li in early:
        for j in range(4):
            me.send(src, rows(dst, f), ss.at[j], rs.at[j]).wait_send()
        for d in (1, 2, 3):
            early_fwd(dst, ss, rs, d).wait_send()
    to_sib.wait_send()
    to_yp.wait_send()
    fwd.wait_send()
    for i, p in enumerate(me.exp_peers):
        me.send(o_s.at[p], attn_recv.at[e], o_ss.at[i], o_rs.at[i]).wait_send()
        me.send(snd.at[p], recv.at[p], d_ss.at[i], d_rs.at[i]).wait()
    for w, (src, full) in enumerate(shards):
        pltpu.make_async_copy(src, full.at[f], loc.at[2 + w]).wait()
        x_send(w, 0, src, xf).wait()

        @pl.when(z <= 2)
        def _():
            up_send(w, 0, src, f).wait_send()

        @pl.when(z >= 1)
        def _():
            down_send(w, 0, src, f).wait_send()

        for p in (1, 2, 3):

            @pl.when(z >= p)
            def _():
                slot = f - 2 * p
                if p <= 2:

                    @pl.when(z <= 2)
                    def _():
                        up_send(w, p, full.at[slot], slot).wait_send()

                x_send(w, p, full.at[slot], xf - 2 * p).wait()

            @pl.when(z + p <= 3)
            def _():
                slot = f + 2 * p
                if p <= 2:

                    @pl.when(z >= 1)
                    def _():
                        down_send(w, p, full.at[slot], slot).wait_send()

                x_send(w, 3 + p, full.at[slot], xf + 2 * p).wait()


def gates_of(logits, routes):
    lane = lane_of(logits.shape)
    chosen = (lane == routes[:, 0:1]) | (lane == routes[:, 1:2])
    top = jnp.max(jnp.where(chosen, logits, NEG), axis=-1, keepdims=True)
    weight = jnp.where(chosen, jnp.exp(logits - top), 0.0)
    return weight / jnp.sum(weight, axis=-1, keepdims=True)


def sds(shape, dtype):
    return jax.ShapeDtypeStruct(shape, dtype)


def vmem():
    return pl.BlockSpec(memory_space=pltpu.VMEM)


def anyspace():
    return pl.BlockSpec(memory_space=pl.ANY)


def call_ka(x, u, wq, wo, wg, wu, wd, gres, routes, routes_t, starts, gain_a, gain_f, router, proj, mix):
    T, D = x.shape
    C = D // 4
    FF = wg.shape[1]
    R = wo.shape[0]
    dma = pltpu.SemaphoreType.DMA
    return pl.pallas_call(
        ka_kernel,
        name="forward",
        out_shape=(
            sds((4, T, D), BF),
            sds((4, T, C), BF), sds((4, T, C), BF), sds((4, T, C), BF), sds((4, T, C), BF),
            sds((4, T, 8), F32),
            sds((T, D), F32),
            sds((T, 8), F32), sds((T, 4), F32),
            sds((4, CAP, T), BF),
            sds((4, 2, CAP, D), BF),
            sds((D, D), BF),
            sds((D, 3 * C), BF),
            sds((8, R, FF), BF), sds((8, R, FF), BF), sds((8, FF // 8, D), BF),
        ),
        in_specs=[vmem(), vmem(), anyspace(), anyspace(), anyspace(), anyspace(), anyspace(), vmem(), vmem(), vmem(),
                  pl.BlockSpec(memory_space=pltpu.SMEM)] + [vmem()] * 5,
        out_specs=tuple([vmem()] * 13 + [anyspace()] * 3),
        scratch_shapes=[
            pltpu.VMEM((4, T, C), BF),
            pltpu.VMEM((T, D), BF),
            pltpu.VMEM((4, 2, CAP, D), BF),
            pltpu.VMEM((T, 1), F32),
            pltpu.VMEM((T, 1), F32),
            pltpu.VMEM((T, C), F32),
            pltpu.VMEM((T, 8), F32),
            dma((7,)), dma((7,)), dma((7,)), dma((7,)),
            dma((3,)), dma((3,)), dma((3,)), dma((3,)), dma((3,)), dma((3,)),
            dma((3, 3)), dma((3, 3)), dma((3, 3)), dma((3, 3)), dma((3, 7)), dma((3, 7)),
            dma((5,)),
        ],
        compiler_params=pltpu.CompilerParams(collective_id=0, has_side_effects=True, vmem_limit_bytes=56 << 20),
    )(x, u, wq, wo, wg, wu, wd, gres, routes, routes_t, starts, gain_a, gain_f, router, proj, mix)


def dot(a, b, ca=1, cb=0):
    return lax.dot_general(a, b, (((ca,), (cb,)), ((), ())), preferred_element_type=F32)


def kf_kernel(
    recv, gate_hbm, up_hbm, down_hbm,
    ret, grad_gate, grad_up, grad_down,
    gate, up, down, gate_pre, up_pre, inner, d_gate, d_up, rows, d_rows_in, acc, out, d_out,
    e_ss, e_rs, r_ss, r_rs, loc,
):
    me = Place()
    e, f = me.e, me.f
    n, _, cap, D = recv.shape
    S = n * cap
    chunks = down.shape[0]
    W = down.shape[1]
    loads = []
    for i, (src, dst) in enumerate(((gate_hbm, gate), (up_hbm, up), (down_hbm, down))):
        loads.append(pltpu.make_async_copy(src, dst, loc.at[i]))
        loads[-1].start()
    sem = pltpu.get_barrier_semaphore()
    for p in me.exp_peers:
        pl.semaphore_signal(sem, inc=1, device_id=(p, f), device_id_type=MESH)
    pl.semaphore_wait(sem, 3)
    for k in range(n):
        rows[k * cap : (k + 1) * cap, :] = recv[k, 0]
        d_rows_in[k * cap : (k + 1) * cap, :] = recv[k, 1]
    acc[...] = jnp.zeros_like(acc)
    for load in loads:
        load.wait()

    def cols(ref, c):
        return ref[:, :, pl.ds(pl.multiple_of(c * W, 256), W)].reshape(D, W)

    def forward_step(c, _):
        g = dot(rows[...], cols(gate, c))
        u = dot(rows[...], cols(up, c))
        gate_pre[c] = g
        up_pre[c] = u
        v = (g / (1.0 + jnp.exp(-g)) * u).astype(BF)
        inner[c] = v
        acc[...] += dot(v, down[c])
        return 0

    lax.fori_loop(0, chunks, forward_step, 0)
    for k in range(n):
        out[k] = acc[k * cap : (k + 1) * cap, :].astype(BF)
    for i, p in enumerate(me.exp_peers):
        me.send(out.at[p], ret.at[e, 0], e_ss.at[i], e_rs.at[i], e=p).start()
    ret[e, 0] = out[e]
    acc[...] = jnp.zeros_like(acc)

    def backward_step(c, _):
        d_inner = dot(d_rows_in[...], down[c], 1, 1)
        g = gate_pre[c]
        sig = 1.0 / (1.0 + jnp.exp(-g))
        silu = g * sig
        du = (d_inner * silu).astype(BF)
        dg = (d_inner * up_pre[c] * (sig + silu * (1.0 - sig))).astype(BF)
        d_up[c] = du
        d_gate[c] = dg
        acc[...] += dot(dg, cols(gate, c), 1, 1) + dot(du, cols(up, c), 1, 1)
        return 0

    lax.fori_loop(0, chunks, backward_step, 0)
    for k in range(n):
        d_out[k] = acc[k * cap : (k + 1) * cap, :].astype(BF)
    for i, p in enumerate(me.exp_peers):
        me.send(d_out.at[p], ret.at[e, 1], r_ss.at[i], r_rs.at[i], e=p).start()
    ret[e, 1] = d_out[e]

    def grad_step(c, _):
        grad_down[c] = dot(inner[c], d_rows_in[...], 0, 0).astype(BF)
        w = pl.ds(pl.multiple_of(c * W, 256), W)
        grad_gate[:, :, w] = dot(rows[...], d_gate[c], 0, 0).astype(BF).reshape(chunks, D // chunks, W)
        grad_up[:, :, w] = dot(rows[...], d_up[c], 0, 0).astype(BF).reshape(chunks, D // chunks, W)
        return 0

    lax.fori_loop(0, chunks, grad_step, 0)
    for i, p in enumerate(me.exp_peers):
        me.send(out.at[p], ret.at[p, 0], e_ss.at[i], e_rs.at[i]).wait()
        me.send(d_out.at[p], ret.at[p, 1], r_ss.at[i], r_rs.at[i]).wait()


def call_kf(recv, gate, up, down):
    n, _, cap, D = recv.shape
    S = n * cap
    chunks, W, _ = down.shape
    dma = pltpu.SemaphoreType.DMA
    return pl.pallas_call(
        kf_kernel,
        name="experts",
        out_shape=(sds(recv.shape, BF), sds(gate.shape, BF), sds(up.shape, BF), sds(down.shape, BF)),
        in_specs=[vmem(), anyspace(), anyspace(), anyspace()],
        out_specs=(vmem(), vmem(), vmem(), vmem()),
        scratch_shapes=[
            pltpu.VMEM(gate.shape, BF), pltpu.VMEM(up.shape, BF), pltpu.VMEM(down.shape, BF),
            pltpu.VMEM((chunks, S, W), F32), pltpu.VMEM((chunks, S, W), F32),
            pltpu.VMEM((chunks, S, W), BF), pltpu.VMEM((chunks, S, W), BF), pltpu.VMEM((chunks, S, W), BF),
            pltpu.VMEM((S, D), BF), pltpu.VMEM((S, D), BF), pltpu.VMEM((S, D), F32),
            pltpu.VMEM((n, cap, D), BF), pltpu.VMEM((n, cap, D), BF),
            dma((3,)), dma((3,)), dma((3,)), dma((3,)), dma((3,)),
        ],
        compiler_params=pltpu.CompilerParams(collective_id=1, has_side_effects=True, vmem_limit_bytes=57 << 20),
    )(recv, gate, up, down)


LN2 = math.log(2.0)


def kb_kernel(
    ret, hidden, u_ref, x_ref, logit_ref, pair_ref, routes_ref, place_ref, gres_ref,
    attn_all, q_s, k_s, v_s, o_s, lse_s, wo, wqkv, gain_a_ref, gain_f_ref, router_ref, proj_ref, mix_ref, cvec_ref, starts_ref,
    g_gate, g_up, g_down,
    layer_out, grad_tokens, d_res, small_out, ag_out, go_out, eg_out, eu_out, ed_out,
    xin_g, xin_u, xin_d, own_g, own_u, own_d, zin_g, zin_u, zin_d,
    dh_all, da, dq, dk, dv, dq_acc, pin, py_in, d_hidden, wk_s, lse_r, del_r, gt, ag_s, ag_in, ag_fin, go_s, go_in, go_b,
    small, sm1, sm2,
    xs, xr, zs, zr, own_sem, dh_ss, dh_rs, go_ss, go_rs, gb_ss, gb_rs, pd_ss, pd_rs, ag_ss, ag_rs, ab_ss, ab_rs, s1_ss, s1_rs, s2_ss, s2_rs,
):
    me = Place()
    e, f, z, x, xf = me.e, me.f, me.z, me.x, me.xf
    T, D = x_ref.shape
    C = D // 4
    R = D // 8

    def fp(r):
        return (f + r) % 8

    sem = pltpu.get_barrier_semaphore()
    for p in me.exp_peers:
        pl.semaphore_signal(sem, inc=1, device_id=(p, f), device_id_type=MESH)
    for r in range(1, 8):
        pl.semaphore_signal(sem, inc=1, device_id=(e, fp(r)), device_id_type=MESH)
    pl.semaphore_wait(sem, 10)

    parts = ((g_gate, xin_g, own_g, zin_g), (g_up, xin_u, own_u, zin_u), (g_down, xin_d, own_d, zin_d))

    def row_of(d):
        return (z + d) % 4

    def x_copy(w, d):
        g, xin = parts[w][0], parts[w][1]
        zz = row_of(d)
        return me.send(g.at[2 * zz + 1 - x], xin.at[zz], xs.at[w, d], xr.at[w, d], f=xf)

    def own_copy(w, d):
        g, own = parts[w][0], parts[w][2]
        return pltpu.make_async_copy(g.at[2 * row_of(d) + x], own, own_sem.at[w])

    def z_copy(w, d):
        xin, zin = parts[w][1], parts[w][3]
        return me.send(xin.at[row_of(d)], zin.at[d - 1], zs.at[w, d - 1], zr.at[w, d - 1], f=me.zf(d))

    def rs_send(d):
        for w in range(3):
            x_copy(w, d).start()

    after = {2: 1, 1: 3, 3: 0}

    def rs_mid(d, w):
        xin, own = parts[w][1], parts[w][2]
        x_copy(w, d).wait_recv()
        own_copy(w, d).wait()
        zz = row_of(d)
        if d:
            xin[zz] = (xin[zz].astype(F32) + own[...].astype(F32)).astype(BF)
            z_copy(w, d).start()
            own_copy(w, after[d]).start()

    def rs_mid_all(d):
        for w in range(3):
            rs_mid(d, w)

    for w in range(3):
        own_copy(w, 2).start()
    rs_send(2)
    rs_send(1)

    small[...] = jnp.zeros_like(small)
    cv0, cv1 = cvec_ref[0:1, :], cvec_ref[1:2, :]
    lane8 = lane_of((128, 8))

    def pick(values, k):
        return jnp.sum(jnp.where(lane_of(values.shape) == k, values, 0.0), axis=-1, keepdims=True)

    def mix_step(i, _):
        r = pl.ds(pl.multiple_of(i * 128, 128), 128)
        h = hidden[r, :]
        u = u_ref[r, :].astype(F32)
        inv = lax.rsqrt(jnp.mean(h * h, axis=-1, keepdims=True) + EPS)
        hn = h * inv
        n = hn * gain_f_ref[...]
        gates = gates_of(logit_ref[r, :], routes_ref[r, :])
        pairs = pair_ref[r, :]
        p0, p1, p2, p3 = pairs[:, 0:1], pairs[:, 1:2], pairs[:, 2:3], pairs[:, 3:4]
        a0 = 1.0 / (1.0 + jnp.exp(p1 - p0))
        b0 = 1.0 / (1.0 + jnp.exp(p0 - p1))
        a1 = 1.0 / (1.0 + jnp.exp(p3 - p2))
        b1 = 1.0 / (1.0 + jnp.exp(p2 - p3))
        g5, g6, g7 = pick(gates, 5), pick(gates, 6), pick(gates, 7)
        c_n = g5 + g6 * a0 + g7 * a1
        c0 = g6 * b0
        c1 = g7 * b1
        mixed = h + c_n * n + c0 * cv0 + c1 * cv1
        dg = jnp.zeros((128, 8), F32)
        dn = c_n * u
        for k in range(4):
            place = place_ref[k, :, r]
            rk = dot(place, ret[k, 0], 0, 0)
            mixed = mixed + pick(gates, k) * rk
            dg = jnp.where(lane8 == k, jnp.sum(u * rk, axis=-1, keepdims=True), dg)
            dn = dn + dot(place, ret[k, 1], 0, 0)
        layer_out[r, :] = mixed.astype(BF)
        un = jnp.sum(u * n, axis=-1, keepdims=True)
        uv0 = jnp.sum(u * cv0, axis=-1, keepdims=True)
        uv1 = jnp.sum(u * cv1, axis=-1, keepdims=True)
        dg = jnp.where(lane8 == 5, un, dg)
        dg = jnp.where(lane8 == 6, a0 * un + b0 * uv0, dg)
        dg = jnp.where(lane8 == 7, a1 * un + b1 * uv1, dg)
        dlog = gates * (dg - jnp.sum(gates * dg, axis=-1, keepdims=True))
        e0 = g6 * a0 * b0 * (un - uv0)
        e1 = g7 * a1 * b1 * (un - uv1)
        lane4 = lane_of((128, 4))
        dpair = jnp.where(lane4 == 0, e0, jnp.where(lane4 == 1, -e0, jnp.where(lane4 == 2, e1, -e1)))
        d_res[r, :] = lax.dot_general(dlog, mix_ref[...], (((1,), (1,)), ((), ())), precision=HIGH, preferred_element_type=F32)
        dn = dn + lax.dot_general(dlog, router_ref[...], (((1,), (1,)), ((), ())), precision=HIGH, preferred_element_type=F32)
        dn = dn + lax.dot_general(dpair, proj_ref[...], (((1,), (1,)), ((), ())), precision=HIGH, preferred_element_type=F32)
        small[0:8, :] += lax.dot_general(dlog, n, (((0,), (0,)), ((), ())), precision=HIGH, preferred_element_type=F32)
        small[8:12, :] += lax.dot_general(dpair, n, (((0,), (0,)), ((), ())), precision=HIGH, preferred_element_type=F32)
        small[12:13, :] += jnp.sum(c0 * u, axis=0, keepdims=True)
        small[13:14, :] += jnp.sum(c1 * u, axis=0, keepdims=True)
        small[14:15, :] += jnp.sum(dn * hn, axis=0, keepdims=True)
        small[16:24, 0:8] += lax.dot_general(gres_ref[r, :], dlog, (((0,), (0,)), ((), ())), precision=HIGH, preferred_element_type=F32)
        gd = dn * gain_f_ref[...]
        dh = u + inv * (gd - hn * jnp.mean(gd * hn, axis=-1, keepdims=True))
        d_hidden[r, :] = dh
        dh_all[e, r, :] = dh.astype(BF)
        return 0

    lax.fori_loop(0, T // 128, mix_step, 0)

    mine = dh_all.at[e]
    me.send(mine, mine, dh_ss.at[1], dh_rs.at[1], e=me.yp).start()
    me.send(mine, mine, dh_ss.at[0], dh_rs.at[0], e=me.sib).start()
    rs_mid_all(2)
    rs_send(3)
    wide = pltpu.roll(wqkv[:, 128:384].astype(F32), 192, 1)
    wk_s[...] = wide[:, 0:C].astype(BF)
    head_of = lane_of((T, C)) // HD
    eye = (lax.broadcasted_iota(jnp.int32, (8, 8), 0) == lane_of((8, 8))).astype(F32)
    heads = (lax.broadcasted_iota(jnp.int32, (8, C), 0) == lane_of((8, C)) // HD).astype(F32)
    dk[...] = jnp.zeros_like(dk)
    dv[...] = jnp.zeros_like(dv)
    for b in range(4):
        lse_r[b] = lax.dot_general(eye, lse_s[b], (((1,), (1,)), ((), ())), precision=HIGH, preferred_element_type=F32)
    slot = dh_all.at[me.yp]
    me.send(slot, slot, dh_ss.at[1], dh_rs.at[1]).wait_recv()
    fwd = me.send(slot, slot, dh_ss.at[2], dh_rs.at[2], e=me.sib)
    fwd.start()
    slot = dh_all.at[me.sib]
    me.send(slot, slot, dh_ss.at[0], dh_rs.at[0]).wait_recv()
    slot = dh_all.at[me.diag]
    me.send(slot, slot, dh_ss.at[2], dh_rs.at[2]).wait_recv()

    gt[0] = jnp.zeros((C, D), F32)

    def da_step(b, _):
        dhb = dh_all[b]
        d = dot(dhb, wo[pl.ds(pl.multiple_of(e * C, 64), C), :], 1, 1)
        low = d.astype(BF)
        da[b] = low
        ob = o_s[b]
        del_r[b] = lax.dot_general(
            heads, low.astype(F32) * ob.astype(F32), (((1,), (1,)), ((), ())), precision=HIGH, preferred_element_type=F32
        )
        gt[0] += dot(ob, dhb, 0, 0)
        return 0

    lax.fori_loop(0, 4, da_step, 0)
    go_s[0] = gt[0, 0:R, :].astype(BF)
    go_s[1] = gt[0, R : 2 * R, :].astype(BF)
    for j in range(2):

        @pl.when(f != 2 * e + j)
        def _():
            me.send(go_s.at[j], go_in.at[f], go_ss.at[j], go_rs.at[f], f=2 * e + j).start()

    rs_mid_all(1)
    rs_send(0)

    def head_step(i, _):
        qb = i // 3
        h = i % 3
        zero = jnp.zeros((T, C), BF)
        qh = jnp.where(head_of == h, q_s[qb], zero)
        dah = jnp.where(head_of == h, da[qb], zero)
        lse = lse_r[qb, pl.ds(h, 1), :]
        delta = del_r[qb, pl.ds(h, 1), :]

        def pair(kb, p):
            dp = dot(v_s[kb], dah, 1, 1)
            ds = (p * (dp - delta)).astype(BF)
            dv[kb] += dot(p.astype(BF), dah)
            dk[kb] += dot(ds, qh)
            return dot(ds, k_s[kb], 0, 0)

        row = lane_of((T, T))
        col = lax.broadcasted_iota(jnp.int32, (T, T), 0)
        first = starts_ref[0, qb] - qb * T
        inside_c = (col >= first) & (col < first + PIECE)
        inside_r = (row >= first) & (row < first + PIECE)
        s = dot(k_s[qb], qh, 1, 1)
        p = jnp.where((col <= row) | (inside_c & inside_r), jnp.exp2(s - lse), 0.0)
        dq_acc[...] = pair(qb, p)

        def kv_step(kb, _):
            s = dot(k_s[kb], qh, 1, 1)
            dq_acc[...] += pair(kb, jnp.exp2(s - lse))
            return 0

        lax.fori_loop(0, qb, kv_step, 0)
        dq[qb] = jnp.where(head_of == h, dq_acc[...], dq[qb])
        return 0

    lax.fori_loop(0, 6, head_step, 0)
    rs_mid_all(3)
    lax.fori_loop(6, 12, head_step, 0)

    @pl.when(z == e)
    def _():
        total = go_s[x].astype(F32)
        for r in range(1, 8):
            s = go_in.at[fp(r)]
            me.send(s, s, go_ss.at[0], go_rs.at[fp(r)]).wait_recv()
            total = total + go_in[fp(r)].astype(F32)
        go_b[...] = total.astype(BF)
        for i, p in enumerate(me.exp_peers):
            me.send(go_b, go_b, gb_ss.at[i], gb_rs.at[0], e=p).start()

    for i in range(3):
        gt[i] = jnp.zeros((C, D), F32)

    def low(b):
        return (
            (dq[b] * (1.0 / math.sqrt(HD))).astype(BF),
            (dk[b] * LN2).astype(BF),
            dv[b].astype(BF),
        )

    def partial_in(b):
        low_q, low_k, low_v = low(b)
        out = dot(low_q, wqkv[:, 0:C], 1, 1)
        out = out + dot(low_k, wk_s[...], 1, 1)
        out = out + dot(low_v, wqkv[:, 2 * C : 3 * C], 1, 1)
        small[15:16, :] += jnp.sum(out * attn_all[b].astype(F32), axis=0, keepdims=True)
        return out

    for i in range(3):
        me.send(dh_all.at[e], dh_all.at[e], dh_ss.at[i], dh_rs.at[i]).wait_send()

    def far_step(i, _):
        b = (me.sib + 2 * i) % 4
        dh_all[b] = partial_in(b).astype(BF)
        return 0

    lax.fori_loop(0, 2, far_step, 0)
    me.send(dh_all.at[me.sib], pin.at[0], pd_ss.at[0], pd_rs.at[0], e=me.sib).start()
    me.send(dh_all.at[me.diag], pin.at[1], pd_ss.at[1], pd_rs.at[1], e=me.sib).start()

    def near_step(i, _):
        b = (e + 2 * (1 - i)) % 4
        dh_all[b] = partial_in(b).astype(BF)
        return 0

    lax.fori_loop(0, 2, near_step, 0)
    me.send(dh_all.at[me.sib], pin.at[0], pd_ss.at[0], pd_rs.at[0]).wait_recv()
    me.send(dh_all.at[me.sib], pin.at[1], pd_ss.at[1], pd_rs.at[1]).wait_recv()
    dh_all[me.yp] = (dh_all[me.yp].astype(F32) + pin[1].astype(F32)).astype(BF)
    me.send(dh_all.at[me.yp], py_in, pd_ss.at[2], pd_rs.at[2], e=me.yp).start()

    small[15:16, :] = small[15:16, :] / gain_a_ref[...]
    sm1[e] = small[...]
    for i, p in enumerate(me.exp_peers):
        me.send(small, sm1.at[e], s1_ss.at[i], s1_rs.at[i], e=p).start()

    def grad_step(b, _):
        a = attn_all[b]
        for i, part in enumerate(low(b)):
            gt[i] += dot(part, a, 0, 0)
        return 0

    lax.fori_loop(0, 4, grad_step, 0)
    for i in range(3):
        ag_s[:, i] = gt[i].T.astype(BF).reshape(8, R, C)
    for r in range(1, 8):
        me.send(ag_s.at[fp(r)], ag_in.at[f], ag_ss.at[r - 1], ag_rs.at[f], f=fp(r)).start()
    ag_in[f] = ag_s[f]

    for i, p in enumerate(me.exp_peers):
        me.send(small, sm1.at[p], s1_ss.at[i], s1_rs.at[i]).wait()
    sm2[f] = sm1[0] + sm1[1] + sm1[2] + sm1[3]
    for r in range(1, 8):
        me.send(sm2.at[f], sm2.at[f], s2_ss.at[r - 1], s2_rs.at[f], f=fp(r)).start()

    rs_mid_all(0)

    for r in range(1, 8):
        s = ag_in.at[fp(r)]
        me.send(s, s, ag_ss.at[r - 1], ag_rs.at[fp(r)]).wait_recv()
    for i in range(3):
        total = ag_in[0, i].astype(F32)
        for r in range(1, 8):
            total = total + ag_in[r, i].astype(F32)
        ag_fin[i] = total.astype(BF)
    for i, p in enumerate(me.exp_peers):
        me.send(ag_fin, ag_out.at[e], ab_ss.at[i], ab_rs.at[i], e=p).start()
    ag_out[e] = ag_fin[...]

    for r in range(1, 8):
        s = sm2.at[fp(r)]
        me.send(s, s, s2_ss.at[r - 1], s2_rs.at[fp(r)]).wait_recv()
    total = sm2[0]
    for r in range(1, 8):
        total = total + sm2[r]
    small_out[...] = total

    me.send(py_in, py_in, pd_ss.at[2], pd_rs.at[2]).wait_recv()

    def token_step(i, _):
        r = pl.ds(pl.multiple_of(i * 256, 256), 256)
        d = dh_all[e, r, :].astype(F32) + pin[0, r, :].astype(F32) + py_in[r, :].astype(F32)
        xv = x_ref[r, :].astype(F32)
        inv = lax.rsqrt(jnp.mean(xv * xv, axis=-1, keepdims=True) + EPS)
        xn = xv * inv
        gd = d * gain_a_ref[...]
        grad_tokens[r, :] = (d_hidden[r, :] + inv * (gd - xn * jnp.mean(gd * xn, axis=-1, keepdims=True))).astype(BF)
        return 0

    lax.fori_loop(0, 2, token_step, 0)

    @pl.when(z != e)
    def _():
        me.send(go_b, go_b, gb_ss.at[0], gb_rs.at[0]).wait_recv()

    go_out[...] = go_b[...].astype(F32)

    outs = (eg_out, eu_out, ed_out)
    for w in range(3):
        g, xin, own, zin = parts[w]
        for d in (1, 2, 3):
            z_copy(w, d).wait_recv()
        total = xin[z].astype(F32) + own[...].astype(F32)
        for d in range(3):
            total = total + zin[d].astype(F32)
        outs[w][...] = total

    for w in range(3):
        for d in range(4):
            x_copy(w, d).wait_send()
            if d:
                z_copy(w, d).wait_send()
    for j in range(2):

        @pl.when(f != 2 * e + j)
        def _():
            me.send(go_s.at[j], go_in.at[f], go_ss.at[j], go_rs.at[f]).wait_send()

    @pl.when(z == e)
    def _():
        for i in range(3):
            me.send(go_b, go_b, gb_ss.at[i], gb_rs.at[0]).wait_send()

    for i in range(3):
        me.send(py_in, py_in, pd_ss.at[i], pd_rs.at[i]).wait_send()
        me.send(ag_fin, ag_out.at[me.exp_peers[i]], ab_ss.at[i], ab_rs.at[i]).wait()
    for r in range(1, 8):
        me.send(ag_s.at[0], ag_in.at[f], ag_ss.at[r - 1], ag_rs.at[f]).wait_send()
        me.send(sm2.at[f], sm2.at[f], s2_ss.at[r - 1], s2_rs.at[f]).wait_send()


def call_kb(ret, hidden, u, x, logits, pair, routes, place, gres, attn_all, q, k, v, o, lse, wo, wqkv,
            gain_a, gain_f, router, proj, mix, cvec, starts, gg, gu, gd):
    T, D = x.shape
    C, R = D // 4, D // 8
    dma = pltpu.SemaphoreType.DMA
    VM = pltpu.VMEM
    shapes = (gg.shape[1:], gu.shape[1:], gd.shape[1:])
    return pl.pallas_call(
        kb_kernel,
        name="backward",
        out_shape=(
            sds((T, D), BF), sds((T, D), BF), sds((T, 8), F32), sds((24, D), F32),
            sds((4, 3, R, C), BF), sds((R, D), F32),
        ) + tuple(sds(s, F32) for s in shapes),
        in_specs=[vmem()] * 23 + [pl.BlockSpec(memory_space=pltpu.SMEM)] + [anyspace()] * 3,
        out_specs=tuple([vmem()] * 9),
        scratch_shapes=[VM((4,) + s, BF) for s in shapes] + [VM(s, BF) for s in shapes] + [VM((3,) + s, BF) for s in shapes] + [
            VM((4, T, D), BF), VM((4, T, C), BF), VM((4, T, C), F32), VM((4, T, C), F32), VM((4, T, C), F32),
            VM((T, C), F32), VM((2, T, D), BF), VM((T, D), BF), VM((T, D), F32),
            VM((D, C), BF), VM((4, 8, T), F32), VM((4, 8, T), F32), VM((3, C, D), F32),
            VM((8, 3, R, C), BF), VM((8, 3, R, C), BF), VM((3, R, C), BF), VM((2, R, D), BF), VM((8, R, D), BF), VM((R, D), BF),
            VM((24, D), F32), VM((4, 24, D), F32), VM((8, 24, D), F32),
            dma((3, 4)), dma((3, 4)), dma((3, 3)), dma((3, 3)), dma((3,)),
            dma((3,)), dma((3,)), dma((2,)), dma((8,)), dma((3,)), dma((1,)), dma((3,)), dma((3,)),
            dma((7,)), dma((8,)), dma((3,)), dma((3,)), dma((3,)), dma((3,)), dma((7,)), dma((8,)),
        ],
        compiler_params=pltpu.CompilerParams(collective_id=2, has_side_effects=True, vmem_limit_bytes=62 << 20),
    )(ret, hidden, u, x, logits, pair, routes, place, gres, attn_all, q, k, v, o, lse, wo, wqkv,
      gain_a, gain_f, router, proj, mix, cvec, starts, gg, gu, gd)


def body_fast(
    tokens, gate_res, routes, piece_starts, norm_attn, norm_ffn, w_query, w_key, w_value, w_out, router, mixing,
    const_proj, const_vec, w_gate, w_up, w_down, cotangent,
):
    x, u, gres, route_ids = tokens[0], cotangent[0], gate_res[0], routes[0]
    D = x.shape[1]
    C = D // 4
    first = lax.axis_index("exp") * C
    wqkv = jnp.concatenate([lax.dynamic_slice_in_dim(w, first, C, 1) for w in (w_query, w_key, w_value)], axis=1)
    gain_a, gain_f = norm_attn[None], norm_ffn[None]
    (attn_all, q, k, v, o, lse, hidden, logits, pair, place, recv, wo, wq, gate, up, down) = call_ka(
        x, u, wqkv, w_out, w_gate[0], w_up[0], w_down[0], gres, route_ids, route_ids.T, piece_starts,
        gain_a, gain_f, router, const_proj, mixing,
    )
    ret, gg, gu, gd = call_kf(recv, gate, up, down)
    layer_out, grad_tokens, d_res, small, ag, go, eg, eu, ed = call_kb(
        ret, hidden, u, x, logits, pair, route_ids, place, gres, attn_all, q, k, v, o, lse, wo, wq,
        gain_a, gain_f, router, const_proj, mixing, const_vec, piece_starts, gg, gu, gd,
    )
    qkv = ag.astype(F32).transpose(1, 2, 0, 3).reshape(3, D // 8, D)
    return (
        layer_out[None], grad_tokens[None], d_res[None], small[15], small[14], qkv[0], qkv[1], qkv[2], go,
        small[0:8].T, small[16:24, 0:8], small[8:12].T, small[12:14], eg[None], eu[None], ed[None],
    )


def solution(mesh):
    placed = (
        P("fsdp", "exp", None),
        P("fsdp", "exp", None),
        P("fsdp", "exp", None),
        P("fsdp", None),
        P(),
        P(),
        P("fsdp", None),
        P("fsdp", None),
        P("fsdp", None),
        P("fsdp", None),
        P(),
        P(),
        P(),
        P(),
        P("exp", "fsdp", None),
        P("exp", "fsdp", None),
        P("exp", "fsdp", None),
        P("fsdp", "exp", None),
    )
    return jax.shard_map(
        body_fast if (mesh.shape['exp'], mesh.shape['fsdp']) == (4, 8) else body,
        mesh=mesh,
        in_specs=placed,
        out_specs=(
            P("fsdp", "exp", None),
            P("fsdp", "exp", None),
            P("fsdp", "exp", None),
            P(),
            P(),
            P("fsdp", None),
            P("fsdp", None),
            P("fsdp", None),
            P("fsdp", None),
            P(),
            P(),
            P(),
            P(),
            P("exp", "fsdp", None),
            P("exp", "fsdp", None),
            P("exp", "fsdp", None),
        ),
        check_vma=False,
    )
```

```python
import math

import jax
import jax.numpy as jnp
from jax import lax
from jax.experimental import pallas as pl
from jax.experimental.pallas import tpu as pltpu
from jax.sharding import PartitionSpec as P

H = 12
HD = 64
PIECE = 256
KBLK = 512
CAP = 160


EPS = 1e-05
HIGH = lax.Precision.HIGHEST
NEG = -1e30


def rms_scale(values, gain_vec):
    inverse = lax.rsqrt(jnp.mean(values * values, axis=-1, keepdims=True) + EPS)
    return values * inverse * gain_vec


def piece_ids(positions, starts, extent):
    inside = (positions[:, None] >= starts[None, :]) & (
        positions[:, None] < starts[None, :] + extent
    )
    labels = jnp.arange(1, starts.shape[0] + 1, dtype=jnp.int32)
    return jnp.sum(jnp.where(inside, labels[None, :], 0), axis=1)


def reach_bounds(positions, starts, extent):
    inside = (positions[:, None] >= starts[None, :]) & (
        positions[:, None] < starts[None, :] + extent
    )
    piece_last = jnp.max(jnp.where(inside, starts[None, :] + extent - 1, 0))
    piece_first = jnp.min(jnp.where(inside, starts[None, :], positions[0]))
    upper = jnp.maximum(positions[-1], piece_last)
    lower = jnp.minimum(positions[0], piece_first)
    return (upper, lower)


def allowed_mask(query_pos, query_ids, key_pos, key_ids):
    causal = key_pos[None, :] <= query_pos[:, None]
    shared = (key_ids[None, :] == query_ids[:, None]) & (query_ids[:, None] > 0)
    return causal | shared


def slot_dest(route_ids, n_ffn, capacity):
    flat_ids = route_ids.reshape(-1)
    onehot = (flat_ids[:, None] == jnp.arange(n_ffn, dtype=jnp.int32)[None, :]).astype(jnp.int32)
    earlier = jnp.cumsum(onehot, axis=0) - onehot
    slot_pos = jnp.sum(earlier * onehot, axis=1)
    return jnp.where(flat_ids < n_ffn, flat_ids * capacity + slot_pos, n_ffn * capacity)


def local_mix(
    normed, res_logits, router, mixing, const_proj, const_vec, expert_rows, route_ids, n_ffn
):
    n_all = router.shape[1]
    logits = jnp.dot(normed, router, precision=HIGH) + jnp.dot(res_logits, mixing, precision=HIGH)
    probs = jax.nn.softmax(logits, axis=-1)
    labels = jnp.arange(n_all, dtype=jnp.int32)
    chosen = jnp.sum(
        jnp.where(route_ids[:, :, None] == labels[None, None, :], probs[:, None, :], 0.0), axis=-1
    )
    gates = chosen / jnp.sum(chosen, axis=1, keepdims=True)
    pair_logits = jnp.dot(normed, const_proj, precision=HIGH)
    first_pair = jax.nn.softmax(pair_logits[:, 0:2], axis=-1)
    second_pair = jax.nn.softmax(pair_logits[:, 2:4], axis=-1)
    first_const = first_pair[:, 0:1] * normed + first_pair[:, 1:2] * const_vec[0][None, :]
    second_const = second_pair[:, 0:1] * normed + second_pair[:, 1:2] * const_vec[1][None, :]
    mixed = jnp.zeros_like(normed)
    for route_k in range(2):
        route_id = route_ids[:, route_k : route_k + 1]
        entry = jnp.where(route_id < n_ffn, expert_rows[:, route_k], 0.0)
        entry = entry + jnp.where(route_id == n_ffn + 1, normed, 0.0)
        entry = entry + jnp.where(route_id == n_ffn + 2, first_const, 0.0)
        entry = entry + jnp.where(route_id == n_ffn + 3, second_const, 0.0)
        mixed = mixed + gates[:, route_k : route_k + 1] * entry
    return mixed


def swiglu_act(gate_pre, up_pre):
    return jax.nn.silu(gate_pre) * up_pre


def body(
    tokens,
    gate_res,
    routes,
    piece_starts,
    norm_attn,
    norm_ffn,
    w_query,
    w_key,
    w_value,
    w_out,
    router,
    mixing,
    const_proj,
    const_vec,
    w_gate,
    w_up,
    w_down,
    cotangent,
):
    n_ffn = lax.axis_size("exp")
    rows_dev = tokens.shape[1]
    model_width = tokens.shape[2]
    seq_length = rows_dev * n_ffn
    score_scale = 1.0 / math.sqrt(HD)
    inputs_f = tokens[0].astype(jnp.float32)
    res_logits = gate_res[0]
    route_ids = routes[0]
    starts = piece_starts[0]
    full_query, full_key, full_value, full_out = (
        lax.all_gather(w_query, "fsdp", axis=0, tiled=True),
        lax.all_gather(w_key, "fsdp", axis=0, tiled=True),
        lax.all_gather(w_value, "fsdp", axis=0, tiled=True),
        lax.all_gather(w_out, "fsdp", axis=0, tiled=True),
    )
    attn_in = rms_scale(inputs_f, norm_attn).astype(jnp.bfloat16)
    query = jnp.dot(attn_in, full_query, preferred_element_type=jnp.float32).astype(jnp.bfloat16)
    key = jnp.dot(attn_in, full_key, preferred_element_type=jnp.float32).astype(jnp.bfloat16)
    value = jnp.dot(attn_in, full_value, preferred_element_type=jnp.float32).astype(jnp.bfloat16)
    keys_all, values_all = (
        lax.all_gather(key, "exp", axis=0, tiled=True),
        lax.all_gather(value, "exp", axis=0, tiled=True),
    )
    query_heads = query.reshape(rows_dev, H, HD)
    key_heads = keys_all.reshape(seq_length, H, HD)
    value_heads = values_all.reshape(seq_length, H, HD)
    query_pos = lax.axis_index("exp") * rows_dev + jnp.arange(rows_dev, dtype=jnp.int32)
    query_ids = piece_ids(query_pos, starts, PIECE)
    key_upper, query_lower = reach_bounds(query_pos, starts, PIECE)
    block_list = jnp.arange(seq_length // KBLK, dtype=jnp.int32)

    def score_block(block_index):
        key_first = block_index * KBLK
        key_block = lax.dynamic_slice_in_dim(key_heads, key_first, KBLK, 0)
        value_block = lax.dynamic_slice_in_dim(value_heads, key_first, KBLK, 0)
        key_pos = key_first + jnp.arange(KBLK, dtype=jnp.int32)
        key_ids = piece_ids(key_pos, starts, PIECE)
        scores = (
            jnp.einsum("qhd,khd->hqk", query_heads, key_block, preferred_element_type=jnp.float32)
            * score_scale
        )
        allowed = allowed_mask(query_pos, query_ids, key_pos, key_ids)[None]
        return (scores, allowed, key_block, value_block)

    def needed(block_index):
        return block_index * KBLK <= key_upper

    def lse_step(carry, block_index):

        def lse_active(state):
            run_max, run_sum = state
            scores, allowed, _, _ = score_block(block_index)
            scores = jnp.where(allowed, scores, NEG)
            new_max = jnp.maximum(run_max, jnp.max(scores, axis=-1))
            exp_terms = jnp.where(allowed, jnp.exp(scores - new_max[..., None]), 0.0)
            return (new_max, run_sum * jnp.exp(run_max - new_max) + jnp.sum(exp_terms, axis=-1))

        return (lax.cond(needed(block_index), lse_active, lambda state: state, carry), None)

    start_carry = (jnp.full((H, rows_dev), NEG, jnp.float32), jnp.zeros((H, rows_dev), jnp.float32))
    (run_max, run_sum), _ = lax.scan(lse_step, start_carry, block_list)
    log_norm = run_max + jnp.log(run_sum)

    def block_probs(scores, allowed):
        return jnp.where(allowed, jnp.exp(scores - log_norm[..., None]), 0.0)

    def out_step(accum, block_index):

        def out_active(total):
            scores, allowed, _, value_block = score_block(block_index)
            probs_low = block_probs(scores, allowed).astype(jnp.bfloat16)
            return total + jnp.einsum(
                "hqk,khd->qhd", probs_low, value_block, preferred_element_type=jnp.float32
            )

        return (lax.cond(needed(block_index), out_active, lambda total: total, accum), None)

    attn_sum, _ = lax.scan(out_step, jnp.zeros((rows_dev, H, HD), jnp.float32), block_list)
    attn_low = attn_sum.astype(jnp.bfloat16).reshape(rows_dev, model_width)
    hidden = inputs_f + jnp.dot(attn_low, full_out, preferred_element_type=jnp.float32)
    normed = rms_scale(hidden, norm_ffn)
    destination = slot_dest(route_ids, n_ffn, CAP)
    sources = jnp.arange(2 * rows_dev, dtype=jnp.int32) // 2
    slot_table = (
        jnp.full((n_ffn * CAP,), rows_dev, jnp.int32).at[destination].set(sources, mode="drop")
    )
    padded = jnp.concatenate(
        [normed.astype(jnp.bfloat16), jnp.zeros((1, model_width), jnp.bfloat16)], axis=0
    )
    dispatched = padded[slot_table].reshape(n_ffn, CAP, model_width)
    received = lax.all_to_all(dispatched, "exp", split_axis=0, concat_axis=0, tiled=True)
    full_gate, full_up, full_down = (
        lax.all_gather(w_gate[0], "fsdp", axis=0, tiled=True),
        lax.all_gather(w_up[0], "fsdp", axis=0, tiled=True),
        lax.all_gather(w_down[0], "fsdp", axis=0, tiled=True),
    )
    slot_rows = received.reshape(n_ffn * CAP, model_width)
    gate_pre = jnp.dot(slot_rows, full_gate, preferred_element_type=jnp.float32)
    up_pre = jnp.dot(slot_rows, full_up, preferred_element_type=jnp.float32)
    inner_act = swiglu_act(gate_pre, up_pre).astype(jnp.bfloat16)
    expert_result = jnp.dot(inner_act, full_down, preferred_element_type=jnp.float32).astype(
        jnp.bfloat16
    )
    returned = lax.all_to_all(
        expert_result.reshape(n_ffn, CAP, model_width),
        "exp",
        split_axis=0,
        concat_axis=0,
        tiled=True,
    )
    returned_pad = jnp.concatenate(
        [returned.reshape(n_ffn * CAP, model_width), jnp.zeros((1, model_width), jnp.bfloat16)],
        axis=0,
    )
    expert_rows = returned_pad[destination].astype(jnp.float32).reshape(rows_dev, 2, model_width)

    def mix_local(normed_in, logits_in, router_in, mixing_in, proj_in, vec_in, rows_in):
        return local_mix(
            normed_in, logits_in, router_in, mixing_in, proj_in, vec_in, rows_in, route_ids, n_ffn
        )

    moe_out, mix_pull = jax.vjp(
        mix_local, normed, res_logits, router, mixing, const_proj, const_vec, expert_rows
    )
    layer_out = (hidden + moe_out).astype(jnp.bfloat16)
    upstream = cotangent[0].astype(jnp.float32)
    d_normed_local, d_res_logits, d_router, d_mixing, d_const_proj, d_const_vec, d_expert_rows = (
        mix_pull(upstream)
    )
    d_rows_low = d_expert_rows.reshape(2 * rows_dev, model_width).astype(jnp.bfloat16)
    d_dispatched = (
        jnp.zeros((n_ffn * CAP, model_width), jnp.bfloat16)
        .at[destination]
        .set(d_rows_low, mode="drop")
    )
    d_received = lax.all_to_all(
        d_dispatched.reshape(n_ffn, CAP, model_width),
        "exp",
        split_axis=0,
        concat_axis=0,
        tiled=True,
    )
    d_received = d_received.reshape(n_ffn * CAP, model_width)
    d_inner = jnp.einsum("rd,fd->rf", d_received, full_down, preferred_element_type=jnp.float32)
    _, act_pull = jax.vjp(swiglu_act, gate_pre, up_pre)
    d_gate_pre, d_up_pre = act_pull(d_inner)
    d_gate_low = d_gate_pre.astype(jnp.bfloat16)
    d_up_low = d_up_pre.astype(jnp.bfloat16)
    grad_down_full = jnp.einsum(
        "rf,rd->fd", inner_act, d_received, preferred_element_type=jnp.float32
    )
    grad_gate_full = jnp.einsum(
        "rd,rf->df", slot_rows, d_gate_low, preferred_element_type=jnp.float32
    )
    grad_up_full = jnp.einsum("rd,rf->df", slot_rows, d_up_low, preferred_element_type=jnp.float32)
    d_slot_rows = (
        jnp.einsum("rf,df->rd", d_gate_low, full_gate, preferred_element_type=jnp.float32)
        + jnp.einsum("rf,df->rd", d_up_low, full_up, preferred_element_type=jnp.float32)
    ).astype(jnp.bfloat16)
    d_sent = lax.all_to_all(
        d_slot_rows.reshape(n_ffn, CAP, model_width), "exp", split_axis=0, concat_axis=0, tiled=True
    )
    d_sent_pad = jnp.concatenate(
        [d_sent.reshape(n_ffn * CAP, model_width), jnp.zeros((1, model_width), jnp.bfloat16)],
        axis=0,
    )
    d_normed_sent = jnp.sum(
        d_sent_pad[destination].astype(jnp.float32).reshape(rows_dev, 2, model_width), axis=1
    )
    _, norm_ffn_pull = jax.vjp(rms_scale, hidden, norm_ffn)
    d_hidden_part, d_norm_ffn = norm_ffn_pull(d_normed_local + d_normed_sent)
    d_hidden = upstream + d_hidden_part
    d_hidden_low = d_hidden.astype(jnp.bfloat16)
    grad_out_full = jnp.einsum(
        "td,te->de", attn_low, d_hidden_low, preferred_element_type=jnp.float32
    )
    d_attn = jnp.einsum(
        "te,de->td", d_hidden_low, full_out, preferred_element_type=jnp.float32
    ).astype(jnp.bfloat16)
    d_attn_heads = d_attn.reshape(rows_dev, H, HD)
    zero_block = jnp.zeros((KBLK, H, HD), jnp.float32)

    def delta_terms(block_index):
        scores, allowed, _, value_block = score_block(block_index)
        probs = block_probs(scores, allowed)
        d_probs = jnp.einsum(
            "qhd,khd->hqk", d_attn_heads, value_block, preferred_element_type=jnp.float32
        )
        part = jnp.sum(probs * d_probs, axis=-1)
        return (
            part,
            jnp.einsum(
                "hqk,qhd->khd",
                probs.astype(jnp.bfloat16),
                d_attn_heads,
                preferred_element_type=jnp.float32,
            ),
        )

    def query_terms(block_index, row_delta):
        scores, allowed, key_block, value_block = score_block(block_index)
        probs = block_probs(scores, allowed)
        d_probs = jnp.einsum(
            "qhd,khd->hqk", d_attn_heads, value_block, preferred_element_type=jnp.float32
        )
        d_scores = (probs * (d_probs - row_delta[..., None])).astype(jnp.bfloat16)
        part = (
            jnp.einsum("hqk,khd->qhd", d_scores, key_block, preferred_element_type=jnp.float32)
            * score_scale
        )
        return (
            part,
            jnp.einsum("hqk,qhd->khd", d_scores, query_heads, preferred_element_type=jnp.float32)
            * score_scale,
        )

    def delta_step(total, block_index):

        def delta_active(running):
            part, grad_block = delta_terms(block_index)
            return (running + part, grad_block)

        return lax.cond(
            needed(block_index), delta_active, lambda running: (running, zero_block), total
        )

    row_delta, grad_values = lax.scan(delta_step, jnp.zeros((H, rows_dev), jnp.float32), block_list)

    def query_step(total, block_index):

        def query_active(running):
            part, grad_block = query_terms(block_index, row_delta)
            return (running + part, grad_block)

        return lax.cond(
            needed(block_index), query_active, lambda running: (running, zero_block), total
        )

    d_query_sum, grad_keys = lax.scan(
        query_step, jnp.zeros((rows_dev, H, HD), jnp.float32), block_list
    )
    grad_keys = grad_keys.reshape(seq_length, model_width)
    grad_values = grad_values.reshape(seq_length, model_width)
    d_key_sum, d_value_sum = (
        lax.psum_scatter(
            grad_keys.astype(jnp.bfloat16), "exp", scatter_dimension=0, tiled=True
        ).astype(jnp.float32),
        lax.psum_scatter(
            grad_values.astype(jnp.bfloat16), "exp", scatter_dimension=0, tiled=True
        ).astype(jnp.float32),
    )
    d_query_low = d_query_sum.reshape(rows_dev, model_width).astype(jnp.bfloat16)
    d_key_low = d_key_sum.astype(jnp.bfloat16)
    d_value_low = d_value_sum.astype(jnp.bfloat16)
    d_attn_in = (
        jnp.einsum("te,de->td", d_query_low, full_query, preferred_element_type=jnp.float32)
        + jnp.einsum("te,de->td", d_key_low, full_key, preferred_element_type=jnp.float32)
        + jnp.einsum("te,de->td", d_value_low, full_value, preferred_element_type=jnp.float32)
    )
    grad_query_full = jnp.einsum(
        "td,te->de", attn_in, d_query_low, preferred_element_type=jnp.float32
    )
    grad_key_full = jnp.einsum("td,te->de", attn_in, d_key_low, preferred_element_type=jnp.float32)
    grad_value_full = jnp.einsum(
        "td,te->de", attn_in, d_value_low, preferred_element_type=jnp.float32
    )
    _, norm_attn_pull = jax.vjp(rms_scale, inputs_f, norm_attn)
    d_inputs_part, d_norm_attn = norm_attn_pull(d_attn_in)
    grad_tokens = (d_hidden + d_inputs_part).astype(jnp.bfloat16)
    attn_shards = (
        lax.psum_scatter(
            grad_query_full.astype(jnp.bfloat16), "fsdp", scatter_dimension=0, tiled=True
        ).astype(jnp.float32),
        lax.psum_scatter(
            grad_key_full.astype(jnp.bfloat16), "fsdp", scatter_dimension=0, tiled=True
        ).astype(jnp.float32),
        lax.psum_scatter(
            grad_value_full.astype(jnp.bfloat16), "fsdp", scatter_dimension=0, tiled=True
        ).astype(jnp.float32),
        lax.psum_scatter(
            grad_out_full.astype(jnp.bfloat16), "fsdp", scatter_dimension=0, tiled=True
        ).astype(jnp.float32),
    )
    attn_shards = (
        lax.psum(attn_shards[0].astype(jnp.bfloat16), "exp").astype(jnp.float32),
        lax.psum(attn_shards[1].astype(jnp.bfloat16), "exp").astype(jnp.float32),
        lax.psum(attn_shards[2].astype(jnp.bfloat16), "exp").astype(jnp.float32),
        lax.psum(attn_shards[3].astype(jnp.bfloat16), "exp").astype(jnp.float32),
    )
    expert_shards = (
        lax.psum_scatter(
            grad_gate_full.astype(jnp.bfloat16), "fsdp", scatter_dimension=0, tiled=True
        ).astype(jnp.float32),
        lax.psum_scatter(
            grad_up_full.astype(jnp.bfloat16), "fsdp", scatter_dimension=0, tiled=True
        ).astype(jnp.float32),
        lax.psum_scatter(
            grad_down_full.astype(jnp.bfloat16), "fsdp", scatter_dimension=0, tiled=True
        ).astype(jnp.float32),
    )
    small_sums = lax.psum(
        (d_norm_attn, d_norm_ffn, d_router, d_mixing, d_const_proj, d_const_vec), ("exp", "fsdp")
    )
    return (
        layer_out[None],
        grad_tokens[None],
        d_res_logits[None],
        small_sums[0],
        small_sums[1],
        attn_shards[0],
        attn_shards[1],
        attn_shards[2],
        attn_shards[3],
        small_sums[2],
        small_sums[3],
        small_sums[4],
        small_sums[5],
        expert_shards[0][None],
        expert_shards[1][None],
        expert_shards[2][None],
    )


MESH = pl.DeviceIdType.MESH
BF = jnp.bfloat16
F32 = jnp.float32
LN2 = math.log(2.0)
QSCALE = 1.0 / (LN2 * math.sqrt(HD))
CHUNKS = 4


class Place:
    def __init__(self):
        self.e = lax.axis_index("exp")
        self.f = lax.axis_index("fsdp")
        self.z = self.f // 2
        self.x = self.f % 2
        self.sib = self.e + 1 - 2 * (self.e % 2)
        self.yp = (self.e + 2) % 4
        self.diag = (self.sib + 2) % 4
        self.xf = self.f + 1 - 2 * self.x
        self.exp_peers = (self.sib, self.yp, self.diag)

    def zf(self, d):
        return ((self.z + d) % 4) * 2 + self.x

    def fp(self, r):
        return (self.f + r) % 8

    def far_first(self, j):
        return (self.e + (j % 2) * (1 - 2 * (self.e % 2)) + 2 * (1 - j // 2)) % 4

    def near_first(self, j):
        return (self.e + (j % 2) * (1 - 2 * (self.e % 2)) + 2 * (j // 2)) % 4

    def barrier(self):
        sem = pltpu.get_barrier_semaphore()
        for p in self.exp_peers:
            pl.semaphore_signal(sem, inc=1, device_id=(p, self.f), device_id_type=MESH)
        for r in range(1, 8):
            pl.semaphore_signal(sem, inc=1, device_id=(self.e, self.fp(r)), device_id_type=MESH)
        pl.semaphore_wait(sem, 10)

    def send(self, src, dst, ss, rs, e=None, f=None):
        return pltpu.make_async_remote_copy(
            src_ref=src,
            dst_ref=dst,
            send_sem=ss,
            recv_sem=rs,
            device_id=(self.e if e is None else e, self.f if f is None else f),
            device_id_type=MESH,
        )


def lane_of(shape):
    return lax.broadcasted_iota(jnp.int32, shape, len(shape) - 1)


def row_of(shape):
    return lax.broadcasted_iota(jnp.int32, shape, 0)


def dot(a, b, ca=1, cb=0, precision=None):
    return lax.dot_general(a, b, (((ca,), (cb,)), ((), ())), precision=precision, preferred_element_type=F32)


def allowed_block(size, first):
    key, query = row_of((size, size)), lane_of((size, size))
    inside_k = (key >= first) & (key < first + PIECE)
    inside_q = (query >= first) & (query < first + PIECE)
    return (key <= query) | (inside_k & inside_q)


def k1_kernel(
    x_ref, u_ref, wq_ref, wk_ref, wv_ref, wo_ref, wg_ref, wu_ref, wd_ref, gres_ref, routes_ref, starts_ref,
    gain_a_ref, gain_f_ref, router_ref, proj_ref, mix_ref,
    attn_all, q_s, k_s, v_s, o_s, lse_s, hidden_ref, aux_ref, place_ref, ret_o, ret_d, wo_full, wq_full,
    grad_gate, grad_up, grad_down, far_gate, far_up, far_down,
    gate_full, up_full, down_full, wq_own, vt_s, attn_recv, nb, snd_r, snd_d, recv_r, recv_d, m_s, l_s, acc_s,
    acc, d_acc, st_gate, st_up, st_down,
    wq_ss, wq_rs, wo_ss, wo_rs, at_ss, at_rs, o_ss, o_rs, dr_ss, dr_rs, dd_ss, dd_rs, ro_ss, ro_rs, rd_ss, rd_rs,
    us, ur, ds, dr, xs, xr, loc, st_sem, fs, fr,
):
    me = Place()
    e, f, z, xf = me.e, me.f, me.z, me.xf
    T, D = x_ref.shape
    C = D // 4
    R = wo_ref.shape[0]
    FF = wg_ref.shape[1]
    W = FF // CHUNKS
    S = 4 * CAP
    for k in range(4):

        @pl.when(e == k)
        def _():
            for i, w in enumerate((wq_ref, wk_ref, wv_ref)):
                wq_own[:, i * C : (i + 1) * C] = w[:, k * C : (k + 1) * C]

    me.barrier()

    def rows(ref, index):
        return ref.at[pl.ds(pl.multiple_of(index * R, 32), R)]

    early = ((wq_own, wq_full, wq_ss, wq_rs, 0), (wo_ref, wo_full, wo_ss, wo_rs, 1))
    for src, dst, ss, rs, li in early:
        for d in (1, 3, 2):
            me.send(src, rows(dst, f), ss.at[d], rs.at[d], f=me.zf(d)).start()
        me.send(src, rows(dst, f), ss.at[0], rs.at[0], f=xf).start()
        pltpu.make_async_copy(src, rows(dst, f), loc.at[li]).start()

    xv = x_ref[...].astype(F32)
    inv = lax.rsqrt(jnp.mean(xv * xv, axis=-1, keepdims=True) + EPS)
    attn_all[e] = (xv * inv * gain_a_ref[...].reshape(1, D)).astype(BF)

    def at_copy(i, block, to=None):
        ref = attn_all.at[block]
        return me.send(ref, ref, at_ss.at[i], at_rs.at[i], e=to)

    at_copy(1, e, me.yp).start()
    at_copy(0, e, me.sib).start()

    def early_slot(dst, d, other):
        return rows(dst, ((z - d + 4) % 4) * 2 + (1 - me.x if other else me.x))

    def early_forward(dst, ss, rs):
        for d in (1, 3, 2):
            slot = early_slot(dst, d, False)
            me.send(slot, slot, ss.at[d], rs.at[d]).wait_recv()
            me.send(slot, slot, ss.at[3 + d], rs.at[3 + d], f=xf).start()

    def early_wait(src, dst, ss, rs, li):
        pltpu.make_async_copy(src, rows(dst, f), loc.at[li]).wait()
        me.send(rows(dst, xf), rows(dst, xf), ss.at[0], rs.at[0]).wait_recv()
        for d in (1, 2, 3):
            slot = early_slot(dst, d, True)
            me.send(slot, slot, ss.at[3 + d], rs.at[3 + d]).wait_recv()

    early_forward(*early[0][1:4])

    units = [(wd_ref, down_full, None)]
    for c in range(CHUNKS):
        units += [(wg_ref, gate_full, c), (wu_ref, up_full, c)]

    def cut(ref, c):
        return ref if c is None else ref.at[:, pl.ds(pl.multiple_of(c * W, W), W)]

    def up_copy(n, p, src, dst, to=None):
        return me.send(src, dst, us.at[n, p], ur.at[n, p], f=to)

    def down_copy(n, p, src, dst, to=None):
        return me.send(src, dst, ds.at[n, p], dr.at[n, p], f=to)

    def x_copy(n, i, src, dst, to=None):
        return me.send(src, dst, xs.at[n, i], xr.at[n, i], f=to)

    def experts(p):
        for n, (src, full, c) in enumerate(units):

            def at(slot):
                return cut(full.at[slot], c)

            own = cut(src, c)
            if p == 0:
                x_copy(n, 0, own, at(f), xf).start()

                @pl.when(z <= 2)
                def _():
                    up_copy(n, 0, own, at(f), f + 2).start()

                @pl.when(z >= 1)
                def _():
                    down_copy(n, 0, own, at(f), f - 2).start()

            else:

                @pl.when(z >= p)
                def _():
                    slot = at(f - 2 * p)
                    up_copy(n, p - 1, slot, slot).wait_recv()
                    if p <= 2:

                        @pl.when(z <= 2)
                        def _():
                            up_copy(n, p, slot, slot, f + 2).start()

                    x_copy(n, p, slot, slot, xf).start()

                @pl.when(z + p <= 3)
                def _():
                    slot = at(f + 2 * p)
                    down_copy(n, p - 1, slot, slot).wait_recv()
                    if p <= 2:

                        @pl.when(z >= 1)
                        def _():
                            down_copy(n, p, slot, slot, f - 2).start()

                    x_copy(n, 3 + p, slot, slot, xf).start()

    own_loads = ((wd_ref, down_full), (wg_ref, gate_full), (wu_ref, up_full))

    def own_load(i):
        src, full = own_loads[i]
        return pltpu.make_async_copy(src, full.at[f], loc.at[2 + i])

    experts(0)
    for i in range(3):
        own_load(i).start()

    at_copy(1, me.yp).wait_recv()
    at_copy(2, me.yp, me.sib).start()
    at_copy(0, me.sib).wait_recv()
    early_wait(*early[0])
    early_forward(*early[1][1:4])
    at_copy(2, me.diag).wait_recv()

    def qkv_step(i, _):
        b = i // 2
        r = pl.ds(pl.multiple_of((i % 2) * 256, 256), 256)
        out = dot(attn_all[b, r, :], wq_full[...])
        q_s[b, r, :] = (out[:, 0:C] * QSCALE).astype(BF)
        k_s[b, r, :] = out[:, C : 2 * C].astype(BF)
        v = out[:, 2 * C : 3 * C]
        v_s[b, r, :] = v.astype(BF)
        vt_s[b, :, r] = v.T.astype(BF)
        return 0

    lax.fori_loop(0, 8, qkv_step, 0)

    head_of = lane_of((T, C)) // HD
    lse_s[...] = jnp.zeros_like(lse_s)

    def query_step(j, _):
        qb = me.far_first(j)
        queries = [jnp.where(head_of == h, q_s[qb], jnp.zeros((T, C), BF)) for h in range(3)]
        allowed = allowed_block(T, starts_ref[0, qb] - qb * T)
        for h in range(3):
            hr = pl.ds(h * HD, HD)
            s = jnp.where(allowed, dot(k_s[qb], queries[h], 1, 1), NEG)
            m = jnp.max(s, axis=0, keepdims=True)
            p = jnp.exp2(s - m)
            m_s[h : h + 1] = m
            l_s[h : h + 1] = jnp.sum(p, axis=0, keepdims=True)
            acc_s[hr] = dot(vt_s[qb, hr, :], p.astype(BF))

        def key_step(kb, _):
            for h in range(3):
                hr = pl.ds(h * HD, HD)
                query = jnp.where(head_of == h, q_s[qb], jnp.zeros((T, C), BF))
                s = dot(k_s[kb], query, 1, 1)
                m_old = m_s[h : h + 1]
                m = jnp.maximum(m_old, jnp.max(s, axis=0, keepdims=True))
                scale = jnp.exp2(m_old - m)
                p = jnp.exp2(s - m)
                m_s[h : h + 1] = m
                l_s[h : h + 1] = l_s[h : h + 1] * scale + jnp.sum(p, axis=0, keepdims=True)
                acc_s[hr] = acc_s[hr] * scale + dot(vt_s[kb, hr, :], p.astype(BF))
            return 0

        lax.fori_loop(0, qb, key_step, 0)
        for h in range(3):
            hr = pl.ds(h * HD, HD)
            total = l_s[h : h + 1]
            acc_s[hr] = acc_s[hr] / total
            lse_s[qb, h : h + 1, :] = m_s[h : h + 1] + jnp.log2(total)
        o_s[qb] = acc_s[...].T.astype(BF)
        return 0

    def o_copy(i, to=None):
        p = me.exp_peers[i]
        if to is None:
            return me.send(o_s.at[p], attn_recv.at[p], o_ss.at[i], o_rs.at[i])
        return me.send(o_s.at[p], attn_recv.at[e], o_ss.at[i], o_rs.at[i], e=p)

    lax.fori_loop(0, 2, query_step, 0)
    o_copy(1, True).start()
    o_copy(2, True).start()
    experts(1)
    lax.fori_loop(2, 4, query_step, 0)
    o_copy(0, True).start()
    attn_recv[e] = o_s[e]

    r0, r1 = routes_ref[0:1, :], routes_ref[1:2, :]
    expert = row_of((8, T))
    chosen = (expert == r0) | (expert == r1)
    earlier = (row_of((T, T)) < lane_of((T, T))).astype(BF)
    count = dot(chosen.astype(BF), earlier).astype(jnp.int32)
    count = jnp.where(chosen, count, -1)
    slot_id = row_of((CAP, T))
    for k in range(4):
        place_ref[k] = jnp.where(slot_id == count[k : k + 1, :], 1.0, 0.0).astype(BF)

    early_wait(*early[1])
    for i in (0, 1, 2):
        o_copy(i).wait_recv()

    def hidden_step(i, _):
        r = pl.ds(pl.multiple_of(i * 256, 256), 256)
        h = x_ref[r, :].astype(F32)
        for b in range(4):
            h = h + dot(attn_recv[b, r, :], wo_full[b * C : (b + 1) * C, :])
        hidden_ref[r, :] = h
        n = h * lax.rsqrt(jnp.mean(h * h, axis=-1, keepdims=True) + EPS) * gain_f_ref[...].reshape(1, D)
        nb[r, :] = n.astype(BF)
        aux_ref[0:8, r] = dot(router_ref[...], n, 1, 1, HIGH) + dot(mix_ref[...], gres_ref[:, r], 0, 0, HIGH)
        aux_ref[8:12, r] = dot(proj_ref[...], n, 1, 1, HIGH)
        return 0

    lax.fori_loop(0, 2, hidden_step, 0)
    experts(2)

    logits = aux_ref[0:8, :]
    top = jnp.max(jnp.where(chosen, logits, NEG), axis=0, keepdims=True)
    weight = jnp.where(chosen, jnp.exp(logits - top), 0.0)
    gates = weight / jnp.sum(weight, axis=0, keepdims=True)
    pairs = aux_ref[8:12, :]
    other = jnp.concatenate([pairs[1:2], pairs[0:1], pairs[3:4], pairs[2:3]], axis=0)
    aux_ref[0:8, :] = gates
    aux_ref[8:12, :] = 1.0 / (1.0 + jnp.exp(other - pairs))
    aux_ref[12:16, :] = jnp.zeros((4, T), F32)

    def d_copy(i, ref, out, ss, rs, k, to=None):
        return me.send(ref.at[k], out.at[e if to is not None else k], ss.at[i], rs.at[i], e=to)

    def dispatch_step(j, _):
        k = me.far_first(j)
        i = (j + 1) % 4
        place = place_ref[k]
        snd_r[k] = dot(place, nb[...]).astype(BF)
        gate = aux_ref[pl.ds(k, 1), :]
        gated = jnp.where(place > 0, gate.astype(BF), jnp.zeros((CAP, T), BF))
        snd_d[k] = dot(gated, u_ref[...]).astype(BF)

        @pl.when(j != 2)
        def _():
            d_copy(i, snd_r, recv_r, dr_ss, dr_rs, k, k).start()
            d_copy(i, snd_d, recv_d, dd_ss, dd_rs, k, k).start()

        @pl.when(j == 2)
        def _():
            recv_r[k] = snd_r[k]
            recv_d[k] = snd_d[k]

        return 0

    lax.fori_loop(0, 4, dispatch_step, 0)
    for i, p in enumerate(me.exp_peers):
        d_copy(i, snd_r, recv_r, dr_ss, dr_rs, p).wait()
        d_copy(i, snd_d, recv_d, dd_ss, dd_rs, p).wait()
    experts(3)

    acc[...] = jnp.zeros_like(acc)
    d_acc[...] = jnp.zeros_like(d_acc)

    def unit_wait(n, full, c):
        def at(slot):
            return cut(full.at[slot], c)

        x_copy(n, 0, at(xf), at(xf)).wait_recv()
        for p in (1, 2, 3):

            @pl.when(z >= p)
            def _():
                x_copy(n, p, at(xf - 2 * p), at(xf - 2 * p)).wait_recv()

            @pl.when(z + p <= 3)
            def _():
                x_copy(n, 3 + p, at(xf + 2 * p), at(xf + 2 * p)).wait_recv()

    stages = ((st_gate, grad_gate, 0), (st_up, grad_up, 1), (st_down, grad_down, 2))

    def stage_copy(c, i):
        st, out, _ = stages[i]
        if i == 2:
            dst = out.at[pl.ds(2 * c, 2)]
        else:
            dst = out.at[:, :, pl.ds(pl.multiple_of(c * W, W), W)]
        return pltpu.make_async_copy(st, dst, st_sem.at[i])

    def ret_copy(i, snd, ret, ss, rs, to=None):
        p = me.exp_peers[i]
        return me.send(snd.at[p], ret.at[e if to else p], ss.at[i], rs.at[i], e=p if to else None)

    def expert_step(c, _):
        @pl.when(c == 0)
        def _():
            for i in range(3):
                own_load(i).wait()
            unit_wait(0, down_full, None)

        unit_wait(1 + 2 * c, gate_full, c)
        unit_wait(2 + 2 * c, up_full, c)
        w = pl.ds(pl.multiple_of(c * W, W), W)
        row_in = recv_r[...].reshape(S, D)
        d_in = recv_d[...].reshape(S, D)
        w_gate = gate_full[:, :, w].reshape(D, W)
        w_up = up_full[:, :, w].reshape(D, W)
        w_down = down_full[pl.ds(2 * c, 2)].reshape(W, D)
        g = dot(row_in, w_gate)
        up = dot(row_in, w_up)
        sig = 1.0 / (1.0 + jnp.exp(-g))
        silu = g * sig
        inner = (silu * up).astype(BF)
        acc[...] += dot(inner, w_down)

        @pl.when(c == CHUNKS - 1)
        def _():
            snd_r[...] = acc[...].astype(BF).reshape(4, CAP, D)
            for i in (1, 2, 0):
                ret_copy(i, snd_r, ret_o, ro_ss, ro_rs, True).start()
            ret_o[e] = snd_r[e]

        d_inner = dot(d_in, w_down, 1, 1)
        d_up = (d_inner * silu).astype(BF)
        d_gate = (d_inner * up * (sig + silu * (1.0 - sig))).astype(BF)
        d_acc[...] += dot(d_gate, w_gate, 1, 1) + dot(d_up, w_up, 1, 1)

        @pl.when(c == CHUNKS - 1)
        def _():
            snd_d[...] = d_acc[...].astype(BF).reshape(4, CAP, D)
            for i in (1, 2, 0):
                ret_copy(i, snd_d, ret_d, rd_ss, rd_rs, True).start()
            ret_d[e] = snd_d[e]

        @pl.when(c > 0)
        def _():
            for i in range(3):
                stage_copy(c - 1, i).wait()

        st_down[...] = dot(inner, d_in, 0, 0).astype(BF).reshape(2, W // 2, D)
        st_gate[...] = dot(row_in, d_gate, 0, 0).astype(BF).reshape(8, R, W)
        st_up[...] = dot(row_in, d_up, 0, 0).astype(BF).reshape(8, R, W)
        for i in range(3):
            stage_copy(c, i).start()
        return 0

    lax.fori_loop(0, CHUNKS, expert_step, 0)
    for i in range(3):
        stage_copy(CHUNKS - 1, i).wait()

    far_row = 2 * ((z + 3 - 2 * (z % 2)) % 4) + 1 - me.x
    far = ((grad_gate, far_gate), (grad_up, far_up), (grad_down, far_down))
    for i, (src, dst) in enumerate(far):
        me.send(src.at[far_row], dst, fs.at[i], fr.at[i], f=xf).start()

    for src, dst, ss, rs, li in early:
        for j in range(7):
            me.send(rows(dst, f), rows(dst, f), ss.at[j], rs.at[j]).wait_send()
    for i in range(3):
        at_copy(i, e).wait_send()
        o_copy(i).wait_send()
    for n, (src, full, c) in enumerate(units):
        slot = cut(full.at[f], c)
        x_copy(n, 0, slot, slot).wait_send()

        @pl.when(z <= 2)
        def _():
            up_copy(n, 0, slot, slot).wait_send()

        @pl.when(z >= 1)
        def _():
            down_copy(n, 0, slot, slot).wait_send()

        for p in (1, 2, 3):

            @pl.when(z >= p)
            def _():
                if p <= 2:

                    @pl.when(z <= 2)
                    def _():
                        up_copy(n, p, slot, slot).wait_send()

                x_copy(n, p, slot, slot).wait_send()

            @pl.when(z + p <= 3)
            def _():
                if p <= 2:

                    @pl.when(z >= 1)
                    def _():
                        down_copy(n, p, slot, slot).wait_send()

                x_copy(n, 3 + p, slot, slot).wait_send()

    for i in range(3):
        ret_copy(i, snd_r, ret_o, ro_ss, ro_rs).wait()
        ret_copy(i, snd_d, ret_d, rd_ss, rd_rs).wait()
    for i, (src, dst) in enumerate(far):
        me.send(src.at[far_row], dst, fs.at[i], fr.at[i]).wait()


def sds(shape, dtype):
    return jax.ShapeDtypeStruct(shape, dtype)


def vmem():
    return pl.BlockSpec(memory_space=pltpu.VMEM)


def anyspace():
    return pl.BlockSpec(memory_space=pl.ANY)


def smem():
    return pl.BlockSpec(memory_space=pltpu.SMEM)


def call_k1(x, u, wq, wk, wv, wo, wg, wu, wd, gres, routes, starts, gain_a, gain_f, router, proj, mix):
    T, D = x.shape
    C, R, FF, S = D // 4, D // 8, wg.shape[1], 4 * CAP
    n = 1 + 2 * CHUNKS
    dma = pltpu.SemaphoreType.DMA
    VM = pltpu.VMEM
    block = VM((4, CAP, D), BF)
    return pl.pallas_call(
        k1_kernel,
        name="forward",
        out_shape=(
            sds((4, T, D), BF), sds((4, T, C), BF), sds((4, T, C), BF), sds((4, T, C), BF), sds((4, T, C), BF),
            sds((4, 8, T), F32), sds((T, D), F32), sds((16, T), F32), sds((4, CAP, T), BF),
            sds((4, CAP, D), BF), sds((4, CAP, D), BF), sds((D, D), BF), sds((D, 3 * C), BF),
            sds((8, R, FF), BF), sds((8, R, FF), BF), sds((8, FF // 8, D), BF),
            sds((R, FF), BF), sds((R, FF), BF), sds((FF // 8, D), BF),
        ),
        in_specs=[vmem()] * 5 + [anyspace()] * 4 + [vmem()] * 2 + [smem()] + [vmem()] * 5,
        out_specs=tuple([vmem()] * 13 + [anyspace()] * 6),
        scratch_shapes=[
            VM((8, R, FF), BF), VM((8, R, FF), BF), VM((8, FF // 8, D), BF), VM((R, 3 * C), BF), VM((4, C, T), BF),
            VM((4, T, C), BF), VM((T, D), BF), block, block, block, block, VM((8, T), F32), VM((8, T), F32), VM((C, T), F32),
            VM((S, D), F32), VM((S, D), F32), VM((8, R, FF // CHUNKS), BF), VM((8, R, FF // CHUNKS), BF), VM((2, FF // 8, D), BF),
            dma((7,)), dma((7,)), dma((7,)), dma((7,)),
        ] + [dma((3,))] * 12 + [
            dma((n, 3)), dma((n, 3)), dma((n, 3)), dma((n, 3)), dma((n, 7)), dma((n, 7)),
            dma((5,)), dma((3,)), dma((3,)), dma((3,)),
        ],
        compiler_params=pltpu.CompilerParams(collective_id=0, has_side_effects=True, vmem_limit_bytes=60 << 20),
    )(x, u, wq, wk, wv, wo, wg, wu, wd, gres, routes, starts, gain_a, gain_f, router, proj, mix)


def k2_kernel(
    ret_o, ret_d, hidden, u_ref, x_ref, aux_ref, place_ref, gres_ref,
    attn_all, q_s, k_s, v_s, o_s, lse_s, wo, wqkv, gain_a_ref, gain_f_ref, router_ref, proj_ref, mix_ref, cvec_ref, starts_ref,
    g_gate, g_up, g_down, far_gate, far_up, far_down,
    layer_out, grad_tokens, d_res, small_out, ag_out, go_b, eg_out, eu_out, ed_out,
    xin_g, xin_u, xin_d, own_g, own_u, own_d, zin_g, zin_u, zin_d,
    dh_all, da, kt_s, dq, dk, dv, dqt, pin, py_in, d_hidden, wk_s, del_r, gt, ag_s, ag_in, ag_fin, go_s, go_in,
    small, sm1, sm2,
    far_sem, xs, xr, zs, zr, own_sem, dh_ss, dh_rs, fw_ss, fw_rs, go_ss, go_rs, gb_ss, gb_rs, pd_ss, pd_rs, ag_ss, ag_rs,
    ab_ss, ab_rs, s1_ss, s1_rs, s2_ss, s2_rs,
):
    me = Place()
    e, f, z, x, xf = me.e, me.f, me.z, me.x, me.xf
    T, D = x_ref.shape
    C = D // 4
    R = D // 8
    M = 128

    partner = z + 1 - 2 * (z % 2)
    order = ((partner + 2) % 4, (z + 2) % 4, partner, z)
    parts = (
        (g_gate, xin_g, own_g, zin_g, far_gate, eg_out),
        (g_up, xin_u, own_u, zin_u, far_up, eu_out),
        (g_down, xin_d, own_d, zin_d, far_down, ed_out),
    )

    def far_copy(w):
        return pltpu.make_async_copy(parts[w][4], parts[w][1].at[0], far_sem.at[w])

    def own_copy(w, i):
        return pltpu.make_async_copy(parts[w][0].at[2 * order[i] + x], parts[w][2], own_sem.at[w])

    def x_copy(w, i):
        return me.send(parts[w][0].at[2 * order[i] + 1 - x], parts[w][1].at[i], xs.at[w, i], xr.at[w, i], f=xf)

    def z_copy(w, i):
        to = order[1] if i == 1 else partner
        return me.send(parts[w][1].at[i], parts[w][3].at[i], zs.at[w, i], zr.at[w, i], f=2 * to + x)

    def x_send(i):
        for w in range(3):
            x_copy(w, i).start()

    def rs_mid(i):
        for w in range(3):
            xin, own, zin = parts[w][1:4]
            if i:
                x_copy(w, i).wait_recv()
            else:
                far_copy(w).wait()
            own_copy(w, i).wait()
            total = xin[i].astype(F32) + own[...].astype(F32)
            if i == 1:
                z_copy(w, 0).wait_recv()
                total = total + zin[0].astype(F32)
            if i == 3:
                z_copy(w, 1).wait_recv()
                z_copy(w, 2).wait_recv()
                total = total + zin[1].astype(F32) + zin[2].astype(F32)
                parts[w][5][...] = total.astype(BF)
            else:
                xin[i] = total.astype(BF)
                z_copy(w, i).start()
                own_copy(w, i + 1).start()

    for w in range(3):
        far_copy(w).start()
        own_copy(w, 0).start()
    me.barrier()
    x_send(1)
    rs_mid(0)
    x_send(2)

    small[...] = jnp.zeros_like(small)
    cv0, cv1 = cvec_ref[0:1, :], cvec_ref[1:2, :]
    maps = jnp.concatenate([router_ref[...], proj_ref[...], jnp.zeros((4, D), F32)], axis=0).astype(BF)
    lane8 = lane_of((M, 8))
    lane4 = lane_of((M, 4))

    def dh_copy(i, c, block, to=None):
        ref = dh_all.at[block, pl.ds(pl.multiple_of(c * M, M), M)]
        return me.send(ref, ref, dh_ss.at[i, c], dh_rs.at[i, c], e=to)

    def mix_step(c, _):
        r = pl.ds(pl.multiple_of(c * M, M), M)
        h = hidden[r, :]
        u = u_ref[r, :].astype(F32)
        inv = lax.rsqrt(jnp.mean(h * h, axis=-1, keepdims=True) + EPS)
        hn = h * inv
        gain = gain_f_ref[...].reshape(1, D)
        n = hn * gain
        cols = aux_ref[:, r].T
        gates = cols[:, 0:8]
        a0, b0, a1, b1 = cols[:, 8:9], cols[:, 9:10], cols[:, 10:11], cols[:, 11:12]
        g5, g6, g7 = cols[:, 5:6], cols[:, 6:7], cols[:, 7:8]
        c_n = g5 + g6 * a0 + g7 * a1
        c0 = g6 * b0
        c1 = g7 * b1
        mixed = h + c_n * n + c0 * cv0 + c1 * cv1
        dg = jnp.zeros((M, 8), F32)
        dn = c_n * u
        for k in range(4):
            place = place_ref[k, :, r]
            rk = dot(place, ret_o[k], 0, 0)
            mixed = mixed + cols[:, k : k + 1] * rk
            dg = jnp.where(lane8 == k, jnp.sum(u * rk, axis=-1, keepdims=True), dg)
            dn = dn + dot(place, ret_d[k], 0, 0)
        layer_out[r, :] = mixed.astype(BF)
        un = jnp.sum(u * n, axis=-1, keepdims=True)
        uv0 = jnp.sum(u * cv0, axis=-1, keepdims=True)
        uv1 = jnp.sum(u * cv1, axis=-1, keepdims=True)
        dg = jnp.where(lane8 == 5, un, dg)
        dg = jnp.where(lane8 == 6, a0 * un + b0 * uv0, dg)
        dg = jnp.where(lane8 == 7, a1 * un + b1 * uv1, dg)
        dlog = gates * (dg - jnp.sum(gates * dg, axis=-1, keepdims=True))
        e0 = g6 * a0 * b0 * (un - uv0)
        e1 = g7 * a1 * b1 * (un - uv1)
        dpair = jnp.where(lane4 == 0, e0, jnp.where(lane4 == 1, -e0, jnp.where(lane4 == 2, e1, -e1)))
        dl = jnp.concatenate([dlog, dpair, c0, c1, jnp.zeros((M, 2), F32)], axis=1)
        low = dl.astype(BF)
        d_res[:, r] = dot(mix_ref[...], dlog, 1, 1, HIGH)
        dn = dn + dot(jnp.where(lane_of((M, 16)) < 12, low, jnp.zeros((M, 16), BF)), maps)
        by_n = dot(low, n.astype(BF), 0, 0)
        by_u = dot(low, u_ref[r, :], 0, 0)
        small[0:12, :] += by_n[0:12]
        small[12:14, :] += by_u[12:14]
        small[14:15, :] += jnp.sum(dn * hn, axis=0, keepdims=True)
        small[16:24, 0:8] += dot(gres_ref[:, r], dlog, 1, 0, HIGH)
        gd = dn * gain
        dh = u + inv * (gd - hn * jnp.mean(gd * hn, axis=-1, keepdims=True))
        d_hidden[r, :] = dh
        dh_all[e, r, :] = dh.astype(BF)
        dh_copy(1, c, e, me.yp).start()
        dh_copy(0, c, e, me.sib).start()
        return 0

    lax.fori_loop(0, T // M, mix_step, 0)
    rs_mid(1)
    x_send(3)

    head_of = lane_of((T, C)) // HD
    heads = (row_of((8, C)) == lane_of((8, C)) // HD).astype(F32)
    wk_s[...] = wqkv[:, C : 2 * C]
    dk[...] = jnp.zeros_like(dk)
    dv[...] = jnp.zeros_like(dv)
    gt[0] = jnp.zeros((C, D), F32)
    for b in range(4):
        kt_s[b] = k_s[b].T

    def fw_copy(block, to=None):
        return me.send(dh_all.at[block], dh_all.at[block], fw_ss.at[0], fw_rs.at[0], e=to)

    def query_step(j, _):
        qb = me.near_first(j)

        @pl.when(j == 1)
        def _():
            for c in range(T // M):
                dh_copy(0, c, me.sib).wait_recv()

        @pl.when(j == 2)
        def _():
            for c in range(T // M):
                dh_copy(1, c, me.yp).wait_recv()
            fw_copy(me.yp, me.sib).start()

        @pl.when(j == 3)
        def _():
            fw_copy(me.diag).wait_recv()

        dhb = dh_all[qb]
        low = dot(dhb, wo[pl.ds(pl.multiple_of(e * C, 64), C), :], 1, 1).astype(BF)
        da[...] = low
        ob = o_s[qb]
        del_r[...] = dot(heads, low.astype(F32) * ob.astype(F32), 1, 1, HIGH)
        gt[0] += dot(ob, dhb, 0, 0)

        def pair(kb, h, masked):
            zero = jnp.zeros((T, C), BF)
            query = jnp.where(head_of == h, q_s[qb], zero)
            d_out = jnp.where(head_of == h, da[...], zero)
            p = jnp.exp2(dot(k_s[kb], query, 1, 1) - lse_s[qb, h : h + 1, :])
            if masked:
                p = jnp.where(allowed_block(T, starts_ref[0, qb] - qb * T), p, 0.0)
            dp = dot(v_s[kb], d_out, 1, 1)
            dsc = (p * (dp - del_r[h : h + 1, :])).astype(BF)
            return dot(p.astype(BF), d_out), dot(dsc, query), dot(kt_s[kb, h * HD : (h + 1) * HD, :], dsc)

        def block(kb, masked):
            r = [pair(kb, h, masked) for h in range(3)]
            dv[kb] += r[0][0] + r[1][0] + r[2][0]
            dk[kb] += r[0][1] + r[1][1] + r[2][1]
            for h in range(3):
                if masked:
                    dqt[h * HD : (h + 1) * HD, :] = r[h][2]
                else:
                    dqt[h * HD : (h + 1) * HD, :] += r[h][2]

        block(qb, True)

        def key_step(kb, _):
            block(kb, False)
            return 0

        lax.fori_loop(0, qb, key_step, 0)
        dq[qb] = (dqt[...].T * (1.0 / math.sqrt(HD))).astype(BF)
        return 0

    lax.fori_loop(0, 3, query_step, 0)
    rs_mid(2)
    lax.fori_loop(3, 4, query_step, 0)

    go_s[0] = gt[0, 0:R, :].astype(BF)
    go_s[1] = gt[0, R : 2 * R, :].astype(BF)
    for j in range(2):

        @pl.when(f != 2 * e + j)
        def _():
            me.send(go_s.at[j], go_in.at[f], go_ss.at[j], go_rs.at[f], f=2 * e + j).start()

    def low(b):
        return dq[b], (dk[b] * LN2).astype(BF), dv[b].astype(BF)

    for i in range(3):
        gt[i] = jnp.zeros((C, D), F32)

    def grad_step(b, _):
        a = attn_all[b]
        for i, part in enumerate(low(b)):
            gt[i] += dot(part, a, 0, 0)
        return 0

    lax.fori_loop(0, 4, grad_step, 0)
    for i in range(3):
        ag_s[:, i] = gt[i].T.astype(BF).reshape(8, R, C)
    for r in range(1, 8):
        me.send(ag_s.at[me.fp(r)], ag_in.at[f], ag_ss.at[r - 1], ag_rs.at[f], f=me.fp(r)).start()
    ag_in[f] = ag_s[f]

    for c in range(T // M):
        dh_copy(0, c, e).wait_send()
        dh_copy(1, c, e).wait_send()
    fw_copy(e).wait_send()

    def share_step(j, _):
        b = (me.sib + 2 * j + (j // 2) * (e - me.sib)) % 4
        low_q, low_k, low_v = low(b)
        out = dot(low_q, wqkv[:, 0:C], 1, 1)
        out = out + dot(low_k, wk_s[...], 1, 1)
        out = out + dot(low_v, wqkv[:, 2 * C : 3 * C], 1, 1)
        small[15:16, :] += jnp.sum(out * attn_all[b].astype(F32), axis=0, keepdims=True)
        dh_all[b] = out.astype(BF)
        return 0

    def pd_copy(i, src, dst, to=None):
        return me.send(src, dst, pd_ss.at[i], pd_rs.at[i], e=to)

    lax.fori_loop(0, 2, share_step, 0)
    pd_copy(1, dh_all.at[me.diag], pin.at[1], me.sib).start()
    pd_copy(0, dh_all.at[me.sib], pin.at[0], me.sib).start()
    lax.fori_loop(2, 4, share_step, 0)
    pd_copy(1, pin.at[1], pin.at[1]).wait_recv()
    dh_all[me.yp] = (dh_all[me.yp].astype(F32) + pin[1].astype(F32)).astype(BF)
    pd_copy(2, dh_all.at[me.yp], py_in, me.yp).start()

    small[15:16, :] = small[15:16, :] / gain_a_ref[...].reshape(1, D)
    sm1[e] = small[...]
    for i, p in enumerate(me.exp_peers):
        me.send(small, sm1.at[e], s1_ss.at[i], s1_rs.at[i], e=p).start()

    @pl.when(z == e)
    def _():
        total = go_s[x].astype(F32)
        for r in range(1, 8):
            s = go_in.at[me.fp(r)]
            me.send(s, s, go_ss.at[0], go_rs.at[me.fp(r)]).wait_recv()
            total = total + go_in[me.fp(r)].astype(F32)
        go_b[...] = total.astype(BF)
        for i, p in enumerate(me.exp_peers):
            me.send(go_b, go_b, gb_ss.at[i], gb_rs.at[0], e=p).start()

    for i, p in enumerate(me.exp_peers):
        me.send(small, sm1.at[p], s1_ss.at[i], s1_rs.at[i]).wait()
    sm2[f] = sm1[0] + sm1[1] + sm1[2] + sm1[3]
    for r in range(1, 8):
        me.send(sm2.at[f], sm2.at[f], s2_ss.at[r - 1], s2_rs.at[f], f=me.fp(r)).start()

    rs_mid(3)

    for r in range(1, 8):
        s = ag_in.at[me.fp(r)]
        me.send(s, s, ag_ss.at[r - 1], ag_rs.at[me.fp(r)]).wait_recv()
    for i in range(3):
        total = ag_in[0, i].astype(F32)
        for r in range(1, 8):
            total = total + ag_in[r, i].astype(F32)
        ag_fin[i] = total.astype(BF)
    for i, p in enumerate(me.exp_peers):
        me.send(ag_fin, ag_out.at[e], ab_ss.at[i], ab_rs.at[i], e=p).start()
    ag_out[e] = ag_fin[...]

    for r in range(1, 8):
        s = sm2.at[me.fp(r)]
        me.send(s, s, s2_ss.at[r - 1], s2_rs.at[me.fp(r)]).wait_recv()
    total = sm2[0]
    for r in range(1, 8):
        total = total + sm2[r]
    small_out[...] = total

    pd_copy(0, pin.at[0], pin.at[0]).wait_recv()
    pd_copy(2, py_in, py_in).wait_recv()

    def token_step(i, _):
        r = pl.ds(pl.multiple_of(i * 256, 256), 256)
        d = dh_all[e, r, :].astype(F32) + pin[0, r, :].astype(F32) + py_in[r, :].astype(F32)
        xv = x_ref[r, :].astype(F32)
        inv = lax.rsqrt(jnp.mean(xv * xv, axis=-1, keepdims=True) + EPS)
        xn = xv * inv
        gd = d * gain_a_ref[...].reshape(1, D)
        grad_tokens[r, :] = (d_hidden[r, :] + inv * (gd - xn * jnp.mean(gd * xn, axis=-1, keepdims=True))).astype(BF)
        return 0

    lax.fori_loop(0, 2, token_step, 0)

    @pl.when(z != e)
    def _():
        me.send(go_b, go_b, gb_ss.at[0], gb_rs.at[0]).wait_recv()

    for w in range(3):
        for i in range(3):
            x_copy(w, i + 1).wait_send()
            z_copy(w, i).wait_send()
    for j in range(2):

        @pl.when(f != 2 * e + j)
        def _():
            me.send(go_s.at[j], go_in.at[f], go_ss.at[j], go_rs.at[f]).wait_send()

    @pl.when(z == e)
    def _():
        for i in range(3):
            me.send(go_b, go_b, gb_ss.at[i], gb_rs.at[0]).wait_send()

    for i in range(3):
        pd_copy(i, py_in, py_in).wait_send()
        me.send(ag_fin, ag_out.at[me.exp_peers[i]], ab_ss.at[i], ab_rs.at[i]).wait()
    for r in range(1, 8):
        me.send(ag_s.at[0], ag_in.at[f], ag_ss.at[r - 1], ag_rs.at[f]).wait_send()
        me.send(sm2.at[f], sm2.at[f], s2_ss.at[r - 1], s2_rs.at[f]).wait_send()


def call_k2(*args):
    x, (gg, gu, gd) = args[4], args[23:26]
    T, D = x.shape
    C, R = D // 4, D // 8
    dma = pltpu.SemaphoreType.DMA
    VM = pltpu.VMEM
    shapes = (gg.shape[1:], gu.shape[1:], gd.shape[1:])
    return pl.pallas_call(
        k2_kernel,
        name="backward",
        out_shape=(
            sds((T, D), BF), sds((T, D), BF), sds((8, T), F32), sds((24, D), F32),
            sds((4, 3, R, C), BF), sds((R, D), BF),
        ) + tuple(sds(s, BF) for s in shapes),
        in_specs=[vmem()] * 22 + [smem()] + [anyspace()] * 6,
        out_specs=tuple([vmem()] * 9),
        scratch_shapes=[VM((4,) + s, BF) for s in shapes] + [VM(s, BF) for s in shapes] + [VM((3,) + s, BF) for s in shapes] + [
            VM((4, T, D), BF), VM((T, C), BF), VM((4, C, T), BF), VM((4, T, C), BF), VM((4, T, C), F32), VM((4, T, C), F32),
            VM((C, T), F32), VM((2, T, D), BF), VM((T, D), BF), VM((T, D), F32), VM((D, C), BF), VM((8, T), F32), VM((3, C, D), F32),
            VM((8, 3, R, C), BF), VM((8, 3, R, C), BF), VM((3, R, C), BF), VM((2, R, D), BF), VM((8, R, D), BF),
            VM((24, D), F32), VM((4, 24, D), F32), VM((8, 24, D), F32),
            dma((3,)), dma((3, 4)), dma((3, 4)), dma((3, 3)), dma((3, 3)), dma((3,)),
            dma((2, 4)), dma((2, 4)), dma((1,)), dma((1,)), dma((2,)), dma((8,)), dma((3,)), dma((1,)), dma((3,)), dma((3,)),
            dma((7,)), dma((8,)), dma((3,)), dma((3,)), dma((3,)), dma((3,)), dma((7,)), dma((8,)),
        ],
        compiler_params=pltpu.CompilerParams(collective_id=1, has_side_effects=True, vmem_limit_bytes=63 << 20),
    )(*args)


def k3_kernel(
    layer_in, tokens_in, res_in, small, ag, go, eg, eu, ed,
    layer_out, tokens_out, res_out, norm_a, norm_f, g_q, g_k, g_v, g_o, router, mixing, proj, cvec, o_gate, o_up, o_down,
):
    layer_out[...] = layer_in[...]
    tokens_out[...] = tokens_in[...]
    res_out[...] = res_in[...]
    norm_a[...] = small[15, :]
    norm_f[...] = small[14, :]
    for i, out in enumerate((g_q, g_k, g_v)):
        out[...] = jnp.concatenate([ag[b, i].astype(F32) for b in range(4)], axis=1)
    g_o[...] = go[...].astype(F32)
    router[...] = small[0:8, :]
    mixing[...] = small[16:24, 0:8]
    proj[...] = small[8:12, :]
    cvec[...] = small[12:14, :]
    o_gate[...] = eg[...].astype(F32)
    o_up[...] = eu[...].astype(F32)
    o_down[...] = ed[...].astype(F32)


def call_k3(*args):
    T, D = args[0].shape
    R = D // 8
    return pl.pallas_call(
        k3_kernel,
        name="finish",
        out_shape=(
            sds((T, D), BF), sds((T, D), BF), sds((8, T), F32), sds((D,), F32), sds((D,), F32),
            sds((R, D), F32), sds((R, D), F32), sds((R, D), F32), sds((R, D), F32),
            sds((8, D), F32), sds((8, 8), F32), sds((4, D), F32), sds((2, D), F32),
        ) + tuple(sds(a.shape, F32) for a in args[6:9]),
        in_specs=[vmem()] * 9,
        out_specs=tuple([vmem()] * 16),
    )(*args)


def body_fast(
    tokens, gate_res, routes, piece_starts, norm_attn, norm_ffn, w_query, w_key, w_value, w_out, router, mixing,
    const_proj, const_vec, w_gate, w_up, w_down, cotangent,
):
    x, u = tokens[0], cotangent[0]
    gres, route_ids = gate_res[0].T, routes[0].T
    (attn_all, q, k, v, o, lse, hidden, aux, place, ret_o, ret_d, wo, wq, gg, gu, gd, fg, fu, fd) = call_k1(
        x, u, w_query, w_key, w_value, w_out, w_gate[0], w_up[0], w_down[0], gres, route_ids, piece_starts,
        norm_attn, norm_ffn, router.T, const_proj.T, mixing,
    )
    outs = call_k2(
        ret_o, ret_d, hidden, u, x, aux, place, gres, attn_all, q, k, v, o, lse, wo, wq,
        norm_attn, norm_ffn, router.T, const_proj.T, mixing, const_vec, piece_starts, gg, gu, gd, fg, fu, fd,
    )
    (layer_out, grad_tokens, d_res, norm_a, norm_f, g_q, g_k, g_v, g_o, g_router, g_mixing, g_proj, g_cvec, eg, eu, ed) = call_k3(*outs)
    return (
        layer_out[None], grad_tokens[None], d_res.T[None], norm_a, norm_f, g_q, g_k, g_v, g_o,
        g_router.T, g_mixing, g_proj.T, g_cvec, eg[None], eu[None], ed[None],
    )


def solution(mesh):
    placed = (
        P("fsdp", "exp", None),
        P("fsdp", "exp", None),
        P("fsdp", "exp", None),
        P("fsdp", None),
        P(),
        P(),
        P("fsdp", None),
        P("fsdp", None),
        P("fsdp", None),
        P("fsdp", None),
        P(),
        P(),
        P(),
        P(),
        P("exp", "fsdp", None),
        P("exp", "fsdp", None),
        P("exp", "fsdp", None),
        P("fsdp", "exp", None),
    )
    return jax.shard_map(
        body_fast if (mesh.shape['exp'], mesh.shape['fsdp']) == (4, 8) else body,
        mesh=mesh,
        in_specs=placed,
        out_specs=(
            P("fsdp", "exp", None),
            P("fsdp", "exp", None),
            P("fsdp", "exp", None),
            P(),
            P(),
            P("fsdp", None),
            P("fsdp", None),
            P("fsdp", None),
            P("fsdp", None),
            P(),
            P(),
            P(),
            P(),
            P("exp", "fsdp", None),
            P("exp", "fsdp", None),
            P("exp", "fsdp", None),
        ),
        check_vma=False,
    )
```

```python
import math

import jax
import jax.numpy as jnp
from jax import lax
from jax.experimental import pallas as pl
from jax.experimental.pallas import tpu as pltpu
from jax.sharding import PartitionSpec as P

H = 12
HD = 64
PIECE = 256
KBLK = 512
CAP = 160


EPS = 1e-05
HIGH = lax.Precision.HIGHEST
NEG = -1e30


def rms_scale(values, gain_vec):
    inverse = lax.rsqrt(jnp.mean(values * values, axis=-1, keepdims=True) + EPS)
    return values * inverse * gain_vec


def piece_ids(positions, starts, extent):
    inside = (positions[:, None] >= starts[None, :]) & (
        positions[:, None] < starts[None, :] + extent
    )
    labels = jnp.arange(1, starts.shape[0] + 1, dtype=jnp.int32)
    return jnp.sum(jnp.where(inside, labels[None, :], 0), axis=1)


def reach_bounds(positions, starts, extent):
    inside = (positions[:, None] >= starts[None, :]) & (
        positions[:, None] < starts[None, :] + extent
    )
    piece_last = jnp.max(jnp.where(inside, starts[None, :] + extent - 1, 0))
    piece_first = jnp.min(jnp.where(inside, starts[None, :], positions[0]))
    upper = jnp.maximum(positions[-1], piece_last)
    lower = jnp.minimum(positions[0], piece_first)
    return (upper, lower)


def allowed_mask(query_pos, query_ids, key_pos, key_ids):
    causal = key_pos[None, :] <= query_pos[:, None]
    shared = (key_ids[None, :] == query_ids[:, None]) & (query_ids[:, None] > 0)
    return causal | shared


def slot_dest(route_ids, n_ffn, capacity):
    flat_ids = route_ids.reshape(-1)
    onehot = (flat_ids[:, None] == jnp.arange(n_ffn, dtype=jnp.int32)[None, :]).astype(jnp.int32)
    earlier = jnp.cumsum(onehot, axis=0) - onehot
    slot_pos = jnp.sum(earlier * onehot, axis=1)
    return jnp.where(flat_ids < n_ffn, flat_ids * capacity + slot_pos, n_ffn * capacity)


def local_mix(
    normed, res_logits, router, mixing, const_proj, const_vec, expert_rows, route_ids, n_ffn
):
    n_all = router.shape[1]
    logits = jnp.dot(normed, router, precision=HIGH) + jnp.dot(res_logits, mixing, precision=HIGH)
    probs = jax.nn.softmax(logits, axis=-1)
    labels = jnp.arange(n_all, dtype=jnp.int32)
    chosen = jnp.sum(
        jnp.where(route_ids[:, :, None] == labels[None, None, :], probs[:, None, :], 0.0), axis=-1
    )
    gates = chosen / jnp.sum(chosen, axis=1, keepdims=True)
    pair_logits = jnp.dot(normed, const_proj, precision=HIGH)
    first_pair = jax.nn.softmax(pair_logits[:, 0:2], axis=-1)
    second_pair = jax.nn.softmax(pair_logits[:, 2:4], axis=-1)
    first_const = first_pair[:, 0:1] * normed + first_pair[:, 1:2] * const_vec[0][None, :]
    second_const = second_pair[:, 0:1] * normed + second_pair[:, 1:2] * const_vec[1][None, :]
    mixed = jnp.zeros_like(normed)
    for route_k in range(2):
        route_id = route_ids[:, route_k : route_k + 1]
        entry = jnp.where(route_id < n_ffn, expert_rows[:, route_k], 0.0)
        entry = entry + jnp.where(route_id == n_ffn + 1, normed, 0.0)
        entry = entry + jnp.where(route_id == n_ffn + 2, first_const, 0.0)
        entry = entry + jnp.where(route_id == n_ffn + 3, second_const, 0.0)
        mixed = mixed + gates[:, route_k : route_k + 1] * entry
    return mixed


def swiglu_act(gate_pre, up_pre):
    return jax.nn.silu(gate_pre) * up_pre


def body(
    tokens,
    gate_res,
    routes,
    piece_starts,
    norm_attn,
    norm_ffn,
    w_query,
    w_key,
    w_value,
    w_out,
    router,
    mixing,
    const_proj,
    const_vec,
    w_gate,
    w_up,
    w_down,
    cotangent,
):
    n_ffn = lax.axis_size("exp")
    rows_dev = tokens.shape[1]
    model_width = tokens.shape[2]
    seq_length = rows_dev * n_ffn
    score_scale = 1.0 / math.sqrt(HD)
    inputs_f = tokens[0].astype(jnp.float32)
    res_logits = gate_res[0]
    route_ids = routes[0]
    starts = piece_starts[0]
    full_query, full_key, full_value, full_out = (
        lax.all_gather(w_query, "fsdp", axis=0, tiled=True),
        lax.all_gather(w_key, "fsdp", axis=0, tiled=True),
        lax.all_gather(w_value, "fsdp", axis=0, tiled=True),
        lax.all_gather(w_out, "fsdp", axis=0, tiled=True),
    )
    attn_in = rms_scale(inputs_f, norm_attn).astype(jnp.bfloat16)
    query = jnp.dot(attn_in, full_query, preferred_element_type=jnp.float32).astype(jnp.bfloat16)
    key = jnp.dot(attn_in, full_key, preferred_element_type=jnp.float32).astype(jnp.bfloat16)
    value = jnp.dot(attn_in, full_value, preferred_element_type=jnp.float32).astype(jnp.bfloat16)
    keys_all, values_all = (
        lax.all_gather(key, "exp", axis=0, tiled=True),
        lax.all_gather(value, "exp", axis=0, tiled=True),
    )
    query_heads = query.reshape(rows_dev, H, HD)
    key_heads = keys_all.reshape(seq_length, H, HD)
    value_heads = values_all.reshape(seq_length, H, HD)
    query_pos = lax.axis_index("exp") * rows_dev + jnp.arange(rows_dev, dtype=jnp.int32)
    query_ids = piece_ids(query_pos, starts, PIECE)
    key_upper, query_lower = reach_bounds(query_pos, starts, PIECE)
    block_list = jnp.arange(seq_length // KBLK, dtype=jnp.int32)

    def score_block(block_index):
        key_first = block_index * KBLK
        key_block = lax.dynamic_slice_in_dim(key_heads, key_first, KBLK, 0)
        value_block = lax.dynamic_slice_in_dim(value_heads, key_first, KBLK, 0)
        key_pos = key_first + jnp.arange(KBLK, dtype=jnp.int32)
        key_ids = piece_ids(key_pos, starts, PIECE)
        scores = (
            jnp.einsum("qhd,khd->hqk", query_heads, key_block, preferred_element_type=jnp.float32)
            * score_scale
        )
        allowed = allowed_mask(query_pos, query_ids, key_pos, key_ids)[None]
        return (scores, allowed, key_block, value_block)

    def needed(block_index):
        return block_index * KBLK <= key_upper

    def lse_step(carry, block_index):

        def lse_active(state):
            run_max, run_sum = state
            scores, allowed, _, _ = score_block(block_index)
            scores = jnp.where(allowed, scores, NEG)
            new_max = jnp.maximum(run_max, jnp.max(scores, axis=-1))
            exp_terms = jnp.where(allowed, jnp.exp(scores - new_max[..., None]), 0.0)
            return (new_max, run_sum * jnp.exp(run_max - new_max) + jnp.sum(exp_terms, axis=-1))

        return (lax.cond(needed(block_index), lse_active, lambda state: state, carry), None)

    start_carry = (jnp.full((H, rows_dev), NEG, jnp.float32), jnp.zeros((H, rows_dev), jnp.float32))
    (run_max, run_sum), _ = lax.scan(lse_step, start_carry, block_list)
    log_norm = run_max + jnp.log(run_sum)

    def block_probs(scores, allowed):
        return jnp.where(allowed, jnp.exp(scores - log_norm[..., None]), 0.0)

    def out_step(accum, block_index):

        def out_active(total):
            scores, allowed, _, value_block = score_block(block_index)
            probs_low = block_probs(scores, allowed).astype(jnp.bfloat16)
            return total + jnp.einsum(
                "hqk,khd->qhd", probs_low, value_block, preferred_element_type=jnp.float32
            )

        return (lax.cond(needed(block_index), out_active, lambda total: total, accum), None)

    attn_sum, _ = lax.scan(out_step, jnp.zeros((rows_dev, H, HD), jnp.float32), block_list)
    attn_low = attn_sum.astype(jnp.bfloat16).reshape(rows_dev, model_width)
    hidden = inputs_f + jnp.dot(attn_low, full_out, preferred_element_type=jnp.float32)
    normed = rms_scale(hidden, norm_ffn)
    destination = slot_dest(route_ids, n_ffn, CAP)
    sources = jnp.arange(2 * rows_dev, dtype=jnp.int32) // 2
    slot_table = (
        jnp.full((n_ffn * CAP,), rows_dev, jnp.int32).at[destination].set(sources, mode="drop")
    )
    padded = jnp.concatenate(
        [normed.astype(jnp.bfloat16), jnp.zeros((1, model_width), jnp.bfloat16)], axis=0
    )
    dispatched = padded[slot_table].reshape(n_ffn, CAP, model_width)
    received = lax.all_to_all(dispatched, "exp", split_axis=0, concat_axis=0, tiled=True)
    full_gate, full_up, full_down = (
        lax.all_gather(w_gate[0], "fsdp", axis=0, tiled=True),
        lax.all_gather(w_up[0], "fsdp", axis=0, tiled=True),
        lax.all_gather(w_down[0], "fsdp", axis=0, tiled=True),
    )
    slot_rows = received.reshape(n_ffn * CAP, model_width)
    gate_pre = jnp.dot(slot_rows, full_gate, preferred_element_type=jnp.float32)
    up_pre = jnp.dot(slot_rows, full_up, preferred_element_type=jnp.float32)
    inner_act = swiglu_act(gate_pre, up_pre).astype(jnp.bfloat16)
    expert_result = jnp.dot(inner_act, full_down, preferred_element_type=jnp.float32).astype(
        jnp.bfloat16
    )
    returned = lax.all_to_all(
        expert_result.reshape(n_ffn, CAP, model_width),
        "exp",
        split_axis=0,
        concat_axis=0,
        tiled=True,
    )
    returned_pad = jnp.concatenate(
        [returned.reshape(n_ffn * CAP, model_width), jnp.zeros((1, model_width), jnp.bfloat16)],
        axis=0,
    )
    expert_rows = returned_pad[destination].astype(jnp.float32).reshape(rows_dev, 2, model_width)

    def mix_local(normed_in, logits_in, router_in, mixing_in, proj_in, vec_in, rows_in):
        return local_mix(
            normed_in, logits_in, router_in, mixing_in, proj_in, vec_in, rows_in, route_ids, n_ffn
        )

    moe_out, mix_pull = jax.vjp(
        mix_local, normed, res_logits, router, mixing, const_proj, const_vec, expert_rows
    )
    layer_out = (hidden + moe_out).astype(jnp.bfloat16)
    upstream = cotangent[0].astype(jnp.float32)
    d_normed_local, d_res_logits, d_router, d_mixing, d_const_proj, d_const_vec, d_expert_rows = (
        mix_pull(upstream)
    )
    d_rows_low = d_expert_rows.reshape(2 * rows_dev, model_width).astype(jnp.bfloat16)
    d_dispatched = (
        jnp.zeros((n_ffn * CAP, model_width), jnp.bfloat16)
        .at[destination]
        .set(d_rows_low, mode="drop")
    )
    d_received = lax.all_to_all(
        d_dispatched.reshape(n_ffn, CAP, model_width),
        "exp",
        split_axis=0,
        concat_axis=0,
        tiled=True,
    )
    d_received = d_received.reshape(n_ffn * CAP, model_width)
    d_inner = jnp.einsum("rd,fd->rf", d_received, full_down, preferred_element_type=jnp.float32)
    _, act_pull = jax.vjp(swiglu_act, gate_pre, up_pre)
    d_gate_pre, d_up_pre = act_pull(d_inner)
    d_gate_low = d_gate_pre.astype(jnp.bfloat16)
    d_up_low = d_up_pre.astype(jnp.bfloat16)
    grad_down_full = jnp.einsum(
        "rf,rd->fd", inner_act, d_received, preferred_element_type=jnp.float32
    )
    grad_gate_full = jnp.einsum(
        "rd,rf->df", slot_rows, d_gate_low, preferred_element_type=jnp.float32
    )
    grad_up_full = jnp.einsum("rd,rf->df", slot_rows, d_up_low, preferred_element_type=jnp.float32)
    d_slot_rows = (
        jnp.einsum("rf,df->rd", d_gate_low, full_gate, preferred_element_type=jnp.float32)
        + jnp.einsum("rf,df->rd", d_up_low, full_up, preferred_element_type=jnp.float32)
    ).astype(jnp.bfloat16)
    d_sent = lax.all_to_all(
        d_slot_rows.reshape(n_ffn, CAP, model_width), "exp", split_axis=0, concat_axis=0, tiled=True
    )
    d_sent_pad = jnp.concatenate(
        [d_sent.reshape(n_ffn * CAP, model_width), jnp.zeros((1, model_width), jnp.bfloat16)],
        axis=0,
    )
    d_normed_sent = jnp.sum(
        d_sent_pad[destination].astype(jnp.float32).reshape(rows_dev, 2, model_width), axis=1
    )
    _, norm_ffn_pull = jax.vjp(rms_scale, hidden, norm_ffn)
    d_hidden_part, d_norm_ffn = norm_ffn_pull(d_normed_local + d_normed_sent)
    d_hidden = upstream + d_hidden_part
    d_hidden_low = d_hidden.astype(jnp.bfloat16)
    grad_out_full = jnp.einsum(
        "td,te->de", attn_low, d_hidden_low, preferred_element_type=jnp.float32
    )
    d_attn = jnp.einsum(
        "te,de->td", d_hidden_low, full_out, preferred_element_type=jnp.float32
    ).astype(jnp.bfloat16)
    d_attn_heads = d_attn.reshape(rows_dev, H, HD)
    zero_block = jnp.zeros((KBLK, H, HD), jnp.float32)

    def delta_terms(block_index):
        scores, allowed, _, value_block = score_block(block_index)
        probs = block_probs(scores, allowed)
        d_probs = jnp.einsum(
            "qhd,khd->hqk", d_attn_heads, value_block, preferred_element_type=jnp.float32
        )
        part = jnp.sum(probs * d_probs, axis=-1)
        return (
            part,
            jnp.einsum(
                "hqk,qhd->khd",
                probs.astype(jnp.bfloat16),
                d_attn_heads,
                preferred_element_type=jnp.float32,
            ),
        )

    def query_terms(block_index, row_delta):
        scores, allowed, key_block, value_block = score_block(block_index)
        probs = block_probs(scores, allowed)
        d_probs = jnp.einsum(
            "qhd,khd->hqk", d_attn_heads, value_block, preferred_element_type=jnp.float32
        )
        d_scores = (probs * (d_probs - row_delta[..., None])).astype(jnp.bfloat16)
        part = (
            jnp.einsum("hqk,khd->qhd", d_scores, key_block, preferred_element_type=jnp.float32)
            * score_scale
        )
        return (
            part,
            jnp.einsum("hqk,qhd->khd", d_scores, query_heads, preferred_element_type=jnp.float32)
            * score_scale,
        )

    def delta_step(total, block_index):

        def delta_active(running):
            part, grad_block = delta_terms(block_index)
            return (running + part, grad_block)

        return lax.cond(
            needed(block_index), delta_active, lambda running: (running, zero_block), total
        )

    row_delta, grad_values = lax.scan(delta_step, jnp.zeros((H, rows_dev), jnp.float32), block_list)

    def query_step(total, block_index):

        def query_active(running):
            part, grad_block = query_terms(block_index, row_delta)
            return (running + part, grad_block)

        return lax.cond(
            needed(block_index), query_active, lambda running: (running, zero_block), total
        )

    d_query_sum, grad_keys = lax.scan(
        query_step, jnp.zeros((rows_dev, H, HD), jnp.float32), block_list
    )
    grad_keys = grad_keys.reshape(seq_length, model_width)
    grad_values = grad_values.reshape(seq_length, model_width)
    d_key_sum, d_value_sum = (
        lax.psum_scatter(
            grad_keys.astype(jnp.bfloat16), "exp", scatter_dimension=0, tiled=True
        ).astype(jnp.float32),
        lax.psum_scatter(
            grad_values.astype(jnp.bfloat16), "exp", scatter_dimension=0, tiled=True
        ).astype(jnp.float32),
    )
    d_query_low = d_query_sum.reshape(rows_dev, model_width).astype(jnp.bfloat16)
    d_key_low = d_key_sum.astype(jnp.bfloat16)
    d_value_low = d_value_sum.astype(jnp.bfloat16)
    d_attn_in = (
        jnp.einsum("te,de->td", d_query_low, full_query, preferred_element_type=jnp.float32)
        + jnp.einsum("te,de->td", d_key_low, full_key, preferred_element_type=jnp.float32)
        + jnp.einsum("te,de->td", d_value_low, full_value, preferred_element_type=jnp.float32)
    )
    grad_query_full = jnp.einsum(
        "td,te->de", attn_in, d_query_low, preferred_element_type=jnp.float32
    )
    grad_key_full = jnp.einsum("td,te->de", attn_in, d_key_low, preferred_element_type=jnp.float32)
    grad_value_full = jnp.einsum(
        "td,te->de", attn_in, d_value_low, preferred_element_type=jnp.float32
    )
    _, norm_attn_pull = jax.vjp(rms_scale, inputs_f, norm_attn)
    d_inputs_part, d_norm_attn = norm_attn_pull(d_attn_in)
    grad_tokens = (d_hidden + d_inputs_part).astype(jnp.bfloat16)
    attn_shards = (
        lax.psum_scatter(
            grad_query_full.astype(jnp.bfloat16), "fsdp", scatter_dimension=0, tiled=True
        ).astype(jnp.float32),
        lax.psum_scatter(
            grad_key_full.astype(jnp.bfloat16), "fsdp", scatter_dimension=0, tiled=True
        ).astype(jnp.float32),
        lax.psum_scatter(
            grad_value_full.astype(jnp.bfloat16), "fsdp", scatter_dimension=0, tiled=True
        ).astype(jnp.float32),
        lax.psum_scatter(
            grad_out_full.astype(jnp.bfloat16), "fsdp", scatter_dimension=0, tiled=True
        ).astype(jnp.float32),
    )
    attn_shards = (
        lax.psum(attn_shards[0].astype(jnp.bfloat16), "exp").astype(jnp.float32),
        lax.psum(attn_shards[1].astype(jnp.bfloat16), "exp").astype(jnp.float32),
        lax.psum(attn_shards[2].astype(jnp.bfloat16), "exp").astype(jnp.float32),
        lax.psum(attn_shards[3].astype(jnp.bfloat16), "exp").astype(jnp.float32),
    )
    expert_shards = (
        lax.psum_scatter(
            grad_gate_full.astype(jnp.bfloat16), "fsdp", scatter_dimension=0, tiled=True
        ).astype(jnp.float32),
        lax.psum_scatter(
            grad_up_full.astype(jnp.bfloat16), "fsdp", scatter_dimension=0, tiled=True
        ).astype(jnp.float32),
        lax.psum_scatter(
            grad_down_full.astype(jnp.bfloat16), "fsdp", scatter_dimension=0, tiled=True
        ).astype(jnp.float32),
    )
    small_sums = lax.psum(
        (d_norm_attn, d_norm_ffn, d_router, d_mixing, d_const_proj, d_const_vec), ("exp", "fsdp")
    )
    return (
        layer_out[None],
        grad_tokens[None],
        d_res_logits[None],
        small_sums[0],
        small_sums[1],
        attn_shards[0],
        attn_shards[1],
        attn_shards[2],
        attn_shards[3],
        small_sums[2],
        small_sums[3],
        small_sums[4],
        small_sums[5],
        expert_shards[0][None],
        expert_shards[1][None],
        expert_shards[2][None],
    )


MESH = pl.DeviceIdType.MESH
BF = jnp.bfloat16
F32 = jnp.float32
LN2 = math.log(2.0)
QSCALE = 1.0 / (LN2 * math.sqrt(HD))
CHUNKS = 4


class Place:
    def __init__(self):
        self.e = lax.axis_index("exp")
        self.f = lax.axis_index("fsdp")
        self.z = self.f // 2
        self.x = self.f % 2
        self.sib = self.e + 1 - 2 * (self.e % 2)
        self.yp = (self.e + 2) % 4
        self.diag = (self.sib + 2) % 4
        self.xf = self.f + 1 - 2 * self.x
        self.exp_peers = (self.sib, self.yp, self.diag)

    def zf(self, d):
        return ((self.z + d) % 4) * 2 + self.x

    def fp(self, r):
        return (self.f + r) % 8

    def far_first(self, j):
        return (self.e + (j % 2) * (1 - 2 * (self.e % 2)) + 2 * (1 - j // 2)) % 4

    def near_first(self, j):
        return (self.e + (j % 2) * (1 - 2 * (self.e % 2)) + 2 * (j // 2)) % 4

    def share_order(self, j):
        return (self.e + (1 - j % 2) * (1 - 2 * (self.e % 2)) + 2 * (1 - j // 2)) % 4

    def barrier(self):
        sem = pltpu.get_barrier_semaphore()
        for p in self.exp_peers:
            pl.semaphore_signal(sem, inc=1, device_id=(p, self.f), device_id_type=MESH)
        for r in range(1, 8):
            pl.semaphore_signal(sem, inc=1, device_id=(self.e, self.fp(r)), device_id_type=MESH)
        pl.semaphore_wait(sem, 10)

    def send(self, src, dst, ss, rs, e=None, f=None):
        return pltpu.make_async_remote_copy(
            src_ref=src,
            dst_ref=dst,
            send_sem=ss,
            recv_sem=rs,
            device_id=(self.e if e is None else e, self.f if f is None else f),
            device_id_type=MESH,
        )


def lane_of(shape):
    return lax.broadcasted_iota(jnp.int32, shape, len(shape) - 1)


def row_of(shape):
    return lax.broadcasted_iota(jnp.int32, shape, 0)


def dot(a, b, ca=1, cb=0, precision=None):
    return lax.dot_general(a, b, (((ca,), (cb,)), ((), ())), precision=precision, preferred_element_type=F32)


def allowed_block(size, first):
    key, query = row_of((size, size)), lane_of((size, size))
    inside_k = (key >= first) & (key < first + PIECE)
    inside_q = (query >= first) & (query < first + PIECE)
    return (key <= query) | (inside_k & inside_q)


def k1_kernel(
    x_ref, u_ref, wq_ref, wk_ref, wv_ref, wo_ref, wg_ref, wu_ref, wd_ref, gres_ref, routes_ref, starts_ref,
    gain_a_ref, gain_f_ref, router_ref, proj_ref, mix_ref,
    attn_all, q_s, k_s, v_s, o_s, lse_s, hidden_ref, aux_ref, place_ref, ret_o, ret_d, wo_full, wq_full,
    grad_gate, grad_up, grad_down, far_gate, next_gate, side_gate, side_up,
    gate_full, up_full, down_full, wq_own, vt_s, attn_recv, nb, snd_r, snd_d, recv_r, recv_d, m_s, l_s, acc_s,
    acc, d_acc, st_gate, st_up, st_down,
    wq_ss, wq_rs, wo_ss, wo_rs, at_ss, at_rs, o_ss, o_rs, dr_ss, dr_rs, dd_ss, dd_rs, ro_ss, ro_rs, rd_ss, rd_rs,
    us, ur, ds, dr, xs, xr, vs, vr, wc_ss, wc_rs, loc, st_sem, fs, fr,
):
    me = Place()
    e, f, z, xf = me.e, me.f, me.z, me.xf
    T, D = x_ref.shape
    C = D // 4
    R = wo_ref.shape[0]
    FF = wg_ref.shape[1]
    W = FF // CHUNKS
    S = 4 * CAP
    for k in range(4):

        @pl.when(e == k)
        def _():
            for i, w in enumerate((wq_ref, wk_ref, wv_ref)):
                wq_own[:, i * C : (i + 1) * C] = w[:, k * C : (k + 1) * C]

    me.barrier()

    def half(core):
        return pl.ds(pl.multiple_of(core * (R // 2), 16), R // 2)

    def wq_slot(index):
        return wq_full.at[pl.ds(pl.multiple_of(index * R, 32), R)]

    def wo_slot(index):
        return wo_full.at[index, half(e % 2)]

    early = (
        (wq_own, wq_slot, wq_ss, wq_rs, 0),
        (wo_ref.at[half(e % 2)], wo_slot, wo_ss, wo_rs, 1),
    )
    for src, slot_of, ss, rs, li in early:
        for d in (1, 3, 2):
            me.send(src, slot_of(f), ss.at[d], rs.at[d], f=me.zf(d)).start()
        me.send(src, slot_of(f), ss.at[0], rs.at[0], f=xf).start()
        pltpu.make_async_copy(src, slot_of(f), loc.at[li]).start()

    xv = x_ref[...].astype(F32)
    inv = lax.rsqrt(jnp.mean(xv * xv, axis=-1, keepdims=True) + EPS)
    attn_all[e] = (xv * inv * gain_a_ref[...].reshape(1, D)).astype(BF)

    def at_copy(i, block, to=None):
        ref = attn_all.at[block]
        return me.send(ref, ref, at_ss.at[i], at_rs.at[i], e=to)

    at_copy(1, e, me.yp).start()
    at_copy(0, e, me.sib).start()

    def early_index(d, other):
        return ((z - d + 4) % 4) * 2 + (1 - me.x if other else me.x)

    def early_forward(src, slot_of, ss, rs, li):
        for d in (1, 3, 2):
            slot = slot_of(early_index(d, False))
            me.send(slot, slot, ss.at[d], rs.at[d]).wait_recv()
            me.send(slot, slot, ss.at[3 + d], rs.at[3 + d], f=xf).start()

    def early_wait(src, slot_of, ss, rs, li):
        pltpu.make_async_copy(src, slot_of(f), loc.at[li]).wait()
        me.send(slot_of(xf), slot_of(xf), ss.at[0], rs.at[0]).wait_recv()
        for d in (1, 2, 3):
            slot = slot_of(early_index(d, True))
            me.send(slot, slot, ss.at[3 + d], rs.at[3 + d]).wait_recv()

    def wo_copy(core, to=None):
        ref = wo_full.at[:, half(core)]
        return me.send(ref, ref, wc_ss.at[0], wc_rs.at[0], e=to)

    def cut(ref, c):
        return ref if c is None else ref.at[:, pl.ds(pl.multiple_of(c * W, W), W)]

    def up_copy(n, p, src, dst, to=None):
        return me.send(src, dst, us.at[n, p], ur.at[n, p], f=to)

    def down_copy(n, p, src, dst, to=None):
        return me.send(src, dst, ds.at[n, p], dr.at[n, p], f=to)

    def x_copy(n, i, src, dst, to=None):
        return me.send(src, dst, xs.at[n, i], xr.at[n, i], f=to)

    def relay(n, p, src, full, c):
        def at(slot):
            return cut(full.at[slot], c)

        if p == 0:
            own = cut(src, c)
            x_copy(n, 0, own, at(f), xf).start()

            @pl.when(z <= 2)
            def _():
                up_copy(n, 0, own, at(f), f + 2).start()

            @pl.when(z >= 1)
            def _():
                down_copy(n, 0, own, at(f), f - 2).start()

            return

        if p == 1 and c is None:
            x_copy(n, 0, at(xf), at(xf)).wait_recv()

            @pl.when(z <= 2)
            def _():
                side_copy(0, at(xf), at(xf), f + 2).start()

            @pl.when(z >= 1)
            def _():
                side_copy(1, at(xf), at(xf), f - 2).start()

        @pl.when(z >= p)
        def _():
            slot = at(f - 2 * p)
            up_copy(n, p - 1, slot, slot).wait_recv()
            if p <= 2:

                @pl.when(z <= 2)
                def _():
                    up_copy(n, p, slot, slot, f + 2).start()

            if p > 1 or c is not None:
                x_copy(n, p, slot, slot, xf).start()

        @pl.when(z + p <= 3)
        def _():
            slot = at(f + 2 * p)
            down_copy(n, p - 1, slot, slot).wait_recv()
            if p <= 2:

                @pl.when(z >= 1)
                def _():
                    down_copy(n, p, slot, slot, f - 2).start()

            if p > 1 or c is not None:
                x_copy(n, 3 + p, slot, slot, xf).start()

    def side_copy(i, src, dst, to=None):
        return me.send(src, dst, vs.at[i], vr.at[i], f=to)

    def relay_chunk(p, c):
        relay(1 + 2 * c, p, wg_ref, gate_full, c)
        relay(2 + 2 * c, p, wu_ref, up_full, c)

    def experts(p):
        relay(0, p, wd_ref, down_full, None)
        for c in range(CHUNKS):
            relay_chunk(p, c)

    own_loads = ((wd_ref, down_full), (wg_ref, gate_full), (wu_ref, up_full))

    def own_load(i):
        src, full = own_loads[i]
        return pltpu.make_async_copy(src, full.at[f], loc.at[2 + i])

    relay(0, 0, wd_ref, down_full, None)
    early_forward(*early[0])
    for c in range(CHUNKS):
        relay_chunk(0, c)
    for i in range(3):
        own_load(i).start()

    at_copy(1, me.yp).wait_recv()
    at_copy(2, me.yp, me.sib).start()
    at_copy(0, me.sib).wait_recv()
    early_wait(*early[0])
    early_forward(*early[1])
    at_copy(2, me.diag).wait_recv()

    def qkv_step(i, _):
        b = i // 2
        r = pl.ds(pl.multiple_of((i % 2) * 256, 256), 256)
        out = dot(attn_all[b, r, :], wq_full[...])
        q_s[b, r, :] = (out[:, 0:C] * QSCALE).astype(BF)
        k_s[b, r, :] = out[:, C : 2 * C].astype(BF)
        v = out[:, 2 * C : 3 * C]
        v_s[b, r, :] = v.astype(BF)
        vt_s[b, :, r] = v.T.astype(BF)
        return 0

    lax.fori_loop(0, 8, qkv_step, 0)

    head_of = lane_of((T, C)) // HD
    lse_s[...] = jnp.zeros_like(lse_s)

    def query_step(j, _):
        qb = me.far_first(j)
        queries = [jnp.where(head_of == h, q_s[qb], jnp.zeros((T, C), BF)) for h in range(3)]
        allowed = allowed_block(T, starts_ref[0, qb] - qb * T)
        for h in range(3):
            hr = pl.ds(h * HD, HD)
            s = jnp.where(allowed, dot(k_s[qb], queries[h], 1, 1), NEG)
            m = jnp.max(s, axis=0, keepdims=True)
            p = jnp.exp2(s - m)
            m_s[h : h + 1] = m
            l_s[h : h + 1] = jnp.sum(p, axis=0, keepdims=True)
            acc_s[hr] = dot(vt_s[qb, hr, :], p.astype(BF))

        def key_step(kb, _):
            for h in range(3):
                hr = pl.ds(h * HD, HD)
                query = jnp.where(head_of == h, q_s[qb], jnp.zeros((T, C), BF))
                s = dot(k_s[kb], query, 1, 1)
                m_old = m_s[h : h + 1]
                m = jnp.maximum(m_old, jnp.max(s, axis=0, keepdims=True))
                scale = jnp.exp2(m_old - m)
                p = jnp.exp2(s - m)
                m_s[h : h + 1] = m
                l_s[h : h + 1] = l_s[h : h + 1] * scale + jnp.sum(p, axis=0, keepdims=True)
                acc_s[hr] = acc_s[hr] * scale + dot(vt_s[kb, hr, :], p.astype(BF))
            return 0

        lax.fori_loop(0, qb, key_step, 0)
        for h in range(3):
            hr = pl.ds(h * HD, HD)
            total = l_s[h : h + 1]
            acc_s[hr] = acc_s[hr] / total
            lse_s[qb, h : h + 1, :] = m_s[h : h + 1] + jnp.log2(total)
        o_s[qb] = acc_s[...].T.astype(BF)
        return 0

    def o_copy(i, to=None):
        p = me.exp_peers[i]
        if to is None:
            return me.send(o_s.at[p], attn_recv.at[p], o_ss.at[i], o_rs.at[i])
        return me.send(o_s.at[p], attn_recv.at[e], o_ss.at[i], o_rs.at[i], e=p)

    lax.fori_loop(0, 2, query_step, 0)
    o_copy(1, True).start()
    o_copy(2, True).start()
    early_wait(*early[1])
    wo_copy(e % 2, me.sib).start()
    experts(1)
    lax.fori_loop(2, 4, query_step, 0)
    o_copy(0, True).start()
    attn_recv[e] = o_s[e]

    r0, r1 = routes_ref[0:1, :], routes_ref[1:2, :]
    expert = row_of((8, T))
    chosen = (expert == r0) | (expert == r1)
    earlier = (row_of((T, T)) < lane_of((T, T))).astype(BF)
    count = dot(chosen.astype(BF), earlier).astype(jnp.int32)
    count = jnp.where(chosen, count, -1)
    slot_id = row_of((CAP, T))
    for k in range(4):
        place_ref[k] = jnp.where(slot_id == count[k : k + 1, :], 1.0, 0.0).astype(BF)

    wo_copy(1 - e % 2).wait_recv()
    for i in (0, 1, 2):
        o_copy(i).wait_recv()

    def hidden_step(i, _):
        r = pl.ds(pl.multiple_of(i * 256, 256), 256)
        h = x_ref[r, :].astype(F32)
        for b in range(4):
            h = h + dot(attn_recv[b, r, :], wo_full[2 * b : 2 * b + 2].reshape(C, D))
        hidden_ref[r, :] = h
        n = h * lax.rsqrt(jnp.mean(h * h, axis=-1, keepdims=True) + EPS) * gain_f_ref[...].reshape(1, D)
        nb[r, :] = n.astype(BF)
        aux_ref[0:8, r] = dot(router_ref[...], n, 1, 1, HIGH) + dot(mix_ref[...], gres_ref[:, r], 0, 0, HIGH)
        aux_ref[8:12, r] = dot(proj_ref[...], n, 1, 1, HIGH)
        return 0

    relay(0, 2, wd_ref, down_full, None)
    lax.fori_loop(0, 2, hidden_step, 0)
    relay_chunk(2, 0)
    relay_chunk(2, 1)

    logits = aux_ref[0:8, :]
    top = jnp.max(jnp.where(chosen, logits, NEG), axis=0, keepdims=True)
    weight = jnp.where(chosen, jnp.exp(logits - top), 0.0)
    gates = weight / jnp.sum(weight, axis=0, keepdims=True)
    pairs = aux_ref[8:12, :]
    other = jnp.concatenate([pairs[1:2], pairs[0:1], pairs[3:4], pairs[2:3]], axis=0)
    aux_ref[0:8, :] = gates
    aux_ref[8:12, :] = 1.0 / (1.0 + jnp.exp(other - pairs))
    aux_ref[12:16, :] = jnp.zeros((4, T), F32)

    def d_copy(i, ref, out, ss, rs, k, to=None):
        return me.send(ref.at[k], out.at[e if to is not None else k], ss.at[i], rs.at[i], e=to)

    def dispatch_step(j, _):
        k = me.far_first(j)
        i = (j + 1) % 4
        place = place_ref[k]
        snd_r[k] = dot(place, nb[...]).astype(BF)
        gate = aux_ref[pl.ds(k, 1), :]
        gated = jnp.where(place > 0, gate.astype(BF), jnp.zeros((CAP, T), BF))
        snd_d[k] = dot(gated, u_ref[...]).astype(BF)

        @pl.when(j != 2)
        def _():
            d_copy(i, snd_r, recv_r, dr_ss, dr_rs, k, k).start()
            d_copy(i, snd_d, recv_d, dd_ss, dd_rs, k, k).start()

        @pl.when(j == 2)
        def _():
            recv_r[k] = snd_r[k]
            recv_d[k] = snd_d[k]

        return 0

    lax.fori_loop(0, 4, dispatch_step, 0)
    relay_chunk(2, 2)
    relay_chunk(2, 3)
    relay(0, 3, wd_ref, down_full, None)
    relay_chunk(3, 0)
    for i, p in enumerate(me.exp_peers):
        d_copy(i, snd_r, recv_r, dr_ss, dr_rs, p).wait()
        d_copy(i, snd_d, recv_d, dd_ss, dd_rs, p).wait()

    acc[...] = jnp.zeros_like(acc)
    d_acc[...] = jnp.zeros_like(d_acc)

    def unit_wait(n, full, c):
        def at(slot):
            return cut(full.at[slot], c)

        if c is None:

            @pl.when(z >= 1)
            def _():
                side_copy(0, at(xf - 2), at(xf - 2)).wait_recv()

            @pl.when(z <= 2)
            def _():
                side_copy(1, at(xf + 2), at(xf + 2)).wait_recv()

        else:
            x_copy(n, 0, at(xf), at(xf)).wait_recv()
        for p in (2, 3) if c is None else (1, 2, 3):

            @pl.when(z >= p)
            def _():
                x_copy(n, p, at(xf - 2 * p), at(xf - 2 * p)).wait_recv()

            @pl.when(z + p <= 3)
            def _():
                x_copy(n, 3 + p, at(xf + 2 * p), at(xf + 2 * p)).wait_recv()

    stages = ((st_gate, grad_gate, 0), (st_up, grad_up, 1), (st_down, grad_down, 2))

    def stage_copy(c, i):
        st, out, _ = stages[i]
        if i == 2:
            dst = out.at[pl.ds(2 * c, 2)]
        else:
            dst = out.at[:, :, pl.ds(pl.multiple_of(c * W, W), W)]
        return pltpu.make_async_copy(st, dst, st_sem.at[i])

    def ret_copy(i, snd, ret, ss, rs, to=None):
        p = me.exp_peers[i]
        return me.send(snd.at[p], ret.at[e if to else p], ss.at[i], rs.at[i], e=p if to else None)

    def expert_step(c, _):
        @pl.when(c < CHUNKS - 1)
        def _():
            relay_chunk(3, c + 1)

        @pl.when(c == 0)
        def _():
            for i in range(3):
                own_load(i).wait()
            unit_wait(0, down_full, None)

        unit_wait(1 + 2 * c, gate_full, c)
        unit_wait(2 + 2 * c, up_full, c)
        w = pl.ds(pl.multiple_of(c * W, W), W)
        row_in = recv_r[...].reshape(S, D)
        d_in = recv_d[...].reshape(S, D)
        w_gate = gate_full[:, :, w].reshape(D, W)
        w_up = up_full[:, :, w].reshape(D, W)
        w_down = down_full[pl.ds(2 * c, 2)].reshape(W, D)
        g = dot(row_in, w_gate)
        up = dot(row_in, w_up)
        sig = 1.0 / (1.0 + jnp.exp(-g))
        silu = g * sig
        inner = (silu * up).astype(BF)
        acc[...] += dot(inner, w_down)

        @pl.when(c == CHUNKS - 1)
        def _():
            snd_r[...] = acc[...].astype(BF).reshape(4, CAP, D)
            for i in (1, 2, 0):
                ret_copy(i, snd_r, ret_o, ro_ss, ro_rs, True).start()
            ret_o[e] = snd_r[e]

        d_inner = dot(d_in, w_down, 1, 1)
        d_up = (d_inner * silu).astype(BF)
        d_gate = (d_inner * up * (sig + silu * (1.0 - sig))).astype(BF)
        d_acc[...] += dot(d_gate, w_gate, 1, 1) + dot(d_up, w_up, 1, 1)

        @pl.when(c == CHUNKS - 1)
        def _():
            snd_d[...] = d_acc[...].astype(BF).reshape(4, CAP, D)
            for i in (1, 2, 0):
                ret_copy(i, snd_d, ret_d, rd_ss, rd_rs, True).start()
            ret_d[e] = snd_d[e]

        @pl.when(c > 0)
        def _():
            for i in range(3):
                stage_copy(c - 1, i).wait()

        st_down[...] = dot(inner, d_in, 0, 0).astype(BF).reshape(2, W // 2, D)
        st_gate[...] = dot(row_in, d_gate, 0, 0).astype(BF).reshape(8, R, W)
        st_up[...] = dot(row_in, d_up, 0, 0).astype(BF).reshape(8, R, W)
        for i in range(3):
            stage_copy(c, i).start()
        return 0

    lax.fori_loop(0, CHUNKS, expert_step, 0)
    for i in range(3):
        stage_copy(CHUNKS - 1, i).wait()

    partner = z + 1 - 2 * (z % 2)
    far_row = 2 * ((partner + 2) % 4) + 1 - me.x
    next_row = 2 * ((z + 2) % 4) + 1 - me.x
    side_row = 2 * partner + 1 - me.x
    far = (
        (grad_gate.at[far_row], far_gate, xf),
        (grad_gate.at[side_row], side_gate, 2 * partner + me.x),
        (grad_gate.at[next_row], next_gate, xf),
        (grad_up.at[side_row], side_up, 2 * partner + me.x),
    )
    for i, (src, dst, to) in enumerate(far):
        me.send(src, dst, fs.at[i], fr.at[i], f=to).start()

    for src, slot_of, ss, rs, li in early:
        for j in range(7):
            me.send(slot_of(f), slot_of(f), ss.at[j], rs.at[j]).wait_send()
    wo_copy(e % 2).wait_send()
    for i in range(3):
        at_copy(i, e).wait_send()
        o_copy(i).wait_send()
    def relay_end(n, full, c):
        slot = cut(full.at[f], c)
        x_copy(n, 0, slot, slot).wait_send()

        @pl.when(z <= 2)
        def _():
            up_copy(n, 0, slot, slot).wait_send()
            if c is None:
                side_copy(0, slot, slot).wait_send()

        @pl.when(z >= 1)
        def _():
            down_copy(n, 0, slot, slot).wait_send()
            if c is None:
                side_copy(1, slot, slot).wait_send()

        for p in (1, 2, 3):

            @pl.when(z >= p)
            def _():
                if p <= 2:

                    @pl.when(z <= 2)
                    def _():
                        up_copy(n, p, slot, slot).wait_send()

                if p > 1 or c is not None:
                    x_copy(n, p, slot, slot).wait_send()

            @pl.when(z + p <= 3)
            def _():
                if p <= 2:

                    @pl.when(z >= 1)
                    def _():
                        down_copy(n, p, slot, slot).wait_send()

                if p > 1 or c is not None:
                    x_copy(n, 3 + p, slot, slot).wait_send()

    relay_end(0, down_full, None)

    def end_step(c, _):
        relay_end(1 + 2 * c, gate_full, c)
        relay_end(2 + 2 * c, up_full, c)
        return 0

    lax.fori_loop(0, CHUNKS, end_step, 0)
    for i in range(3):
        ret_copy(i, snd_r, ret_o, ro_ss, ro_rs).wait()
        ret_copy(i, snd_d, ret_d, rd_ss, rd_rs).wait()
    for i, (src, dst, to) in enumerate(far):
        me.send(src, dst, fs.at[i], fr.at[i]).wait()


def sds(shape, dtype):
    return jax.ShapeDtypeStruct(shape, dtype)


def vmem():
    return pl.BlockSpec(memory_space=pltpu.VMEM)


def anyspace():
    return pl.BlockSpec(memory_space=pl.ANY)


def smem():
    return pl.BlockSpec(memory_space=pltpu.SMEM)


def call_k1(x, u, wq, wk, wv, wo, wg, wu, wd, gres, routes, starts, gain_a, gain_f, router, proj, mix):
    T, D = x.shape
    C, R, FF, S = D // 4, D // 8, wg.shape[1], 4 * CAP
    n = 1 + 2 * CHUNKS
    dma = pltpu.SemaphoreType.DMA
    VM = pltpu.VMEM
    block = VM((4, CAP, D), BF)
    return pl.pallas_call(
        k1_kernel,
        name="forward",
        out_shape=(
            sds((4, T, D), BF), sds((4, T, C), BF), sds((4, T, C), BF), sds((4, T, C), BF), sds((4, T, C), BF),
            sds((4, 8, T), F32), sds((T, D), F32), sds((16, T), F32), sds((4, CAP, T), BF),
            sds((4, CAP, D), BF), sds((4, CAP, D), BF), sds((8, R, D), BF), sds((D, 3 * C), BF),
            sds((8, R, FF), BF), sds((8, R, FF), BF), sds((8, FF // 8, D), BF),
            sds((R, FF), BF), sds((R, FF), BF), sds((R, FF), BF), sds((R, FF), BF),
        ),
        in_specs=[vmem()] * 5 + [anyspace()] * 4 + [vmem()] * 2 + [smem()] + [vmem()] * 5,
        out_specs=tuple([vmem()] * 13 + [anyspace()] * 7),
        scratch_shapes=[
            VM((8, R, FF), BF), VM((8, R, FF), BF), VM((8, FF // 8, D), BF), VM((R, 3 * C), BF), VM((4, C, T), BF),
            VM((4, T, C), BF), VM((T, D), BF), block, block, block, block, VM((8, T), F32), VM((8, T), F32), VM((C, T), F32),
            VM((S, D), F32), VM((S, D), F32), VM((8, R, FF // CHUNKS), BF), VM((8, R, FF // CHUNKS), BF), VM((2, FF // 8, D), BF),
            dma((7,)), dma((7,)), dma((7,)), dma((7,)),
        ] + [dma((3,))] * 12 + [
            dma((n, 3)), dma((n, 3)), dma((n, 3)), dma((n, 3)), dma((n, 7)), dma((n, 7)),
            dma((2,)), dma((2,)), dma((1,)), dma((1,)), dma((5,)), dma((3,)), dma((4,)), dma((4,)),
        ],
        compiler_params=pltpu.CompilerParams(collective_id=0, has_side_effects=True, vmem_limit_bytes=60 << 20),
    )(x, u, wq, wk, wv, wo, wg, wu, wd, gres, routes, starts, gain_a, gain_f, router, proj, mix)


def k2_kernel(
    ret_o, ret_d, hidden, u_ref, x_ref, aux_ref, place_ref, gres_ref,
    attn_hbm, q_hbm, k_hbm, v_hbm, o_hbm, lse_s, wo_hbm, wqkv_hbm, gain_a_ref, gain_f_ref, router_ref, proj_ref, mix_ref, cvec_ref, starts_ref,
    g_gate, g_up, g_down, far_gate, next_gate, side_gate, side_up,
    layer_out, grad_tokens, d_res, small_out, ag_out, go_b, eg_out, eu_out, ed_out,
    xin_g, xin_u, xin_d, own_g, own_u, own_d, zin_g, zin_u, zin_d, cross_g, cross_u, cross_d,
    attn_all, q_s, k_s, v_s, o_s, wo, wqkv,
    dh_all, da, kt_s, dq, dk, dv, dqt, pin, py_in, d_hidden, wk_s, del_r, gt, go_acc, ag_s, ag_in, ag_fin, go_s, go_in,
    small, sm1, sm2,
    load_sem, late_sem, xs, xr, zs, zr, own_sem, dh_ss, dh_rs, fw_ss, fw_rs, go_ss, go_rs, gb_ss, gb_rs, pd_ss, pd_rs, ag_ss, ag_rs,
    ab_ss, ab_rs, s1_ss, s1_rs, s2_ss, s2_rs,
):
    me = Place()
    e, f, z, x, xf = me.e, me.f, me.z, me.x, me.xf
    T, D = x_ref.shape
    C = D // 4
    R = D // 8
    M = 128

    partner = z + 1 - 2 * (z % 2)
    targets = ((partner + 2) % 4, (z + 2) % 4, z, partner)
    parts = (
        (g_gate, xin_g, own_g, zin_g, cross_g, eg_out),
        (g_up, xin_u, own_u, zin_u, cross_u, eu_out),
        (g_down, xin_d, own_d, zin_d, cross_d, ed_out),
    )

    def load_copy(i):
        src, dst = ((far_gate, xin_g.at[0]), (next_gate, xin_g.at[1]), (side_gate, cross_g), (side_up, cross_u))[i]
        return pltpu.make_async_copy(src, dst, load_sem.at[i])

    def own_copy(w, i, column):
        return pltpu.make_async_copy(parts[w][0].at[2 * targets[i] + column], parts[w][2], own_sem.at[w])

    def x_copy(w, i):
        src = parts[w][4] if i == 2 and w < 2 else parts[w][0].at[2 * targets[i] + 1 - x]
        dst = parts[w][4] if i == 3 else parts[w][1].at[i]
        return me.send(src, dst, xs.at[w, i], xr.at[w, i], f=xf)

    def z_copy(w, i):
        if i == 2:
            src = parts[w][0].at[2 * partner + x] if w < 2 else parts[w][4]
        else:
            src = parts[w][1].at[i]
        to = targets[1] if i == 1 else partner
        return me.send(src, parts[w][3].at[i], zs.at[w, i], zr.at[w, i], f=2 * to + x)

    def add(dst, *terms):
        total = dst.astype(F32)
        for term in terms:
            total = total + term.astype(F32)
        return total.astype(BF)

    def rs_far(w):
        xin, own = parts[w][1:3]
        if w:
            x_copy(w, 0).wait_recv()
        else:
            load_copy(0).wait()
        own_copy(w, 0, x).wait()
        xin[0] = add(xin[0], own[...])
        z_copy(w, 0).start()
        own_copy(w, 1, x).start()

    def rs_cross(w):
        xin, own, zin = parts[w][1:4]
        if w:
            x_copy(w, 1).wait_recv()
        else:
            load_copy(1).wait()
        own_copy(w, 1, x).wait()
        z_copy(w, 0).wait_recv()
        xin[1] = add(xin[1], own[...], zin[0])
        z_copy(w, 1).start()
        if w < 2:
            own_copy(w, 2, 1 - x).start()
        else:
            own_copy(w, 3, x).start()

    def rs_side(w):
        own, cross = parts[w][2], parts[w][4]
        if w < 2:
            load_copy(2 + w).wait()
            own_copy(w, 2, 1 - x).wait()
        else:
            x_copy(w, 3).wait_recv()
            own_copy(w, 3, x).wait()
        cross[...] = add(cross[...], own[...])
        if w < 2:
            x_copy(w, 2).start()
        z_copy(w, 2).start()
        own_copy(w, 2, x).start()

    def rs_end(w):
        xin, own, zin = parts[w][1:4]
        x_copy(w, 2).wait_recv()
        own_copy(w, 2, x).wait()
        z_copy(w, 1).wait_recv()
        z_copy(w, 2).wait_recv()
        parts[w][5][...] = add(xin[2], own[...], zin[1], zin[2])

    for i in range(4):
        load_copy(i).start()
    for w in range(3):
        own_copy(w, 0, x).start()
    late = ((attn_hbm, attn_all), (q_hbm, q_s), (k_hbm, k_s), (v_hbm, v_s), (o_hbm, o_s), (wo_hbm, wo), (wqkv_hbm, wqkv))

    def late_copy(i):
        return pltpu.make_async_copy(late[i][0], late[i][1], late_sem.at[i])

    for i in (5, 2, 4, 1, 3, 6, 0):
        late_copy(i).start()
    me.barrier()
    for w, i in ((1, 0), (2, 0), (1, 1), (2, 1), (2, 3), (2, 2)):
        x_copy(w, i).start()
    rs_far(0)

    small[...] = jnp.zeros_like(small)
    cv0, cv1 = cvec_ref[0:1, :], cvec_ref[1:2, :]
    maps = jnp.concatenate([router_ref[...], proj_ref[...], jnp.zeros((4, D), F32)], axis=0).astype(BF)
    lane8 = lane_of((M, 8))
    lane4 = lane_of((M, 4))

    def dh_copy(i, c, block, to=None):
        ref = dh_all.at[block, pl.ds(pl.multiple_of(c * M, M), M)]
        return me.send(ref, ref, dh_ss.at[i, c], dh_rs.at[i, c], e=to)

    def mix_step(c, _):
        r = pl.ds(pl.multiple_of(c * M, M), M)
        h = hidden[r, :]
        u = u_ref[r, :].astype(F32)
        inv = lax.rsqrt(jnp.mean(h * h, axis=-1, keepdims=True) + EPS)
        hn = h * inv
        gain = gain_f_ref[...].reshape(1, D)
        n = hn * gain
        cols = aux_ref[:, r].T
        gates = cols[:, 0:8]
        a0, b0, a1, b1 = cols[:, 8:9], cols[:, 9:10], cols[:, 10:11], cols[:, 11:12]
        g5, g6, g7 = cols[:, 5:6], cols[:, 6:7], cols[:, 7:8]
        c_n = g5 + g6 * a0 + g7 * a1
        c0 = g6 * b0
        c1 = g7 * b1
        mixed = h + c_n * n + c0 * cv0 + c1 * cv1
        dg = jnp.zeros((M, 8), F32)
        dn = c_n * u
        for k in range(4):
            place = place_ref[k, :, r]
            rk = dot(place, ret_o[k], 0, 0)
            mixed = mixed + cols[:, k : k + 1] * rk
            dg = jnp.where(lane8 == k, jnp.sum(u * rk, axis=-1, keepdims=True), dg)
            dn = dn + dot(place, ret_d[k], 0, 0)
        layer_out[r, :] = mixed.astype(BF)
        un = jnp.sum(u * n, axis=-1, keepdims=True)
        uv0 = jnp.sum(u * cv0, axis=-1, keepdims=True)
        uv1 = jnp.sum(u * cv1, axis=-1, keepdims=True)
        dg = jnp.where(lane8 == 5, un, dg)
        dg = jnp.where(lane8 == 6, a0 * un + b0 * uv0, dg)
        dg = jnp.where(lane8 == 7, a1 * un + b1 * uv1, dg)
        dlog = gates * (dg - jnp.sum(gates * dg, axis=-1, keepdims=True))
        e0 = g6 * a0 * b0 * (un - uv0)
        e1 = g7 * a1 * b1 * (un - uv1)
        dpair = jnp.where(lane4 == 0, e0, jnp.where(lane4 == 1, -e0, jnp.where(lane4 == 2, e1, -e1)))
        dl = jnp.concatenate([dlog, dpair, c0, c1, jnp.zeros((M, 2), F32)], axis=1)
        low = dl.astype(BF)
        d_res[:, r] = dot(mix_ref[...], dlog, 1, 1, HIGH)
        dn = dn + dot(jnp.where(lane_of((M, 16)) < 12, low, jnp.zeros((M, 16), BF)), maps)
        by_n = dot(low, n.astype(BF), 0, 0)
        by_u = dot(low, u_ref[r, :], 0, 0)
        small[0:12, :] += by_n[0:12]
        small[12:14, :] += by_u[12:14]
        small[14:15, :] += jnp.sum(dn * hn, axis=0, keepdims=True)
        small[16:24, 0:8] += dot(gres_ref[:, r], dlog, 1, 0, HIGH)
        gd = dn * gain
        dh = u + inv * (gd - hn * jnp.mean(gd * hn, axis=-1, keepdims=True))
        d_hidden[r, :] = dh
        dh_all[e, r, :] = dh.astype(BF)
        dh_copy(1, c, e, me.yp).start()
        dh_copy(0, c, e, me.sib).start()
        return 0

    lax.fori_loop(0, T // M, mix_step, 0)
    rs_far(1)
    rs_cross(0)
    for i in range(7):
        late_copy(i).wait()

    head_of = lane_of((T, C)) // HD
    heads = (row_of((8, C)) == lane_of((8, C)) // HD).astype(F32)
    wk_s[...] = wqkv[:, C : 2 * C]
    dk[...] = jnp.zeros_like(dk)
    dv[...] = jnp.zeros_like(dv)
    go_acc[...] = jnp.zeros_like(go_acc)
    for b in range(4):
        kt_s[b] = k_s[b].T

    def fw_copy(block, to=None):
        return me.send(dh_all.at[block], dh_all.at[block], fw_ss.at[0], fw_rs.at[0], e=to)

    def d_out_step(j, qb):
        @pl.when(j == 1)
        def _():
            for c in range(T // M):
                dh_copy(0, c, me.sib).wait_recv()

        @pl.when(j == 2)
        def _():
            for c in range(T // M):
                dh_copy(1, c, me.yp).wait_recv()
            fw_copy(me.yp, me.sib).start()

        @pl.when(j == 3)
        def _():
            fw_copy(me.diag).wait_recv()

        dhb = dh_all[qb]
        low = dot(dhb, wo[pl.ds(2 * e, 2)].reshape(C, D), 1, 1).astype(BF)
        da[qb] = low
        ob = o_s[qb]
        del_r[qb] = dot(heads, low.astype(F32) * ob.astype(F32), 1, 1, HIGH)
        go_acc[...] += dot(ob, dhb, 0, 0)

    def head_block(qb, h):
        hr = pl.ds(pl.multiple_of(h * HD, HD), HD)
        mine = head_of == h

        def block(kb, masked):
            zero = jnp.zeros((T, C), BF)
            query = jnp.where(mine, q_s[qb], zero)
            d_out = jnp.where(mine, da[qb], zero)
            p = jnp.exp2(dot(k_s[kb], query, 1, 1) - lse_s[qb, pl.ds(h, 1), :])
            if masked:
                p = jnp.where(allowed_block(T, starts_ref[0, qb] - qb * T), p, 0.0)
            dp = dot(v_s[kb], d_out, 1, 1)
            dsc = (p * (dp - del_r[qb, pl.ds(h, 1), :])).astype(BF)
            dv[kb] += dot(p.astype(BF), d_out)
            dk[kb] += dot(dsc, query)
            return dot(kt_s[kb, hr, :], dsc)

        dqt[...] = block(qb, True)

        def key_step(kb, _):
            dqt[...] += block(kb, False)
            return 0

        lax.fori_loop(0, qb, key_step, 0)
        dq[qb, hr, :] = (dqt[...] * (1.0 / math.sqrt(HD))).astype(BF)

    def near_step(i, _):
        j = i // 3
        qb = me.near_first(j)

        @pl.when(i % 3 == 0)
        def _():
            d_out_step(j, qb)

        head_block(qb, i % 3)
        return 0

    def far_pass(h):
        def far_step(j, _):
            qb = me.near_first(j)
            if h == 0:
                d_out_step(j, qb)
            head_block(qb, h)
            return 0

        lax.fori_loop(2, 4, far_step, 0)

    def ag_copy(h, r, src, dst, to=None):
        return me.send(src, dst, ag_ss.at[h, r - 1], ag_rs.at[h, r - 1], f=to)

    def weight_grads(h):
        cols = slice(h * HD, (h + 1) * HD)
        gt[...] = jnp.zeros_like(gt)

        def grad_step(b, _):
            low_k = (dk[b, :, cols] * LN2).T.astype(BF)
            low_v = dv[b, :, cols].T.astype(BF)
            gt[...] += dot(jnp.concatenate([dq[b, cols, :], low_k, low_v], axis=0), attn_all[b])
            return 0

        lax.fori_loop(0, 4, grad_step, 0)
        ag_s[:, h] = gt[...].T.astype(BF).reshape(8, R, C)
        for r in range(1, 8):
            ag_copy(h, r, ag_s.at[me.fp(r), h], ag_in.at[r, h], me.fp(r)).start()
        ag_in[0, h] = ag_s[f, h]

    lax.fori_loop(0, 6, near_step, 0)
    rs_far(2)
    far_pass(0)
    rs_cross(1)

    go_s[0] = go_acc[0:R, :].astype(BF)
    go_s[1] = go_acc[R : 2 * R, :].astype(BF)
    for j in range(2):

        @pl.when(f != 2 * e + j)
        def _():
            me.send(go_s.at[j], go_in.at[f], go_ss.at[j], go_rs.at[f], f=2 * e + j).start()

    weight_grads(0)
    far_pass(1)
    weight_grads(1)
    rs_cross(2)
    rs_side(0)
    rs_side(1)
    far_pass(2)

    for c in range(T // M):
        dh_copy(0, c, e).wait_send()
        dh_copy(1, c, e).wait_send()
    fw_copy(e).wait_send()

    def share_step(j, _):
        b = me.share_order(j)
        out = dot(dq[b], wqkv[:, 0:C], 0, 1)
        out = out + dot((dk[b] * LN2).astype(BF), wk_s[...], 1, 1)
        out = out + dot(dv[b].astype(BF), wqkv[:, 2 * C : 3 * C], 1, 1)
        small[15:16, :] += jnp.sum(out * attn_all[b].astype(F32), axis=0, keepdims=True)
        dh_all[b] = out.astype(BF)
        return 0

    def pd_copy(i, src, dst, to=None):
        return me.send(src, dst, pd_ss.at[i], pd_rs.at[i], e=to)

    lax.fori_loop(0, 1, share_step, 0)
    pd_copy(1, dh_all.at[me.diag], pin.at[1], me.sib).start()
    lax.fori_loop(1, 2, share_step, 0)
    pd_copy(1, pin.at[1], pin.at[1]).wait_recv()
    dh_all[me.yp] = add(dh_all[me.yp], pin[1])
    pd_copy(2, dh_all.at[me.yp], py_in, me.yp).start()
    weight_grads(2)
    lax.fori_loop(2, 3, share_step, 0)
    pd_copy(0, dh_all.at[me.sib], pin.at[0], me.sib).start()
    lax.fori_loop(3, 4, share_step, 0)

    rs_side(2)
    small[15:16, :] = small[15:16, :] / gain_a_ref[...].reshape(1, D)
    sm1[e] = small[...]
    for i, p in enumerate(me.exp_peers):
        me.send(small, sm1.at[e], s1_ss.at[i], s1_rs.at[i], e=p).start()

    @pl.when(z == e)
    def _():
        total = go_s[x].astype(F32)
        for r in range(1, 8):
            s = go_in.at[me.fp(r)]
            me.send(s, s, go_ss.at[0], go_rs.at[me.fp(r)]).wait_recv()
            total = total + go_in[me.fp(r)].astype(F32)
        go_b[...] = total.astype(BF)
        for i, p in enumerate(me.exp_peers):
            me.send(go_b, go_b, gb_ss.at[i], gb_rs.at[0], e=p).start()

    for i, p in enumerate(me.exp_peers):
        me.send(small, sm1.at[p], s1_ss.at[i], s1_rs.at[i]).wait()
    sm2[f] = sm1[0] + sm1[1] + sm1[2] + sm1[3]
    for r in range(1, 8):
        me.send(sm2.at[f], sm2.at[f], s2_ss.at[r - 1], s2_rs.at[f], f=me.fp(r)).start()

    for h in range(3):
        total = ag_in[0, h].astype(F32)
        for r in range(1, 8):
            ag_copy(h, r, ag_in.at[r, h], ag_in.at[r, h]).wait_recv()
            total = total + ag_in[r, h].astype(F32)
        ag_fin[h] = total.astype(BF)
        for i, p in enumerate(me.exp_peers):
            me.send(ag_fin.at[h], ag_out.at[e, h], ab_ss.at[h, i], ab_rs.at[h, i], e=p).start()
        ag_out[e, h] = ag_fin[h]

    for r in range(1, 8):
        s = sm2.at[me.fp(r)]
        me.send(s, s, s2_ss.at[r - 1], s2_rs.at[me.fp(r)]).wait_recv()
    total = sm2[0]
    for r in range(1, 8):
        total = total + sm2[r]
    small_out[...] = total

    pd_copy(0, pin.at[0], pin.at[0]).wait_recv()
    pd_copy(2, py_in, py_in).wait_recv()

    def token_step(i, _):
        r = pl.ds(pl.multiple_of(i * 256, 256), 256)
        d = dh_all[e, r, :].astype(F32) + pin[0, r, :].astype(F32) + py_in[r, :].astype(F32)
        xv = x_ref[r, :].astype(F32)
        inv = lax.rsqrt(jnp.mean(xv * xv, axis=-1, keepdims=True) + EPS)
        xn = xv * inv
        gd = d * gain_a_ref[...].reshape(1, D)
        grad_tokens[r, :] = (d_hidden[r, :] + inv * (gd - xn * jnp.mean(gd * xn, axis=-1, keepdims=True))).astype(BF)
        return 0

    lax.fori_loop(0, 2, token_step, 0)
    for w in range(3):
        rs_end(w)

    @pl.when(z != e)
    def _():
        me.send(go_b, go_b, gb_ss.at[0], gb_rs.at[0]).wait_recv()

    for w in range(3):
        for i in range(3):
            if w or i == 2:
                x_copy(w, i).wait_send()
            z_copy(w, i).wait_send()
    x_copy(2, 3).wait_send()
    for j in range(2):

        @pl.when(f != 2 * e + j)
        def _():
            me.send(go_s.at[j], go_in.at[f], go_ss.at[j], go_rs.at[f]).wait_send()

    @pl.when(z == e)
    def _():
        for i in range(3):
            me.send(go_b, go_b, gb_ss.at[i], gb_rs.at[0]).wait_send()

    for i in range(3):
        pd_copy(i, py_in, py_in).wait_send()
        for h in range(3):
            me.send(ag_fin.at[h], ag_out.at[me.exp_peers[i], h], ab_ss.at[h, i], ab_rs.at[h, i]).wait()
    for r in range(1, 8):
        for h in range(3):
            ag_copy(h, r, ag_s.at[0, h], ag_in.at[r, h]).wait_send()
        me.send(sm2.at[f], sm2.at[f], s2_ss.at[r - 1], s2_rs.at[f]).wait_send()


def call_k2(*args):
    x, (gg, gu, gd) = args[4], args[23:26]
    late = args[8:13] + args[14:16]
    T, D = x.shape
    C, R = D // 4, D // 8
    dma = pltpu.SemaphoreType.DMA
    VM = pltpu.VMEM
    shapes = (gg.shape[1:], gu.shape[1:], gd.shape[1:])
    return pl.pallas_call(
        k2_kernel,
        name="backward",
        out_shape=(
            sds((T, D), BF), sds((T, D), BF), sds((8, T), F32), sds((24, D), F32),
            sds((4, 3, R, C), BF), sds((R, D), BF),
        ) + tuple(sds(s, BF) for s in shapes),
        in_specs=[vmem()] * 8 + [anyspace()] * 5 + [vmem()] + [anyspace()] * 2 + [vmem()] * 6 + [smem()] + [anyspace()] * 7,
        out_specs=tuple([vmem()] * 9),
        scratch_shapes=[VM((3,) + s, BF) for s in shapes] + [VM(s, BF) for s in shapes] + [VM((3,) + s, BF) for s in shapes] + [VM(s, BF) for s in shapes] + [VM(a.shape, BF) for a in late] + [
            VM((4, T, D), BF), VM((4, T, C), BF), VM((4, C, T), BF), VM((4, C, T), BF), VM((4, T, C), F32), VM((4, T, C), F32),
            VM((HD, T), F32), VM((2, T, D), BF), VM((T, D), BF), VM((T, D), F32), VM((D, C), BF), VM((4, 8, T), F32), VM((C, D), F32), VM((C, D), F32),
            VM((8, 3, R, C), BF), VM((8, 3, R, C), BF), VM((3, R, C), BF), VM((2, R, D), BF), VM((8, R, D), BF),
            VM((24, D), F32), VM((4, 24, D), F32), VM((8, 24, D), F32),
            dma((4,)), dma((7,)), dma((3, 4)), dma((3, 4)), dma((3, 3)), dma((3, 3)), dma((3,)),
            dma((2, 4)), dma((2, 4)), dma((1,)), dma((1,)), dma((2,)), dma((8,)), dma((3,)), dma((1,)), dma((3,)), dma((3,)),
            dma((3, 7)), dma((3, 7)), dma((3, 3)), dma((3, 3)), dma((3,)), dma((3,)), dma((7,)), dma((8,)),
        ],
        compiler_params=pltpu.CompilerParams(collective_id=1, has_side_effects=True, vmem_limit_bytes=63 << 20),
    )(*args)


def k3_kernel(
    layer_in, tokens_in, res_in, small, ag, go, eg, eu, ed,
    layer_out, tokens_out, res_out, norm_a, norm_f, g_q, g_k, g_v, g_o, router, mixing, proj, cvec, o_gate, o_up, o_down,
):
    layer_out[...] = layer_in[...]
    tokens_out[...] = tokens_in[...]
    res_out[...] = res_in[...]
    norm_a[...] = small[15, :]
    norm_f[...] = small[14, :]
    for i, out in enumerate((g_q, g_k, g_v)):
        out[...] = jnp.concatenate(
            [ag[b, h, :, i * HD : (i + 1) * HD].astype(F32) for b in range(4) for h in range(3)], axis=1
        )
    g_o[...] = go[...].astype(F32)
    router[...] = small[0:8, :]
    mixing[...] = small[16:24, 0:8]
    proj[...] = small[8:12, :]
    cvec[...] = small[12:14, :]
    o_gate[...] = eg[...].astype(F32)
    o_up[...] = eu[...].astype(F32)
    o_down[...] = ed[...].astype(F32)


def call_k3(*args):
    T, D = args[0].shape
    R = D // 8
    return pl.pallas_call(
        k3_kernel,
        name="finish",
        out_shape=(
            sds((T, D), BF), sds((T, D), BF), sds((8, T), F32), sds((D,), F32), sds((D,), F32),
            sds((R, D), F32), sds((R, D), F32), sds((R, D), F32), sds((R, D), F32),
            sds((8, D), F32), sds((8, 8), F32), sds((4, D), F32), sds((2, D), F32),
        ) + tuple(sds(a.shape, F32) for a in args[6:9]),
        in_specs=[vmem()] * 9,
        out_specs=tuple([vmem()] * 16),
    )(*args)


def body_fast(
    tokens, gate_res, routes, piece_starts, norm_attn, norm_ffn, w_query, w_key, w_value, w_out, router, mixing,
    const_proj, const_vec, w_gate, w_up, w_down, cotangent,
):
    x, u = tokens[0], cotangent[0]
    gres, route_ids = gate_res[0].T, routes[0].T
    (attn_all, q, k, v, o, lse, hidden, aux, place, ret_o, ret_d, wo, wq, gg, gu, gd, fg, ng, sg, su) = call_k1(
        x, u, w_query, w_key, w_value, w_out, w_gate[0], w_up[0], w_down[0], gres, route_ids, piece_starts,
        norm_attn, norm_ffn, router.T, const_proj.T, mixing,
    )
    outs = call_k2(
        ret_o, ret_d, hidden, u, x, aux, place, gres, attn_all, q, k, v, o, lse, wo, wq,
        norm_attn, norm_ffn, router.T, const_proj.T, mixing, const_vec, piece_starts, gg, gu, gd, fg, ng, sg, su,
    )
    (layer_out, grad_tokens, d_res, norm_a, norm_f, g_q, g_k, g_v, g_o, g_router, g_mixing, g_proj, g_cvec, eg, eu, ed) = call_k3(*outs)
    return (
        layer_out[None], grad_tokens[None], d_res.T[None], norm_a, norm_f, g_q, g_k, g_v, g_o,
        g_router.T, g_mixing, g_proj.T, g_cvec, eg[None], eu[None], ed[None],
    )


def solution(mesh):
    placed = (
        P("fsdp", "exp", None),
        P("fsdp", "exp", None),
        P("fsdp", "exp", None),
        P("fsdp", None),
        P(),
        P(),
        P("fsdp", None),
        P("fsdp", None),
        P("fsdp", None),
        P("fsdp", None),
        P(),
        P(),
        P(),
        P(),
        P("exp", "fsdp", None),
        P("exp", "fsdp", None),
        P("exp", "fsdp", None),
        P("fsdp", "exp", None),
    )
    return jax.shard_map(
        body_fast if (mesh.shape['exp'], mesh.shape['fsdp']) == (4, 8) else body,
        mesh=mesh,
        in_specs=placed,
        out_specs=(
            P("fsdp", "exp", None),
            P("fsdp", "exp", None),
            P("fsdp", "exp", None),
            P(),
            P(),
            P("fsdp", None),
            P("fsdp", None),
            P("fsdp", None),
            P("fsdp", None),
            P(),
            P(),
            P(),
            P(),
            P("exp", "fsdp", None),
            P("exp", "fsdp", None),
            P("exp", "fsdp", None),
        ),
        check_vma=False,
    )
```

```python
import math

import jax
import jax.numpy as jnp
from jax import lax
from jax.experimental import pallas as pl
from jax.experimental.pallas import tpu as pltpu
from jax.sharding import PartitionSpec as P

H = 12
HD = 64
PIECE = 256
KBLK = 512
CAP = 160


EPS = 1e-05
HIGH = lax.Precision.HIGHEST
NEG = -1e30


def rms_scale(values, gain_vec):
    inverse = lax.rsqrt(jnp.mean(values * values, axis=-1, keepdims=True) + EPS)
    return values * inverse * gain_vec


def piece_ids(positions, starts, extent):
    inside = (positions[:, None] >= starts[None, :]) & (
        positions[:, None] < starts[None, :] + extent
    )
    labels = jnp.arange(1, starts.shape[0] + 1, dtype=jnp.int32)
    return jnp.sum(jnp.where(inside, labels[None, :], 0), axis=1)


def reach_bounds(positions, starts, extent):
    inside = (positions[:, None] >= starts[None, :]) & (
        positions[:, None] < starts[None, :] + extent
    )
    piece_last = jnp.max(jnp.where(inside, starts[None, :] + extent - 1, 0))
    piece_first = jnp.min(jnp.where(inside, starts[None, :], positions[0]))
    upper = jnp.maximum(positions[-1], piece_last)
    lower = jnp.minimum(positions[0], piece_first)
    return (upper, lower)


def allowed_mask(query_pos, query_ids, key_pos, key_ids):
    causal = key_pos[None, :] <= query_pos[:, None]
    shared = (key_ids[None, :] == query_ids[:, None]) & (query_ids[:, None] > 0)
    return causal | shared


def slot_dest(route_ids, n_ffn, capacity):
    flat_ids = route_ids.reshape(-1)
    onehot = (flat_ids[:, None] == jnp.arange(n_ffn, dtype=jnp.int32)[None, :]).astype(jnp.int32)
    earlier = jnp.cumsum(onehot, axis=0) - onehot
    slot_pos = jnp.sum(earlier * onehot, axis=1)
    return jnp.where(flat_ids < n_ffn, flat_ids * capacity + slot_pos, n_ffn * capacity)


def local_mix(
    normed, res_logits, router, mixing, const_proj, const_vec, expert_rows, route_ids, n_ffn
):
    n_all = router.shape[1]
    logits = jnp.dot(normed, router, precision=HIGH) + jnp.dot(res_logits, mixing, precision=HIGH)
    probs = jax.nn.softmax(logits, axis=-1)
    labels = jnp.arange(n_all, dtype=jnp.int32)
    chosen = jnp.sum(
        jnp.where(route_ids[:, :, None] == labels[None, None, :], probs[:, None, :], 0.0), axis=-1
    )
    gates = chosen / jnp.sum(chosen, axis=1, keepdims=True)
    pair_logits = jnp.dot(normed, const_proj, precision=HIGH)
    first_pair = jax.nn.softmax(pair_logits[:, 0:2], axis=-1)
    second_pair = jax.nn.softmax(pair_logits[:, 2:4], axis=-1)
    first_const = first_pair[:, 0:1] * normed + first_pair[:, 1:2] * const_vec[0][None, :]
    second_const = second_pair[:, 0:1] * normed + second_pair[:, 1:2] * const_vec[1][None, :]
    mixed = jnp.zeros_like(normed)
    for route_k in range(2):
        route_id = route_ids[:, route_k : route_k + 1]
        entry = jnp.where(route_id < n_ffn, expert_rows[:, route_k], 0.0)
        entry = entry + jnp.where(route_id == n_ffn + 1, normed, 0.0)
        entry = entry + jnp.where(route_id == n_ffn + 2, first_const, 0.0)
        entry = entry + jnp.where(route_id == n_ffn + 3, second_const, 0.0)
        mixed = mixed + gates[:, route_k : route_k + 1] * entry
    return mixed


def swiglu_act(gate_pre, up_pre):
    return jax.nn.silu(gate_pre) * up_pre


def body(
    tokens,
    gate_res,
    routes,
    piece_starts,
    norm_attn,
    norm_ffn,
    w_query,
    w_key,
    w_value,
    w_out,
    router,
    mixing,
    const_proj,
    const_vec,
    w_gate,
    w_up,
    w_down,
    cotangent,
):
    n_ffn = lax.axis_size("exp")
    rows_dev = tokens.shape[1]
    model_width = tokens.shape[2]
    seq_length = rows_dev * n_ffn
    score_scale = 1.0 / math.sqrt(HD)
    inputs_f = tokens[0].astype(jnp.float32)
    res_logits = gate_res[0]
    route_ids = routes[0]
    starts = piece_starts[0]
    full_query, full_key, full_value, full_out = (
        lax.all_gather(w_query, "fsdp", axis=0, tiled=True),
        lax.all_gather(w_key, "fsdp", axis=0, tiled=True),
        lax.all_gather(w_value, "fsdp", axis=0, tiled=True),
        lax.all_gather(w_out, "fsdp", axis=0, tiled=True),
    )
    attn_in = rms_scale(inputs_f, norm_attn).astype(jnp.bfloat16)
    query = jnp.dot(attn_in, full_query, preferred_element_type=jnp.float32).astype(jnp.bfloat16)
    key = jnp.dot(attn_in, full_key, preferred_element_type=jnp.float32).astype(jnp.bfloat16)
    value = jnp.dot(attn_in, full_value, preferred_element_type=jnp.float32).astype(jnp.bfloat16)
    keys_all, values_all = (
        lax.all_gather(key, "exp", axis=0, tiled=True),
        lax.all_gather(value, "exp", axis=0, tiled=True),
    )
    query_heads = query.reshape(rows_dev, H, HD)
    key_heads = keys_all.reshape(seq_length, H, HD)
    value_heads = values_all.reshape(seq_length, H, HD)
    query_pos = lax.axis_index("exp") * rows_dev + jnp.arange(rows_dev, dtype=jnp.int32)
    query_ids = piece_ids(query_pos, starts, PIECE)
    key_upper, query_lower = reach_bounds(query_pos, starts, PIECE)
    block_list = jnp.arange(seq_length // KBLK, dtype=jnp.int32)

    def score_block(block_index):
        key_first = block_index * KBLK
        key_block = lax.dynamic_slice_in_dim(key_heads, key_first, KBLK, 0)
        value_block = lax.dynamic_slice_in_dim(value_heads, key_first, KBLK, 0)
        key_pos = key_first + jnp.arange(KBLK, dtype=jnp.int32)
        key_ids = piece_ids(key_pos, starts, PIECE)
        scores = (
            jnp.einsum("qhd,khd->hqk", query_heads, key_block, preferred_element_type=jnp.float32)
            * score_scale
        )
        allowed = allowed_mask(query_pos, query_ids, key_pos, key_ids)[None]
        return (scores, allowed, key_block, value_block)

    def needed(block_index):
        return block_index * KBLK <= key_upper

    def lse_step(carry, block_index):

        def lse_active(state):
            run_max, run_sum = state
            scores, allowed, _, _ = score_block(block_index)
            scores = jnp.where(allowed, scores, NEG)
            new_max = jnp.maximum(run_max, jnp.max(scores, axis=-1))
            exp_terms = jnp.where(allowed, jnp.exp(scores - new_max[..., None]), 0.0)
            return (new_max, run_sum * jnp.exp(run_max - new_max) + jnp.sum(exp_terms, axis=-1))

        return (lax.cond(needed(block_index), lse_active, lambda state: state, carry), None)

    start_carry = (jnp.full((H, rows_dev), NEG, jnp.float32), jnp.zeros((H, rows_dev), jnp.float32))
    (run_max, run_sum), _ = lax.scan(lse_step, start_carry, block_list)
    log_norm = run_max + jnp.log(run_sum)

    def block_probs(scores, allowed):
        return jnp.where(allowed, jnp.exp(scores - log_norm[..., None]), 0.0)

    def out_step(accum, block_index):

        def out_active(total):
            scores, allowed, _, value_block = score_block(block_index)
            probs_low = block_probs(scores, allowed).astype(jnp.bfloat16)
            return total + jnp.einsum(
                "hqk,khd->qhd", probs_low, value_block, preferred_element_type=jnp.float32
            )

        return (lax.cond(needed(block_index), out_active, lambda total: total, accum), None)

    attn_sum, _ = lax.scan(out_step, jnp.zeros((rows_dev, H, HD), jnp.float32), block_list)
    attn_low = attn_sum.astype(jnp.bfloat16).reshape(rows_dev, model_width)
    hidden = inputs_f + jnp.dot(attn_low, full_out, preferred_element_type=jnp.float32)
    normed = rms_scale(hidden, norm_ffn)
    destination = slot_dest(route_ids, n_ffn, CAP)
    sources = jnp.arange(2 * rows_dev, dtype=jnp.int32) // 2
    slot_table = (
        jnp.full((n_ffn * CAP,), rows_dev, jnp.int32).at[destination].set(sources, mode="drop")
    )
    padded = jnp.concatenate(
        [normed.astype(jnp.bfloat16), jnp.zeros((1, model_width), jnp.bfloat16)], axis=0
    )
    dispatched = padded[slot_table].reshape(n_ffn, CAP, model_width)
    received = lax.all_to_all(dispatched, "exp", split_axis=0, concat_axis=0, tiled=True)
    full_gate, full_up, full_down = (
        lax.all_gather(w_gate[0], "fsdp", axis=0, tiled=True),
        lax.all_gather(w_up[0], "fsdp", axis=0, tiled=True),
        lax.all_gather(w_down[0], "fsdp", axis=0, tiled=True),
    )
    slot_rows = received.reshape(n_ffn * CAP, model_width)
    gate_pre = jnp.dot(slot_rows, full_gate, preferred_element_type=jnp.float32)
    up_pre = jnp.dot(slot_rows, full_up, preferred_element_type=jnp.float32)
    inner_act = swiglu_act(gate_pre, up_pre).astype(jnp.bfloat16)
    expert_result = jnp.dot(inner_act, full_down, preferred_element_type=jnp.float32).astype(
        jnp.bfloat16
    )
    returned = lax.all_to_all(
        expert_result.reshape(n_ffn, CAP, model_width),
        "exp",
        split_axis=0,
        concat_axis=0,
        tiled=True,
    )
    returned_pad = jnp.concatenate(
        [returned.reshape(n_ffn * CAP, model_width), jnp.zeros((1, model_width), jnp.bfloat16)],
        axis=0,
    )
    expert_rows = returned_pad[destination].astype(jnp.float32).reshape(rows_dev, 2, model_width)

    def mix_local(normed_in, logits_in, router_in, mixing_in, proj_in, vec_in, rows_in):
        return local_mix(
            normed_in, logits_in, router_in, mixing_in, proj_in, vec_in, rows_in, route_ids, n_ffn
        )

    moe_out, mix_pull = jax.vjp(
        mix_local, normed, res_logits, router, mixing, const_proj, const_vec, expert_rows
    )
    layer_out = (hidden + moe_out).astype(jnp.bfloat16)
    upstream = cotangent[0].astype(jnp.float32)
    d_normed_local, d_res_logits, d_router, d_mixing, d_const_proj, d_const_vec, d_expert_rows = (
        mix_pull(upstream)
    )
    d_rows_low = d_expert_rows.reshape(2 * rows_dev, model_width).astype(jnp.bfloat16)
    d_dispatched = (
        jnp.zeros((n_ffn * CAP, model_width), jnp.bfloat16)
        .at[destination]
        .set(d_rows_low, mode="drop")
    )
    d_received = lax.all_to_all(
        d_dispatched.reshape(n_ffn, CAP, model_width),
        "exp",
        split_axis=0,
        concat_axis=0,
        tiled=True,
    )
    d_received = d_received.reshape(n_ffn * CAP, model_width)
    d_inner = jnp.einsum("rd,fd->rf", d_received, full_down, preferred_element_type=jnp.float32)
    _, act_pull = jax.vjp(swiglu_act, gate_pre, up_pre)
    d_gate_pre, d_up_pre = act_pull(d_inner)
    d_gate_low = d_gate_pre.astype(jnp.bfloat16)
    d_up_low = d_up_pre.astype(jnp.bfloat16)
    grad_down_full = jnp.einsum(
        "rf,rd->fd", inner_act, d_received, preferred_element_type=jnp.float32
    )
    grad_gate_full = jnp.einsum(
        "rd,rf->df", slot_rows, d_gate_low, preferred_element_type=jnp.float32
    )
    grad_up_full = jnp.einsum("rd,rf->df", slot_rows, d_up_low, preferred_element_type=jnp.float32)
    d_slot_rows = (
        jnp.einsum("rf,df->rd", d_gate_low, full_gate, preferred_element_type=jnp.float32)
        + jnp.einsum("rf,df->rd", d_up_low, full_up, preferred_element_type=jnp.float32)
    ).astype(jnp.bfloat16)
    d_sent = lax.all_to_all(
        d_slot_rows.reshape(n_ffn, CAP, model_width), "exp", split_axis=0, concat_axis=0, tiled=True
    )
    d_sent_pad = jnp.concatenate(
        [d_sent.reshape(n_ffn * CAP, model_width), jnp.zeros((1, model_width), jnp.bfloat16)],
        axis=0,
    )
    d_normed_sent = jnp.sum(
        d_sent_pad[destination].astype(jnp.float32).reshape(rows_dev, 2, model_width), axis=1
    )
    _, norm_ffn_pull = jax.vjp(rms_scale, hidden, norm_ffn)
    d_hidden_part, d_norm_ffn = norm_ffn_pull(d_normed_local + d_normed_sent)
    d_hidden = upstream + d_hidden_part
    d_hidden_low = d_hidden.astype(jnp.bfloat16)
    grad_out_full = jnp.einsum(
        "td,te->de", attn_low, d_hidden_low, preferred_element_type=jnp.float32
    )
    d_attn = jnp.einsum(
        "te,de->td", d_hidden_low, full_out, preferred_element_type=jnp.float32
    ).astype(jnp.bfloat16)
    d_attn_heads = d_attn.reshape(rows_dev, H, HD)
    zero_block = jnp.zeros((KBLK, H, HD), jnp.float32)

    def delta_terms(block_index):
        scores, allowed, _, value_block = score_block(block_index)
        probs = block_probs(scores, allowed)
        d_probs = jnp.einsum(
            "qhd,khd->hqk", d_attn_heads, value_block, preferred_element_type=jnp.float32
        )
        part = jnp.sum(probs * d_probs, axis=-1)
        return (
            part,
            jnp.einsum(
                "hqk,qhd->khd",
                probs.astype(jnp.bfloat16),
                d_attn_heads,
                preferred_element_type=jnp.float32,
            ),
        )

    def query_terms(block_index, row_delta):
        scores, allowed, key_block, value_block = score_block(block_index)
        probs = block_probs(scores, allowed)
        d_probs = jnp.einsum(
            "qhd,khd->hqk", d_attn_heads, value_block, preferred_element_type=jnp.float32
        )
        d_scores = (probs * (d_probs - row_delta[..., None])).astype(jnp.bfloat16)
        part = (
            jnp.einsum("hqk,khd->qhd", d_scores, key_block, preferred_element_type=jnp.float32)
            * score_scale
        )
        return (
            part,
            jnp.einsum("hqk,qhd->khd", d_scores, query_heads, preferred_element_type=jnp.float32)
            * score_scale,
        )

    def delta_step(total, block_index):

        def delta_active(running):
            part, grad_block = delta_terms(block_index)
            return (running + part, grad_block)

        return lax.cond(
            needed(block_index), delta_active, lambda running: (running, zero_block), total
        )

    row_delta, grad_values = lax.scan(delta_step, jnp.zeros((H, rows_dev), jnp.float32), block_list)

    def query_step(total, block_index):

        def query_active(running):
            part, grad_block = query_terms(block_index, row_delta)
            return (running + part, grad_block)

        return lax.cond(
            needed(block_index), query_active, lambda running: (running, zero_block), total
        )

    d_query_sum, grad_keys = lax.scan(
        query_step, jnp.zeros((rows_dev, H, HD), jnp.float32), block_list
    )
    grad_keys = grad_keys.reshape(seq_length, model_width)
    grad_values = grad_values.reshape(seq_length, model_width)
    d_key_sum, d_value_sum = (
        lax.psum_scatter(
            grad_keys.astype(jnp.bfloat16), "exp", scatter_dimension=0, tiled=True
        ).astype(jnp.float32),
        lax.psum_scatter(
            grad_values.astype(jnp.bfloat16), "exp", scatter_dimension=0, tiled=True
        ).astype(jnp.float32),
    )
    d_query_low = d_query_sum.reshape(rows_dev, model_width).astype(jnp.bfloat16)
    d_key_low = d_key_sum.astype(jnp.bfloat16)
    d_value_low = d_value_sum.astype(jnp.bfloat16)
    d_attn_in = (
        jnp.einsum("te,de->td", d_query_low, full_query, preferred_element_type=jnp.float32)
        + jnp.einsum("te,de->td", d_key_low, full_key, preferred_element_type=jnp.float32)
        + jnp.einsum("te,de->td", d_value_low, full_value, preferred_element_type=jnp.float32)
    )
    grad_query_full = jnp.einsum(
        "td,te->de", attn_in, d_query_low, preferred_element_type=jnp.float32
    )
    grad_key_full = jnp.einsum("td,te->de", attn_in, d_key_low, preferred_element_type=jnp.float32)
    grad_value_full = jnp.einsum(
        "td,te->de", attn_in, d_value_low, preferred_element_type=jnp.float32
    )
    _, norm_attn_pull = jax.vjp(rms_scale, inputs_f, norm_attn)
    d_inputs_part, d_norm_attn = norm_attn_pull(d_attn_in)
    grad_tokens = (d_hidden + d_inputs_part).astype(jnp.bfloat16)
    attn_shards = (
        lax.psum_scatter(
            grad_query_full.astype(jnp.bfloat16), "fsdp", scatter_dimension=0, tiled=True
        ).astype(jnp.float32),
        lax.psum_scatter(
            grad_key_full.astype(jnp.bfloat16), "fsdp", scatter_dimension=0, tiled=True
        ).astype(jnp.float32),
        lax.psum_scatter(
            grad_value_full.astype(jnp.bfloat16), "fsdp", scatter_dimension=0, tiled=True
        ).astype(jnp.float32),
        lax.psum_scatter(
            grad_out_full.astype(jnp.bfloat16), "fsdp", scatter_dimension=0, tiled=True
        ).astype(jnp.float32),
    )
    attn_shards = (
        lax.psum(attn_shards[0].astype(jnp.bfloat16), "exp").astype(jnp.float32),
        lax.psum(attn_shards[1].astype(jnp.bfloat16), "exp").astype(jnp.float32),
        lax.psum(attn_shards[2].astype(jnp.bfloat16), "exp").astype(jnp.float32),
        lax.psum(attn_shards[3].astype(jnp.bfloat16), "exp").astype(jnp.float32),
    )
    expert_shards = (
        lax.psum_scatter(
            grad_gate_full.astype(jnp.bfloat16), "fsdp", scatter_dimension=0, tiled=True
        ).astype(jnp.float32),
        lax.psum_scatter(
            grad_up_full.astype(jnp.bfloat16), "fsdp", scatter_dimension=0, tiled=True
        ).astype(jnp.float32),
        lax.psum_scatter(
            grad_down_full.astype(jnp.bfloat16), "fsdp", scatter_dimension=0, tiled=True
        ).astype(jnp.float32),
    )
    small_sums = lax.psum(
        (d_norm_attn, d_norm_ffn, d_router, d_mixing, d_const_proj, d_const_vec), ("exp", "fsdp")
    )
    return (
        layer_out[None],
        grad_tokens[None],
        d_res_logits[None],
        small_sums[0],
        small_sums[1],
        attn_shards[0],
        attn_shards[1],
        attn_shards[2],
        attn_shards[3],
        small_sums[2],
        small_sums[3],
        small_sums[4],
        small_sums[5],
        expert_shards[0][None],
        expert_shards[1][None],
        expert_shards[2][None],
    )


MESH = pl.DeviceIdType.MESH
BF = jnp.bfloat16
F32 = jnp.float32
LN2 = math.log(2.0)
QSCALE = 1.0 / (LN2 * math.sqrt(HD))
CHUNKS = 4


class Place:
    def __init__(self):
        self.e = lax.axis_index("exp")
        self.f = lax.axis_index("fsdp")
        self.z = self.f // 2
        self.x = self.f % 2
        self.sib = self.e + 1 - 2 * (self.e % 2)
        self.yp = (self.e + 2) % 4
        self.diag = (self.sib + 2) % 4
        self.xf = self.f + 1 - 2 * self.x
        self.exp_peers = (self.sib, self.yp, self.diag)

    def zf(self, d):
        return ((self.z + d) % 4) * 2 + self.x

    def fp(self, r):
        return (self.f + r) % 8

    def far_first(self, j):
        return (self.e + (j % 2) * (1 - 2 * (self.e % 2)) + 2 * (1 - j // 2)) % 4

    def near_first(self, j):
        return (self.e + (j % 2) * (1 - 2 * (self.e % 2)) + 2 * (j // 2)) % 4

    def share_order(self, j):
        return (self.e + (1 - j % 2) * (1 - 2 * (self.e % 2)) + 2 * (1 - j // 2)) % 4

    def barrier(self):
        sem = pltpu.get_barrier_semaphore()
        for p in self.exp_peers:
            pl.semaphore_signal(sem, inc=1, device_id=(p, self.f), device_id_type=MESH)
        for r in range(1, 8):
            pl.semaphore_signal(sem, inc=1, device_id=(self.e, self.fp(r)), device_id_type=MESH)
        pl.semaphore_wait(sem, 10)

    def send(self, src, dst, ss, rs, e=None, f=None):
        return pltpu.make_async_remote_copy(
            src_ref=src,
            dst_ref=dst,
            send_sem=ss,
            recv_sem=rs,
            device_id=(self.e if e is None else e, self.f if f is None else f),
            device_id_type=MESH,
        )


def lane_of(shape):
    return lax.broadcasted_iota(jnp.int32, shape, len(shape) - 1)


def row_of(shape):
    return lax.broadcasted_iota(jnp.int32, shape, 0)


def dot(a, b, ca=1, cb=0, precision=None):
    return lax.dot_general(a, b, (((ca,), (cb,)), ((), ())), precision=precision, preferred_element_type=F32)


def allowed_block(size, first):
    key, query = row_of((size, size)), lane_of((size, size))
    inside_k = (key >= first) & (key < first + PIECE)
    inside_q = (query >= first) & (query < first + PIECE)
    return (key <= query) | (inside_k & inside_q)


def k1_kernel(
    x_ref, u_ref, wq_ref, wk_ref, wv_ref, wo_ref, wg_ref, wu_ref, wd_ref, gres_ref, routes_ref, starts_ref,
    gain_a_ref, gain_f_ref, router_ref, proj_ref, mix_ref,
    attn_hbm, q_hbm, k_hbm, v_hbm, o_hbm, lse_s, hidden_ref, aux_ref, place_ref, ret_o, ret_d, wo_hbm, wq_hbm,
    grad_gate, grad_up, grad_down, far_gate, next_gate, near_gate, side_gate, far_up, side_up,
    attn_all, q_s, k_s, v_s, o_s, wo_full, wq_full,
    gate_full, up_full, down_full, wq_own, vt_s, attn_recv, nb, snd_r, snd_d, recv_r, recv_d, m_s, l_s, acc_s,
    acc, d_acc, st_gate, st_up, st_down,
    wq_ss, wq_rs, wo_ss, wo_rs, at_ss, at_rs, o_ss, o_rs, dr_ss, dr_rs, dd_ss, dd_rs, ro_ss, ro_rs, rd_ss, rd_rs,
    us, ur, ds, dr, xs, xr, vs, vr, wc_ss, wc_rs, loc, st_sem, fs, fr, keep_sem,
):
    me = Place()
    e, f, z, xf = me.e, me.f, me.z, me.xf
    T, D = x_ref.shape
    C = D // 4
    R = wo_ref.shape[0]
    FF = wg_ref.shape[1]
    W = FF // CHUNKS
    S = 4 * CAP
    for k in range(4):

        @pl.when(e == k)
        def _():
            for i, w in enumerate((wq_ref, wk_ref, wv_ref)):
                wq_own[:, i * C : (i + 1) * C] = w[:, k * C : (k + 1) * C]

    me.barrier()

    def half(core):
        return pl.ds(pl.multiple_of(core * (R // 2), 16), R // 2)

    def wq_slot(index):
        return wq_full.at[pl.ds(pl.multiple_of(index * R, 32), R)]

    def wo_slot(index):
        return wo_full.at[index, half(e % 2)]

    early = (
        (wq_own, wq_slot, wq_ss, wq_rs, 0),
        (wo_ref.at[half(e % 2)], wo_slot, wo_ss, wo_rs, 1),
    )
    for src, slot_of, ss, rs, li in early:
        for d in (1, 3, 2):
            me.send(src, slot_of(f), ss.at[d], rs.at[d], f=me.zf(d)).start()
        me.send(src, slot_of(f), ss.at[0], rs.at[0], f=xf).start()
        pltpu.make_async_copy(src, slot_of(f), loc.at[li]).start()

    xv = x_ref[...].astype(F32)
    inv = lax.rsqrt(jnp.mean(xv * xv, axis=-1, keepdims=True) + EPS)
    attn_all[e] = (xv * inv * gain_a_ref[...].reshape(1, D)).astype(BF)

    def at_copy(i, block, to=None):
        ref = attn_all.at[block]
        return me.send(ref, ref, at_ss.at[i], at_rs.at[i], e=to)

    at_copy(1, e, me.yp).start()
    at_copy(0, e, me.sib).start()

    def early_index(d, other):
        return ((z - d + 4) % 4) * 2 + (1 - me.x if other else me.x)

    def early_forward(src, slot_of, ss, rs, li):
        for d in (1, 3, 2):
            slot = slot_of(early_index(d, False))
            me.send(slot, slot, ss.at[d], rs.at[d]).wait_recv()
            me.send(slot, slot, ss.at[3 + d], rs.at[3 + d], f=xf).start()

    def early_wait(src, slot_of, ss, rs, li):
        pltpu.make_async_copy(src, slot_of(f), loc.at[li]).wait()
        me.send(slot_of(xf), slot_of(xf), ss.at[0], rs.at[0]).wait_recv()
        for d in (1, 2, 3):
            slot = slot_of(early_index(d, True))
            me.send(slot, slot, ss.at[3 + d], rs.at[3 + d]).wait_recv()

    def wo_copy(core, to=None):
        ref = wo_full.at[:, half(core)]
        return me.send(ref, ref, wc_ss.at[0], wc_rs.at[0], e=to)

    def cut(ref, c):
        return ref if c is None else ref.at[:, pl.ds(pl.multiple_of(c * W, W), W)]

    def up_copy(n, p, src, dst, to=None):
        return me.send(src, dst, us.at[n, p], ur.at[n, p], f=to)

    def down_copy(n, p, src, dst, to=None):
        return me.send(src, dst, ds.at[n, p], dr.at[n, p], f=to)

    def x_copy(n, i, src, dst, to=None):
        return me.send(src, dst, xs.at[n, i], xr.at[n, i], f=to)

    def relay(n, p, src, full, c):
        def at(slot):
            return cut(full.at[slot], c)

        if p == 0:
            own = cut(src, c)
            x_copy(n, 0, own, at(f), xf).start()

            @pl.when(z <= 2)
            def _():
                up_copy(n, 0, own, at(f), f + 2).start()

            @pl.when(z >= 1)
            def _():
                down_copy(n, 0, own, at(f), f - 2).start()

            return

        if p == 1 and c is None:
            x_copy(n, 0, at(xf), at(xf)).wait_recv()

            @pl.when(z <= 2)
            def _():
                side_copy(0, at(xf), at(xf), f + 2).start()

            @pl.when(z >= 1)
            def _():
                side_copy(1, at(xf), at(xf), f - 2).start()

        @pl.when(z >= p)
        def _():
            slot = at(f - 2 * p)
            up_copy(n, p - 1, slot, slot).wait_recv()
            if p <= 2:

                @pl.when(z <= 2)
                def _():
                    up_copy(n, p, slot, slot, f + 2).start()

            if p > 1 or c is not None:
                x_copy(n, p, slot, slot, xf).start()

        @pl.when(z + p <= 3)
        def _():
            slot = at(f + 2 * p)
            down_copy(n, p - 1, slot, slot).wait_recv()
            if p <= 2:

                @pl.when(z >= 1)
                def _():
                    down_copy(n, p, slot, slot, f - 2).start()

            if p > 1 or c is not None:
                x_copy(n, 3 + p, slot, slot, xf).start()

    def side_copy(i, src, dst, to=None):
        return me.send(src, dst, vs.at[i], vr.at[i], f=to)

    def relay_chunk(p, c):
        relay(1 + 2 * c, p, wg_ref, gate_full, c)
        relay(2 + 2 * c, p, wu_ref, up_full, c)

    def experts(p):
        relay(0, p, wd_ref, down_full, None)
        for c in range(CHUNKS):
            relay_chunk(p, c)

    own_loads = ((wd_ref, down_full), (wg_ref, gate_full), (wu_ref, up_full))

    def own_load(i):
        src, full = own_loads[i]
        return pltpu.make_async_copy(src, full.at[f], loc.at[2 + i])

    relay(0, 0, wd_ref, down_full, None)
    early_forward(*early[0])
    for c in range(CHUNKS):
        relay_chunk(0, c)
    for i in range(3):
        own_load(i).start()

    at_copy(1, me.yp).wait_recv()
    at_copy(2, me.yp, me.sib).start()
    at_copy(0, me.sib).wait_recv()
    early_wait(*early[0])
    early_forward(*early[1])
    at_copy(2, me.diag).wait_recv()

    kept = (
        (attn_all, attn_hbm), (wq_full, wq_hbm), (q_s, q_hbm), (k_s, k_hbm), (v_s, v_hbm), (wo_full, wo_hbm), (o_s, o_hbm),
    )

    def keep_copy(i):
        return pltpu.make_async_copy(kept[i][0], kept[i][1], keep_sem.at[i])

    keep_copy(0).start()
    keep_copy(1).start()

    def qkv_step(i, _):
        b = i // 2
        r = pl.ds(pl.multiple_of((i % 2) * 256, 256), 256)
        out = dot(attn_all[b, r, :], wq_full[...])
        q_s[b, r, :] = (out[:, 0:C] * QSCALE).astype(BF)
        k_s[b, r, :] = out[:, C : 2 * C].astype(BF)
        v = out[:, 2 * C : 3 * C]
        v_s[b, r, :] = v.astype(BF)
        vt_s[b, :, r] = v.T.astype(BF)
        return 0

    lax.fori_loop(0, 8, qkv_step, 0)
    for i in (2, 3, 4):
        keep_copy(i).start()

    head_of = lane_of((T, C)) // HD
    lse_s[...] = jnp.zeros_like(lse_s)

    def query_step(j, _):
        qb = me.far_first(j)
        queries = [jnp.where(head_of == h, q_s[qb], jnp.zeros((T, C), BF)) for h in range(3)]
        allowed = allowed_block(T, starts_ref[0, qb] - qb * T)
        for h in range(3):
            hr = pl.ds(h * HD, HD)
            s = jnp.where(allowed, dot(k_s[qb], queries[h], 1, 1), NEG)
            m = jnp.max(s, axis=0, keepdims=True)
            p = jnp.exp2(s - m)
            m_s[h : h + 1] = m
            l_s[h : h + 1] = jnp.sum(p, axis=0, keepdims=True)
            acc_s[hr] = dot(vt_s[qb, hr, :], p.astype(BF))

        def key_step(kb, _):
            for h in range(3):
                hr = pl.ds(h * HD, HD)
                query = jnp.where(head_of == h, q_s[qb], jnp.zeros((T, C), BF))
                s = dot(k_s[kb], query, 1, 1)
                m_old = m_s[h : h + 1]
                m = jnp.maximum(m_old, jnp.max(s, axis=0, keepdims=True))
                scale = jnp.exp2(m_old - m)
                p = jnp.exp2(s - m)
                m_s[h : h + 1] = m
                l_s[h : h + 1] = l_s[h : h + 1] * scale + jnp.sum(p, axis=0, keepdims=True)
                acc_s[hr] = acc_s[hr] * scale + dot(vt_s[kb, hr, :], p.astype(BF))
            return 0

        lax.fori_loop(0, qb, key_step, 0)
        for h in range(3):
            hr = pl.ds(h * HD, HD)
            total = l_s[h : h + 1]
            acc_s[hr] = acc_s[hr] / total
            lse_s[qb, h : h + 1, :] = m_s[h : h + 1] + jnp.log2(total)
        o_s[qb] = acc_s[...].T.astype(BF)
        return 0

    def o_copy(i, to=None):
        p = me.exp_peers[i]
        if to is None:
            return me.send(o_s.at[p], attn_recv.at[p], o_ss.at[i], o_rs.at[i])
        return me.send(o_s.at[p], attn_recv.at[e], o_ss.at[i], o_rs.at[i], e=p)

    lax.fori_loop(0, 2, query_step, 0)
    o_copy(1, True).start()
    o_copy(2, True).start()
    early_wait(*early[1])
    wo_copy(e % 2, me.sib).start()
    experts(1)
    lax.fori_loop(2, 4, query_step, 0)
    o_copy(0, True).start()
    attn_recv[e] = o_s[e]
    keep_copy(6).start()

    r0, r1 = routes_ref[0:1, :], routes_ref[1:2, :]
    expert = row_of((8, T))
    chosen = (expert == r0) | (expert == r1)
    earlier = (row_of((T, T)) < lane_of((T, T))).astype(BF)
    count = dot(chosen.astype(BF), earlier).astype(jnp.int32)
    count = jnp.where(chosen, count, -1)
    slot_id = row_of((CAP, T))
    for k in range(4):
        place_ref[k] = jnp.where(slot_id == count[k : k + 1, :], 1.0, 0.0).astype(BF)

    wo_copy(1 - e % 2).wait_recv()
    keep_copy(5).start()
    for i in (0, 1, 2):
        o_copy(i).wait_recv()

    def hidden_step(i, _):
        r = pl.ds(pl.multiple_of(i * 256, 256), 256)
        h = x_ref[r, :].astype(F32)
        for b in range(4):
            h = h + dot(attn_recv[b, r, :], wo_full[2 * b : 2 * b + 2].reshape(C, D))
        hidden_ref[r, :] = h
        n = h * lax.rsqrt(jnp.mean(h * h, axis=-1, keepdims=True) + EPS) * gain_f_ref[...].reshape(1, D)
        nb[r, :] = n.astype(BF)
        aux_ref[0:8, r] = dot(router_ref[...], n, 1, 1, HIGH) + dot(mix_ref[...], gres_ref[:, r], 0, 0, HIGH)
        aux_ref[8:12, r] = dot(proj_ref[...], n, 1, 1, HIGH)
        return 0

    relay(0, 2, wd_ref, down_full, None)
    lax.fori_loop(0, 2, hidden_step, 0)
    relay_chunk(2, 0)
    relay_chunk(2, 1)

    logits = aux_ref[0:8, :]
    top = jnp.max(jnp.where(chosen, logits, NEG), axis=0, keepdims=True)
    weight = jnp.where(chosen, jnp.exp(logits - top), 0.0)
    gates = weight / jnp.sum(weight, axis=0, keepdims=True)
    pairs = aux_ref[8:12, :]
    other = jnp.concatenate([pairs[1:2], pairs[0:1], pairs[3:4], pairs[2:3]], axis=0)
    aux_ref[0:8, :] = gates
    aux_ref[8:12, :] = 1.0 / (1.0 + jnp.exp(other - pairs))
    aux_ref[12:16, :] = jnp.zeros((4, T), F32)

    def d_copy(i, ref, out, ss, rs, k, to=None):
        return me.send(ref.at[k], out.at[e if to is not None else k], ss.at[i], rs.at[i], e=to)

    def dispatch_step(j, _):
        k = me.far_first(j)
        i = (j + 1) % 4
        place = place_ref[k]
        snd_r[k] = dot(place, nb[...]).astype(BF)
        gate = aux_ref[pl.ds(k, 1), :]
        gated = jnp.where(place > 0, gate.astype(BF), jnp.zeros((CAP, T), BF))
        snd_d[k] = dot(gated, u_ref[...]).astype(BF)

        @pl.when(j != 2)
        def _():
            d_copy(i, snd_r, recv_r, dr_ss, dr_rs, k, k).start()
            d_copy(i, snd_d, recv_d, dd_ss, dd_rs, k, k).start()

        @pl.when(j == 2)
        def _():
            recv_r[k] = snd_r[k]
            recv_d[k] = snd_d[k]

        return 0

    lax.fori_loop(0, 4, dispatch_step, 0)
    relay_chunk(2, 2)
    relay_chunk(2, 3)
    relay(0, 3, wd_ref, down_full, None)
    relay_chunk(3, 0)
    for i, p in enumerate(me.exp_peers):
        d_copy(i, snd_r, recv_r, dr_ss, dr_rs, p).wait()
        d_copy(i, snd_d, recv_d, dd_ss, dd_rs, p).wait()

    partner = z + 1 - 2 * (z % 2)
    far_row = 2 * ((partner + 2) % 4) + 1 - me.x
    next_row = 2 * ((z + 2) % 4) + 1 - me.x
    side_row = 2 * partner + 1 - me.x
    near_row = 2 * partner + me.x
    first = (
        (grad_gate, far_row, far_gate, xf),
        (grad_gate, side_row, side_gate, near_row),
        (grad_up, far_row, far_up, xf),
        (grad_up, side_row, side_up, near_row),
        (grad_gate, next_row, next_gate, xf),
        (grad_gate, near_row, near_gate, near_row),
    )

    def first_copy(i, c, to=None):
        src, row, dst, _ = first[i]
        return me.send(cut(src.at[row], c), cut(dst, c), fs.at[i, c], fr.at[i, c], f=to)

    def first_send(c):
        for i in range(6):
            first_copy(i, c, first[i][3]).start()

    acc[...] = jnp.zeros_like(acc)
    d_acc[...] = jnp.zeros_like(d_acc)

    def unit_wait(n, full, c):
        def at(slot):
            return cut(full.at[slot], c)

        if c is None:

            @pl.when(z >= 1)
            def _():
                side_copy(0, at(xf - 2), at(xf - 2)).wait_recv()

            @pl.when(z <= 2)
            def _():
                side_copy(1, at(xf + 2), at(xf + 2)).wait_recv()

        else:
            x_copy(n, 0, at(xf), at(xf)).wait_recv()
        for p in (2, 3) if c is None else (1, 2, 3):

            @pl.when(z >= p)
            def _():
                x_copy(n, p, at(xf - 2 * p), at(xf - 2 * p)).wait_recv()

            @pl.when(z + p <= 3)
            def _():
                x_copy(n, 3 + p, at(xf + 2 * p), at(xf + 2 * p)).wait_recv()

    stages = ((st_gate, grad_gate, 0), (st_up, grad_up, 1), (st_down, grad_down, 2))

    def stage_copy(c, i):
        st, out, _ = stages[i]
        if i == 2:
            dst = out.at[pl.ds(2 * c, 2)]
        else:
            dst = out.at[:, :, pl.ds(pl.multiple_of(c * W, W), W)]
        return pltpu.make_async_copy(st, dst, st_sem.at[i])

    def ret_copy(i, snd, ret, ss, rs, to=None):
        p = me.exp_peers[i]
        return me.send(snd.at[p], ret.at[e if to else p], ss.at[i], rs.at[i], e=p if to else None)

    def expert_step(c, _):
        @pl.when(c < CHUNKS - 1)
        def _():
            relay_chunk(3, c + 1)

        @pl.when(c == 0)
        def _():
            for i in range(3):
                own_load(i).wait()
            unit_wait(0, down_full, None)

        unit_wait(1 + 2 * c, gate_full, c)
        unit_wait(2 + 2 * c, up_full, c)
        w = pl.ds(pl.multiple_of(c * W, W), W)
        row_in = recv_r[...].reshape(S, D)
        d_in = recv_d[...].reshape(S, D)
        w_gate = gate_full[:, :, w].reshape(D, W)
        w_up = up_full[:, :, w].reshape(D, W)
        w_down = down_full[pl.ds(2 * c, 2)].reshape(W, D)
        g = dot(row_in, w_gate)
        up = dot(row_in, w_up)
        sig = 1.0 / (1.0 + jnp.exp(-g))
        silu = g * sig
        inner = (silu * up).astype(BF)
        acc[...] += dot(inner, w_down)

        @pl.when(c == CHUNKS - 1)
        def _():
            snd_r[...] = acc[...].astype(BF).reshape(4, CAP, D)
            for i in (1, 2, 0):
                ret_copy(i, snd_r, ret_o, ro_ss, ro_rs, True).start()
            ret_o[e] = snd_r[e]

        d_inner = dot(d_in, w_down, 1, 1)
        d_up = (d_inner * silu).astype(BF)
        d_gate = (d_inner * up * (sig + silu * (1.0 - sig))).astype(BF)
        d_acc[...] += dot(d_gate, w_gate, 1, 1) + dot(d_up, w_up, 1, 1)

        @pl.when(c == CHUNKS - 1)
        def _():
            snd_d[...] = d_acc[...].astype(BF).reshape(4, CAP, D)
            for i in (1, 2, 0):
                ret_copy(i, snd_d, ret_d, rd_ss, rd_rs, True).start()
            ret_d[e] = snd_d[e]

        @pl.when(c > 0)
        def _():
            for i in range(3):
                stage_copy(c - 1, i).wait()
            first_send(c - 1)

        st_down[...] = dot(inner, d_in, 0, 0).astype(BF).reshape(2, W // 2, D)
        st_gate[...] = dot(row_in, d_gate, 0, 0).astype(BF).reshape(8, R, W)
        st_up[...] = dot(row_in, d_up, 0, 0).astype(BF).reshape(8, R, W)
        for i in range(3):
            stage_copy(c, i).start()
        return 0

    lax.fori_loop(0, CHUNKS, expert_step, 0)
    for i in range(3):
        stage_copy(CHUNKS - 1, i).wait()
    first_send(CHUNKS - 1)

    for src, slot_of, ss, rs, li in early:
        for j in range(7):
            me.send(slot_of(f), slot_of(f), ss.at[j], rs.at[j]).wait_send()
    wo_copy(e % 2).wait_send()
    for i in range(3):
        at_copy(i, e).wait_send()
        o_copy(i).wait_send()
    def relay_end(n, full, c):
        slot = cut(full.at[f], c)
        x_copy(n, 0, slot, slot).wait_send()

        @pl.when(z <= 2)
        def _():
            up_copy(n, 0, slot, slot).wait_send()
            if c is None:
                side_copy(0, slot, slot).wait_send()

        @pl.when(z >= 1)
        def _():
            down_copy(n, 0, slot, slot).wait_send()
            if c is None:
                side_copy(1, slot, slot).wait_send()

        for p in (1, 2, 3):

            @pl.when(z >= p)
            def _():
                if p <= 2:

                    @pl.when(z <= 2)
                    def _():
                        up_copy(n, p, slot, slot).wait_send()

                if p > 1 or c is not None:
                    x_copy(n, p, slot, slot).wait_send()

            @pl.when(z + p <= 3)
            def _():
                if p <= 2:

                    @pl.when(z >= 1)
                    def _():
                        down_copy(n, p, slot, slot).wait_send()

                if p > 1 or c is not None:
                    x_copy(n, 3 + p, slot, slot).wait_send()

    relay_end(0, down_full, None)

    def end_step(c, _):
        relay_end(1 + 2 * c, gate_full, c)
        relay_end(2 + 2 * c, up_full, c)
        return 0

    lax.fori_loop(0, CHUNKS, end_step, 0)
    for i in range(3):
        ret_copy(i, snd_r, ret_o, ro_ss, ro_rs).wait()
        ret_copy(i, snd_d, ret_d, rd_ss, rd_rs).wait()

    def first_end(c, _):
        for i in range(6):
            first_copy(i, c).wait()
        return 0

    lax.fori_loop(0, CHUNKS, first_end, 0)
    for i in range(7):
        keep_copy(i).wait()


def sds(shape, dtype):
    return jax.ShapeDtypeStruct(shape, dtype)


def vmem():
    return pl.BlockSpec(memory_space=pltpu.VMEM)


def anyspace():
    return pl.BlockSpec(memory_space=pl.ANY)


def smem():
    return pl.BlockSpec(memory_space=pltpu.SMEM)


def call_k1(x, u, wq, wk, wv, wo, wg, wu, wd, gres, routes, starts, gain_a, gain_f, router, proj, mix):
    T, D = x.shape
    C, R, FF, S = D // 4, D // 8, wg.shape[1], 4 * CAP
    n = 1 + 2 * CHUNKS
    dma = pltpu.SemaphoreType.DMA
    VM = pltpu.VMEM
    block = VM((4, CAP, D), BF)
    return pl.pallas_call(
        k1_kernel,
        name="forward",
        out_shape=(
            sds((4, T, D), BF), sds((4, T, C), BF), sds((4, T, C), BF), sds((4, T, C), BF), sds((4, T, C), BF),
            sds((4, 8, T), F32), sds((T, D), F32), sds((16, T), F32), sds((4, CAP, T), BF),
            sds((4, CAP, D), BF), sds((4, CAP, D), BF), sds((8, R, D), BF), sds((D, 3 * C), BF),
            sds((8, R, FF), BF), sds((8, R, FF), BF), sds((8, FF // 8, D), BF),
            sds((R, FF), BF), sds((R, FF), BF), sds((R, FF), BF), sds((R, FF), BF), sds((R, FF), BF), sds((R, FF), BF),
        ),
        in_specs=[vmem()] * 5 + [anyspace()] * 4 + [vmem()] * 2 + [smem()] + [vmem()] * 5,
        out_specs=tuple([anyspace()] * 5 + [vmem()] * 6 + [anyspace()] * 11),
        scratch_shapes=[
            VM((4, T, D), BF), VM((4, T, C), BF), VM((4, T, C), BF), VM((4, T, C), BF), VM((4, T, C), BF), VM((8, R, D), BF), VM((D, 3 * C), BF),
            VM((8, R, FF), BF), VM((8, R, FF), BF), VM((8, FF // 8, D), BF), VM((R, 3 * C), BF), VM((4, C, T), BF),
            VM((4, T, C), BF), VM((T, D), BF), block, block, block, block, VM((8, T), F32), VM((8, T), F32), VM((C, T), F32),
            VM((S, D), F32), VM((S, D), F32), VM((8, R, FF // CHUNKS), BF), VM((8, R, FF // CHUNKS), BF), VM((2, FF // 8, D), BF),
            dma((7,)), dma((7,)), dma((7,)), dma((7,)),
        ] + [dma((3,))] * 12 + [
            dma((n, 3)), dma((n, 3)), dma((n, 3)), dma((n, 3)), dma((n, 7)), dma((n, 7)),
            dma((2,)), dma((2,)), dma((1,)), dma((1,)), dma((5,)), dma((3,)), dma((6, CHUNKS)), dma((6, CHUNKS)), dma((7,)),
        ],
        compiler_params=pltpu.CompilerParams(collective_id=0, has_side_effects=True, vmem_limit_bytes=60 << 20),
    )(x, u, wq, wk, wv, wo, wg, wu, wd, gres, routes, starts, gain_a, gain_f, router, proj, mix)


def k2_kernel(
    ret_o, ret_d, hidden, u_ref, x_ref, aux_ref, place_ref, gres_ref,
    attn_hbm, q_hbm, k_hbm, v_hbm, o_hbm, lse_s, wo_hbm, wqkv_hbm, gain_a_ref, gain_f_ref, router_ref, proj_ref, mix_ref, cvec_ref, starts_ref,
    g_gate, g_up, g_down, far_gate, next_gate, near_gate, side_gate, far_up, side_up,
    layer_out, grad_tokens, d_res, small_out, ag_out, go_b, eg_out, eu_out, ed_out,
    xin_g, xin_u, xin_d, own_g, own_u, own_d, zin_g, zin_u, zin_d, cross_g, cross_u, cross_d,
    attn_all, q_s, k_s, v_s, o_s, wo, wqkv,
    dh_all, da, kt_s, dq, dk, dv, dqt, pin, py_in, d_hidden, wk_s, del_r, gt, go_acc, ag_s, bx_in, bz_in, ag_fin, go_s, go_in,
    small, sm1, sm2,
    load_sem, late_sem, xs, xr, zs, zr, own_sem, dh_ss, dh_rs, fw_ss, fw_rs, go_ss, go_rs, gb_ss, gb_rs, pd_ss, pd_rs, bx_ss, bx_rs, bz_ss, bz_rs,
    ab_ss, ab_rs, s1_ss, s1_rs, s2_ss, s2_rs,
):
    me = Place()
    e, f, z, x, xf = me.e, me.f, me.z, me.x, me.xf
    T, D = x_ref.shape
    C = D // 4
    R = D // 8
    M = 128

    partner = z + 1 - 2 * (z % 2)
    targets = ((partner + 2) % 4, (z + 2) % 4, z, partner)
    parts = (
        (g_gate, xin_g, own_g, zin_g, cross_g, eg_out),
        (g_up, xin_u, own_u, zin_u, cross_u, eu_out),
        (g_down, xin_d, own_d, zin_d, cross_d, ed_out),
    )

    def load_copy(i):
        src, dst = (
            (far_gate, xin_g.at[0]), (far_up, xin_u.at[0]), (next_gate, xin_g.at[1]),
            (side_gate, cross_g), (side_up, cross_u), (near_gate, zin_g.at[2]),
        )[i]
        return pltpu.make_async_copy(src, dst, load_sem.at[i])

    def own_copy(w, i, column):
        return pltpu.make_async_copy(parts[w][0].at[2 * targets[i] + column], parts[w][2], own_sem.at[w])

    def x_copy(w, i):
        src = parts[w][4] if i == 2 and w < 2 else parts[w][0].at[2 * targets[i] + 1 - x]
        dst = parts[w][4] if i == 3 else parts[w][1].at[i]
        return me.send(src, dst, xs.at[w, i], xr.at[w, i], f=xf)

    def z_copy(w, i):
        if i == 2:
            src = parts[w][0].at[2 * partner + x] if w < 2 else parts[w][4]
        else:
            src = parts[w][1].at[i]
        to = targets[1] if i == 1 else partner
        return me.send(src, parts[w][3].at[i], zs.at[w, i], zr.at[w, i], f=2 * to + x)

    def add(dst, *terms):
        total = dst.astype(F32)
        for term in terms:
            total = total + term.astype(F32)
        return total.astype(BF)

    def rs_far(w):
        xin, own = parts[w][1:3]
        if w == 2:
            x_copy(w, 0).wait_recv()
        else:
            load_copy(w).wait()
        own_copy(w, 0, x).wait()
        xin[0] = add(xin[0], own[...])
        z_copy(w, 0).start()
        own_copy(w, 1, x).start()

    def rs_cross(w):
        xin, own, zin = parts[w][1:4]
        if w:
            x_copy(w, 1).wait_recv()
        else:
            load_copy(2).wait()
        own_copy(w, 1, x).wait()
        z_copy(w, 0).wait_recv()
        xin[1] = add(xin[1], own[...], zin[0])
        z_copy(w, 1).start()
        if w < 2:
            own_copy(w, 2, 1 - x).start()
        else:
            own_copy(w, 3, x).start()

    def rs_side(w):
        own, cross = parts[w][2], parts[w][4]
        if w < 2:
            load_copy(3 + w).wait()
            own_copy(w, 2, 1 - x).wait()
        else:
            x_copy(w, 3).wait_recv()
            own_copy(w, 3, x).wait()
        cross[...] = add(cross[...], own[...])
        if w:
            z_copy(w, 2).start()
        own_copy(w, 2, x).start()

    def rs_end(w):
        xin, own, zin = parts[w][1:4]
        x_copy(w, 2).wait_recv()
        own_copy(w, 2, x).wait()
        z_copy(w, 1).wait_recv()
        if w:
            z_copy(w, 2).wait_recv()
        else:
            load_copy(5).wait()
        parts[w][5][...] = add(xin[2], own[...], zin[1], zin[2])

    for i in range(6):
        load_copy(i).start()
    for w in range(3):
        own_copy(w, 0, x).start()
    late = ((attn_hbm, attn_all), (q_hbm, q_s), (k_hbm, k_s), (v_hbm, v_s), (o_hbm, o_s), (wo_hbm, wo), (wqkv_hbm, wqkv))

    def late_copy(i):
        return pltpu.make_async_copy(late[i][0], late[i][1], late_sem.at[i])

    for i in (5, 2, 4, 1, 3, 6, 0):
        late_copy(i).start()
    me.barrier()
    for w, i in ((2, 0), (1, 1), (2, 1)):
        x_copy(w, i).start()
    rs_far(0)
    rs_far(1)

    small[...] = jnp.zeros_like(small)
    cv0, cv1 = cvec_ref[0:1, :], cvec_ref[1:2, :]
    maps = jnp.concatenate([router_ref[...], proj_ref[...], jnp.zeros((4, D), F32)], axis=0).astype(BF)
    lane8 = lane_of((M, 8))
    lane4 = lane_of((M, 4))

    def dh_copy(i, c, block, to=None):
        ref = dh_all.at[block, pl.ds(pl.multiple_of(c * M, M), M)]
        return me.send(ref, ref, dh_ss.at[i, c], dh_rs.at[i, c], e=to)

    def mix_step(c, _):
        r = pl.ds(pl.multiple_of(c * M, M), M)
        h = hidden[r, :]
        u = u_ref[r, :].astype(F32)
        inv = lax.rsqrt(jnp.mean(h * h, axis=-1, keepdims=True) + EPS)
        hn = h * inv
        gain = gain_f_ref[...].reshape(1, D)
        n = hn * gain
        cols = aux_ref[:, r].T
        gates = cols[:, 0:8]
        a0, b0, a1, b1 = cols[:, 8:9], cols[:, 9:10], cols[:, 10:11], cols[:, 11:12]
        g5, g6, g7 = cols[:, 5:6], cols[:, 6:7], cols[:, 7:8]
        c_n = g5 + g6 * a0 + g7 * a1
        c0 = g6 * b0
        c1 = g7 * b1
        mixed = h + c_n * n + c0 * cv0 + c1 * cv1
        dg = jnp.zeros((M, 8), F32)
        dn = c_n * u
        for k in range(4):
            place = place_ref[k, :, r]
            rk = dot(place, ret_o[k], 0, 0)
            mixed = mixed + cols[:, k : k + 1] * rk
            dg = jnp.where(lane8 == k, jnp.sum(u * rk, axis=-1, keepdims=True), dg)
            dn = dn + dot(place, ret_d[k], 0, 0)
        layer_out[r, :] = mixed.astype(BF)
        un = jnp.sum(u * n, axis=-1, keepdims=True)
        uv0 = jnp.sum(u * cv0, axis=-1, keepdims=True)
        uv1 = jnp.sum(u * cv1, axis=-1, keepdims=True)
        dg = jnp.where(lane8 == 5, un, dg)
        dg = jnp.where(lane8 == 6, a0 * un + b0 * uv0, dg)
        dg = jnp.where(lane8 == 7, a1 * un + b1 * uv1, dg)
        dlog = gates * (dg - jnp.sum(gates * dg, axis=-1, keepdims=True))
        e0 = g6 * a0 * b0 * (un - uv0)
        e1 = g7 * a1 * b1 * (un - uv1)
        dpair = jnp.where(lane4 == 0, e0, jnp.where(lane4 == 1, -e0, jnp.where(lane4 == 2, e1, -e1)))
        dl = jnp.concatenate([dlog, dpair, c0, c1, jnp.zeros((M, 2), F32)], axis=1)
        low = dl.astype(BF)
        d_res[:, r] = dot(mix_ref[...], dlog, 1, 1, HIGH)
        dn = dn + dot(jnp.where(lane_of((M, 16)) < 12, low, jnp.zeros((M, 16), BF)), maps)
        by_n = dot(low, n.astype(BF), 0, 0)
        by_u = dot(low, u_ref[r, :], 0, 0)
        small[0:12, :] += by_n[0:12]
        small[12:14, :] += by_u[12:14]
        small[14:15, :] += jnp.sum(dn * hn, axis=0, keepdims=True)
        small[16:24, 0:8] += dot(gres_ref[:, r], dlog, 1, 0, HIGH)
        gd = dn * gain
        dh = u + inv * (gd - hn * jnp.mean(gd * hn, axis=-1, keepdims=True))
        d_hidden[r, :] = dh
        dh_all[e, r, :] = dh.astype(BF)
        dh_copy(1, c, e, me.yp).start()
        dh_copy(0, c, e, me.sib).start()
        return 0

    lax.fori_loop(0, T // M, mix_step, 0)
    rs_cross(0)
    for i in range(7):
        late_copy(i).wait()

    head_of = lane_of((T, C)) // HD
    heads = (row_of((8, C)) == lane_of((8, C)) // HD).astype(F32)
    wk_s[...] = wqkv[:, C : 2 * C]
    dk[...] = jnp.zeros_like(dk)
    dv[...] = jnp.zeros_like(dv)
    go_acc[...] = jnp.zeros_like(go_acc)
    for b in range(4):
        kt_s[b] = k_s[b].T

    def fw_copy(block, to=None):
        return me.send(dh_all.at[block], dh_all.at[block], fw_ss.at[0], fw_rs.at[0], e=to)

    def d_out_step(j, qb):
        @pl.when(j == 1)
        def _():
            for c in range(T // M):
                dh_copy(0, c, me.sib).wait_recv()

        @pl.when(j == 2)
        def _():
            for c in range(T // M):
                dh_copy(1, c, me.yp).wait_recv()
            fw_copy(me.yp, me.sib).start()

        @pl.when(j == 3)
        def _():
            fw_copy(me.diag).wait_recv()

        dhb = dh_all[qb]
        low = dot(dhb, wo[pl.ds(2 * e, 2)].reshape(C, D), 1, 1).astype(BF)
        da[qb] = low
        ob = o_s[qb]
        del_r[qb] = dot(heads, low.astype(F32) * ob.astype(F32), 1, 1, HIGH)
        go_acc[...] += dot(ob, dhb, 0, 0)

    def head_block(qb, h):
        hr = pl.ds(pl.multiple_of(h * HD, HD), HD)
        mine = head_of == h

        def block(kb, masked):
            zero = jnp.zeros((T, C), BF)
            query = jnp.where(mine, q_s[qb], zero)
            d_out = jnp.where(mine, da[qb], zero)
            p = jnp.exp2(dot(k_s[kb], query, 1, 1) - lse_s[qb, pl.ds(h, 1), :])
            if masked:
                p = jnp.where(allowed_block(T, starts_ref[0, qb] - qb * T), p, 0.0)
            dp = dot(v_s[kb], d_out, 1, 1)
            dsc = (p * (dp - del_r[qb, pl.ds(h, 1), :])).astype(BF)
            dv[kb] += dot(p.astype(BF), d_out)
            dk[kb] += dot(dsc, query)
            return dot(kt_s[kb, hr, :], dsc)

        dqt[...] = block(qb, True)

        def key_step(kb, _):
            dqt[...] += block(kb, False)
            return 0

        lax.fori_loop(0, qb, key_step, 0)
        dq[qb, hr, :] = (dqt[...] * (1.0 / math.sqrt(HD))).astype(BF)

    def near_step(i, _):
        j = i // 3
        qb = me.near_first(j)

        @pl.when(i % 3 == 0)
        def _():
            d_out_step(j, qb)

        head_block(qb, i % 3)
        return 0

    def far_pass(h):
        def far_step(j, _):
            qb = me.near_first(j)
            if h == 0:
                d_out_step(j, qb)
            head_block(qb, h)
            return 0

        lax.fori_loop(2, 4, far_step, 0)

    def bx_copy(h, to=None):
        return me.send(ag_s.at[1 - x, h], bx_in.at[h], bx_ss.at[h], bx_rs.at[h], f=to)

    def bz_copy(h, d, to=None):
        return me.send(bx_in.at[h, (z + d) % 4], bz_in.at[h, d - 1], bz_ss.at[h, d - 1], bz_rs.at[h, d - 1], f=to)

    def ab_copy(h, i, to=None):
        return me.send(ag_fin.at[h], ag_out.at[e if to is not None else me.exp_peers[i], h], ab_ss.at[h, i], ab_rs.at[h, i], e=to)

    def weight_grads(h):
        cols = slice(h * HD, (h + 1) * HD)
        gt[...] = jnp.zeros_like(gt)

        def grad_step(b, _):
            low_k = (dk[b, :, cols] * LN2).T.astype(BF)
            low_v = dv[b, :, cols].T.astype(BF)
            gt[...] += dot(jnp.concatenate([dq[b, cols, :], low_k, low_v], axis=0), attn_all[b])
            return 0

        lax.fori_loop(0, 4, grad_step, 0)
        grads = gt[...].T.astype(BF).reshape(8, R, C)
        for k in range(8):
            ag_s[k % 2, h, k // 2] = grads[k]
        bx_copy(h, xf).start()

    def weight_rows(h):
        bx_copy(h).wait_recv()
        bx_in[h] = add(bx_in[h], ag_s[x, h])
        for d in (2, 1, 3):
            bz_copy(h, d, me.zf(d)).start()

    def weight_sum(h):
        total = bx_in[h, z].astype(F32)
        for d in (1, 2, 3):
            bz_copy(h, d).wait_recv()
            total = total + bz_in[h, d - 1].astype(F32)
        ag_fin[h] = total.astype(BF)
        for i, p in enumerate(me.exp_peers):
            ab_copy(h, i, p).start()
        ag_out[e, h] = ag_fin[h]

    lax.fori_loop(0, 6, near_step, 0)
    rs_far(2)
    far_pass(0)
    rs_cross(1)

    go_s[0] = go_acc[0:R, :].astype(BF)
    go_s[1] = go_acc[R : 2 * R, :].astype(BF)
    for j in range(2):

        @pl.when(f != 2 * e + j)
        def _():
            me.send(go_s.at[j], go_in.at[f], go_ss.at[j], go_rs.at[f], f=2 * e + j).start()

    weight_grads(0)
    x_copy(2, 3).start()
    far_pass(1)
    weight_grads(1)
    x_copy(2, 2).start()
    weight_rows(0)
    rs_cross(2)
    rs_side(0)
    rs_side(1)
    far_pass(2)

    for c in range(T // M):
        dh_copy(0, c, e).wait_send()
        dh_copy(1, c, e).wait_send()
    fw_copy(e).wait_send()

    def share_step(j, _):
        b = me.share_order(j)
        out = dot(dq[b], wqkv[:, 0:C], 0, 1)
        out = out + dot((dk[b] * LN2).astype(BF), wk_s[...], 1, 1)
        out = out + dot(dv[b].astype(BF), wqkv[:, 2 * C : 3 * C], 1, 1)
        small[15:16, :] += jnp.sum(out * attn_all[b].astype(F32), axis=0, keepdims=True)
        dh_all[b] = out.astype(BF)
        return 0

    def pd_copy(i, src, dst, to=None):
        return me.send(src, dst, pd_ss.at[i], pd_rs.at[i], e=to)

    lax.fori_loop(0, 1, share_step, 0)
    pd_copy(1, dh_all.at[me.diag], pin.at[1], me.sib).start()
    lax.fori_loop(1, 2, share_step, 0)
    pd_copy(1, pin.at[1], pin.at[1]).wait_recv()
    dh_all[me.yp] = add(dh_all[me.yp], pin[1])
    pd_copy(2, dh_all.at[me.yp], py_in, me.yp).start()
    weight_grads(2)
    x_copy(0, 2).start()
    x_copy(1, 2).start()
    lax.fori_loop(2, 3, share_step, 0)
    pd_copy(0, dh_all.at[me.sib], pin.at[0], me.sib).start()
    lax.fori_loop(3, 4, share_step, 0)

    small[15:16, :] = small[15:16, :] / gain_a_ref[...].reshape(1, D)
    sm1[e] = small[...].astype(BF)
    for i, p in enumerate(me.exp_peers):
        me.send(sm1.at[e], sm1.at[e], s1_ss.at[i], s1_rs.at[i], e=p).start()
    weight_rows(1)
    rs_side(2)
    weight_sum(0)
    for i, p in enumerate(me.exp_peers):
        me.send(sm1.at[p], sm1.at[p], s1_ss.at[i], s1_rs.at[i]).wait()
    sm2[f] = add(sm1[0], sm1[1], sm1[2], sm1[3])
    for r in range(1, 8):
        me.send(sm2.at[f], sm2.at[f], s2_ss.at[r - 1], s2_rs.at[f], f=me.fp(r)).start()
    weight_rows(2)

    @pl.when(z == e)
    def _():
        total = go_s[x].astype(F32)
        for r in range(1, 8):
            s = go_in.at[me.fp(r)]
            me.send(s, s, go_ss.at[0], go_rs.at[me.fp(r)]).wait_recv()
            total = total + go_in[me.fp(r)].astype(F32)
        go_b[...] = total.astype(BF)
        for i, p in enumerate(me.exp_peers):
            me.send(go_b, go_b, gb_ss.at[i], gb_rs.at[0], e=p).start()

    weight_sum(1)
    weight_sum(2)
    for r in range(1, 8):
        s = sm2.at[me.fp(r)]
        me.send(s, s, s2_ss.at[r - 1], s2_rs.at[me.fp(r)]).wait_recv()
    total = sm2[0].astype(F32)
    for r in range(1, 8):
        total = total + sm2[r].astype(F32)
    small_out[...] = total

    pd_copy(0, pin.at[0], pin.at[0]).wait_recv()
    pd_copy(2, py_in, py_in).wait_recv()

    def token_step(i, _):
        r = pl.ds(pl.multiple_of(i * 256, 256), 256)
        d = dh_all[e, r, :].astype(F32) + pin[0, r, :].astype(F32) + py_in[r, :].astype(F32)
        xv = x_ref[r, :].astype(F32)
        inv = lax.rsqrt(jnp.mean(xv * xv, axis=-1, keepdims=True) + EPS)
        xn = xv * inv
        gd = d * gain_a_ref[...].reshape(1, D)
        grad_tokens[r, :] = (d_hidden[r, :] + inv * (gd - xn * jnp.mean(gd * xn, axis=-1, keepdims=True))).astype(BF)
        return 0

    lax.fori_loop(0, 2, token_step, 0)
    for w in range(3):
        rs_end(w)

    @pl.when(z != e)
    def _():
        me.send(go_b, go_b, gb_ss.at[0], gb_rs.at[0]).wait_recv()

    for w in range(3):
        for i in range(3):
            if (w, i) not in ((0, 0), (0, 1), (1, 0)):
                x_copy(w, i).wait_send()
            if (w, i) != (0, 2):
                z_copy(w, i).wait_send()
    x_copy(2, 3).wait_send()
    for j in range(2):

        @pl.when(f != 2 * e + j)
        def _():
            me.send(go_s.at[j], go_in.at[f], go_ss.at[j], go_rs.at[f]).wait_send()

    @pl.when(z == e)
    def _():
        for i in range(3):
            me.send(go_b, go_b, gb_ss.at[i], gb_rs.at[0]).wait_send()

    for i in range(3):
        pd_copy(i, py_in, py_in).wait_send()
        for h in range(3):
            ab_copy(h, i).wait()
    for h in range(3):
        bx_copy(h).wait_send()
        for d in (1, 2, 3):
            bz_copy(h, d).wait_send()
    for r in range(1, 8):
        me.send(sm2.at[f], sm2.at[f], s2_ss.at[r - 1], s2_rs.at[f]).wait_send()


def call_k2(*args):
    x, (gg, gu, gd) = args[4], args[23:26]
    late = args[8:13] + args[14:16]
    T, D = x.shape
    C, R = D // 4, D // 8
    dma = pltpu.SemaphoreType.DMA
    VM = pltpu.VMEM
    shapes = (gg.shape[1:], gu.shape[1:], gd.shape[1:])
    return pl.pallas_call(
        k2_kernel,
        name="backward",
        out_shape=(
            sds((T, D), BF), sds((T, D), BF), sds((8, T), F32), sds((24, D), F32),
            sds((4, 3, R, C), BF), sds((R, D), BF),
        ) + tuple(sds(s, BF) for s in shapes),
        in_specs=[vmem()] * 8 + [anyspace()] * 5 + [vmem()] + [anyspace()] * 2 + [vmem()] * 6 + [smem()] + [anyspace()] * 9,
        out_specs=tuple([vmem()] * 9),
        scratch_shapes=[VM((3,) + s, BF) for s in shapes] + [VM(s, BF) for s in shapes] + [VM((3,) + s, BF) for s in shapes] + [VM(s, BF) for s in shapes] + [VM(a.shape, BF) for a in late] + [
            VM((4, T, D), BF), VM((4, T, C), BF), VM((4, C, T), BF), VM((4, C, T), BF), VM((4, T, C), F32), VM((4, T, C), F32),
            VM((HD, T), F32), VM((2, T, D), BF), VM((T, D), BF), VM((T, D), F32), VM((D, C), BF), VM((4, 8, T), F32), VM((C, D), F32), VM((C, D), F32),
            VM((2, 3, 4, R, C), BF), VM((3, 4, R, C), BF), VM((3, 3, R, C), BF), VM((3, R, C), BF), VM((2, R, D), BF), VM((8, R, D), BF),
            VM((24, D), F32), VM((4, 24, D), BF), VM((8, 24, D), BF),
            dma((6,)), dma((7,)), dma((3, 4)), dma((3, 4)), dma((3, 3)), dma((3, 3)), dma((3,)),
            dma((2, 4)), dma((2, 4)), dma((1,)), dma((1,)), dma((2,)), dma((8,)), dma((3,)), dma((1,)), dma((3,)), dma((3,)),
            dma((3,)), dma((3,)), dma((3, 3)), dma((3, 3)), dma((3, 3)), dma((3, 3)), dma((3,)), dma((3,)), dma((7,)), dma((8,)),
        ],
        compiler_params=pltpu.CompilerParams(collective_id=1, has_side_effects=True, vmem_limit_bytes=63 << 20),
    )(*args)


def k3_kernel(
    layer_in, tokens_in, res_in, small, ag, go, eg, eu, ed,
    layer_out, tokens_out, res_out, norm_a, norm_f, g_q, g_k, g_v, g_o, router, mixing, proj, cvec, o_gate, o_up, o_down,
):
    layer_out[...] = layer_in[...]
    tokens_out[...] = tokens_in[...]
    res_out[...] = res_in[...]
    norm_a[...] = small[15, :]
    norm_f[...] = small[14, :]
    for i, out in enumerate((g_q, g_k, g_v)):
        out[...] = jnp.concatenate(
            [ag[b, h, :, i * HD : (i + 1) * HD].astype(F32) for b in range(4) for h in range(3)], axis=1
        )
    g_o[...] = go[...].astype(F32)
    router[...] = small[0:8, :]
    mixing[...] = small[16:24, 0:8]
    proj[...] = small[8:12, :]
    cvec[...] = small[12:14, :]
    o_gate[...] = eg[...].astype(F32)
    o_up[...] = eu[...].astype(F32)
    o_down[...] = ed[...].astype(F32)


def call_k3(*args):
    T, D = args[0].shape
    R = D // 8
    return pl.pallas_call(
        k3_kernel,
        name="finish",
        out_shape=(
            sds((T, D), BF), sds((T, D), BF), sds((8, T), F32), sds((D,), F32), sds((D,), F32),
            sds((R, D), F32), sds((R, D), F32), sds((R, D), F32), sds((R, D), F32),
            sds((8, D), F32), sds((8, 8), F32), sds((4, D), F32), sds((2, D), F32),
        ) + tuple(sds(a.shape, F32) for a in args[6:9]),
        in_specs=[vmem()] * 9,
        out_specs=tuple([vmem()] * 16),
    )(*args)


def body_fast(
    tokens, gate_res, routes, piece_starts, norm_attn, norm_ffn, w_query, w_key, w_value, w_out, router, mixing,
    const_proj, const_vec, w_gate, w_up, w_down, cotangent,
):
    x, u = tokens[0], cotangent[0]
    gres, route_ids = gate_res[0].T, routes[0].T
    (attn_all, q, k, v, o, lse, hidden, aux, place, ret_o, ret_d, wo, wq, gg, gu, gd, fg, ng, eg1, sg, fu, su) = call_k1(
        x, u, w_query, w_key, w_value, w_out, w_gate[0], w_up[0], w_down[0], gres, route_ids, piece_starts,
        norm_attn, norm_ffn, router.T, const_proj.T, mixing,
    )
    outs = call_k2(
        ret_o, ret_d, hidden, u, x, aux, place, gres, attn_all, q, k, v, o, lse, wo, wq,
        norm_attn, norm_ffn, router.T, const_proj.T, mixing, const_vec, piece_starts, gg, gu, gd, fg, ng, eg1, sg, fu, su,
    )
    (layer_out, grad_tokens, d_res, norm_a, norm_f, g_q, g_k, g_v, g_o, g_router, g_mixing, g_proj, g_cvec, eg, eu, ed) = call_k3(*outs)
    return (
        layer_out[None], grad_tokens[None], d_res.T[None], norm_a, norm_f, g_q, g_k, g_v, g_o,
        g_router.T, g_mixing, g_proj.T, g_cvec, eg[None], eu[None], ed[None],
    )


def solution(mesh):
    placed = (
        P("fsdp", "exp", None),
        P("fsdp", "exp", None),
        P("fsdp", "exp", None),
        P("fsdp", None),
        P(),
        P(),
        P("fsdp", None),
        P("fsdp", None),
        P("fsdp", None),
        P("fsdp", None),
        P(),
        P(),
        P(),
        P(),
        P("exp", "fsdp", None),
        P("exp", "fsdp", None),
        P("exp", "fsdp", None),
        P("fsdp", "exp", None),
    )
    return jax.shard_map(
        body_fast if (mesh.shape['exp'], mesh.shape['fsdp']) == (4, 8) else body,
        mesh=mesh,
        in_specs=placed,
        out_specs=(
            P("fsdp", "exp", None),
            P("fsdp", "exp", None),
            P("fsdp", "exp", None),
            P(),
            P(),
            P("fsdp", None),
            P("fsdp", None),
            P("fsdp", None),
            P("fsdp", None),
            P(),
            P(),
            P(),
            P(),
            P("exp", "fsdp", None),
            P("exp", "fsdp", None),
            P("exp", "fsdp", None),
        ),
        check_vma=False,
    )
```

```python
import math

import jax
import jax.numpy as jnp
from jax import lax
from jax.experimental import pallas as pl
from jax.experimental.pallas import tpu as pltpu
from jax.sharding import PartitionSpec as P

H = 12
HD = 64
PIECE = 256
KBLK = 512
CAP = 160


EPS = 1e-05
HIGH = lax.Precision.HIGHEST
NEG = -1e30


def rms_scale(values, gain_vec):
    inverse = lax.rsqrt(jnp.mean(values * values, axis=-1, keepdims=True) + EPS)
    return values * inverse * gain_vec


def piece_ids(positions, starts, extent):
    inside = (positions[:, None] >= starts[None, :]) & (
        positions[:, None] < starts[None, :] + extent
    )
    labels = jnp.arange(1, starts.shape[0] + 1, dtype=jnp.int32)
    return jnp.sum(jnp.where(inside, labels[None, :], 0), axis=1)


def reach_bounds(positions, starts, extent):
    inside = (positions[:, None] >= starts[None, :]) & (
        positions[:, None] < starts[None, :] + extent
    )
    piece_last = jnp.max(jnp.where(inside, starts[None, :] + extent - 1, 0))
    piece_first = jnp.min(jnp.where(inside, starts[None, :], positions[0]))
    upper = jnp.maximum(positions[-1], piece_last)
    lower = jnp.minimum(positions[0], piece_first)
    return (upper, lower)


def allowed_mask(query_pos, query_ids, key_pos, key_ids):
    causal = key_pos[None, :] <= query_pos[:, None]
    shared = (key_ids[None, :] == query_ids[:, None]) & (query_ids[:, None] > 0)
    return causal | shared


def slot_dest(route_ids, n_ffn, capacity):
    flat_ids = route_ids.reshape(-1)
    onehot = (flat_ids[:, None] == jnp.arange(n_ffn, dtype=jnp.int32)[None, :]).astype(jnp.int32)
    earlier = jnp.cumsum(onehot, axis=0) - onehot
    slot_pos = jnp.sum(earlier * onehot, axis=1)
    return jnp.where(flat_ids < n_ffn, flat_ids * capacity + slot_pos, n_ffn * capacity)


def local_mix(
    normed, res_logits, router, mixing, const_proj, const_vec, expert_rows, route_ids, n_ffn
):
    n_all = router.shape[1]
    logits = jnp.dot(normed, router, precision=HIGH) + jnp.dot(res_logits, mixing, precision=HIGH)
    probs = jax.nn.softmax(logits, axis=-1)
    labels = jnp.arange(n_all, dtype=jnp.int32)
    chosen = jnp.sum(
        jnp.where(route_ids[:, :, None] == labels[None, None, :], probs[:, None, :], 0.0), axis=-1
    )
    gates = chosen / jnp.sum(chosen, axis=1, keepdims=True)
    pair_logits = jnp.dot(normed, const_proj, precision=HIGH)
    first_pair = jax.nn.softmax(pair_logits[:, 0:2], axis=-1)
    second_pair = jax.nn.softmax(pair_logits[:, 2:4], axis=-1)
    first_const = first_pair[:, 0:1] * normed + first_pair[:, 1:2] * const_vec[0][None, :]
    second_const = second_pair[:, 0:1] * normed + second_pair[:, 1:2] * const_vec[1][None, :]
    mixed = jnp.zeros_like(normed)
    for route_k in range(2):
        route_id = route_ids[:, route_k : route_k + 1]
        entry = jnp.where(route_id < n_ffn, expert_rows[:, route_k], 0.0)
        entry = entry + jnp.where(route_id == n_ffn + 1, normed, 0.0)
        entry = entry + jnp.where(route_id == n_ffn + 2, first_const, 0.0)
        entry = entry + jnp.where(route_id == n_ffn + 3, second_const, 0.0)
        mixed = mixed + gates[:, route_k : route_k + 1] * entry
    return mixed


def swiglu_act(gate_pre, up_pre):
    return jax.nn.silu(gate_pre) * up_pre


def body(
    tokens,
    gate_res,
    routes,
    piece_starts,
    norm_attn,
    norm_ffn,
    w_query,
    w_key,
    w_value,
    w_out,
    router,
    mixing,
    const_proj,
    const_vec,
    w_gate,
    w_up,
    w_down,
    cotangent,
):
    n_ffn = lax.axis_size("exp")
    rows_dev = tokens.shape[1]
    model_width = tokens.shape[2]
    seq_length = rows_dev * n_ffn
    score_scale = 1.0 / math.sqrt(HD)
    inputs_f = tokens[0].astype(jnp.float32)
    res_logits = gate_res[0]
    route_ids = routes[0]
    starts = piece_starts[0]
    full_query, full_key, full_value, full_out = (
        lax.all_gather(w_query, "fsdp", axis=0, tiled=True),
        lax.all_gather(w_key, "fsdp", axis=0, tiled=True),
        lax.all_gather(w_value, "fsdp", axis=0, tiled=True),
        lax.all_gather(w_out, "fsdp", axis=0, tiled=True),
    )
    attn_in = rms_scale(inputs_f, norm_attn).astype(jnp.bfloat16)
    query = jnp.dot(attn_in, full_query, preferred_element_type=jnp.float32).astype(jnp.bfloat16)
    key = jnp.dot(attn_in, full_key, preferred_element_type=jnp.float32).astype(jnp.bfloat16)
    value = jnp.dot(attn_in, full_value, preferred_element_type=jnp.float32).astype(jnp.bfloat16)
    keys_all, values_all = (
        lax.all_gather(key, "exp", axis=0, tiled=True),
        lax.all_gather(value, "exp", axis=0, tiled=True),
    )
    query_heads = query.reshape(rows_dev, H, HD)
    key_heads = keys_all.reshape(seq_length, H, HD)
    value_heads = values_all.reshape(seq_length, H, HD)
    query_pos = lax.axis_index("exp") * rows_dev + jnp.arange(rows_dev, dtype=jnp.int32)
    query_ids = piece_ids(query_pos, starts, PIECE)
    key_upper, query_lower = reach_bounds(query_pos, starts, PIECE)
    block_list = jnp.arange(seq_length // KBLK, dtype=jnp.int32)

    def score_block(block_index):
        key_first = block_index * KBLK
        key_block = lax.dynamic_slice_in_dim(key_heads, key_first, KBLK, 0)
        value_block = lax.dynamic_slice_in_dim(value_heads, key_first, KBLK, 0)
        key_pos = key_first + jnp.arange(KBLK, dtype=jnp.int32)
        key_ids = piece_ids(key_pos, starts, PIECE)
        scores = (
            jnp.einsum("qhd,khd->hqk", query_heads, key_block, preferred_element_type=jnp.float32)
            * score_scale
        )
        allowed = allowed_mask(query_pos, query_ids, key_pos, key_ids)[None]
        return (scores, allowed, key_block, value_block)

    def needed(block_index):
        return block_index * KBLK <= key_upper

    def lse_step(carry, block_index):

        def lse_active(state):
            run_max, run_sum = state
            scores, allowed, _, _ = score_block(block_index)
            scores = jnp.where(allowed, scores, NEG)
            new_max = jnp.maximum(run_max, jnp.max(scores, axis=-1))
            exp_terms = jnp.where(allowed, jnp.exp(scores - new_max[..., None]), 0.0)
            return (new_max, run_sum * jnp.exp(run_max - new_max) + jnp.sum(exp_terms, axis=-1))

        return (lax.cond(needed(block_index), lse_active, lambda state: state, carry), None)

    start_carry = (jnp.full((H, rows_dev), NEG, jnp.float32), jnp.zeros((H, rows_dev), jnp.float32))
    (run_max, run_sum), _ = lax.scan(lse_step, start_carry, block_list)
    log_norm = run_max + jnp.log(run_sum)

    def block_probs(scores, allowed):
        return jnp.where(allowed, jnp.exp(scores - log_norm[..., None]), 0.0)

    def out_step(accum, block_index):

        def out_active(total):
            scores, allowed, _, value_block = score_block(block_index)
            probs_low = block_probs(scores, allowed).astype(jnp.bfloat16)
            return total + jnp.einsum(
                "hqk,khd->qhd", probs_low, value_block, preferred_element_type=jnp.float32
            )

        return (lax.cond(needed(block_index), out_active, lambda total: total, accum), None)

    attn_sum, _ = lax.scan(out_step, jnp.zeros((rows_dev, H, HD), jnp.float32), block_list)
    attn_low = attn_sum.astype(jnp.bfloat16).reshape(rows_dev, model_width)
    hidden = inputs_f + jnp.dot(attn_low, full_out, preferred_element_type=jnp.float32)
    normed = rms_scale(hidden, norm_ffn)
    destination = slot_dest(route_ids, n_ffn, CAP)
    sources = jnp.arange(2 * rows_dev, dtype=jnp.int32) // 2
    slot_table = (
        jnp.full((n_ffn * CAP,), rows_dev, jnp.int32).at[destination].set(sources, mode="drop")
    )
    padded = jnp.concatenate(
        [normed.astype(jnp.bfloat16), jnp.zeros((1, model_width), jnp.bfloat16)], axis=0
    )
    dispatched = padded[slot_table].reshape(n_ffn, CAP, model_width)
    received = lax.all_to_all(dispatched, "exp", split_axis=0, concat_axis=0, tiled=True)
    full_gate, full_up, full_down = (
        lax.all_gather(w_gate[0], "fsdp", axis=0, tiled=True),
        lax.all_gather(w_up[0], "fsdp", axis=0, tiled=True),
        lax.all_gather(w_down[0], "fsdp", axis=0, tiled=True),
    )
    slot_rows = received.reshape(n_ffn * CAP, model_width)
    gate_pre = jnp.dot(slot_rows, full_gate, preferred_element_type=jnp.float32)
    up_pre = jnp.dot(slot_rows, full_up, preferred_element_type=jnp.float32)
    inner_act = swiglu_act(gate_pre, up_pre).astype(jnp.bfloat16)
    expert_result = jnp.dot(inner_act, full_down, preferred_element_type=jnp.float32).astype(
        jnp.bfloat16
    )
    returned = lax.all_to_all(
        expert_result.reshape(n_ffn, CAP, model_width),
        "exp",
        split_axis=0,
        concat_axis=0,
        tiled=True,
    )
    returned_pad = jnp.concatenate(
        [returned.reshape(n_ffn * CAP, model_width), jnp.zeros((1, model_width), jnp.bfloat16)],
        axis=0,
    )
    expert_rows = returned_pad[destination].astype(jnp.float32).reshape(rows_dev, 2, model_width)

    def mix_local(normed_in, logits_in, router_in, mixing_in, proj_in, vec_in, rows_in):
        return local_mix(
            normed_in, logits_in, router_in, mixing_in, proj_in, vec_in, rows_in, route_ids, n_ffn
        )

    moe_out, mix_pull = jax.vjp(
        mix_local, normed, res_logits, router, mixing, const_proj, const_vec, expert_rows
    )
    layer_out = (hidden + moe_out).astype(jnp.bfloat16)
    upstream = cotangent[0].astype(jnp.float32)
    d_normed_local, d_res_logits, d_router, d_mixing, d_const_proj, d_const_vec, d_expert_rows = (
        mix_pull(upstream)
    )
    d_rows_low = d_expert_rows.reshape(2 * rows_dev, model_width).astype(jnp.bfloat16)
    d_dispatched = (
        jnp.zeros((n_ffn * CAP, model_width), jnp.bfloat16)
        .at[destination]
        .set(d_rows_low, mode="drop")
    )
    d_received = lax.all_to_all(
        d_dispatched.reshape(n_ffn, CAP, model_width),
        "exp",
        split_axis=0,
        concat_axis=0,
        tiled=True,
    )
    d_received = d_received.reshape(n_ffn * CAP, model_width)
    d_inner = jnp.einsum("rd,fd->rf", d_received, full_down, preferred_element_type=jnp.float32)
    _, act_pull = jax.vjp(swiglu_act, gate_pre, up_pre)
    d_gate_pre, d_up_pre = act_pull(d_inner)
    d_gate_low = d_gate_pre.astype(jnp.bfloat16)
    d_up_low = d_up_pre.astype(jnp.bfloat16)
    grad_down_full = jnp.einsum(
        "rf,rd->fd", inner_act, d_received, preferred_element_type=jnp.float32
    )
    grad_gate_full = jnp.einsum(
        "rd,rf->df", slot_rows, d_gate_low, preferred_element_type=jnp.float32
    )
    grad_up_full = jnp.einsum("rd,rf->df", slot_rows, d_up_low, preferred_element_type=jnp.float32)
    d_slot_rows = (
        jnp.einsum("rf,df->rd", d_gate_low, full_gate, preferred_element_type=jnp.float32)
        + jnp.einsum("rf,df->rd", d_up_low, full_up, preferred_element_type=jnp.float32)
    ).astype(jnp.bfloat16)
    d_sent = lax.all_to_all(
        d_slot_rows.reshape(n_ffn, CAP, model_width), "exp", split_axis=0, concat_axis=0, tiled=True
    )
    d_sent_pad = jnp.concatenate(
        [d_sent.reshape(n_ffn * CAP, model_width), jnp.zeros((1, model_width), jnp.bfloat16)],
        axis=0,
    )
    d_normed_sent = jnp.sum(
        d_sent_pad[destination].astype(jnp.float32).reshape(rows_dev, 2, model_width), axis=1
    )
    _, norm_ffn_pull = jax.vjp(rms_scale, hidden, norm_ffn)
    d_hidden_part, d_norm_ffn = norm_ffn_pull(d_normed_local + d_normed_sent)
    d_hidden = upstream + d_hidden_part
    d_hidden_low = d_hidden.astype(jnp.bfloat16)
    grad_out_full = jnp.einsum(
        "td,te->de", attn_low, d_hidden_low, preferred_element_type=jnp.float32
    )
    d_attn = jnp.einsum(
        "te,de->td", d_hidden_low, full_out, preferred_element_type=jnp.float32
    ).astype(jnp.bfloat16)
    d_attn_heads = d_attn.reshape(rows_dev, H, HD)
    zero_block = jnp.zeros((KBLK, H, HD), jnp.float32)

    def delta_terms(block_index):
        scores, allowed, _, value_block = score_block(block_index)
        probs = block_probs(scores, allowed)
        d_probs = jnp.einsum(
            "qhd,khd->hqk", d_attn_heads, value_block, preferred_element_type=jnp.float32
        )
        part = jnp.sum(probs * d_probs, axis=-1)
        return (
            part,
            jnp.einsum(
                "hqk,qhd->khd",
                probs.astype(jnp.bfloat16),
                d_attn_heads,
                preferred_element_type=jnp.float32,
            ),
        )

    def query_terms(block_index, row_delta):
        scores, allowed, key_block, value_block = score_block(block_index)
        probs = block_probs(scores, allowed)
        d_probs = jnp.einsum(
            "qhd,khd->hqk", d_attn_heads, value_block, preferred_element_type=jnp.float32
        )
        d_scores = (probs * (d_probs - row_delta[..., None])).astype(jnp.bfloat16)
        part = (
            jnp.einsum("hqk,khd->qhd", d_scores, key_block, preferred_element_type=jnp.float32)
            * score_scale
        )
        return (
            part,
            jnp.einsum("hqk,qhd->khd", d_scores, query_heads, preferred_element_type=jnp.float32)
            * score_scale,
        )

    def delta_step(total, block_index):

        def delta_active(running):
            part, grad_block = delta_terms(block_index)
            return (running + part, grad_block)

        return lax.cond(
            needed(block_index), delta_active, lambda running: (running, zero_block), total
        )

    row_delta, grad_values = lax.scan(delta_step, jnp.zeros((H, rows_dev), jnp.float32), block_list)

    def query_step(total, block_index):

        def query_active(running):
            part, grad_block = query_terms(block_index, row_delta)
            return (running + part, grad_block)

        return lax.cond(
            needed(block_index), query_active, lambda running: (running, zero_block), total
        )

    d_query_sum, grad_keys = lax.scan(
        query_step, jnp.zeros((rows_dev, H, HD), jnp.float32), block_list
    )
    grad_keys = grad_keys.reshape(seq_length, model_width)
    grad_values = grad_values.reshape(seq_length, model_width)
    d_key_sum, d_value_sum = (
        lax.psum_scatter(
            grad_keys.astype(jnp.bfloat16), "exp", scatter_dimension=0, tiled=True
        ).astype(jnp.float32),
        lax.psum_scatter(
            grad_values.astype(jnp.bfloat16), "exp", scatter_dimension=0, tiled=True
        ).astype(jnp.float32),
    )
    d_query_low = d_query_sum.reshape(rows_dev, model_width).astype(jnp.bfloat16)
    d_key_low = d_key_sum.astype(jnp.bfloat16)
    d_value_low = d_value_sum.astype(jnp.bfloat16)
    d_attn_in = (
        jnp.einsum("te,de->td", d_query_low, full_query, preferred_element_type=jnp.float32)
        + jnp.einsum("te,de->td", d_key_low, full_key, preferred_element_type=jnp.float32)
        + jnp.einsum("te,de->td", d_value_low, full_value, preferred_element_type=jnp.float32)
    )
    grad_query_full = jnp.einsum(
        "td,te->de", attn_in, d_query_low, preferred_element_type=jnp.float32
    )
    grad_key_full = jnp.einsum("td,te->de", attn_in, d_key_low, preferred_element_type=jnp.float32)
    grad_value_full = jnp.einsum(
        "td,te->de", attn_in, d_value_low, preferred_element_type=jnp.float32
    )
    _, norm_attn_pull = jax.vjp(rms_scale, inputs_f, norm_attn)
    d_inputs_part, d_norm_attn = norm_attn_pull(d_attn_in)
    grad_tokens = (d_hidden + d_inputs_part).astype(jnp.bfloat16)
    attn_shards = (
        lax.psum_scatter(
            grad_query_full.astype(jnp.bfloat16), "fsdp", scatter_dimension=0, tiled=True
        ).astype(jnp.float32),
        lax.psum_scatter(
            grad_key_full.astype(jnp.bfloat16), "fsdp", scatter_dimension=0, tiled=True
        ).astype(jnp.float32),
        lax.psum_scatter(
            grad_value_full.astype(jnp.bfloat16), "fsdp", scatter_dimension=0, tiled=True
        ).astype(jnp.float32),
        lax.psum_scatter(
            grad_out_full.astype(jnp.bfloat16), "fsdp", scatter_dimension=0, tiled=True
        ).astype(jnp.float32),
    )
    attn_shards = (
        lax.psum(attn_shards[0].astype(jnp.bfloat16), "exp").astype(jnp.float32),
        lax.psum(attn_shards[1].astype(jnp.bfloat16), "exp").astype(jnp.float32),
        lax.psum(attn_shards[2].astype(jnp.bfloat16), "exp").astype(jnp.float32),
        lax.psum(attn_shards[3].astype(jnp.bfloat16), "exp").astype(jnp.float32),
    )
    expert_shards = (
        lax.psum_scatter(
            grad_gate_full.astype(jnp.bfloat16), "fsdp", scatter_dimension=0, tiled=True
        ).astype(jnp.float32),
        lax.psum_scatter(
            grad_up_full.astype(jnp.bfloat16), "fsdp", scatter_dimension=0, tiled=True
        ).astype(jnp.float32),
        lax.psum_scatter(
            grad_down_full.astype(jnp.bfloat16), "fsdp", scatter_dimension=0, tiled=True
        ).astype(jnp.float32),
    )
    small_sums = lax.psum(
        (d_norm_attn, d_norm_ffn, d_router, d_mixing, d_const_proj, d_const_vec), ("exp", "fsdp")
    )
    return (
        layer_out[None],
        grad_tokens[None],
        d_res_logits[None],
        small_sums[0],
        small_sums[1],
        attn_shards[0],
        attn_shards[1],
        attn_shards[2],
        attn_shards[3],
        small_sums[2],
        small_sums[3],
        small_sums[4],
        small_sums[5],
        expert_shards[0][None],
        expert_shards[1][None],
        expert_shards[2][None],
    )


MESH = pl.DeviceIdType.MESH
BF = jnp.bfloat16
F32 = jnp.float32
LN2 = math.log(2.0)
QSCALE = 1.0 / (LN2 * math.sqrt(HD))
CHUNKS = 4


class Place:
    def __init__(self):
        self.e = lax.axis_index("exp")
        self.f = lax.axis_index("fsdp")
        self.z = self.f // 2
        self.x = self.f % 2
        self.sib = self.e + 1 - 2 * (self.e % 2)
        self.yp = (self.e + 2) % 4
        self.diag = (self.sib + 2) % 4
        self.xf = self.f + 1 - 2 * self.x
        self.exp_peers = (self.sib, self.yp, self.diag)

    def zf(self, d):
        return ((self.z + d) % 4) * 2 + self.x

    def fp(self, r):
        return (self.f + r) % 8

    def far_first(self, j):
        return (self.e + (j % 2) * (1 - 2 * (self.e % 2)) + 2 * (1 - j // 2)) % 4

    def near_first(self, j):
        return (self.e + (j % 2) * (1 - 2 * (self.e % 2)) + 2 * (j // 2)) % 4

    def share_order(self, j):
        return (self.e + (1 - j % 2) * (1 - 2 * (self.e % 2)) + 2 * (1 - j // 2)) % 4

    def barrier(self):
        sem = pltpu.get_barrier_semaphore()
        for p in self.exp_peers:
            pl.semaphore_signal(sem, inc=1, device_id=(p, self.f), device_id_type=MESH)
        for r in range(1, 8):
            pl.semaphore_signal(sem, inc=1, device_id=(self.e, self.fp(r)), device_id_type=MESH)
        pl.semaphore_wait(sem, 10)

    def send(self, src, dst, ss, rs, e=None, f=None):
        return pltpu.make_async_remote_copy(
            src_ref=src,
            dst_ref=dst,
            send_sem=ss,
            recv_sem=rs,
            device_id=(self.e if e is None else e, self.f if f is None else f),
            device_id_type=MESH,
        )


def lane_of(shape):
    return lax.broadcasted_iota(jnp.int32, shape, len(shape) - 1)


def row_of(shape):
    return lax.broadcasted_iota(jnp.int32, shape, 0)


def dot(a, b, ca=1, cb=0, precision=None):
    return lax.dot_general(a, b, (((ca,), (cb,)), ((), ())), precision=precision, preferred_element_type=F32)


def allowed_block(size, first):
    key, query = row_of((size, size)), lane_of((size, size))
    inside_k = (key >= first) & (key < first + PIECE)
    inside_q = (query >= first) & (query < first + PIECE)
    return (key <= query) | (inside_k & inside_q)


def k1_kernel(
    x_ref, u_ref, wq_ref, wk_ref, wv_ref, wo_ref, wg_ref, wu_ref, wd_ref, gres_ref, routes_ref, starts_ref,
    gain_a_ref, gain_f_ref, router_ref, proj_ref, mix_ref,
    attn_hbm, q_hbm, k_hbm, v_hbm, o_hbm, lse_s, hidden_ref, aux_ref, place_ref, ret_o, ret_d, wo_hbm, wq_hbm,
    grad_gate, grad_up, grad_down, far_gate, next_gate, near_gate, side_gate, far_up, side_up,
    attn_all, q_s, k_s, v_s, o_s, wo_full, wq_full,
    gate_full, up_full, down_full, wq_own, vt_s, attn_recv, nb, snd_r, snd_d, recv_r, recv_d, m_s, l_s, acc_s,
    acc, d_acc, st_gate, st_up, st_down,
    wq_ss, wq_rs, wo_ss, wo_rs, at_ss, at_rs, o_ss, o_rs, dr_ss, dr_rs, dd_ss, dd_rs, ro_ss, ro_rs, rd_ss, rd_rs,
    us, ur, ds, dr, xs, xr, vs, vr, wc_ss, wc_rs, loc, st_sem, fs, fr, keep_sem,
):
    me = Place()
    e, f, z, xf = me.e, me.f, me.z, me.xf
    T, D = x_ref.shape
    C = D // 4
    R = wo_ref.shape[0]
    FF = wg_ref.shape[1]
    W = FF // CHUNKS
    S = 4 * CAP
    for k in range(4):

        @pl.when(e == k)
        def _():
            for i, w in enumerate((wq_ref, wk_ref, wv_ref)):
                wq_own[:, i * C : (i + 1) * C] = w[:, k * C : (k + 1) * C]

    me.barrier()

    def half(core):
        return pl.ds(pl.multiple_of(core * (R // 2), 16), R // 2)

    def wq_slot(index):
        return wq_full.at[pl.ds(pl.multiple_of(index * R, 32), R)]

    def wo_slot(index):
        return wo_full.at[index, half(e % 2)]

    early = (
        (wq_own, wq_slot, wq_ss, wq_rs, 0),
        (wo_ref.at[half(e % 2)], wo_slot, wo_ss, wo_rs, 1),
    )
    for src, slot_of, ss, rs, li in early:
        for d in (1, 3, 2):
            me.send(src, slot_of(f), ss.at[d], rs.at[d], f=me.zf(d)).start()
        me.send(src, slot_of(f), ss.at[0], rs.at[0], f=xf).start()
        pltpu.make_async_copy(src, slot_of(f), loc.at[li]).start()

    xv = x_ref[...].astype(F32)
    inv = lax.rsqrt(jnp.mean(xv * xv, axis=-1, keepdims=True) + EPS)
    attn_all[e] = (xv * inv * gain_a_ref[...].reshape(1, D)).astype(BF)

    def at_copy(i, block, to=None):
        ref = attn_all.at[block]
        return me.send(ref, ref, at_ss.at[i], at_rs.at[i], e=to)

    at_copy(1, e, me.yp).start()
    at_copy(0, e, me.sib).start()

    def early_index(d, other):
        return ((z - d + 4) % 4) * 2 + (1 - me.x if other else me.x)

    def early_forward(src, slot_of, ss, rs, li):
        for d in (1, 3, 2):
            slot = slot_of(early_index(d, False))
            me.send(slot, slot, ss.at[d], rs.at[d]).wait_recv()
            me.send(slot, slot, ss.at[3 + d], rs.at[3 + d], f=xf).start()

    def early_wait(src, slot_of, ss, rs, li):
        pltpu.make_async_copy(src, slot_of(f), loc.at[li]).wait()
        me.send(slot_of(xf), slot_of(xf), ss.at[0], rs.at[0]).wait_recv()
        for d in (1, 2, 3):
            slot = slot_of(early_index(d, True))
            me.send(slot, slot, ss.at[3 + d], rs.at[3 + d]).wait_recv()

    def wo_copy(core, to=None):
        ref = wo_full.at[:, half(core)]
        return me.send(ref, ref, wc_ss.at[0], wc_rs.at[0], e=to)

    def cut(ref, c):
        return ref if c is None else ref.at[:, pl.ds(pl.multiple_of(c * W, W), W)]

    def up_copy(n, p, src, dst, to=None):
        return me.send(src, dst, us.at[n, p], ur.at[n, p], f=to)

    def down_copy(n, p, src, dst, to=None):
        return me.send(src, dst, ds.at[n, p], dr.at[n, p], f=to)

    def x_copy(n, i, src, dst, to=None):
        return me.send(src, dst, xs.at[n, i], xr.at[n, i], f=to)

    def relay(n, p, src, full, c):
        def at(slot):
            return cut(full.at[slot], c)

        if p == 0:
            own = cut(src, c)
            x_copy(n, 0, own, at(f), xf).start()

            @pl.when(z <= 2)
            def _():
                up_copy(n, 0, own, at(f), f + 2).start()

            @pl.when(z >= 1)
            def _():
                down_copy(n, 0, own, at(f), f - 2).start()

            return

        if p == 1 and c is None:
            x_copy(n, 0, at(xf), at(xf)).wait_recv()

            @pl.when(z <= 2)
            def _():
                side_copy(0, at(xf), at(xf), f + 2).start()

            @pl.when(z >= 1)
            def _():
                side_copy(1, at(xf), at(xf), f - 2).start()

        @pl.when(z >= p)
        def _():
            slot = at(f - 2 * p)
            up_copy(n, p - 1, slot, slot).wait_recv()
            if p <= 2:

                @pl.when(z <= 2)
                def _():
                    up_copy(n, p, slot, slot, f + 2).start()

            if p > 1 or c is not None:
                x_copy(n, p, slot, slot, xf).start()

        @pl.when(z + p <= 3)
        def _():
            slot = at(f + 2 * p)
            down_copy(n, p - 1, slot, slot).wait_recv()
            if p <= 2:

                @pl.when(z >= 1)
                def _():
                    down_copy(n, p, slot, slot, f - 2).start()

            if p > 1 or c is not None:
                x_copy(n, 3 + p, slot, slot, xf).start()

    def side_copy(i, src, dst, to=None):
        return me.send(src, dst, vs.at[i], vr.at[i], f=to)

    def relay_chunk(p, c):
        relay(1 + 2 * c, p, wg_ref, gate_full, c)
        relay(2 + 2 * c, p, wu_ref, up_full, c)

    def experts(p):
        relay(0, p, wd_ref, down_full, None)
        for c in range(CHUNKS):
            relay_chunk(p, c)

    own_loads = ((wd_ref, down_full), (wg_ref, gate_full), (wu_ref, up_full))

    def own_load(i):
        src, full = own_loads[i]
        return pltpu.make_async_copy(src, full.at[f], loc.at[2 + i])

    relay(0, 0, wd_ref, down_full, None)
    early_forward(*early[0])
    for c in range(CHUNKS):
        relay_chunk(0, c)
    for i in range(3):
        own_load(i).start()

    at_copy(1, me.yp).wait_recv()
    at_copy(2, me.yp, me.sib).start()
    at_copy(0, me.sib).wait_recv()
    early_wait(*early[0])
    early_forward(*early[1])
    at_copy(2, me.diag).wait_recv()

    kept = (
        (attn_all, attn_hbm), (wq_full, wq_hbm), (q_s, q_hbm), (k_s, k_hbm), (v_s, v_hbm), (wo_full, wo_hbm), (o_s, o_hbm),
    )

    def keep_copy(i):
        return pltpu.make_async_copy(kept[i][0], kept[i][1], keep_sem.at[i])

    keep_copy(0).start()
    keep_copy(1).start()

    def qkv_step(i, _):
        b = i // 2
        r = pl.ds(pl.multiple_of((i % 2) * 256, 256), 256)
        out = dot(attn_all[b, r, :], wq_full[...])
        q_s[b, r, :] = (out[:, 0:C] * QSCALE).astype(BF)
        k_s[b, r, :] = out[:, C : 2 * C].astype(BF)
        v = out[:, 2 * C : 3 * C]
        v_s[b, r, :] = v.astype(BF)
        vt_s[b, :, r] = v.T.astype(BF)
        return 0

    lax.fori_loop(0, 8, qkv_step, 0)
    for i in (2, 3, 4):
        keep_copy(i).start()

    head_of = lane_of((T, C)) // HD
    lse_s[...] = jnp.zeros_like(lse_s)

    def query_step(j, _):
        qb = me.far_first(j)
        queries = [jnp.where(head_of == h, q_s[qb], jnp.zeros((T, C), BF)) for h in range(3)]
        allowed = allowed_block(T, starts_ref[0, qb] - qb * T)
        for h in range(3):
            hr = pl.ds(h * HD, HD)
            s = jnp.where(allowed, dot(k_s[qb], queries[h], 1, 1), NEG)
            m = jnp.max(s, axis=0, keepdims=True)
            p = jnp.exp2(s - m)
            m_s[h : h + 1] = m
            l_s[h : h + 1] = jnp.sum(p, axis=0, keepdims=True)
            acc_s[hr] = dot(vt_s[qb, hr, :], p.astype(BF))

        def key_step(kb, _):
            for h in range(3):
                hr = pl.ds(h * HD, HD)
                query = jnp.where(head_of == h, q_s[qb], jnp.zeros((T, C), BF))
                s = dot(k_s[kb], query, 1, 1)
                m_old = m_s[h : h + 1]
                m = jnp.maximum(m_old, jnp.max(s, axis=0, keepdims=True))
                scale = jnp.exp2(m_old - m)
                p = jnp.exp2(s - m)
                m_s[h : h + 1] = m
                l_s[h : h + 1] = l_s[h : h + 1] * scale + jnp.sum(p, axis=0, keepdims=True)
                acc_s[hr] = acc_s[hr] * scale + dot(vt_s[kb, hr, :], p.astype(BF))
            return 0

        lax.fori_loop(0, qb, key_step, 0)
        for h in range(3):
            hr = pl.ds(h * HD, HD)
            total = l_s[h : h + 1]
            acc_s[hr] = acc_s[hr] / total
            lse_s[qb, h : h + 1, :] = m_s[h : h + 1] + jnp.log2(total)
        o_s[qb] = acc_s[...].T.astype(BF)
        return 0

    def o_copy(i, to=None):
        p = me.exp_peers[i]
        if to is None:
            return me.send(o_s.at[p], attn_recv.at[p], o_ss.at[i], o_rs.at[i])
        return me.send(o_s.at[p], attn_recv.at[e], o_ss.at[i], o_rs.at[i], e=p)

    lax.fori_loop(0, 2, query_step, 0)
    o_copy(1, True).start()
    o_copy(2, True).start()
    early_wait(*early[1])
    wo_copy(e % 2, me.sib).start()
    experts(1)
    lax.fori_loop(2, 4, query_step, 0)
    o_copy(0, True).start()
    attn_recv[e] = o_s[e]
    keep_copy(6).start()

    r0, r1 = routes_ref[0:1, :], routes_ref[1:2, :]
    expert = row_of((8, T))
    chosen = (expert == r0) | (expert == r1)
    earlier = (row_of((T, T)) < lane_of((T, T))).astype(BF)
    count = dot(chosen.astype(BF), earlier).astype(jnp.int32)
    count = jnp.where(chosen, count, -1)
    slot_id = row_of((CAP, T))
    for k in range(4):
        place_ref[k] = jnp.where(slot_id == count[k : k + 1, :], 1.0, 0.0).astype(BF)

    wo_copy(1 - e % 2).wait_recv()
    keep_copy(5).start()
    for i in (0, 1, 2):
        o_copy(i).wait_recv()

    def hidden_step(i, _):
        r = pl.ds(pl.multiple_of(i * 256, 256), 256)
        h = x_ref[r, :].astype(F32)
        for b in range(4):
            h = h + dot(attn_recv[b, r, :], wo_full[2 * b : 2 * b + 2].reshape(C, D))
        hidden_ref[r, :] = h
        n = h * lax.rsqrt(jnp.mean(h * h, axis=-1, keepdims=True) + EPS) * gain_f_ref[...].reshape(1, D)
        nb[r, :] = n.astype(BF)
        aux_ref[0:8, r] = dot(router_ref[...], n, 1, 1, HIGH) + dot(mix_ref[...], gres_ref[:, r], 0, 0, HIGH)
        aux_ref[8:12, r] = dot(proj_ref[...], n, 1, 1, HIGH)
        return 0

    relay(0, 2, wd_ref, down_full, None)
    lax.fori_loop(0, 2, hidden_step, 0)
    relay_chunk(2, 0)
    relay_chunk(2, 1)

    logits = aux_ref[0:8, :]
    top = jnp.max(jnp.where(chosen, logits, NEG), axis=0, keepdims=True)
    weight = jnp.where(chosen, jnp.exp(logits - top), 0.0)
    gates = weight / jnp.sum(weight, axis=0, keepdims=True)
    pairs = aux_ref[8:12, :]
    other = jnp.concatenate([pairs[1:2], pairs[0:1], pairs[3:4], pairs[2:3]], axis=0)
    aux_ref[0:8, :] = gates
    aux_ref[8:12, :] = 1.0 / (1.0 + jnp.exp(other - pairs))
    aux_ref[12:16, :] = jnp.zeros((4, T), F32)

    def d_copy(i, ref, out, ss, rs, k, to=None):
        return me.send(ref.at[k], out.at[e if to is not None else k], ss.at[i], rs.at[i], e=to)

    def dispatch_step(j, _):
        k = me.far_first(j)
        i = (j + 1) % 4
        place = place_ref[k]
        snd_r[k] = dot(place, nb[...]).astype(BF)
        gate = aux_ref[pl.ds(k, 1), :]
        gated = jnp.where(place > 0, gate.astype(BF), jnp.zeros((CAP, T), BF))
        snd_d[k] = dot(gated, u_ref[...]).astype(BF)

        @pl.when(j != 2)
        def _():
            d_copy(i, snd_r, recv_r, dr_ss, dr_rs, k, k).start()
            d_copy(i, snd_d, recv_d, dd_ss, dd_rs, k, k).start()

        @pl.when(j == 2)
        def _():
            recv_r[k] = snd_r[k]
            recv_d[k] = snd_d[k]

        return 0

    lax.fori_loop(0, 4, dispatch_step, 0)
    relay_chunk(2, 2)
    relay_chunk(2, 3)
    relay(0, 3, wd_ref, down_full, None)
    relay_chunk(3, 0)
    for i, p in enumerate(me.exp_peers):
        d_copy(i, snd_r, recv_r, dr_ss, dr_rs, p).wait()
        d_copy(i, snd_d, recv_d, dd_ss, dd_rs, p).wait()

    partner = z + 1 - 2 * (z % 2)
    far_row = 2 * ((partner + 2) % 4) + 1 - me.x
    next_row = 2 * ((z + 2) % 4) + 1 - me.x
    side_row = 2 * partner + 1 - me.x
    near_row = 2 * partner + me.x
    first = (
        (grad_gate, far_row, far_gate, xf),
        (grad_gate, side_row, side_gate, near_row),
        (grad_up, far_row, far_up, xf),
        (grad_up, side_row, side_up, near_row),
        (grad_gate, next_row, next_gate, xf),
        (grad_gate, near_row, near_gate, near_row),
    )

    def first_copy(i, c, to=None):
        src, row, dst, _ = first[i]
        return me.send(cut(src.at[row], c), cut(dst, c), fs.at[i, c], fr.at[i, c], f=to)

    def first_send(c):
        for i in range(6):
            first_copy(i, c, first[i][3]).start()

    acc[...] = jnp.zeros_like(acc)
    d_acc[...] = jnp.zeros_like(d_acc)

    def unit_wait(n, full, c):
        def at(slot):
            return cut(full.at[slot], c)

        if c is None:

            @pl.when(z >= 1)
            def _():
                side_copy(0, at(xf - 2), at(xf - 2)).wait_recv()

            @pl.when(z <= 2)
            def _():
                side_copy(1, at(xf + 2), at(xf + 2)).wait_recv()

        else:
            x_copy(n, 0, at(xf), at(xf)).wait_recv()
        for p in (2, 3) if c is None else (1, 2, 3):

            @pl.when(z >= p)
            def _():
                x_copy(n, p, at(xf - 2 * p), at(xf - 2 * p)).wait_recv()

            @pl.when(z + p <= 3)
            def _():
                x_copy(n, 3 + p, at(xf + 2 * p), at(xf + 2 * p)).wait_recv()

    stages = ((st_gate, grad_gate, 0), (st_up, grad_up, 1), (st_down, grad_down, 2))

    def stage_copy(c, i):
        st, out, _ = stages[i]
        if i == 2:
            dst = out.at[pl.ds(2 * c, 2)]
        else:
            dst = out.at[:, :, pl.ds(pl.multiple_of(c * W, W), W)]
        return pltpu.make_async_copy(st, dst, st_sem.at[i])

    def ret_copy(i, snd, ret, ss, rs, to=None):
        p = me.exp_peers[i]
        return me.send(snd.at[p], ret.at[e if to else p], ss.at[i], rs.at[i], e=p if to else None)

    def expert_step(c, _):
        @pl.when(c < CHUNKS - 1)
        def _():
            relay_chunk(3, c + 1)

        @pl.when(c == 0)
        def _():
            for i in range(3):
                own_load(i).wait()
            unit_wait(0, down_full, None)

        unit_wait(1 + 2 * c, gate_full, c)
        unit_wait(2 + 2 * c, up_full, c)
        w = pl.ds(pl.multiple_of(c * W, W), W)
        row_in = recv_r[...].reshape(S, D)
        d_in = recv_d[...].reshape(S, D)
        w_gate = gate_full[:, :, w].reshape(D, W)
        w_up = up_full[:, :, w].reshape(D, W)
        w_down = down_full[pl.ds(2 * c, 2)].reshape(W, D)
        g = dot(row_in, w_gate)
        up = dot(row_in, w_up)
        sig = 1.0 / (1.0 + jnp.exp(-g))
        silu = g * sig
        inner = (silu * up).astype(BF)
        acc[...] += dot(inner, w_down)

        @pl.when(c == CHUNKS - 1)
        def _():
            snd_r[...] = acc[...].astype(BF).reshape(4, CAP, D)
            for i in (1, 2, 0):
                ret_copy(i, snd_r, ret_o, ro_ss, ro_rs, True).start()
            ret_o[e] = snd_r[e]

        d_inner = dot(d_in, w_down, 1, 1)
        d_up = (d_inner * silu).astype(BF)
        d_gate = (d_inner * up * (sig + silu * (1.0 - sig))).astype(BF)
        d_acc[...] += dot(d_gate, w_gate, 1, 1) + dot(d_up, w_up, 1, 1)

        @pl.when(c == CHUNKS - 1)
        def _():
            snd_d[...] = d_acc[...].astype(BF).reshape(4, CAP, D)
            for i in (1, 2, 0):
                ret_copy(i, snd_d, ret_d, rd_ss, rd_rs, True).start()
            ret_d[e] = snd_d[e]

        @pl.when(c > 0)
        def _():
            for i in range(3):
                stage_copy(c - 1, i).wait()
            first_send(c - 1)

        st_down[...] = dot(inner, d_in, 0, 0).astype(BF).reshape(2, W // 2, D)
        st_gate[...] = dot(row_in, d_gate, 0, 0).astype(BF).reshape(8, R, W)
        st_up[...] = dot(row_in, d_up, 0, 0).astype(BF).reshape(8, R, W)
        for i in range(3):
            stage_copy(c, i).start()
        return 0

    lax.fori_loop(0, CHUNKS, expert_step, 0)
    for i in range(3):
        stage_copy(CHUNKS - 1, i).wait()
    first_send(CHUNKS - 1)

    for src, slot_of, ss, rs, li in early:
        for j in range(7):
            me.send(slot_of(f), slot_of(f), ss.at[j], rs.at[j]).wait_send()
    wo_copy(e % 2).wait_send()
    for i in range(3):
        at_copy(i, e).wait_send()
        o_copy(i).wait_send()
    def relay_end(n, full, c):
        slot = cut(full.at[f], c)
        x_copy(n, 0, slot, slot).wait_send()

        @pl.when(z <= 2)
        def _():
            up_copy(n, 0, slot, slot).wait_send()
            if c is None:
                side_copy(0, slot, slot).wait_send()

        @pl.when(z >= 1)
        def _():
            down_copy(n, 0, slot, slot).wait_send()
            if c is None:
                side_copy(1, slot, slot).wait_send()

        for p in (1, 2, 3):

            @pl.when(z >= p)
            def _():
                if p <= 2:

                    @pl.when(z <= 2)
                    def _():
                        up_copy(n, p, slot, slot).wait_send()

                if p > 1 or c is not None:
                    x_copy(n, p, slot, slot).wait_send()

            @pl.when(z + p <= 3)
            def _():
                if p <= 2:

                    @pl.when(z >= 1)
                    def _():
                        down_copy(n, p, slot, slot).wait_send()

                if p > 1 or c is not None:
                    x_copy(n, 3 + p, slot, slot).wait_send()

    relay_end(0, down_full, None)

    def end_step(c, _):
        relay_end(1 + 2 * c, gate_full, c)
        relay_end(2 + 2 * c, up_full, c)
        return 0

    lax.fori_loop(0, CHUNKS, end_step, 0)
    for i in range(3):
        ret_copy(i, snd_r, ret_o, ro_ss, ro_rs).wait()
        ret_copy(i, snd_d, ret_d, rd_ss, rd_rs).wait()

    def first_end(c, _):
        for i in range(6):
            first_copy(i, c).wait()
        return 0

    lax.fori_loop(0, CHUNKS, first_end, 0)
    for i in range(7):
        keep_copy(i).wait()


def sds(shape, dtype):
    return jax.ShapeDtypeStruct(shape, dtype)


def vmem():
    return pl.BlockSpec(memory_space=pltpu.VMEM)


def anyspace():
    return pl.BlockSpec(memory_space=pl.ANY)


def smem():
    return pl.BlockSpec(memory_space=pltpu.SMEM)


def call_k1(x, u, wq, wk, wv, wo, wg, wu, wd, gres, routes, starts, gain_a, gain_f, router, proj, mix):
    T, D = x.shape
    C, R, FF, S = D // 4, D // 8, wg.shape[1], 4 * CAP
    n = 1 + 2 * CHUNKS
    dma = pltpu.SemaphoreType.DMA
    VM = pltpu.VMEM
    block = VM((4, CAP, D), BF)
    return pl.pallas_call(
        k1_kernel,
        name="forward",
        out_shape=(
            sds((4, T, D), BF), sds((4, T, C), BF), sds((4, T, C), BF), sds((4, T, C), BF), sds((4, T, C), BF),
            sds((4, 8, T), F32), sds((T, D), F32), sds((16, T), F32), sds((4, CAP, T), BF),
            sds((4, CAP, D), BF), sds((4, CAP, D), BF), sds((8, R, D), BF), sds((D, 3 * C), BF),
            sds((8, R, FF), BF), sds((8, R, FF), BF), sds((8, FF // 8, D), BF),
            sds((R, FF), BF), sds((R, FF), BF), sds((R, FF), BF), sds((R, FF), BF), sds((R, FF), BF), sds((R, FF), BF),
        ),
        in_specs=[vmem()] * 5 + [anyspace()] * 4 + [vmem()] * 2 + [smem()] + [vmem()] * 5,
        out_specs=tuple([anyspace()] * 5 + [vmem()] * 6 + [anyspace()] * 11),
        scratch_shapes=[
            VM((4, T, D), BF), VM((4, T, C), BF), VM((4, T, C), BF), VM((4, T, C), BF), VM((4, T, C), BF), VM((8, R, D), BF), VM((D, 3 * C), BF),
            VM((8, R, FF), BF), VM((8, R, FF), BF), VM((8, FF // 8, D), BF), VM((R, 3 * C), BF), VM((4, C, T), BF),
            VM((4, T, C), BF), VM((T, D), BF), block, block, block, block, VM((8, T), F32), VM((8, T), F32), VM((C, T), F32),
            VM((S, D), F32), VM((S, D), F32), VM((8, R, FF // CHUNKS), BF), VM((8, R, FF // CHUNKS), BF), VM((2, FF // 8, D), BF),
            dma((7,)), dma((7,)), dma((7,)), dma((7,)),
        ] + [dma((3,))] * 12 + [
            dma((n, 3)), dma((n, 3)), dma((n, 3)), dma((n, 3)), dma((n, 7)), dma((n, 7)),
            dma((2,)), dma((2,)), dma((1,)), dma((1,)), dma((5,)), dma((3,)), dma((6, CHUNKS)), dma((6, CHUNKS)), dma((7,)),
        ],
        compiler_params=pltpu.CompilerParams(collective_id=0, has_side_effects=True, vmem_limit_bytes=60 << 20),
    )(x, u, wq, wk, wv, wo, wg, wu, wd, gres, routes, starts, gain_a, gain_f, router, proj, mix)


def k2_kernel(
    ret_o, ret_d, hidden, u_ref, x_ref, aux_ref, place_ref, gres_ref,
    attn_hbm, q_hbm, k_hbm, v_hbm, o_hbm, lse_s, wo_hbm, wqkv_hbm, gain_a_ref, gain_f_ref, router_ref, proj_ref, mix_ref, cvec_ref, starts_ref,
    g_gate, g_up, g_down, far_gate, next_gate, near_gate, side_gate, far_up, side_up,
    layer_out, grad_tokens, d_res, small_out, ag_out, go_b, eg_out, eu_out, ed_out,
    xin_g, xin_u, xin_d, own_g, own_u, own_d, zin_g, zin_u, zin_d, cross_g, cross_u, cross_d,
    attn_all, q_s, k_s, v_s, o_s, wo, wqkv,
    dh_all, da, kt_s, dq, dk, dv, dqt, pin, py_in, d_hidden, wk_s, del_r, gt, go_acc, ag_s, bx_in, bz_in, ag_fin, go_s, go_in,
    small, sm1, sm2,
    load_sem, late_sem, xs, xr, zs, zr, own_sem, dh_ss, dh_rs, fw_ss, fw_rs, go_ss, go_rs, gb_ss, gb_rs, pd_ss, pd_rs, bx_ss, bx_rs, bz_ss, bz_rs,
    ab_ss, ab_rs, s1_ss, s1_rs, s2_ss, s2_rs,
):
    me = Place()
    e, f, z, x, xf = me.e, me.f, me.z, me.x, me.xf
    T, D = x_ref.shape
    C = D // 4
    R = D // 8
    M = 128

    partner = z + 1 - 2 * (z % 2)
    targets = ((partner + 2) % 4, (z + 2) % 4, z, partner)
    parts = (
        (g_gate, xin_g, own_g, zin_g, cross_g, eg_out),
        (g_up, xin_u, own_u, zin_u, cross_u, eu_out),
        (g_down, xin_d, own_d, zin_d, cross_d, ed_out),
    )

    def load_copy(i):
        src, dst = (
            (far_gate, xin_g.at[0]), (far_up, xin_u.at[0]), (next_gate, xin_g.at[1]),
            (side_gate, cross_g), (side_up, cross_u), (near_gate, zin_g.at[2]),
        )[i]
        return pltpu.make_async_copy(src, dst, load_sem.at[i])

    def own_copy(w, i, column):
        return pltpu.make_async_copy(parts[w][0].at[2 * targets[i] + column], parts[w][2], own_sem.at[w])

    def x_copy(w, i):
        src = parts[w][4] if i == 2 and w < 2 else parts[w][0].at[2 * targets[i] + 1 - x]
        dst = parts[w][4] if i == 3 else parts[w][1].at[i]
        return me.send(src, dst, xs.at[w, i], xr.at[w, i], f=xf)

    def z_copy(w, i):
        if i == 2:
            src = parts[w][0].at[2 * partner + x] if w < 2 else parts[w][4]
        else:
            src = parts[w][1].at[i]
        to = targets[1] if i == 1 else partner
        return me.send(src, parts[w][3].at[i], zs.at[w, i], zr.at[w, i], f=2 * to + x)

    def add(dst, *terms):
        total = dst.astype(F32)
        for term in terms:
            total = total + term.astype(F32)
        return total.astype(BF)

    def rs_far(w):
        xin, own = parts[w][1:3]
        if w == 2:
            x_copy(w, 0).wait_recv()
        else:
            load_copy(w).wait()
        own_copy(w, 0, x).wait()
        xin[0] = add(xin[0], own[...])
        z_copy(w, 0).start()
        own_copy(w, 1, x).start()

    def rs_cross(w):
        xin, own, zin = parts[w][1:4]
        if w:
            x_copy(w, 1).wait_recv()
        else:
            load_copy(2).wait()
        own_copy(w, 1, x).wait()
        z_copy(w, 0).wait_recv()
        xin[1] = add(xin[1], own[...], zin[0])
        z_copy(w, 1).start()
        if w < 2:
            own_copy(w, 2, 1 - x).start()
        else:
            own_copy(w, 3, x).start()

    def rs_side(w):
        own, cross = parts[w][2], parts[w][4]
        if w < 2:
            load_copy(3 + w).wait()
            own_copy(w, 2, 1 - x).wait()
        else:
            x_copy(w, 3).wait_recv()
            own_copy(w, 3, x).wait()
        cross[...] = add(cross[...], own[...])
        if w:
            z_copy(w, 2).start()
        own_copy(w, 2, x).start()

    def rs_end(w):
        xin, own, zin = parts[w][1:4]
        x_copy(w, 2).wait_recv()
        own_copy(w, 2, x).wait()
        z_copy(w, 1).wait_recv()
        if w:
            z_copy(w, 2).wait_recv()
        else:
            load_copy(5).wait()
        parts[w][5][...] = add(xin[2], own[...], zin[1], zin[2])

    for i in range(6):
        load_copy(i).start()
    for w in range(3):
        own_copy(w, 0, x).start()
    late = ((attn_hbm, attn_all), (q_hbm, q_s), (k_hbm, k_s), (v_hbm, v_s), (o_hbm, o_s), (wo_hbm, wo), (wqkv_hbm, wqkv))

    def late_copy(i):
        return pltpu.make_async_copy(late[i][0], late[i][1], late_sem.at[i])

    for i in (5, 2, 4, 1, 3, 6, 0):
        late_copy(i).start()
    me.barrier()
    for w, i in ((2, 0), (1, 1), (2, 1)):
        x_copy(w, i).start()
    rs_far(0)
    rs_far(1)

    small[...] = jnp.zeros_like(small)
    cv0, cv1 = cvec_ref[0:1, :], cvec_ref[1:2, :]
    maps = jnp.concatenate([router_ref[...], proj_ref[...], jnp.zeros((4, D), F32)], axis=0).astype(BF)
    lane8 = lane_of((M, 8))
    lane4 = lane_of((M, 4))

    def dh_copy(i, c, block, to=None):
        ref = dh_all.at[block, pl.ds(pl.multiple_of(c * M, M), M)]
        return me.send(ref, ref, dh_ss.at[i, c], dh_rs.at[i, c], e=to)

    def mix_step(c, _):
        r = pl.ds(pl.multiple_of(c * M, M), M)
        h = hidden[r, :]
        u = u_ref[r, :].astype(F32)
        inv = lax.rsqrt(jnp.mean(h * h, axis=-1, keepdims=True) + EPS)
        hn = h * inv
        gain = gain_f_ref[...].reshape(1, D)
        n = hn * gain
        cols = aux_ref[:, r].T
        gates = cols[:, 0:8]
        a0, b0, a1, b1 = cols[:, 8:9], cols[:, 9:10], cols[:, 10:11], cols[:, 11:12]
        g5, g6, g7 = cols[:, 5:6], cols[:, 6:7], cols[:, 7:8]
        c_n = g5 + g6 * a0 + g7 * a1
        c0 = g6 * b0
        c1 = g7 * b1
        mixed = h + c_n * n + c0 * cv0 + c1 * cv1
        dg = jnp.zeros((M, 8), F32)
        dn = c_n * u
        for k in range(4):
            place = place_ref[k, :, r]
            rk = dot(place, ret_o[k], 0, 0)
            mixed = mixed + cols[:, k : k + 1] * rk
            dg = jnp.where(lane8 == k, jnp.sum(u * rk, axis=-1, keepdims=True), dg)
            dn = dn + dot(place, ret_d[k], 0, 0)
        layer_out[r, :] = mixed.astype(BF)
        un = jnp.sum(u * n, axis=-1, keepdims=True)
        uv0 = jnp.sum(u * cv0, axis=-1, keepdims=True)
        uv1 = jnp.sum(u * cv1, axis=-1, keepdims=True)
        dg = jnp.where(lane8 == 5, un, dg)
        dg = jnp.where(lane8 == 6, a0 * un + b0 * uv0, dg)
        dg = jnp.where(lane8 == 7, a1 * un + b1 * uv1, dg)
        dlog = gates * (dg - jnp.sum(gates * dg, axis=-1, keepdims=True))
        e0 = g6 * a0 * b0 * (un - uv0)
        e1 = g7 * a1 * b1 * (un - uv1)
        dpair = jnp.where(lane4 == 0, e0, jnp.where(lane4 == 1, -e0, jnp.where(lane4 == 2, e1, -e1)))
        dl = jnp.concatenate([dlog, dpair, c0, c1, jnp.zeros((M, 2), F32)], axis=1)
        low = dl.astype(BF)
        d_res[:, r] = dot(mix_ref[...], dlog, 1, 1, HIGH)
        dn = dn + dot(jnp.where(lane_of((M, 16)) < 12, low, jnp.zeros((M, 16), BF)), maps)
        by_n = dot(low, n.astype(BF), 0, 0)
        by_u = dot(low, u_ref[r, :], 0, 0)
        small[0:12, :] += by_n[0:12]
        small[12:14, :] += by_u[12:14]
        small[14:15, :] += jnp.sum(dn * hn, axis=0, keepdims=True)
        small[16:24, 0:8] += dot(gres_ref[:, r], dlog, 1, 0, HIGH)
        gd = dn * gain
        dh = u + inv * (gd - hn * jnp.mean(gd * hn, axis=-1, keepdims=True))
        d_hidden[r, :] = dh
        dh_all[e, r, :] = dh.astype(BF)
        dh_copy(1, c, e, me.yp).start()
        dh_copy(0, c, e, me.sib).start()
        return 0

    lax.fori_loop(0, T // M, mix_step, 0)
    rs_cross(0)
    for i in range(7):
        late_copy(i).wait()

    head_of = lane_of((T, C)) // HD
    heads = (row_of((8, C)) == lane_of((8, C)) // HD).astype(F32)
    wk_s[...] = wqkv[:, C : 2 * C]
    dk[...] = jnp.zeros_like(dk)
    dv[...] = jnp.zeros_like(dv)
    go_acc[...] = jnp.zeros_like(go_acc)
    for b in range(4):
        kt_s[b] = k_s[b].T

    def fw_copy(block, to=None):
        return me.send(dh_all.at[block], dh_all.at[block], fw_ss.at[0], fw_rs.at[0], e=to)

    def d_out_step(j, qb):
        @pl.when(j == 1)
        def _():
            for c in range(T // M):
                dh_copy(0, c, me.sib).wait_recv()

        @pl.when(j == 2)
        def _():
            for c in range(T // M):
                dh_copy(1, c, me.yp).wait_recv()
            fw_copy(me.yp, me.sib).start()

        @pl.when(j == 3)
        def _():
            fw_copy(me.diag).wait_recv()

        dhb = dh_all[qb]
        low = dot(dhb, wo[pl.ds(2 * e, 2)].reshape(C, D), 1, 1).astype(BF)
        da[qb] = low
        ob = o_s[qb]
        del_r[qb] = dot(heads, low.astype(F32) * ob.astype(F32), 1, 1, HIGH)
        go_acc[...] += dot(ob, dhb, 0, 0)

    def head_block(qb, h):
        hr = pl.ds(pl.multiple_of(h * HD, HD), HD)
        mine = head_of == h

        def block(kb, masked):
            zero = jnp.zeros((T, C), BF)
            query = jnp.where(mine, q_s[qb], zero)
            d_out = jnp.where(mine, da[qb], zero)
            p = jnp.exp2(dot(k_s[kb], query, 1, 1) - lse_s[qb, pl.ds(h, 1), :])
            if masked:
                p = jnp.where(allowed_block(T, starts_ref[0, qb] - qb * T), p, 0.0)
            dp = dot(v_s[kb], d_out, 1, 1)
            dsc = (p * (dp - del_r[qb, pl.ds(h, 1), :])).astype(BF)
            dv[kb] += dot(p.astype(BF), d_out)
            dk[kb] += dot(dsc, query)
            return dot(kt_s[kb, hr, :], dsc)

        dqt[...] = block(qb, True)

        def key_step(kb, _):
            dqt[...] += block(kb, False)
            return 0

        lax.fori_loop(0, qb, key_step, 0)
        dq[qb, hr, :] = (dqt[...] * (1.0 / math.sqrt(HD))).astype(BF)

    def near_step(i, _):
        j = i // 3
        qb = me.near_first(j)

        @pl.when(i % 3 == 0)
        def _():
            d_out_step(j, qb)

        head_block(qb, i % 3)
        return 0

    def far_pass(h):
        def far_step(j, _):
            qb = me.near_first(j)
            if h == 0:
                d_out_step(j, qb)
            head_block(qb, h)
            return 0

        lax.fori_loop(2, 4, far_step, 0)

    def bx_copy(h, to=None):
        return me.send(ag_s.at[1 - x, h], bx_in.at[h], bx_ss.at[h], bx_rs.at[h], f=to)

    def bz_copy(h, d, to=None):
        return me.send(bx_in.at[h, (z + d) % 4], bz_in.at[h, d - 1], bz_ss.at[h, d - 1], bz_rs.at[h, d - 1], f=to)

    def ab_copy(h, i, to=None):
        return me.send(ag_fin.at[h], ag_out.at[e if to is not None else me.exp_peers[i], h], ab_ss.at[h, i], ab_rs.at[h, i], e=to)

    def weight_grads(h):
        cols = slice(h * HD, (h + 1) * HD)
        gt[...] = jnp.zeros_like(gt)

        def grad_step(b, _):
            low_k = (dk[b, :, cols] * LN2).T.astype(BF)
            low_v = dv[b, :, cols].T.astype(BF)
            gt[...] += dot(jnp.concatenate([dq[b, cols, :], low_k, low_v], axis=0), attn_all[b])
            return 0

        lax.fori_loop(0, 4, grad_step, 0)
        grads = gt[...].T.astype(BF).reshape(8, R, C)
        for k in range(8):
            ag_s[k % 2, h, k // 2] = grads[k]
        bx_copy(h, xf).start()

    def weight_rows(h):
        bx_copy(h).wait_recv()
        bx_in[h] = add(bx_in[h], ag_s[x, h])
        for d in (2, 1, 3):
            bz_copy(h, d, me.zf(d)).start()

    def weight_sum(h):
        total = bx_in[h, z].astype(F32)
        for d in (1, 2, 3):
            bz_copy(h, d).wait_recv()
            total = total + bz_in[h, d - 1].astype(F32)
        ag_fin[h] = total.astype(BF)
        for i, p in enumerate(me.exp_peers):
            ab_copy(h, i, p).start()
        ag_out[e, h] = ag_fin[h]

    lax.fori_loop(0, 6, near_step, 0)
    rs_far(2)
    rs_cross(1)
    far_pass(0)

    go_s[0] = go_acc[0:R, :].astype(BF)
    go_s[1] = go_acc[R : 2 * R, :].astype(BF)
    for j in range(2):

        @pl.when(f != 2 * e + j)
        def _():
            me.send(go_s.at[j], go_in.at[f], go_ss.at[j], go_rs.at[f], f=2 * e + j).start()

    weight_grads(0)
    x_copy(2, 3).start()
    far_pass(1)
    weight_grads(1)
    x_copy(2, 2).start()
    weight_rows(0)
    rs_cross(2)
    rs_side(0)
    rs_side(1)
    far_pass(2)

    for c in range(T // M):
        dh_copy(0, c, e).wait_send()
        dh_copy(1, c, e).wait_send()
    fw_copy(e).wait_send()

    def share_step(j, _):
        b = me.share_order(j)
        out = dot(dq[b], wqkv[:, 0:C], 0, 1)
        out = out + dot((dk[b] * LN2).astype(BF), wk_s[...], 1, 1)
        out = out + dot(dv[b].astype(BF), wqkv[:, 2 * C : 3 * C], 1, 1)
        small[15:16, :] += jnp.sum(out * attn_all[b].astype(F32), axis=0, keepdims=True)
        dh_all[b] = out.astype(BF)
        return 0

    def pd_copy(i, src, dst, to=None):
        return me.send(src, dst, pd_ss.at[i], pd_rs.at[i], e=to)

    lax.fori_loop(0, 1, share_step, 0)
    pd_copy(1, dh_all.at[me.diag], pin.at[1], me.sib).start()
    lax.fori_loop(1, 2, share_step, 0)
    pd_copy(1, pin.at[1], pin.at[1]).wait_recv()
    dh_all[me.yp] = add(dh_all[me.yp], pin[1])
    pd_copy(2, dh_all.at[me.yp], py_in, me.yp).start()
    weight_grads(2)
    x_copy(0, 2).start()
    x_copy(1, 2).start()
    lax.fori_loop(2, 3, share_step, 0)
    pd_copy(0, dh_all.at[me.sib], pin.at[0], me.sib).start()
    lax.fori_loop(3, 4, share_step, 0)

    small[15:16, :] = small[15:16, :] / gain_a_ref[...].reshape(1, D)
    sm1[e] = small[...].astype(BF)
    for i, p in enumerate(me.exp_peers):
        me.send(sm1.at[e], sm1.at[e], s1_ss.at[i], s1_rs.at[i], e=p).start()
    weight_rows(1)
    rs_side(2)
    weight_sum(0)
    weight_rows(2)
    for i, p in enumerate(me.exp_peers):
        me.send(sm1.at[p], sm1.at[p], s1_ss.at[i], s1_rs.at[i]).wait()
    sm2[f] = add(sm1[0], sm1[1], sm1[2], sm1[3])
    for r in range(1, 8):
        me.send(sm2.at[f], sm2.at[f], s2_ss.at[r - 1], s2_rs.at[f], f=me.fp(r)).start()

    @pl.when(z == e)
    def _():
        total = go_s[x].astype(F32)
        for r in range(1, 8):
            s = go_in.at[me.fp(r)]
            me.send(s, s, go_ss.at[0], go_rs.at[me.fp(r)]).wait_recv()
            total = total + go_in[me.fp(r)].astype(F32)
        go_b[...] = total.astype(BF)
        for i, p in enumerate(me.exp_peers):
            me.send(go_b, go_b, gb_ss.at[i], gb_rs.at[0], e=p).start()

    weight_sum(1)
    weight_sum(2)
    for r in range(1, 8):
        s = sm2.at[me.fp(r)]
        me.send(s, s, s2_ss.at[r - 1], s2_rs.at[me.fp(r)]).wait_recv()
    total = sm2[0].astype(F32)
    for r in range(1, 8):
        total = total + sm2[r].astype(F32)
    small_out[...] = total

    pd_copy(0, pin.at[0], pin.at[0]).wait_recv()
    pd_copy(2, py_in, py_in).wait_recv()

    def token_step(i, _):
        r = pl.ds(pl.multiple_of(i * 256, 256), 256)
        d = dh_all[e, r, :].astype(F32) + pin[0, r, :].astype(F32) + py_in[r, :].astype(F32)
        xv = x_ref[r, :].astype(F32)
        inv = lax.rsqrt(jnp.mean(xv * xv, axis=-1, keepdims=True) + EPS)
        xn = xv * inv
        gd = d * gain_a_ref[...].reshape(1, D)
        grad_tokens[r, :] = (d_hidden[r, :] + inv * (gd - xn * jnp.mean(gd * xn, axis=-1, keepdims=True))).astype(BF)
        return 0

    lax.fori_loop(0, 2, token_step, 0)
    for w in range(3):
        rs_end(w)

    @pl.when(z != e)
    def _():
        me.send(go_b, go_b, gb_ss.at[0], gb_rs.at[0]).wait_recv()

    for w in range(3):
        for i in range(3):
            if (w, i) not in ((0, 0), (0, 1), (1, 0)):
                x_copy(w, i).wait_send()
            if (w, i) != (0, 2):
                z_copy(w, i).wait_send()
    x_copy(2, 3).wait_send()
    for j in range(2):

        @pl.when(f != 2 * e + j)
        def _():
            me.send(go_s.at[j], go_in.at[f], go_ss.at[j], go_rs.at[f]).wait_send()

    @pl.when(z == e)
    def _():
        for i in range(3):
            me.send(go_b, go_b, gb_ss.at[i], gb_rs.at[0]).wait_send()

    for i in range(3):
        pd_copy(i, py_in, py_in).wait_send()
        for h in range(3):
            ab_copy(h, i).wait()
    for h in range(3):
        bx_copy(h).wait_send()
        for d in (1, 2, 3):
            bz_copy(h, d).wait_send()
    for r in range(1, 8):
        me.send(sm2.at[f], sm2.at[f], s2_ss.at[r - 1], s2_rs.at[f]).wait_send()


def call_k2(*args):
    x, (gg, gu, gd) = args[4], args[23:26]
    late = args[8:13] + args[14:16]
    T, D = x.shape
    C, R = D // 4, D // 8
    dma = pltpu.SemaphoreType.DMA
    VM = pltpu.VMEM
    shapes = (gg.shape[1:], gu.shape[1:], gd.shape[1:])
    return pl.pallas_call(
        k2_kernel,
        name="backward",
        out_shape=(
            sds((T, D), BF), sds((T, D), BF), sds((8, T), F32), sds((24, D), F32),
            sds((4, 3, R, C), BF), sds((R, D), BF),
        ) + tuple(sds(s, BF) for s in shapes),
        in_specs=[vmem()] * 8 + [anyspace()] * 5 + [vmem()] + [anyspace()] * 2 + [vmem()] * 6 + [smem()] + [anyspace()] * 9,
        out_specs=tuple([vmem()] * 9),
        scratch_shapes=[VM((3,) + s, BF) for s in shapes] + [VM(s, BF) for s in shapes] + [VM((3,) + s, BF) for s in shapes] + [VM(s, BF) for s in shapes] + [VM(a.shape, BF) for a in late] + [
            VM((4, T, D), BF), VM((4, T, C), BF), VM((4, C, T), BF), VM((4, C, T), BF), VM((4, T, C), F32), VM((4, T, C), F32),
            VM((HD, T), F32), VM((2, T, D), BF), VM((T, D), BF), VM((T, D), F32), VM((D, C), BF), VM((4, 8, T), F32), VM((C, D), F32), VM((C, D), F32),
            VM((2, 3, 4, R, C), BF), VM((3, 4, R, C), BF), VM((3, 3, R, C), BF), VM((3, R, C), BF), VM((2, R, D), BF), VM((8, R, D), BF),
            VM((24, D), F32), VM((4, 24, D), BF), VM((8, 24, D), BF),
            dma((6,)), dma((7,)), dma((3, 4)), dma((3, 4)), dma((3, 3)), dma((3, 3)), dma((3,)),
            dma((2, 4)), dma((2, 4)), dma((1,)), dma((1,)), dma((2,)), dma((8,)), dma((3,)), dma((1,)), dma((3,)), dma((3,)),
            dma((3,)), dma((3,)), dma((3, 3)), dma((3, 3)), dma((3, 3)), dma((3, 3)), dma((3,)), dma((3,)), dma((7,)), dma((8,)),
        ],
        compiler_params=pltpu.CompilerParams(collective_id=1, has_side_effects=True, vmem_limit_bytes=63 << 20),
    )(*args)


def k3_kernel(
    layer_in, tokens_in, res_in, small, ag, go, eg, eu, ed,
    layer_out, tokens_out, res_out, norm_a, norm_f, g_q, g_k, g_v, g_o, router, mixing, proj, cvec, o_gate, o_up, o_down,
):
    layer_out[...] = layer_in[...]
    tokens_out[...] = tokens_in[...]
    res_out[...] = res_in[...]
    norm_a[...] = small[15, :]
    norm_f[...] = small[14, :]
    for i, out in enumerate((g_q, g_k, g_v)):
        out[...] = jnp.concatenate(
            [ag[b, h, :, i * HD : (i + 1) * HD].astype(F32) for b in range(4) for h in range(3)], axis=1
        )
    g_o[...] = go[...].astype(F32)
    router[...] = small[0:8, :]
    mixing[...] = small[16:24, 0:8]
    proj[...] = small[8:12, :]
    cvec[...] = small[12:14, :]
    o_gate[...] = eg[...].astype(F32)
    o_up[...] = eu[...].astype(F32)
    o_down[...] = ed[...].astype(F32)


def call_k3(*args):
    T, D = args[0].shape
    R = D // 8
    return pl.pallas_call(
        k3_kernel,
        name="finish",
        out_shape=(
            sds((T, D), BF), sds((T, D), BF), sds((8, T), F32), sds((D,), F32), sds((D,), F32),
            sds((R, D), F32), sds((R, D), F32), sds((R, D), F32), sds((R, D), F32),
            sds((8, D), F32), sds((8, 8), F32), sds((4, D), F32), sds((2, D), F32),
        ) + tuple(sds(a.shape, F32) for a in args[6:9]),
        in_specs=[vmem()] * 9,
        out_specs=tuple([vmem()] * 16),
    )(*args)


def body_fast(
    tokens, gate_res, routes, piece_starts, norm_attn, norm_ffn, w_query, w_key, w_value, w_out, router, mixing,
    const_proj, const_vec, w_gate, w_up, w_down, cotangent,
):
    x, u = tokens[0], cotangent[0]
    gres, route_ids = gate_res[0].T, routes[0].T
    (attn_all, q, k, v, o, lse, hidden, aux, place, ret_o, ret_d, wo, wq, gg, gu, gd, fg, ng, eg1, sg, fu, su) = call_k1(
        x, u, w_query, w_key, w_value, w_out, w_gate[0], w_up[0], w_down[0], gres, route_ids, piece_starts,
        norm_attn, norm_ffn, router.T, const_proj.T, mixing,
    )
    outs = call_k2(
        ret_o, ret_d, hidden, u, x, aux, place, gres, attn_all, q, k, v, o, lse, wo, wq,
        norm_attn, norm_ffn, router.T, const_proj.T, mixing, const_vec, piece_starts, gg, gu, gd, fg, ng, eg1, sg, fu, su,
    )
    (layer_out, grad_tokens, d_res, norm_a, norm_f, g_q, g_k, g_v, g_o, g_router, g_mixing, g_proj, g_cvec, eg, eu, ed) = call_k3(*outs)
    return (
        layer_out[None], grad_tokens[None], d_res.T[None], norm_a, norm_f, g_q, g_k, g_v, g_o,
        g_router.T, g_mixing, g_proj.T, g_cvec, eg[None], eu[None], ed[None],
    )


def solution(mesh):
    placed = (
        P("fsdp", "exp", None),
        P("fsdp", "exp", None),
        P("fsdp", "exp", None),
        P("fsdp", None),
        P(),
        P(),
        P("fsdp", None),
        P("fsdp", None),
        P("fsdp", None),
        P("fsdp", None),
        P(),
        P(),
        P(),
        P(),
        P("exp", "fsdp", None),
        P("exp", "fsdp", None),
        P("exp", "fsdp", None),
        P("fsdp", "exp", None),
    )
    return jax.shard_map(
        body_fast if (mesh.shape['exp'], mesh.shape['fsdp']) == (4, 8) else body,
        mesh=mesh,
        in_specs=placed,
        out_specs=(
            P("fsdp", "exp", None),
            P("fsdp", "exp", None),
            P("fsdp", "exp", None),
            P(),
            P(),
            P("fsdp", None),
            P("fsdp", None),
            P("fsdp", None),
            P("fsdp", None),
            P(),
            P(),
            P(),
            P(),
            P("exp", "fsdp", None),
            P("exp", "fsdp", None),
            P("exp", "fsdp", None),
        ),
        check_vma=False,
    )
```

```python
import math

import jax
import jax.numpy as jnp
from jax import lax
from jax.experimental import pallas as pl
from jax.experimental.pallas import tpu as pltpu
from jax.sharding import PartitionSpec as P

H = 12
HD = 64
PIECE = 256
KBLK = 512
CAP = 160


EPS = 1e-05
HIGH = lax.Precision.HIGHEST
NEG = -1e30


def rms_scale(values, gain_vec):
    inverse = lax.rsqrt(jnp.mean(values * values, axis=-1, keepdims=True) + EPS)
    return values * inverse * gain_vec


def piece_ids(positions, starts, extent):
    inside = (positions[:, None] >= starts[None, :]) & (
        positions[:, None] < starts[None, :] + extent
    )
    labels = jnp.arange(1, starts.shape[0] + 1, dtype=jnp.int32)
    return jnp.sum(jnp.where(inside, labels[None, :], 0), axis=1)


def reach_bounds(positions, starts, extent):
    inside = (positions[:, None] >= starts[None, :]) & (
        positions[:, None] < starts[None, :] + extent
    )
    piece_last = jnp.max(jnp.where(inside, starts[None, :] + extent - 1, 0))
    piece_first = jnp.min(jnp.where(inside, starts[None, :], positions[0]))
    upper = jnp.maximum(positions[-1], piece_last)
    lower = jnp.minimum(positions[0], piece_first)
    return (upper, lower)


def allowed_mask(query_pos, query_ids, key_pos, key_ids):
    causal = key_pos[None, :] <= query_pos[:, None]
    shared = (key_ids[None, :] == query_ids[:, None]) & (query_ids[:, None] > 0)
    return causal | shared


def slot_dest(route_ids, n_ffn, capacity):
    flat_ids = route_ids.reshape(-1)
    onehot = (flat_ids[:, None] == jnp.arange(n_ffn, dtype=jnp.int32)[None, :]).astype(jnp.int32)
    earlier = jnp.cumsum(onehot, axis=0) - onehot
    slot_pos = jnp.sum(earlier * onehot, axis=1)
    return jnp.where(flat_ids < n_ffn, flat_ids * capacity + slot_pos, n_ffn * capacity)


def local_mix(
    normed, res_logits, router, mixing, const_proj, const_vec, expert_rows, route_ids, n_ffn
):
    n_all = router.shape[1]
    logits = jnp.dot(normed, router, precision=HIGH) + jnp.dot(res_logits, mixing, precision=HIGH)
    probs = jax.nn.softmax(logits, axis=-1)
    labels = jnp.arange(n_all, dtype=jnp.int32)
    chosen = jnp.sum(
        jnp.where(route_ids[:, :, None] == labels[None, None, :], probs[:, None, :], 0.0), axis=-1
    )
    gates = chosen / jnp.sum(chosen, axis=1, keepdims=True)
    pair_logits = jnp.dot(normed, const_proj, precision=HIGH)
    first_pair = jax.nn.softmax(pair_logits[:, 0:2], axis=-1)
    second_pair = jax.nn.softmax(pair_logits[:, 2:4], axis=-1)
    first_const = first_pair[:, 0:1] * normed + first_pair[:, 1:2] * const_vec[0][None, :]
    second_const = second_pair[:, 0:1] * normed + second_pair[:, 1:2] * const_vec[1][None, :]
    mixed = jnp.zeros_like(normed)
    for route_k in range(2):
        route_id = route_ids[:, route_k : route_k + 1]
        entry = jnp.where(route_id < n_ffn, expert_rows[:, route_k], 0.0)
        entry = entry + jnp.where(route_id == n_ffn + 1, normed, 0.0)
        entry = entry + jnp.where(route_id == n_ffn + 2, first_const, 0.0)
        entry = entry + jnp.where(route_id == n_ffn + 3, second_const, 0.0)
        mixed = mixed + gates[:, route_k : route_k + 1] * entry
    return mixed


def swiglu_act(gate_pre, up_pre):
    return jax.nn.silu(gate_pre) * up_pre


def body(
    tokens,
    gate_res,
    routes,
    piece_starts,
    norm_attn,
    norm_ffn,
    w_query,
    w_key,
    w_value,
    w_out,
    router,
    mixing,
    const_proj,
    const_vec,
    w_gate,
    w_up,
    w_down,
    cotangent,
):
    n_ffn = lax.axis_size("exp")
    rows_dev = tokens.shape[1]
    model_width = tokens.shape[2]
    seq_length = rows_dev * n_ffn
    score_scale = 1.0 / math.sqrt(HD)
    inputs_f = tokens[0].astype(jnp.float32)
    res_logits = gate_res[0]
    route_ids = routes[0]
    starts = piece_starts[0]
    full_query, full_key, full_value, full_out = (
        lax.all_gather(w_query, "fsdp", axis=0, tiled=True),
        lax.all_gather(w_key, "fsdp", axis=0, tiled=True),
        lax.all_gather(w_value, "fsdp", axis=0, tiled=True),
        lax.all_gather(w_out, "fsdp", axis=0, tiled=True),
    )
    attn_in = rms_scale(inputs_f, norm_attn).astype(jnp.bfloat16)
    query = jnp.dot(attn_in, full_query, preferred_element_type=jnp.float32).astype(jnp.bfloat16)
    key = jnp.dot(attn_in, full_key, preferred_element_type=jnp.float32).astype(jnp.bfloat16)
    value = jnp.dot(attn_in, full_value, preferred_element_type=jnp.float32).astype(jnp.bfloat16)
    keys_all, values_all = (
        lax.all_gather(key, "exp", axis=0, tiled=True),
        lax.all_gather(value, "exp", axis=0, tiled=True),
    )
    query_heads = query.reshape(rows_dev, H, HD)
    key_heads = keys_all.reshape(seq_length, H, HD)
    value_heads = values_all.reshape(seq_length, H, HD)
    query_pos = lax.axis_index("exp") * rows_dev + jnp.arange(rows_dev, dtype=jnp.int32)
    query_ids = piece_ids(query_pos, starts, PIECE)
    key_upper, query_lower = reach_bounds(query_pos, starts, PIECE)
    block_list = jnp.arange(seq_length // KBLK, dtype=jnp.int32)

    def score_block(block_index):
        key_first = block_index * KBLK
        key_block = lax.dynamic_slice_in_dim(key_heads, key_first, KBLK, 0)
        value_block = lax.dynamic_slice_in_dim(value_heads, key_first, KBLK, 0)
        key_pos = key_first + jnp.arange(KBLK, dtype=jnp.int32)
        key_ids = piece_ids(key_pos, starts, PIECE)
        scores = (
            jnp.einsum("qhd,khd->hqk", query_heads, key_block, preferred_element_type=jnp.float32)
            * score_scale
        )
        allowed = allowed_mask(query_pos, query_ids, key_pos, key_ids)[None]
        return (scores, allowed, key_block, value_block)

    def needed(block_index):
        return block_index * KBLK <= key_upper

    def lse_step(carry, block_index):

        def lse_active(state):
            run_max, run_sum = state
            scores, allowed, _, _ = score_block(block_index)
            scores = jnp.where(allowed, scores, NEG)
            new_max = jnp.maximum(run_max, jnp.max(scores, axis=-1))
            exp_terms = jnp.where(allowed, jnp.exp(scores - new_max[..., None]), 0.0)
            return (new_max, run_sum * jnp.exp(run_max - new_max) + jnp.sum(exp_terms, axis=-1))

        return (lax.cond(needed(block_index), lse_active, lambda state: state, carry), None)

    start_carry = (jnp.full((H, rows_dev), NEG, jnp.float32), jnp.zeros((H, rows_dev), jnp.float32))
    (run_max, run_sum), _ = lax.scan(lse_step, start_carry, block_list)
    log_norm = run_max + jnp.log(run_sum)

    def block_probs(scores, allowed):
        return jnp.where(allowed, jnp.exp(scores - log_norm[..., None]), 0.0)

    def out_step(accum, block_index):

        def out_active(total):
            scores, allowed, _, value_block = score_block(block_index)
            probs_low = block_probs(scores, allowed).astype(jnp.bfloat16)
            return total + jnp.einsum(
                "hqk,khd->qhd", probs_low, value_block, preferred_element_type=jnp.float32
            )

        return (lax.cond(needed(block_index), out_active, lambda total: total, accum), None)

    attn_sum, _ = lax.scan(out_step, jnp.zeros((rows_dev, H, HD), jnp.float32), block_list)
    attn_low = attn_sum.astype(jnp.bfloat16).reshape(rows_dev, model_width)
    hidden = inputs_f + jnp.dot(attn_low, full_out, preferred_element_type=jnp.float32)
    normed = rms_scale(hidden, norm_ffn)
    destination = slot_dest(route_ids, n_ffn, CAP)
    sources = jnp.arange(2 * rows_dev, dtype=jnp.int32) // 2
    slot_table = (
        jnp.full((n_ffn * CAP,), rows_dev, jnp.int32).at[destination].set(sources, mode="drop")
    )
    padded = jnp.concatenate(
        [normed.astype(jnp.bfloat16), jnp.zeros((1, model_width), jnp.bfloat16)], axis=0
    )
    dispatched = padded[slot_table].reshape(n_ffn, CAP, model_width)
    received = lax.all_to_all(dispatched, "exp", split_axis=0, concat_axis=0, tiled=True)
    full_gate, full_up, full_down = (
        lax.all_gather(w_gate[0], "fsdp", axis=0, tiled=True),
        lax.all_gather(w_up[0], "fsdp", axis=0, tiled=True),
        lax.all_gather(w_down[0], "fsdp", axis=0, tiled=True),
    )
    slot_rows = received.reshape(n_ffn * CAP, model_width)
    gate_pre = jnp.dot(slot_rows, full_gate, preferred_element_type=jnp.float32)
    up_pre = jnp.dot(slot_rows, full_up, preferred_element_type=jnp.float32)
    inner_act = swiglu_act(gate_pre, up_pre).astype(jnp.bfloat16)
    expert_result = jnp.dot(inner_act, full_down, preferred_element_type=jnp.float32).astype(
        jnp.bfloat16
    )
    returned = lax.all_to_all(
        expert_result.reshape(n_ffn, CAP, model_width),
        "exp",
        split_axis=0,
        concat_axis=0,
        tiled=True,
    )
    returned_pad = jnp.concatenate(
        [returned.reshape(n_ffn * CAP, model_width), jnp.zeros((1, model_width), jnp.bfloat16)],
        axis=0,
    )
    expert_rows = returned_pad[destination].astype(jnp.float32).reshape(rows_dev, 2, model_width)

    def mix_local(normed_in, logits_in, router_in, mixing_in, proj_in, vec_in, rows_in):
        return local_mix(
            normed_in, logits_in, router_in, mixing_in, proj_in, vec_in, rows_in, route_ids, n_ffn
        )

    moe_out, mix_pull = jax.vjp(
        mix_local, normed, res_logits, router, mixing, const_proj, const_vec, expert_rows
    )
    layer_out = (hidden + moe_out).astype(jnp.bfloat16)
    upstream = cotangent[0].astype(jnp.float32)
    d_normed_local, d_res_logits, d_router, d_mixing, d_const_proj, d_const_vec, d_expert_rows = (
        mix_pull(upstream)
    )
    d_rows_low = d_expert_rows.reshape(2 * rows_dev, model_width).astype(jnp.bfloat16)
    d_dispatched = (
        jnp.zeros((n_ffn * CAP, model_width), jnp.bfloat16)
        .at[destination]
        .set(d_rows_low, mode="drop")
    )
    d_received = lax.all_to_all(
        d_dispatched.reshape(n_ffn, CAP, model_width),
        "exp",
        split_axis=0,
        concat_axis=0,
        tiled=True,
    )
    d_received = d_received.reshape(n_ffn * CAP, model_width)
    d_inner = jnp.einsum("rd,fd->rf", d_received, full_down, preferred_element_type=jnp.float32)
    _, act_pull = jax.vjp(swiglu_act, gate_pre, up_pre)
    d_gate_pre, d_up_pre = act_pull(d_inner)
    d_gate_low = d_gate_pre.astype(jnp.bfloat16)
    d_up_low = d_up_pre.astype(jnp.bfloat16)
    grad_down_full = jnp.einsum(
        "rf,rd->fd", inner_act, d_received, preferred_element_type=jnp.float32
    )
    grad_gate_full = jnp.einsum(
        "rd,rf->df", slot_rows, d_gate_low, preferred_element_type=jnp.float32
    )
    grad_up_full = jnp.einsum("rd,rf->df", slot_rows, d_up_low, preferred_element_type=jnp.float32)
    d_slot_rows = (
        jnp.einsum("rf,df->rd", d_gate_low, full_gate, preferred_element_type=jnp.float32)
        + jnp.einsum("rf,df->rd", d_up_low, full_up, preferred_element_type=jnp.float32)
    ).astype(jnp.bfloat16)
    d_sent = lax.all_to_all(
        d_slot_rows.reshape(n_ffn, CAP, model_width), "exp", split_axis=0, concat_axis=0, tiled=True
    )
    d_sent_pad = jnp.concatenate(
        [d_sent.reshape(n_ffn * CAP, model_width), jnp.zeros((1, model_width), jnp.bfloat16)],
        axis=0,
    )
    d_normed_sent = jnp.sum(
        d_sent_pad[destination].astype(jnp.float32).reshape(rows_dev, 2, model_width), axis=1
    )
    _, norm_ffn_pull = jax.vjp(rms_scale, hidden, norm_ffn)
    d_hidden_part, d_norm_ffn = norm_ffn_pull(d_normed_local + d_normed_sent)
    d_hidden = upstream + d_hidden_part
    d_hidden_low = d_hidden.astype(jnp.bfloat16)
    grad_out_full = jnp.einsum(
        "td,te->de", attn_low, d_hidden_low, preferred_element_type=jnp.float32
    )
    d_attn = jnp.einsum(
        "te,de->td", d_hidden_low, full_out, preferred_element_type=jnp.float32
    ).astype(jnp.bfloat16)
    d_attn_heads = d_attn.reshape(rows_dev, H, HD)
    zero_block = jnp.zeros((KBLK, H, HD), jnp.float32)

    def delta_terms(block_index):
        scores, allowed, _, value_block = score_block(block_index)
        probs = block_probs(scores, allowed)
        d_probs = jnp.einsum(
            "qhd,khd->hqk", d_attn_heads, value_block, preferred_element_type=jnp.float32
        )
        part = jnp.sum(probs * d_probs, axis=-1)
        return (
            part,
            jnp.einsum(
                "hqk,qhd->khd",
                probs.astype(jnp.bfloat16),
                d_attn_heads,
                preferred_element_type=jnp.float32,
            ),
        )

    def query_terms(block_index, row_delta):
        scores, allowed, key_block, value_block = score_block(block_index)
        probs = block_probs(scores, allowed)
        d_probs = jnp.einsum(
            "qhd,khd->hqk", d_attn_heads, value_block, preferred_element_type=jnp.float32
        )
        d_scores = (probs * (d_probs - row_delta[..., None])).astype(jnp.bfloat16)
        part = (
            jnp.einsum("hqk,khd->qhd", d_scores, key_block, preferred_element_type=jnp.float32)
            * score_scale
        )
        return (
            part,
            jnp.einsum("hqk,qhd->khd", d_scores, query_heads, preferred_element_type=jnp.float32)
            * score_scale,
        )

    def delta_step(total, block_index):

        def delta_active(running):
            part, grad_block = delta_terms(block_index)
            return (running + part, grad_block)

        return lax.cond(
            needed(block_index), delta_active, lambda running: (running, zero_block), total
        )

    row_delta, grad_values = lax.scan(delta_step, jnp.zeros((H, rows_dev), jnp.float32), block_list)

    def query_step(total, block_index):

        def query_active(running):
            part, grad_block = query_terms(block_index, row_delta)
            return (running + part, grad_block)

        return lax.cond(
            needed(block_index), query_active, lambda running: (running, zero_block), total
        )

    d_query_sum, grad_keys = lax.scan(
        query_step, jnp.zeros((rows_dev, H, HD), jnp.float32), block_list
    )
    grad_keys = grad_keys.reshape(seq_length, model_width)
    grad_values = grad_values.reshape(seq_length, model_width)
    d_key_sum, d_value_sum = (
        lax.psum_scatter(
            grad_keys.astype(jnp.bfloat16), "exp", scatter_dimension=0, tiled=True
        ).astype(jnp.float32),
        lax.psum_scatter(
            grad_values.astype(jnp.bfloat16), "exp", scatter_dimension=0, tiled=True
        ).astype(jnp.float32),
    )
    d_query_low = d_query_sum.reshape(rows_dev, model_width).astype(jnp.bfloat16)
    d_key_low = d_key_sum.astype(jnp.bfloat16)
    d_value_low = d_value_sum.astype(jnp.bfloat16)
    d_attn_in = (
        jnp.einsum("te,de->td", d_query_low, full_query, preferred_element_type=jnp.float32)
        + jnp.einsum("te,de->td", d_key_low, full_key, preferred_element_type=jnp.float32)
        + jnp.einsum("te,de->td", d_value_low, full_value, preferred_element_type=jnp.float32)
    )
    grad_query_full = jnp.einsum(
        "td,te->de", attn_in, d_query_low, preferred_element_type=jnp.float32
    )
    grad_key_full = jnp.einsum("td,te->de", attn_in, d_key_low, preferred_element_type=jnp.float32)
    grad_value_full = jnp.einsum(
        "td,te->de", attn_in, d_value_low, preferred_element_type=jnp.float32
    )
    _, norm_attn_pull = jax.vjp(rms_scale, inputs_f, norm_attn)
    d_inputs_part, d_norm_attn = norm_attn_pull(d_attn_in)
    grad_tokens = (d_hidden + d_inputs_part).astype(jnp.bfloat16)
    attn_shards = (
        lax.psum_scatter(
            grad_query_full.astype(jnp.bfloat16), "fsdp", scatter_dimension=0, tiled=True
        ).astype(jnp.float32),
        lax.psum_scatter(
            grad_key_full.astype(jnp.bfloat16), "fsdp", scatter_dimension=0, tiled=True
        ).astype(jnp.float32),
        lax.psum_scatter(
            grad_value_full.astype(jnp.bfloat16), "fsdp", scatter_dimension=0, tiled=True
        ).astype(jnp.float32),
        lax.psum_scatter(
            grad_out_full.astype(jnp.bfloat16), "fsdp", scatter_dimension=0, tiled=True
        ).astype(jnp.float32),
    )
    attn_shards = (
        lax.psum(attn_shards[0].astype(jnp.bfloat16), "exp").astype(jnp.float32),
        lax.psum(attn_shards[1].astype(jnp.bfloat16), "exp").astype(jnp.float32),
        lax.psum(attn_shards[2].astype(jnp.bfloat16), "exp").astype(jnp.float32),
        lax.psum(attn_shards[3].astype(jnp.bfloat16), "exp").astype(jnp.float32),
    )
    expert_shards = (
        lax.psum_scatter(
            grad_gate_full.astype(jnp.bfloat16), "fsdp", scatter_dimension=0, tiled=True
        ).astype(jnp.float32),
        lax.psum_scatter(
            grad_up_full.astype(jnp.bfloat16), "fsdp", scatter_dimension=0, tiled=True
        ).astype(jnp.float32),
        lax.psum_scatter(
            grad_down_full.astype(jnp.bfloat16), "fsdp", scatter_dimension=0, tiled=True
        ).astype(jnp.float32),
    )
    small_sums = lax.psum(
        (d_norm_attn, d_norm_ffn, d_router, d_mixing, d_const_proj, d_const_vec), ("exp", "fsdp")
    )
    return (
        layer_out[None],
        grad_tokens[None],
        d_res_logits[None],
        small_sums[0],
        small_sums[1],
        attn_shards[0],
        attn_shards[1],
        attn_shards[2],
        attn_shards[3],
        small_sums[2],
        small_sums[3],
        small_sums[4],
        small_sums[5],
        expert_shards[0][None],
        expert_shards[1][None],
        expert_shards[2][None],
    )


MESH = pl.DeviceIdType.MESH
BF = jnp.bfloat16
F32 = jnp.float32
LN2 = math.log(2.0)
QSCALE = 1.0 / (LN2 * math.sqrt(HD))
CHUNKS = 4


class Place:
    def __init__(self):
        self.e = lax.axis_index("exp")
        self.f = lax.axis_index("fsdp")
        self.z = self.f // 2
        self.x = self.f % 2
        self.sib = self.e + 1 - 2 * (self.e % 2)
        self.yp = (self.e + 2) % 4
        self.diag = (self.sib + 2) % 4
        self.xf = self.f + 1 - 2 * self.x
        self.exp_peers = (self.sib, self.yp, self.diag)

    def zf(self, d):
        return ((self.z + d) % 4) * 2 + self.x

    def fp(self, r):
        return (self.f + r) % 8

    def far_first(self, j):
        return (self.e + (j % 2) * (1 - 2 * (self.e % 2)) + 2 * (1 - j // 2)) % 4

    def near_first(self, j):
        return (self.e + (j % 2) * (1 - 2 * (self.e % 2)) + 2 * (j // 2)) % 4

    def share_order(self, j):
        return (self.e + (1 - j % 2) * (1 - 2 * (self.e % 2)) + 2 * (1 - j // 2)) % 4

    def barrier(self):
        sem = pltpu.get_barrier_semaphore()
        for p in self.exp_peers:
            pl.semaphore_signal(sem, inc=1, device_id=(p, self.f), device_id_type=MESH)
        for r in range(1, 8):
            pl.semaphore_signal(sem, inc=1, device_id=(self.e, self.fp(r)), device_id_type=MESH)
        pl.semaphore_wait(sem, 10)

    def send(self, src, dst, ss, rs, e=None, f=None):
        return pltpu.make_async_remote_copy(
            src_ref=src,
            dst_ref=dst,
            send_sem=ss,
            recv_sem=rs,
            device_id=(self.e if e is None else e, self.f if f is None else f),
            device_id_type=MESH,
        )


def lane_of(shape):
    return lax.broadcasted_iota(jnp.int32, shape, len(shape) - 1)


def row_of(shape):
    return lax.broadcasted_iota(jnp.int32, shape, 0)


def dot(a, b, ca=1, cb=0, precision=None):
    return lax.dot_general(a, b, (((ca,), (cb,)), ((), ())), precision=precision, preferred_element_type=F32)


def allowed_block(size, first):
    key, query = row_of((size, size)), lane_of((size, size))
    inside_k = (key >= first) & (key < first + PIECE)
    inside_q = (query >= first) & (query < first + PIECE)
    return (key <= query) | (inside_k & inside_q)


def k1_kernel(
    x_ref, u_ref, wq_ref, wk_ref, wv_ref, wo_ref, wg_ref, wu_ref, wd_ref, gres_ref, routes_ref, starts_ref,
    gain_a_ref, gain_f_ref, router_ref, proj_ref, mix_ref,
    attn_hbm, q_hbm, k_hbm, v_hbm, o_hbm, lse_s, hidden_ref, aux_ref, place_ref, ret_o, ret_d, wo_hbm, wq_hbm,
    grad_gate, grad_up, grad_down, far_gate, next_gate, near_gate, side_gate, far_up, side_up,
    attn_all, q_s, k_s, v_s, o_s, wo_full, wq_full,
    gate_full, up_full, down_full, wq_own, vt_s, attn_recv, nb, snd_r, snd_d, recv_r, recv_d, m_s, l_s, acc_s,
    acc, d_acc, st_gate, st_up, st_down,
    wq_ss, wq_rs, wo_ss, wo_rs, at_ss, at_rs, o_ss, o_rs, dr_ss, dr_rs, dd_ss, dd_rs, ro_ss, ro_rs, rd_ss, rd_rs,
    us, ur, ds, dr, xs, xr, vs, vr, wc_ss, wc_rs, loc, st_sem, fs, fr, keep_sem,
):
    me = Place()
    e, f, z, xf = me.e, me.f, me.z, me.xf
    T, D = x_ref.shape
    C = D // 4
    R = wo_ref.shape[0]
    FF = wg_ref.shape[1]
    W = FF // CHUNKS
    S = 4 * CAP
    for k in range(4):

        @pl.when(e == k)
        def _():
            for i, w in enumerate((wq_ref, wk_ref, wv_ref)):
                wq_own[:, i * C : (i + 1) * C] = w[:, k * C : (k + 1) * C]

    me.barrier()

    def half(core):
        return pl.ds(pl.multiple_of(core * (R // 2), 16), R // 2)

    def wq_slot(index):
        return wq_full.at[pl.ds(pl.multiple_of(index * R, 32), R)]

    def wo_slot(index):
        return wo_full.at[index, half(e % 2)]

    early = (
        (wq_own, wq_slot, wq_ss, wq_rs, 0),
        (wo_ref.at[half(e % 2)], wo_slot, wo_ss, wo_rs, 1),
    )
    for src, slot_of, ss, rs, li in early:
        for d in (1, 3, 2):
            me.send(src, slot_of(f), ss.at[d], rs.at[d], f=me.zf(d)).start()
        me.send(src, slot_of(f), ss.at[0], rs.at[0], f=xf).start()
        pltpu.make_async_copy(src, slot_of(f), loc.at[li]).start()

    xv = x_ref[...].astype(F32)
    inv = lax.rsqrt(jnp.mean(xv * xv, axis=-1, keepdims=True) + EPS)
    attn_all[e] = (xv * inv * gain_a_ref[...].reshape(1, D)).astype(BF)

    def at_copy(i, block, to=None):
        ref = attn_all.at[block]
        return me.send(ref, ref, at_ss.at[i], at_rs.at[i], e=to)

    at_copy(1, e, me.yp).start()
    at_copy(0, e, me.sib).start()

    def early_index(d, other):
        return ((z - d + 4) % 4) * 2 + (1 - me.x if other else me.x)

    def early_forward(src, slot_of, ss, rs, li):
        for d in (1, 3, 2):
            slot = slot_of(early_index(d, False))
            me.send(slot, slot, ss.at[d], rs.at[d]).wait_recv()
            me.send(slot, slot, ss.at[3 + d], rs.at[3 + d], f=xf).start()

    def early_wait(src, slot_of, ss, rs, li):
        pltpu.make_async_copy(src, slot_of(f), loc.at[li]).wait()
        me.send(slot_of(xf), slot_of(xf), ss.at[0], rs.at[0]).wait_recv()
        for d in (1, 2, 3):
            slot = slot_of(early_index(d, True))
            me.send(slot, slot, ss.at[3 + d], rs.at[3 + d]).wait_recv()

    def wo_copy(core, to=None):
        ref = wo_full.at[:, half(core)]
        return me.send(ref, ref, wc_ss.at[0], wc_rs.at[0], e=to)

    def cut(ref, c):
        return ref if c is None else ref.at[:, pl.ds(pl.multiple_of(c * W, W), W)]

    def up_copy(n, p, src, dst, to=None):
        return me.send(src, dst, us.at[n, p], ur.at[n, p], f=to)

    def down_copy(n, p, src, dst, to=None):
        return me.send(src, dst, ds.at[n, p], dr.at[n, p], f=to)

    def x_copy(n, i, src, dst, to=None):
        return me.send(src, dst, xs.at[n, i], xr.at[n, i], f=to)

    def relay(n, p, src, full, c):
        def at(slot):
            return cut(full.at[slot], c)

        if p == 0:
            own = cut(src, c)
            x_copy(n, 0, own, at(f), xf).start()

            @pl.when(z <= 2)
            def _():
                up_copy(n, 0, own, at(f), f + 2).start()

            @pl.when(z >= 1)
            def _():
                down_copy(n, 0, own, at(f), f - 2).start()

            return

        if p == 1 and c is None:
            x_copy(n, 0, at(xf), at(xf)).wait_recv()

            @pl.when(z <= 2)
            def _():
                side_copy(0, at(xf), at(xf), f + 2).start()

            @pl.when(z >= 1)
            def _():
                side_copy(1, at(xf), at(xf), f - 2).start()

        @pl.when(z >= p)
        def _():
            slot = at(f - 2 * p)
            up_copy(n, p - 1, slot, slot).wait_recv()
            if p <= 2:

                @pl.when(z <= 2)
                def _():
                    up_copy(n, p, slot, slot, f + 2).start()

            if p > 1 or c is not None:
                x_copy(n, p, slot, slot, xf).start()

        @pl.when(z + p <= 3)
        def _():
            slot = at(f + 2 * p)
            down_copy(n, p - 1, slot, slot).wait_recv()
            if p <= 2:

                @pl.when(z >= 1)
                def _():
                    down_copy(n, p, slot, slot, f - 2).start()

            if p > 1 or c is not None:
                x_copy(n, 3 + p, slot, slot, xf).start()

    def side_copy(i, src, dst, to=None):
        return me.send(src, dst, vs.at[i], vr.at[i], f=to)

    def relay_chunk(p, c):
        relay(1 + 2 * c, p, wg_ref, gate_full, c)
        relay(2 + 2 * c, p, wu_ref, up_full, c)

    def experts(p):
        relay(0, p, wd_ref, down_full, None)
        for c in range(CHUNKS):
            relay_chunk(p, c)

    own_loads = ((wd_ref, down_full), (wg_ref, gate_full), (wu_ref, up_full))

    def own_load(i):
        src, full = own_loads[i]
        return pltpu.make_async_copy(src, full.at[f], loc.at[2 + i])

    relay(0, 0, wd_ref, down_full, None)
    early_forward(*early[0])
    for c in range(CHUNKS):
        relay_chunk(0, c)
    for i in range(3):
        own_load(i).start()

    at_copy(1, me.yp).wait_recv()
    at_copy(2, me.yp, me.sib).start()
    at_copy(0, me.sib).wait_recv()
    early_wait(*early[0])
    early_forward(*early[1])
    at_copy(2, me.diag).wait_recv()

    kept = (
        (attn_all, attn_hbm), (wq_full, wq_hbm), (q_s, q_hbm), (k_s, k_hbm), (v_s, v_hbm), (wo_full, wo_hbm), (o_s, o_hbm),
    )

    def keep_copy(i):
        return pltpu.make_async_copy(kept[i][0], kept[i][1], keep_sem.at[i])

    keep_copy(0).start()
    keep_copy(1).start()

    def qkv_step(i, _):
        b = i // 2
        r = pl.ds(pl.multiple_of((i % 2) * 256, 256), 256)
        out = dot(attn_all[b, r, :], wq_full[...])
        q_s[b, r, :] = (out[:, 0:C] * QSCALE).astype(BF)
        k_s[b, r, :] = out[:, C : 2 * C].astype(BF)
        v = out[:, 2 * C : 3 * C]
        v_s[b, r, :] = v.astype(BF)
        vt_s[b, :, r] = v.T.astype(BF)
        return 0

    lax.fori_loop(0, 8, qkv_step, 0)
    for i in (2, 3, 4):
        keep_copy(i).start()

    head_of = lane_of((T, C)) // HD
    lse_s[...] = jnp.zeros_like(lse_s)

    def query_step(j, _):
        qb = me.far_first(j)
        queries = [jnp.where(head_of == h, q_s[qb], jnp.zeros((T, C), BF)) for h in range(3)]
        allowed = allowed_block(T, starts_ref[0, qb] - qb * T)
        for h in range(3):
            hr = pl.ds(h * HD, HD)
            s = jnp.where(allowed, dot(k_s[qb], queries[h], 1, 1), NEG)
            m = jnp.max(s, axis=0, keepdims=True)
            p = jnp.exp2(s - m)
            m_s[h : h + 1] = m
            l_s[h : h + 1] = jnp.sum(p, axis=0, keepdims=True)
            acc_s[hr] = dot(vt_s[qb, hr, :], p.astype(BF))

        def key_step(kb, _):
            for h in range(3):
                hr = pl.ds(h * HD, HD)
                query = jnp.where(head_of == h, q_s[qb], jnp.zeros((T, C), BF))
                s = dot(k_s[kb], query, 1, 1)
                m_old = m_s[h : h + 1]
                m = jnp.maximum(m_old, jnp.max(s, axis=0, keepdims=True))
                scale = jnp.exp2(m_old - m)
                p = jnp.exp2(s - m)
                m_s[h : h + 1] = m
                l_s[h : h + 1] = l_s[h : h + 1] * scale + jnp.sum(p, axis=0, keepdims=True)
                acc_s[hr] = acc_s[hr] * scale + dot(vt_s[kb, hr, :], p.astype(BF))
            return 0

        lax.fori_loop(0, qb, key_step, 0)
        for h in range(3):
            hr = pl.ds(h * HD, HD)
            total = l_s[h : h + 1]
            acc_s[hr] = acc_s[hr] / total
            lse_s[qb, h : h + 1, :] = m_s[h : h + 1] + jnp.log2(total)
        o_s[qb] = acc_s[...].T.astype(BF)
        return 0

    def o_copy(i, to=None):
        p = me.exp_peers[i]
        if to is None:
            return me.send(o_s.at[p], attn_recv.at[p], o_ss.at[i], o_rs.at[i])
        return me.send(o_s.at[p], attn_recv.at[e], o_ss.at[i], o_rs.at[i], e=p)

    lax.fori_loop(0, 2, query_step, 0)
    o_copy(1, True).start()
    o_copy(2, True).start()
    early_wait(*early[1])
    wo_copy(e % 2, me.sib).start()
    experts(1)
    lax.fori_loop(2, 4, query_step, 0)
    o_copy(0, True).start()
    attn_recv[e] = o_s[e]
    keep_copy(6).start()

    r0, r1 = routes_ref[0:1, :], routes_ref[1:2, :]
    expert = row_of((8, T))
    chosen = (expert == r0) | (expert == r1)
    earlier = (row_of((T, T)) < lane_of((T, T))).astype(BF)
    count = dot(chosen.astype(BF), earlier).astype(jnp.int32)
    count = jnp.where(chosen, count, -1)
    slot_id = row_of((CAP, T))
    for k in range(4):
        place_ref[k] = jnp.where(slot_id == count[k : k + 1, :], 1.0, 0.0).astype(BF)

    wo_copy(1 - e % 2).wait_recv()
    keep_copy(5).start()
    for i in (0, 1, 2):
        o_copy(i).wait_recv()

    def hidden_step(i, _):
        r = pl.ds(pl.multiple_of(i * 256, 256), 256)
        h = x_ref[r, :].astype(F32)
        for b in range(4):
            h = h + dot(attn_recv[b, r, :], wo_full[2 * b : 2 * b + 2].reshape(C, D))
        hidden_ref[r, :] = h
        n = h * lax.rsqrt(jnp.mean(h * h, axis=-1, keepdims=True) + EPS) * gain_f_ref[...].reshape(1, D)
        nb[r, :] = n.astype(BF)
        aux_ref[0:8, r] = dot(router_ref[...], n, 1, 1, HIGH) + dot(mix_ref[...], gres_ref[:, r], 0, 0, HIGH)
        aux_ref[8:12, r] = dot(proj_ref[...], n, 1, 1, HIGH)
        return 0

    relay(0, 2, wd_ref, down_full, None)
    lax.fori_loop(0, 2, hidden_step, 0)
    relay_chunk(2, 0)
    relay_chunk(2, 1)

    logits = aux_ref[0:8, :]
    top = jnp.max(jnp.where(chosen, logits, NEG), axis=0, keepdims=True)
    weight = jnp.where(chosen, jnp.exp(logits - top), 0.0)
    gates = weight / jnp.sum(weight, axis=0, keepdims=True)
    pairs = aux_ref[8:12, :]
    other = jnp.concatenate([pairs[1:2], pairs[0:1], pairs[3:4], pairs[2:3]], axis=0)
    aux_ref[0:8, :] = gates
    aux_ref[8:12, :] = 1.0 / (1.0 + jnp.exp(other - pairs))
    aux_ref[12:16, :] = jnp.zeros((4, T), F32)

    def d_copy(i, ref, out, ss, rs, k, to=None):
        return me.send(ref.at[k], out.at[e if to is not None else k], ss.at[i], rs.at[i], e=to)

    def dispatch_step(j, _):
        k = me.far_first(j)
        i = (j + 1) % 4
        place = place_ref[k]
        snd_r[k] = dot(place, nb[...]).astype(BF)
        gate = aux_ref[pl.ds(k, 1), :]
        gated = jnp.where(place > 0, gate.astype(BF), jnp.zeros((CAP, T), BF))
        snd_d[k] = dot(gated, u_ref[...]).astype(BF)

        @pl.when(j != 2)
        def _():
            d_copy(i, snd_r, recv_r, dr_ss, dr_rs, k, k).start()
            d_copy(i, snd_d, recv_d, dd_ss, dd_rs, k, k).start()

        @pl.when(j == 2)
        def _():
            recv_r[k] = snd_r[k]
            recv_d[k] = snd_d[k]

        return 0

    lax.fori_loop(0, 4, dispatch_step, 0)
    relay_chunk(2, 2)
    relay_chunk(2, 3)
    relay(0, 3, wd_ref, down_full, None)
    relay_chunk(3, 0)
    for i, p in enumerate(me.exp_peers):
        d_copy(i, snd_r, recv_r, dr_ss, dr_rs, p).wait()
        d_copy(i, snd_d, recv_d, dd_ss, dd_rs, p).wait()

    partner = z + 1 - 2 * (z % 2)
    far_row = 2 * ((partner + 2) % 4) + 1 - me.x
    next_row = 2 * ((z + 2) % 4) + 1 - me.x
    side_row = 2 * partner + 1 - me.x
    near_row = 2 * partner + me.x
    first = (
        (grad_gate, far_row, far_gate, xf),
        (grad_gate, side_row, side_gate, near_row),
        (grad_up, far_row, far_up, xf),
        (grad_up, side_row, side_up, near_row),
        (grad_gate, next_row, next_gate, xf),
        (grad_gate, near_row, near_gate, near_row),
    )

    def first_copy(i, c, to=None):
        src, row, dst, _ = first[i]
        return me.send(cut(src.at[row], c), cut(dst, c), fs.at[i, c], fr.at[i, c], f=to)

    def first_send(c):
        for i in range(6):
            first_copy(i, c, first[i][3]).start()

    acc[...] = jnp.zeros_like(acc)
    d_acc[...] = jnp.zeros_like(d_acc)

    def unit_wait(n, full, c):
        def at(slot):
            return cut(full.at[slot], c)

        if c is None:

            @pl.when(z >= 1)
            def _():
                side_copy(0, at(xf - 2), at(xf - 2)).wait_recv()

            @pl.when(z <= 2)
            def _():
                side_copy(1, at(xf + 2), at(xf + 2)).wait_recv()

        else:
            x_copy(n, 0, at(xf), at(xf)).wait_recv()
        for p in (2, 3) if c is None else (1, 2, 3):

            @pl.when(z >= p)
            def _():
                x_copy(n, p, at(xf - 2 * p), at(xf - 2 * p)).wait_recv()

            @pl.when(z + p <= 3)
            def _():
                x_copy(n, 3 + p, at(xf + 2 * p), at(xf + 2 * p)).wait_recv()

    stages = ((st_gate, grad_gate, 0), (st_up, grad_up, 1), (st_down, grad_down, 2))

    def stage_copy(c, i):
        st, out, _ = stages[i]
        if i == 2:
            dst = out.at[pl.ds(2 * c, 2)]
        else:
            dst = out.at[:, :, pl.ds(pl.multiple_of(c * W, W), W)]
        return pltpu.make_async_copy(st, dst, st_sem.at[i])

    def ret_copy(i, snd, ret, ss, rs, to=None):
        p = me.exp_peers[i]
        return me.send(snd.at[p], ret.at[e if to else p], ss.at[i], rs.at[i], e=p if to else None)

    def expert_step(c, _):
        @pl.when(c < CHUNKS - 1)
        def _():
            relay_chunk(3, c + 1)

        @pl.when(c == 0)
        def _():
            for i in range(3):
                own_load(i).wait()
            unit_wait(0, down_full, None)

        unit_wait(1 + 2 * c, gate_full, c)
        unit_wait(2 + 2 * c, up_full, c)
        w = pl.ds(pl.multiple_of(c * W, W), W)
        row_in = recv_r[...].reshape(S, D)
        d_in = recv_d[...].reshape(S, D)
        w_gate = gate_full[:, :, w].reshape(D, W)
        w_up = up_full[:, :, w].reshape(D, W)
        w_down = down_full[pl.ds(2 * c, 2)].reshape(W, D)
        g = dot(row_in, w_gate)
        up = dot(row_in, w_up)
        sig = 1.0 / (1.0 + jnp.exp(-g))
        silu = g * sig
        inner = (silu * up).astype(BF)
        acc[...] += dot(inner, w_down)

        @pl.when(c == CHUNKS - 1)
        def _():
            snd_r[...] = acc[...].astype(BF).reshape(4, CAP, D)
            for i in (1, 2, 0):
                ret_copy(i, snd_r, ret_o, ro_ss, ro_rs, True).start()
            ret_o[e] = snd_r[e]

        d_inner = dot(d_in, w_down, 1, 1)
        d_up = (d_inner * silu).astype(BF)
        d_gate = (d_inner * up * (sig + silu * (1.0 - sig))).astype(BF)
        d_acc[...] += dot(d_gate, w_gate, 1, 1) + dot(d_up, w_up, 1, 1)

        @pl.when(c == CHUNKS - 1)
        def _():
            snd_d[...] = d_acc[...].astype(BF).reshape(4, CAP, D)
            for i in (1, 2, 0):
                ret_copy(i, snd_d, ret_d, rd_ss, rd_rs, True).start()
            ret_d[e] = snd_d[e]

        @pl.when(c > 0)
        def _():
            for i in range(3):
                stage_copy(c - 1, i).wait()
            first_send(c - 1)

        st_down[...] = dot(inner, d_in, 0, 0).astype(BF).reshape(2, W // 2, D)
        st_gate[...] = dot(row_in, d_gate, 0, 0).astype(BF).reshape(8, R, W)
        st_up[...] = dot(row_in, d_up, 0, 0).astype(BF).reshape(8, R, W)
        for i in range(3):
            stage_copy(c, i).start()
        return 0

    lax.fori_loop(0, CHUNKS, expert_step, 0)
    for i in range(3):
        stage_copy(CHUNKS - 1, i).wait()
    first_send(CHUNKS - 1)

    for src, slot_of, ss, rs, li in early:
        for j in range(7):
            me.send(slot_of(f), slot_of(f), ss.at[j], rs.at[j]).wait_send()
    wo_copy(e % 2).wait_send()
    for i in range(3):
        at_copy(i, e).wait_send()
        o_copy(i).wait_send()
    def relay_end(n, full, c):
        slot = cut(full.at[f], c)
        x_copy(n, 0, slot, slot).wait_send()

        @pl.when(z <= 2)
        def _():
            up_copy(n, 0, slot, slot).wait_send()
            if c is None:
                side_copy(0, slot, slot).wait_send()

        @pl.when(z >= 1)
        def _():
            down_copy(n, 0, slot, slot).wait_send()
            if c is None:
                side_copy(1, slot, slot).wait_send()

        for p in (1, 2, 3):

            @pl.when(z >= p)
            def _():
                if p <= 2:

                    @pl.when(z <= 2)
                    def _():
                        up_copy(n, p, slot, slot).wait_send()

                if p > 1 or c is not None:
                    x_copy(n, p, slot, slot).wait_send()

            @pl.when(z + p <= 3)
            def _():
                if p <= 2:

                    @pl.when(z >= 1)
                    def _():
                        down_copy(n, p, slot, slot).wait_send()

                if p > 1 or c is not None:
                    x_copy(n, 3 + p, slot, slot).wait_send()

    relay_end(0, down_full, None)

    def end_step(c, _):
        relay_end(1 + 2 * c, gate_full, c)
        relay_end(2 + 2 * c, up_full, c)
        return 0

    lax.fori_loop(0, CHUNKS, end_step, 0)
    for i in range(3):
        ret_copy(i, snd_r, ret_o, ro_ss, ro_rs).wait()
        ret_copy(i, snd_d, ret_d, rd_ss, rd_rs).wait()

    def first_end(c, _):
        for i in range(6):
            first_copy(i, c).wait()
        return 0

    lax.fori_loop(0, CHUNKS, first_end, 0)
    for i in range(7):
        keep_copy(i).wait()


def sds(shape, dtype):
    return jax.ShapeDtypeStruct(shape, dtype)


def vmem():
    return pl.BlockSpec(memory_space=pltpu.VMEM)


def anyspace():
    return pl.BlockSpec(memory_space=pl.ANY)


def smem():
    return pl.BlockSpec(memory_space=pltpu.SMEM)


def call_k1(x, u, wq, wk, wv, wo, wg, wu, wd, gres, routes, starts, gain_a, gain_f, router, proj, mix):
    T, D = x.shape
    C, R, FF, S = D // 4, D // 8, wg.shape[1], 4 * CAP
    n = 1 + 2 * CHUNKS
    dma = pltpu.SemaphoreType.DMA
    VM = pltpu.VMEM
    block = VM((4, CAP, D), BF)
    return pl.pallas_call(
        k1_kernel,
        name="forward",
        out_shape=(
            sds((4, T, D), BF), sds((4, T, C), BF), sds((4, T, C), BF), sds((4, T, C), BF), sds((4, T, C), BF),
            sds((4, 8, T), F32), sds((T, D), F32), sds((16, T), F32), sds((4, CAP, T), BF),
            sds((4, CAP, D), BF), sds((4, CAP, D), BF), sds((8, R, D), BF), sds((D, 3 * C), BF),
            sds((8, R, FF), BF), sds((8, R, FF), BF), sds((8, FF // 8, D), BF),
            sds((R, FF), BF), sds((R, FF), BF), sds((R, FF), BF), sds((R, FF), BF), sds((R, FF), BF), sds((R, FF), BF),
        ),
        in_specs=[vmem()] * 5 + [anyspace()] * 4 + [vmem()] * 2 + [smem()] + [vmem()] * 5,
        out_specs=tuple([anyspace()] * 5 + [vmem()] * 6 + [anyspace()] * 11),
        scratch_shapes=[
            VM((4, T, D), BF), VM((4, T, C), BF), VM((4, T, C), BF), VM((4, T, C), BF), VM((4, T, C), BF), VM((8, R, D), BF), VM((D, 3 * C), BF),
            VM((8, R, FF), BF), VM((8, R, FF), BF), VM((8, FF // 8, D), BF), VM((R, 3 * C), BF), VM((4, C, T), BF),
            VM((4, T, C), BF), VM((T, D), BF), block, block, block, block, VM((8, T), F32), VM((8, T), F32), VM((C, T), F32),
            VM((S, D), F32), VM((S, D), F32), VM((8, R, FF // CHUNKS), BF), VM((8, R, FF // CHUNKS), BF), VM((2, FF // 8, D), BF),
            dma((7,)), dma((7,)), dma((7,)), dma((7,)),
        ] + [dma((3,))] * 12 + [
            dma((n, 3)), dma((n, 3)), dma((n, 3)), dma((n, 3)), dma((n, 7)), dma((n, 7)),
            dma((2,)), dma((2,)), dma((1,)), dma((1,)), dma((5,)), dma((3,)), dma((6, CHUNKS)), dma((6, CHUNKS)), dma((7,)),
        ],
        compiler_params=pltpu.CompilerParams(collective_id=0, has_side_effects=True, vmem_limit_bytes=60 << 20),
    )(x, u, wq, wk, wv, wo, wg, wu, wd, gres, routes, starts, gain_a, gain_f, router, proj, mix)


def k2_kernel(
    ret_o, ret_d, hidden, u_ref, x_ref, aux_ref, place_ref, gres_ref,
    attn_hbm, q_hbm, k_hbm, v_hbm, o_hbm, lse_s, wo_hbm, wqkv_hbm, gain_a_ref, gain_f_ref, router_ref, proj_ref, mix_ref, cvec_ref, starts_ref,
    g_gate, g_up, g_down, far_gate, next_gate, near_gate, side_gate, far_up, side_up,
    layer_out, grad_tokens, d_res, small_out, ag_out, go_b, eg_out, eu_out, ed_out,
    xin_g, xin_u, xin_d, own_g, own_u, own_d, zin_g, zin_u, zin_d, cross_g, cross_u, cross_d,
    attn_all, q_s, k_s, v_s, o_s, wo, wqkv,
    dh_all, da, kt_s, dq, dk, dv, dqt, pin, py_in, d_hidden, wk_s, del_r, gt, go_acc, ag_s, bx_in, bz_in, ag_fin, go_s, go_in,
    small, sm1, sm2,
    load_sem, late_sem, xs, xr, zs, zr, own_sem, dh_ss, dh_rs, fw_ss, fw_rs, go_ss, go_rs, gb_ss, gb_rs, pd_ss, pd_rs, bx_ss, bx_rs, bz_ss, bz_rs,
    ab_ss, ab_rs, s1_ss, s1_rs, s2_ss, s2_rs,
):
    me = Place()
    e, f, z, x, xf = me.e, me.f, me.z, me.x, me.xf
    T, D = x_ref.shape
    C = D // 4
    R = D // 8
    M = 128

    partner = z + 1 - 2 * (z % 2)
    targets = ((partner + 2) % 4, (z + 2) % 4, z, partner)
    parts = (
        (g_gate, xin_g, own_g, zin_g, cross_g, eg_out),
        (g_up, xin_u, own_u, zin_u, cross_u, eu_out),
        (g_down, xin_d, own_d, zin_d, cross_d, ed_out),
    )

    def load_copy(i):
        src, dst = (
            (far_gate, xin_g.at[0]), (far_up, xin_u.at[0]), (next_gate, xin_g.at[1]),
            (side_gate, cross_g), (side_up, cross_u), (near_gate, zin_g.at[2]),
        )[i]
        return pltpu.make_async_copy(src, dst, load_sem.at[i])

    def own_copy(w, i, column):
        return pltpu.make_async_copy(parts[w][0].at[2 * targets[i] + column], parts[w][2], own_sem.at[w])

    def x_copy(w, i):
        src = parts[w][4] if i == 2 and w < 2 else parts[w][0].at[2 * targets[i] + 1 - x]
        dst = parts[w][4] if i == 3 else parts[w][1].at[i]
        return me.send(src, dst, xs.at[w, i], xr.at[w, i], f=xf)

    def z_copy(w, i):
        if i == 2:
            src = parts[w][0].at[2 * partner + x] if w < 2 else parts[w][4]
        else:
            src = parts[w][1].at[i]
        to = targets[1] if i == 1 else partner
        return me.send(src, parts[w][3].at[i], zs.at[w, i], zr.at[w, i], f=2 * to + x)

    def add(dst, *terms):
        total = dst.astype(F32)
        for term in terms:
            total = total + term.astype(F32)
        return total.astype(BF)

    def rs_far(w):
        xin, own = parts[w][1:3]
        if w == 2:
            x_copy(w, 0).wait_recv()
        else:
            load_copy(w).wait()
        own_copy(w, 0, x).wait()
        xin[0] = add(xin[0], own[...])
        z_copy(w, 0).start()
        own_copy(w, 1, x).start()

    def rs_cross(w):
        xin, own, zin = parts[w][1:4]
        if w:
            x_copy(w, 1).wait_recv()
        else:
            load_copy(2).wait()
        own_copy(w, 1, x).wait()
        z_copy(w, 0).wait_recv()
        xin[1] = add(xin[1], own[...], zin[0])
        z_copy(w, 1).start()
        if w < 2:
            own_copy(w, 2, 1 - x).start()
        else:
            own_copy(w, 3, x).start()

    def rs_side(w):
        own, cross = parts[w][2], parts[w][4]
        if w < 2:
            load_copy(3 + w).wait()
            own_copy(w, 2, 1 - x).wait()
        else:
            x_copy(w, 3).wait_recv()
            own_copy(w, 3, x).wait()
        cross[...] = add(cross[...], own[...])
        if w:
            z_copy(w, 2).start()
        own_copy(w, 2, x).start()

    def rs_end(w):
        xin, own, zin = parts[w][1:4]
        x_copy(w, 2).wait_recv()
        own_copy(w, 2, x).wait()
        z_copy(w, 1).wait_recv()
        if w:
            z_copy(w, 2).wait_recv()
        else:
            load_copy(5).wait()
        parts[w][5][...] = add(xin[2], own[...], zin[1], zin[2])

    for i in range(6):
        load_copy(i).start()
    for w in range(3):
        own_copy(w, 0, x).start()
    late = ((attn_hbm, attn_all), (q_hbm, q_s), (k_hbm, k_s), (v_hbm, v_s), (o_hbm, o_s), (wo_hbm, wo), (wqkv_hbm, wqkv))

    def late_copy(i):
        return pltpu.make_async_copy(late[i][0], late[i][1], late_sem.at[i])

    for i in (5, 2, 4, 1, 3, 6, 0):
        late_copy(i).start()
    me.barrier()
    for w, i in ((2, 0), (1, 1), (2, 1)):
        x_copy(w, i).start()
    rs_far(0)
    rs_far(1)

    small[...] = jnp.zeros_like(small)
    cv0, cv1 = cvec_ref[0:1, :], cvec_ref[1:2, :]
    maps = jnp.concatenate([router_ref[...], proj_ref[...], jnp.zeros((4, D), F32)], axis=0).astype(BF)
    lane8 = lane_of((M, 8))
    lane4 = lane_of((M, 4))

    def dh_copy(i, c, block, to=None):
        ref = dh_all.at[block, pl.ds(pl.multiple_of(c * M, M), M)]
        return me.send(ref, ref, dh_ss.at[i, c], dh_rs.at[i, c], e=to)

    def mix_step(c, _):
        r = pl.ds(pl.multiple_of(c * M, M), M)
        h = hidden[r, :]
        u = u_ref[r, :].astype(F32)
        inv = lax.rsqrt(jnp.mean(h * h, axis=-1, keepdims=True) + EPS)
        hn = h * inv
        gain = gain_f_ref[...].reshape(1, D)
        n = hn * gain
        cols = aux_ref[:, r].T
        gates = cols[:, 0:8]
        a0, b0, a1, b1 = cols[:, 8:9], cols[:, 9:10], cols[:, 10:11], cols[:, 11:12]
        g5, g6, g7 = cols[:, 5:6], cols[:, 6:7], cols[:, 7:8]
        c_n = g5 + g6 * a0 + g7 * a1
        c0 = g6 * b0
        c1 = g7 * b1
        mixed = h + c_n * n + c0 * cv0 + c1 * cv1
        dg = jnp.zeros((M, 8), F32)
        dn = c_n * u
        for k in range(4):
            place = place_ref[k, :, r]
            rk = dot(place, ret_o[k], 0, 0)
            mixed = mixed + cols[:, k : k + 1] * rk
            dg = jnp.where(lane8 == k, jnp.sum(u * rk, axis=-1, keepdims=True), dg)
            dn = dn + dot(place, ret_d[k], 0, 0)
        layer_out[r, :] = mixed.astype(BF)
        un = jnp.sum(u * n, axis=-1, keepdims=True)
        uv0 = jnp.sum(u * cv0, axis=-1, keepdims=True)
        uv1 = jnp.sum(u * cv1, axis=-1, keepdims=True)
        dg = jnp.where(lane8 == 5, un, dg)
        dg = jnp.where(lane8 == 6, a0 * un + b0 * uv0, dg)
        dg = jnp.where(lane8 == 7, a1 * un + b1 * uv1, dg)
        dlog = gates * (dg - jnp.sum(gates * dg, axis=-1, keepdims=True))
        e0 = g6 * a0 * b0 * (un - uv0)
        e1 = g7 * a1 * b1 * (un - uv1)
        dpair = jnp.where(lane4 == 0, e0, jnp.where(lane4 == 1, -e0, jnp.where(lane4 == 2, e1, -e1)))
        dl = jnp.concatenate([dlog, dpair, c0, c1, jnp.zeros((M, 2), F32)], axis=1)
        low = dl.astype(BF)
        d_res[:, r] = dot(mix_ref[...], dlog, 1, 1, HIGH)
        dn = dn + dot(jnp.where(lane_of((M, 16)) < 12, low, jnp.zeros((M, 16), BF)), maps)
        by_n = dot(low, n.astype(BF), 0, 0)
        by_u = dot(low, u_ref[r, :], 0, 0)
        small[0:12, :] += by_n[0:12]
        small[12:14, :] += by_u[12:14]
        small[14:15, :] += jnp.sum(dn * hn, axis=0, keepdims=True)
        small[16:24, 0:8] += dot(gres_ref[:, r], dlog, 1, 0, HIGH)
        gd = dn * gain
        dh = u + inv * (gd - hn * jnp.mean(gd * hn, axis=-1, keepdims=True))
        d_hidden[r, :] = dh
        dh_all[e, r, :] = dh.astype(BF)
        dh_copy(1, c, e, me.yp).start()
        dh_copy(0, c, e, me.sib).start()
        return 0

    lax.fori_loop(0, T // M, mix_step, 0)
    rs_cross(0)
    for i in range(7):
        late_copy(i).wait()

    head_of = lane_of((T, C)) // HD
    heads = (row_of((8, C)) == lane_of((8, C)) // HD).astype(F32)
    wk_s[...] = wqkv[:, C : 2 * C]
    dk[...] = jnp.zeros_like(dk)
    dv[...] = jnp.zeros_like(dv)
    go_acc[...] = jnp.zeros_like(go_acc)
    for b in range(4):
        kt_s[b] = k_s[b].T

    def fw_copy(block, to=None):
        return me.send(dh_all.at[block], dh_all.at[block], fw_ss.at[0], fw_rs.at[0], e=to)

    def d_out_step(j, qb):
        @pl.when(j == 1)
        def _():
            for c in range(T // M):
                dh_copy(0, c, me.sib).wait_recv()

        @pl.when(j == 2)
        def _():
            for c in range(T // M):
                dh_copy(1, c, me.yp).wait_recv()
            fw_copy(me.yp, me.sib).start()

        @pl.when(j == 3)
        def _():
            fw_copy(me.diag).wait_recv()

        dhb = dh_all[qb]
        low = dot(dhb, wo[pl.ds(2 * e, 2)].reshape(C, D), 1, 1).astype(BF)
        da[qb] = low
        ob = o_s[qb]
        del_r[qb] = dot(heads, low.astype(F32) * ob.astype(F32), 1, 1, HIGH)
        go_acc[...] += dot(ob, dhb, 0, 0)

    def head_block(qb, h):
        hr = pl.ds(pl.multiple_of(h * HD, HD), HD)
        mine = head_of == h

        def block(kb, masked):
            zero = jnp.zeros((T, C), BF)
            query = jnp.where(mine, q_s[qb], zero)
            d_out = jnp.where(mine, da[qb], zero)
            p = jnp.exp2(dot(k_s[kb], query, 1, 1) - lse_s[qb, pl.ds(h, 1), :])
            if masked:
                p = jnp.where(allowed_block(T, starts_ref[0, qb] - qb * T), p, 0.0)
            dp = dot(v_s[kb], d_out, 1, 1)
            dsc = (p * (dp - del_r[qb, pl.ds(h, 1), :])).astype(BF)
            dv[kb] += dot(p.astype(BF), d_out)
            dk[kb] += dot(dsc, query)
            return dot(kt_s[kb, hr, :], dsc)

        dqt[...] = block(qb, True)

        def key_step(kb, _):
            dqt[...] += block(kb, False)
            return 0

        lax.fori_loop(0, qb, key_step, 0)
        dq[qb, hr, :] = (dqt[...] * (1.0 / math.sqrt(HD))).astype(BF)

    def near_step(i, _):
        j = i // 3
        qb = me.near_first(j)

        @pl.when(i % 3 == 0)
        def _():
            d_out_step(j, qb)

        head_block(qb, i % 3)
        return 0

    def far_pass(h):
        def far_step(j, _):
            qb = me.near_first(j)
            if h == 0:
                d_out_step(j, qb)
            head_block(qb, h)
            return 0

        lax.fori_loop(2, 4, far_step, 0)

    def bx_copy(h, to=None):
        return me.send(ag_s.at[1 - x, h], bx_in.at[h], bx_ss.at[h], bx_rs.at[h], f=to)

    def bz_copy(h, d, to=None):
        return me.send(bx_in.at[h, (z + d) % 4], bz_in.at[h, d - 1], bz_ss.at[h, d - 1], bz_rs.at[h, d - 1], f=to)

    def ab_copy(h, i, to=None):
        return me.send(ag_fin.at[h], ag_out.at[e if to is not None else me.exp_peers[i], h], ab_ss.at[h, i], ab_rs.at[h, i], e=to)

    def weight_grads(h):
        cols = slice(h * HD, (h + 1) * HD)
        gt[...] = jnp.zeros_like(gt)

        def grad_step(b, _):
            low_k = (dk[b, :, cols] * LN2).T.astype(BF)
            low_v = dv[b, :, cols].T.astype(BF)
            gt[...] += dot(jnp.concatenate([dq[b, cols, :], low_k, low_v], axis=0), attn_all[b])
            return 0

        lax.fori_loop(0, 4, grad_step, 0)
        grads = gt[...].T.astype(BF).reshape(8, R, C)
        for k in range(8):
            ag_s[k % 2, h, k // 2] = grads[k]
        bx_copy(h, xf).start()

    def weight_rows(h):
        bx_copy(h).wait_recv()
        bx_in[h] = add(bx_in[h], ag_s[x, h])
        for d in (2, 1, 3):
            bz_copy(h, d, me.zf(d)).start()

    def weight_sum(h):
        total = bx_in[h, z].astype(F32)
        for d in (1, 2, 3):
            bz_copy(h, d).wait_recv()
            total = total + bz_in[h, d - 1].astype(F32)
        ag_fin[h] = total.astype(BF)
        for i, p in enumerate(me.exp_peers):
            ab_copy(h, i, p).start()
        ag_out[e, h] = ag_fin[h]

    lax.fori_loop(0, 6, near_step, 0)
    rs_far(2)
    rs_cross(1)
    far_pass(0)

    go_s[0] = go_acc[0:R, :].astype(BF)
    go_s[1] = go_acc[R : 2 * R, :].astype(BF)
    for j in range(2):

        @pl.when(f != 2 * e + j)
        def _():
            me.send(go_s.at[j], go_in.at[f], go_ss.at[j], go_rs.at[f], f=2 * e + j).start()

    weight_grads(0)
    x_copy(2, 3).start()
    far_pass(1)
    weight_grads(1)
    x_copy(2, 2).start()
    weight_rows(0)
    rs_cross(2)
    rs_side(0)
    rs_side(1)
    far_pass(2)

    for c in range(T // M):
        dh_copy(0, c, e).wait_send()
        dh_copy(1, c, e).wait_send()
    fw_copy(e).wait_send()

    def share_step(j, _):
        b = me.share_order(j)
        out = dot(dq[b], wqkv[:, 0:C], 0, 1)
        out = out + dot((dk[b] * LN2).astype(BF), wk_s[...], 1, 1)
        out = out + dot(dv[b].astype(BF), wqkv[:, 2 * C : 3 * C], 1, 1)
        small[15:16, :] += jnp.sum(out * attn_all[b].astype(F32), axis=0, keepdims=True)
        dh_all[b] = out.astype(BF)
        return 0

    def pd_copy(i, src, dst, to=None):
        return me.send(src, dst, pd_ss.at[i], pd_rs.at[i], e=to)

    lax.fori_loop(0, 1, share_step, 0)
    pd_copy(1, dh_all.at[me.diag], pin.at[1], me.sib).start()
    lax.fori_loop(1, 2, share_step, 0)
    pd_copy(1, pin.at[1], pin.at[1]).wait_recv()
    dh_all[me.yp] = add(dh_all[me.yp], pin[1])
    pd_copy(2, dh_all.at[me.yp], py_in, me.yp).start()
    weight_grads(2)
    x_copy(0, 2).start()
    x_copy(1, 2).start()
    lax.fori_loop(2, 3, share_step, 0)
    pd_copy(0, dh_all.at[me.sib], pin.at[0], me.sib).start()
    lax.fori_loop(3, 4, share_step, 0)

    small[15:16, :] = small[15:16, :] / gain_a_ref[...].reshape(1, D)
    sm1[e] = small[...].astype(BF)
    for i, p in enumerate(me.exp_peers):
        me.send(sm1.at[e], sm1.at[e], s1_ss.at[i], s1_rs.at[i], e=p).start()
    weight_rows(1)
    rs_side(2)
    weight_sum(0)
    weight_rows(2)
    for i, p in enumerate(me.exp_peers):
        me.send(sm1.at[p], sm1.at[p], s1_ss.at[i], s1_rs.at[i]).wait()
    sm2[f] = add(sm1[0], sm1[1], sm1[2], sm1[3])
    for r in range(1, 8):
        me.send(sm2.at[f], sm2.at[f], s2_ss.at[r - 1], s2_rs.at[f], f=me.fp(r)).start()

    @pl.when(z == e)
    def _():
        total = go_s[x].astype(F32)
        for r in range(1, 8):
            s = go_in.at[me.fp(r)]
            me.send(s, s, go_ss.at[0], go_rs.at[me.fp(r)]).wait_recv()
            total = total + go_in[me.fp(r)].astype(F32)
        go_b[...] = total.astype(BF)
        for i, p in enumerate(me.exp_peers):
            me.send(go_b, go_b, gb_ss.at[i], gb_rs.at[0], e=p).start()

    weight_sum(1)
    weight_sum(2)
    for r in range(1, 8):
        s = sm2.at[me.fp(r)]
        me.send(s, s, s2_ss.at[r - 1], s2_rs.at[me.fp(r)]).wait_recv()
    total = sm2[0].astype(F32)
    for r in range(1, 8):
        total = total + sm2[r].astype(F32)
    small_out[...] = total

    pd_copy(0, pin.at[0], pin.at[0]).wait_recv()
    pd_copy(2, py_in, py_in).wait_recv()

    def token_step(i, _):
        r = pl.ds(pl.multiple_of(i * 256, 256), 256)
        d = dh_all[e, r, :].astype(F32) + pin[0, r, :].astype(F32) + py_in[r, :].astype(F32)
        xv = x_ref[r, :].astype(F32)
        inv = lax.rsqrt(jnp.mean(xv * xv, axis=-1, keepdims=True) + EPS)
        xn = xv * inv
        gd = d * gain_a_ref[...].reshape(1, D)
        grad_tokens[r, :] = (d_hidden[r, :] + inv * (gd - xn * jnp.mean(gd * xn, axis=-1, keepdims=True))).astype(BF)
        return 0

    lax.fori_loop(0, 2, token_step, 0)
    for w in range(3):
        rs_end(w)

    @pl.when(z != e)
    def _():
        me.send(go_b, go_b, gb_ss.at[0], gb_rs.at[0]).wait_recv()

    for w in range(3):
        for i in range(3):
            if (w, i) not in ((0, 0), (0, 1), (1, 0)):
                x_copy(w, i).wait_send()
            if (w, i) != (0, 2):
                z_copy(w, i).wait_send()
    x_copy(2, 3).wait_send()
    for j in range(2):

        @pl.when(f != 2 * e + j)
        def _():
            me.send(go_s.at[j], go_in.at[f], go_ss.at[j], go_rs.at[f]).wait_send()

    @pl.when(z == e)
    def _():
        for i in range(3):
            me.send(go_b, go_b, gb_ss.at[i], gb_rs.at[0]).wait_send()

    for i in range(3):
        pd_copy(i, py_in, py_in).wait_send()
        for h in range(3):
            ab_copy(h, i).wait()
    for h in range(3):
        bx_copy(h).wait_send()
        for d in (1, 2, 3):
            bz_copy(h, d).wait_send()
    for r in range(1, 8):
        me.send(sm2.at[f], sm2.at[f], s2_ss.at[r - 1], s2_rs.at[f]).wait_send()


def call_k2(*args):
    x, (gg, gu, gd) = args[4], args[23:26]
    late = args[8:13] + args[14:16]
    T, D = x.shape
    C, R = D // 4, D // 8
    dma = pltpu.SemaphoreType.DMA
    VM = pltpu.VMEM
    shapes = (gg.shape[1:], gu.shape[1:], gd.shape[1:])
    return pl.pallas_call(
        k2_kernel,
        name="backward",
        out_shape=(
            sds((T, D), BF), sds((T, D), BF), sds((8, T), F32), sds((24, D), F32),
            sds((4, 3, R, C), BF), sds((R, D), BF),
        ) + tuple(sds(s, BF) for s in shapes),
        in_specs=[vmem()] * 8 + [anyspace()] * 5 + [vmem()] + [anyspace()] * 2 + [vmem()] * 6 + [smem()] + [anyspace()] * 9,
        out_specs=tuple([vmem()] * 9),
        scratch_shapes=[VM((3,) + s, BF) for s in shapes] + [VM(s, BF) for s in shapes] + [VM((3,) + s, BF) for s in shapes] + [VM(s, BF) for s in shapes] + [VM(a.shape, BF) for a in late] + [
            VM((4, T, D), BF), VM((4, T, C), BF), VM((4, C, T), BF), VM((4, C, T), BF), VM((4, T, C), F32), VM((4, T, C), F32),
            VM((HD, T), F32), VM((2, T, D), BF), VM((T, D), BF), VM((T, D), F32), VM((D, C), BF), VM((4, 8, T), F32), VM((C, D), F32), VM((C, D), F32),
            VM((2, 3, 4, R, C), BF), VM((3, 4, R, C), BF), VM((3, 3, R, C), BF), VM((3, R, C), BF), VM((2, R, D), BF), VM((8, R, D), BF),
            VM((24, D), F32), VM((4, 24, D), BF), VM((8, 24, D), BF),
            dma((6,)), dma((7,)), dma((3, 4)), dma((3, 4)), dma((3, 3)), dma((3, 3)), dma((3,)),
            dma((2, 4)), dma((2, 4)), dma((1,)), dma((1,)), dma((2,)), dma((8,)), dma((3,)), dma((1,)), dma((3,)), dma((3,)),
            dma((3,)), dma((3,)), dma((3, 3)), dma((3, 3)), dma((3, 3)), dma((3, 3)), dma((3,)), dma((3,)), dma((7,)), dma((8,)),
        ],
        compiler_params=pltpu.CompilerParams(collective_id=1, has_side_effects=True, vmem_limit_bytes=63 << 20),
    )(*args)


def k3_kernel(
    layer_in, tokens_in, eg, eu, ed, res_in, small, ag, go,
    layer_out, tokens_out, o_gate, o_up, o_down, res_out, norm_a, norm_f, g_q, g_k, g_v, g_o, router, mixing, proj, cvec,
    layer_s, tokens_s, eg_s, eu_s, ed_s, gate_s, up_s, down_s, in_sem, out_sem,
):
    loads = ((layer_in, layer_s), (tokens_in, tokens_s), (eg, eg_s), (eu, eu_s), (ed, ed_s))
    stores = ((layer_s, layer_out), (tokens_s, tokens_out), (gate_s, o_gate), (up_s, o_up), (down_s, o_down))

    def load(i):
        return pltpu.make_async_copy(loads[i][0], loads[i][1], in_sem.at[i])

    def store(i):
        return pltpu.make_async_copy(stores[i][0], stores[i][1], out_sem.at[i])

    order = (2, 3, 4, 0, 1)
    for i in order:
        load(i).start()
    for i in order:
        load(i).wait()
        if i >= 2:
            stores[i][0][...] = loads[i][1][...].astype(F32)
        store(i).start()
    res_out[...] = res_in[...]
    norm_a[...] = small[15, :]
    norm_f[...] = small[14, :]
    for i, out in enumerate((g_q, g_k, g_v)):
        out[...] = jnp.concatenate(
            [ag[b, h, :, i * HD : (i + 1) * HD].astype(F32) for b in range(4) for h in range(3)], axis=1
        )
    g_o[...] = go[...].astype(F32)
    router[...] = small[0:8, :]
    mixing[...] = small[16:24, 0:8]
    proj[...] = small[8:12, :]
    cvec[...] = small[12:14, :]
    for i in order:
        store(i).wait()


def call_k3(layer, tokens, res, small, ag, go, eg, eu, ed):
    T, D = layer.shape
    R = D // 8
    dma = pltpu.SemaphoreType.DMA
    VM = pltpu.VMEM
    experts = (eg, eu, ed)
    outs = pl.pallas_call(
        k3_kernel,
        name="finish",
        out_shape=(sds((T, D), BF), sds((T, D), BF)) + tuple(sds(a.shape, F32) for a in experts) + (
            sds((8, T), F32), sds((D,), F32), sds((D,), F32),
            sds((R, D), F32), sds((R, D), F32), sds((R, D), F32), sds((R, D), F32),
            sds((8, D), F32), sds((8, 8), F32), sds((4, D), F32), sds((2, D), F32),
        ),
        in_specs=[anyspace()] * 5 + [vmem()] * 4,
        out_specs=tuple([anyspace()] * 5 + [vmem()] * 11),
        scratch_shapes=[VM((T, D), BF), VM((T, D), BF)] + [VM(a.shape, BF) for a in experts] + [VM(a.shape, F32) for a in experts]
        + [dma((5,)), dma((5,))],
    )(layer, tokens, eg, eu, ed, res, small, ag, go)
    return outs[:2] + outs[5:] + outs[2:5]


def body_fast(
    tokens, gate_res, routes, piece_starts, norm_attn, norm_ffn, w_query, w_key, w_value, w_out, router, mixing,
    const_proj, const_vec, w_gate, w_up, w_down, cotangent,
):
    x, u = tokens[0], cotangent[0]
    gres, route_ids = gate_res[0].T, routes[0].T
    (attn_all, q, k, v, o, lse, hidden, aux, place, ret_o, ret_d, wo, wq, gg, gu, gd, fg, ng, eg1, sg, fu, su) = call_k1(
        x, u, w_query, w_key, w_value, w_out, w_gate[0], w_up[0], w_down[0], gres, route_ids, piece_starts,
        norm_attn, norm_ffn, router.T, const_proj.T, mixing,
    )
    outs = call_k2(
        ret_o, ret_d, hidden, u, x, aux, place, gres, attn_all, q, k, v, o, lse, wo, wq,
        norm_attn, norm_ffn, router.T, const_proj.T, mixing, const_vec, piece_starts, gg, gu, gd, fg, ng, eg1, sg, fu, su,
    )
    (layer_out, grad_tokens, d_res, norm_a, norm_f, g_q, g_k, g_v, g_o, g_router, g_mixing, g_proj, g_cvec, eg, eu, ed) = call_k3(*outs)
    return (
        layer_out[None], grad_tokens[None], d_res.T[None], norm_a, norm_f, g_q, g_k, g_v, g_o,
        g_router.T, g_mixing, g_proj.T, g_cvec, eg[None], eu[None], ed[None],
    )


def solution(mesh):
    placed = (
        P("fsdp", "exp", None),
        P("fsdp", "exp", None),
        P("fsdp", "exp", None),
        P("fsdp", None),
        P(),
        P(),
        P("fsdp", None),
        P("fsdp", None),
        P("fsdp", None),
        P("fsdp", None),
        P(),
        P(),
        P(),
        P(),
        P("exp", "fsdp", None),
        P("exp", "fsdp", None),
        P("exp", "fsdp", None),
        P("fsdp", "exp", None),
    )
    return jax.shard_map(
        body_fast if (mesh.shape['exp'], mesh.shape['fsdp']) == (4, 8) else body,
        mesh=mesh,
        in_specs=placed,
        out_specs=(
            P("fsdp", "exp", None),
            P("fsdp", "exp", None),
            P("fsdp", "exp", None),
            P(),
            P(),
            P("fsdp", None),
            P("fsdp", None),
            P("fsdp", None),
            P("fsdp", None),
            P(),
            P(),
            P(),
            P(),
            P("exp", "fsdp", None),
            P("exp", "fsdp", None),
            P("exp", "fsdp", None),
        ),
        check_vma=False,
    )
```
